32 devices in a mesh: seq: 4 (over z), fsdp: 8 (over y, x, core).
Axes of the slice: x: 2, y: 2, z: 4, core: 2. Of those that a mesh axis runs over, the one named last changes fastest.
Arguments:
- hidden_in: bfloat16 [16, 1024, 1024], P('fsdp', 'seq'), may hold values from -6 to 6
- document_labels: int32 [16, 1024], P('fsdp', 'seq'), may hold values from 0 to 2, never falling along the last dimension, each value on 1 to 512 neighbouring positions
- cotangent: bfloat16 [16, 1024, 1024], P('fsdp', 'seq'), may hold values from -6 to 6
- ln_gain: bfloat16 [1024], P(('seq', 'fsdp')), may hold values from 0.5 to 1.5
- ln_bias: bfloat16 [1024], P(('seq', 'fsdp')), may hold values from -1 to 1
- qkv_weight: bfloat16 [1024, 3072], P(('seq', 'fsdp')), may hold values from -0.1875 to 0.1875
- qkv_bias: bfloat16 [3072], P(('seq', 'fsdp')), may hold values from -1 to 1
- out_weight: bfloat16 [1024, 1024], P(('seq', 'fsdp')), may hold values from -1.5 to 1.5
- out_bias: bfloat16 [1024], P(('seq', 'fsdp')), may hold values from -1 to 1
- fc_in_weight: bfloat16 [1024, 4096], P(('seq', 'fsdp')), may hold values from -0.1875 to 0.1875
- fc_in_bias: bfloat16 [4096], P(('seq', 'fsdp')), may hold values from -1 to 1
- fc_out_weight: bfloat16 [4096, 1024], P(('seq', 'fsdp')), may hold values from -0.09375 to 0.09375
- fc_out_bias: bfloat16 [1024], P(('seq', 'fsdp')), may hold values from -1 to 1
Outputs:
- output: bfloat16 [16, 1024, 1024], P('fsdp', 'seq')
- input_grad: bfloat16 [16, 1024, 1024], P('fsdp', 'seq')
- ln_gain_grad: float32 [1024], P(('seq', 'fsdp'))
- ln_bias_grad: float32 [1024], P(('seq', 'fsdp'))
- qkv_weight_grad: float32 [1024, 3072], P(('seq', 'fsdp'))
- qkv_bias_grad: float32 [3072], P(('seq', 'fsdp'))
- out_weight_grad: float32 [1024, 1024], P(('seq', 'fsdp'))
- out_bias_grad: float32 [1024], P(('seq', 'fsdp'))
- fc_in_weight_grad: float32 [1024, 4096], P(('seq', 'fsdp'))
- fc_in_bias_grad: float32 [4096], P(('seq', 'fsdp'))
- fc_out_weight_grad: float32 [4096, 1024], P(('seq', 'fsdp'))
- fc_out_bias_grad: float32 [1024], P(('seq', 'fsdp'))
The draws below stay inside these ranges and needn't reach their ends.
Inputs may be any that keep to these rules, and one draw needn't show every extreme that they name: `document_labels`: along each sequence the numbers never fall; every document (a run of equal numbers) has 1 to 512 tokens, and one has exactly 512.
All inputs are finite; a program needn't handle non-finite values.
Results may differ from the reference program's by a relative error of at most 0.009.
Values may be sent and summed in bfloat16 or wider, within the bound.
No kernel may reach another device: no remote copies, remote signals or barrier semaphores. Data moves between devices by JAX's collectives and lax.ppermute only.
A program may use at most 256 MiB of HBM per device.

```python
import math
import jax
import jax.numpy as jnp
import numpy as np
from jax import lax

D = 1024
H = 16
HD = 64
FF = 4096
ROT = 16
LENGTH = 1024
SEQS = 16
DOCS = 3
DOC_MOST = 512


def steps_of(own_key, extent, cuts, least, top_value):
    def one(position, parts):
        steps = jax.random.uniform(jax.random.fold_in(jax.random.fold_in(own_key, 6), position), (parts,), jnp.float32, least / len(cuts), top_value / len(cuts))
        return jnp.repeat(jnp.exp(steps), extent[position] // parts).reshape((-1,) + (1,) * (len(extent) - position - 1))

    gain = one(*cuts[0])
    for cut in cuts[1:]:
        gain = gain * one(*cut)
    return gain


def length_profile(amount, total, reach, slope):
    weights = [(1 << 20) // math.isqrt(standing ** slope) + 1 for standing in range(2, amount + 1)]
    surplus, counts = total - reach - (amount - 1), [1] * (amount - 1)
    while surplus > 0:
        free = [i for i in range(amount - 1) if counts[i] < reach]
        pool, budget = sum([weights[i] for i in free]), surplus
        for i in free:
            extra = min(reach - counts[i], max(1, budget * weights[i] // pool), surplus)
            counts[i] = counts[i] + extra
            surplus = surplus - extra
    return np.array([reach] + counts)


def uneven_parts(key, number_of, total, most, skew):
    if number_of == 2:
        one = jax.random.randint(key, (), max(1, total - most), min(most, total - 1) + 1)
        return jnp.stack([one, total - one])
    tallies = jnp.asarray(length_profile(number_of, total, most, skew), jnp.int32)
    pairs = (number_of - 1) // 2
    giver, sink = tallies[1:1 + 2 * pairs:2], tallies[2:2 + 2 * pairs:2]
    room = jnp.minimum(giver - 1, most - sink)
    moved = jax.random.randint(jax.random.fold_in(key, 1), (pairs,), 0, 1 << 20) % (room + 1)
    tallies = tallies.at[1:1 + 2 * pairs:2].set(giver - moved).at[2:2 + 2 * pairs:2].set(sink + moved)
    return tallies[jax.random.permutation(jax.random.fold_in(key, 2), number_of)]


def noise(key, dims, scale, reach, split=(), held_as=jnp.bfloat16):
    drawn = jax.random.normal(key, dims, jnp.float32) * scale
    if len(split) > 0:
        drawn = steps_of(key, dims, split, -0.22, 0.18) * drawn
    return jnp.clip(drawn, min=-reach, max=reach).astype(held_as)


def setup_inputs(seed: int = 0) -> dict:
    streams_of = jax.random.split(jax.random.key(seed), 14)
    return {
        "hidden_in": noise(streams_of[0], (SEQS, LENGTH, D), 1.0, 6.0, ((0, 8), (1, 4))),
        "document_labels": jax.vmap(lambda own: jnp.searchsorted(jnp.cumsum(uneven_parts(own, DOCS, LENGTH, DOC_MOST, 2)), jnp.arange(LENGTH), side="right"))(jax.random.split(streams_of[1], SEQS)).reshape((SEQS, LENGTH)).astype(jnp.int32),
        "cotangent": noise(streams_of[2], (SEQS, LENGTH, D), 1.0, 6.0, ((0, 8), (1, 4))),
        "ln_gain": jnp.clip(1.0 + 0.1 * jax.random.normal(streams_of[3], (D,), jnp.float32), 0.5, 1.5).astype(jnp.bfloat16),
        "ln_bias": noise(streams_of[4], (D,), 0.2, 1.0, ((0, 32),)),
        "qkv_weight": noise(streams_of[5], (D, 3 * D), D ** -0.5, 0.1875, ((0, 32),)),
        "qkv_bias": noise(streams_of[6], (3 * D,), 0.2, 1.0, ((0, 32),)),
        "out_weight": noise(streams_of[7], (D, D), (D // 64) ** -0.5, 1.5, ((0, 32),)),
        "out_bias": noise(streams_of[8], (D,), 0.2, 1.0, ((0, 32),)),
        "fc_in_weight": noise(streams_of[9], (D, FF), D ** -0.5, 0.1875, ((0, 32),)),
        "fc_in_bias": noise(streams_of[10], (FF,), 0.2, 1.0, ((0, 32),)),
        "fc_out_weight": noise(streams_of[11], (FF, D), FF ** -0.5, 0.09375, ((0, 32),)),
        "fc_out_bias": noise(streams_of[12], (D,), 0.2, 1.0, ((0, 32),)),
    }


@jax.custom_vjp
def low(v):
    return lax.optimization_barrier(v.astype(jnp.bfloat16)).astype(jnp.float32)

@jax.custom_vjp
def low_back(v):
    return v

def low_keep(v):
    return (low(v), None)

def low_pass(kept, grad):
    return (grad,)

def back_keep(v):
    return (v, None)

def back_low(kept, grad):
    return (low(grad),)
low.defvjp(low_keep, low_pass)
low_back.defvjp(back_keep, back_low)

def rotate(values, cosine, sine_part):
    half_rot = ROT // 2
    first_part = values[..., :half_rot]
    second_part = values[..., half_rot:ROT]
    return jnp.concatenate([first_part * cosine - second_part * sine_part, second_part * cosine + first_part * sine_part, values[..., ROT:]], axis=-1)

def position_angles(segments):
    length = segments.shape[0]
    places = jnp.arange(length, dtype=jnp.int32)
    boundary = jnp.concatenate([jnp.ones((1,), dtype=jnp.bool_), segments[1:] != segments[:-1]])
    starts = lax.cummax(jnp.where(boundary, places, 0), axis=0)
    positions = (places - starts).astype(jnp.float32)
    inverse = 1.0 / 10000.0 ** (jnp.arange(0, ROT, 2, dtype=jnp.float32) / ROT)
    return positions[:, None] * inverse[None, :]

def make_mask(segments, first_row, block_rows):
    length = segments.shape[0]
    query_index = first_row + jnp.arange(block_rows, dtype=jnp.int32)
    key_index = jnp.arange(length, dtype=jnp.int32)
    query_segments = lax.dynamic_slice_in_dim(segments, first_row, block_rows, 0)
    return (key_index[None, :] <= query_index[:, None]) & (query_segments[:, None] == segments[None, :])

def block_forward(params, hidden, segments):
    norm_multiplier, norm_shift, w_qkv, b_qkv, w_out, b_out, w_in, b_in, w_fc, b_fc = params
    highest = lax.Precision.HIGHEST
    length = hidden.shape[0]
    average = lax.optimization_barrier(jnp.mean(hidden, axis=-1, keepdims=True))
    centered = hidden - average
    spread = lax.optimization_barrier(jnp.mean(centered * centered, axis=-1, keepdims=True))
    rescaled_rows = centered * lax.rsqrt(spread + 1e-05)
    normed = low(rescaled_rows * norm_multiplier + norm_shift)
    projected = low_back(jnp.dot(normed, w_qkv, precision=highest) + b_qkv)
    head_parts = projected.reshape(length, H, 3, HD)
    angles = position_angles(segments)
    cosine = jnp.cos(angles)[:, None, None, :]
    sine_part = jnp.sin(angles)[:, None, None, :]
    turned = jnp.concatenate([rotate(head_parts[:, :, :2], cosine, sine_part), head_parts[:, :, 2:]], axis=2)
    turned = low(low_back(turned))
    query_all = turned[:, :, 0]
    key_everywhere = turned[:, :, 1]
    value_all = turned[:, :, 2]
    block_rows = min(512, length)
    scale_factor = 1.0 / math.sqrt(HD)

    def attend(block_index):
        first_row = block_index * block_rows
        query_rows = lax.dynamic_slice_in_dim(query_all, first_row, block_rows, 0)
        scores = low_back(jnp.einsum('qhd,khd->hqk', query_rows, key_everywhere, precision=highest) * scale_factor)
        allowed = make_mask(segments, first_row, block_rows)
        probabilities = jax.nn.softmax(jnp.where(allowed[None], scores, -1e+30), axis=-1)
        return jnp.einsum('hqk,khd->qhd', low(probabilities), value_all, precision=highest)
    context = lax.map(jax.checkpoint(attend), jnp.arange(length // block_rows, dtype=jnp.int32))
    context = low(low_back(context.reshape(length, D)))
    attn_out = jnp.dot(context, w_out, precision=highest) + b_out
    hidden_pre = low_back(jnp.dot(normed, w_in, precision=highest) + b_in)
    activated = low(jax.nn.gelu(hidden_pre, approximate=False))
    mlp_out = jnp.dot(activated, w_fc, precision=highest) + b_fc
    return hidden + attn_out + mlp_out

def reference(hidden_in, document_labels, cotangent, ln_gain, ln_bias, qkv_weight, qkv_bias, out_weight, out_bias, fc_in_weight, fc_in_bias, fc_out_weight, fc_out_bias):
    params = tuple((member.astype(jnp.float32) for member in (ln_gain, ln_bias, qkv_weight, qkv_bias, out_weight, out_bias, fc_in_weight, fc_in_bias, fc_out_weight, fc_out_bias)))
    initial = tuple((jnp.zeros_like(member) for member in params))

    def one_sequence(totals, inputs):
        hidden, segments, grad_out = inputs

        def forward(weights, activations):
            return block_forward(weights, activations, segments)
        result, pullback = jax.vjp(forward, params, hidden.astype(jnp.float32))
        weight_grads, hidden_grad = pullback(grad_out.astype(jnp.float32))
        totals = tuple((left + right for left, right in zip(totals, weight_grads)))
        return (totals, (result.astype(jnp.bfloat16), hidden_grad.astype(jnp.bfloat16)))
    totals, (output, input_grad) = lax.scan(one_sequence, initial, (hidden_in, document_labels, cotangent))
    return (output, input_grad, totals[0], totals[1], totals[2], totals[3], totals[4], totals[5], totals[6], totals[7], totals[8], totals[9])
```

```python
from functools import partial
import math

import jax
import jax.numpy as jnp
import numpy as np
from jax import lax
from jax.experimental import pallas as pl
from jax.experimental.pallas import tpu as pltpu
from jax.sharding import PartitionSpec as P

D = 1024
H = 16
HD = 64
ROT = 16
GROUPS = 4
BF = jnp.bfloat16
F32 = jnp.float32


def dot(left, right):
    return jnp.dot(left, right, preferred_element_type=F32)


def outer_product(left, right):
    return lax.dot_general(left, right, (((0,), (0,)), ((), ())), preferred_element_type=F32)


def times_transposed(left, right):
    return lax.dot_general(left, right, (((1,), (1,)), ((), ())), preferred_element_type=F32)


def swap(value, axis, bit):
    return lax.ppermute(value, axis, [(i, i ^ bit) for i in range(lax.axis_size(axis))])


def shift(value, by):
    count = lax.axis_size("seq")
    return lax.ppermute(
        value, "seq", [(i, i + by) for i in range(count) if 0 <= i + by < count]
    )


def far_bits(count):
    bits = []
    while count > 1:
        count //= 2
        bits.append(count)
    return bits


class Clock:
    def __init__(self, token):
        self.token = token

    def gate(self, *values):
        return lax.optimization_barrier((values, self.token))[0]

    def tick(self, *values):
        self.token = lax.optimization_barrier((self.token, values))[0]


class Chips:
    def __init__(self):
        self.nz, self.nf = lax.axis_size("seq"), lax.axis_size("fsdp")
        self.per = self.nf // 2
        self.count = self.nz * self.per
        self.core = lax.axis_index("fsdp") % 2
        self.me = lax.axis_index("seq") * self.per + lax.axis_index("fsdp") // 2
        self.line = [bit * self.per for bit in far_bits(self.nz)]
        self.plane = list(reversed(far_bits(self.per)))
        self.cube = len(self.plane) == 2 and self.nz == 4
        far, near = self.line[0], self.line[-1]
        if self.cube:
            bx, by = self.plane
            a, b = [0, far], [near, near ^ far]

            def over(chips, to):
                return [chip ^ to for chip in chips]

            ax, yb = a + over(a, bx), b + over(b, by)
            self.pieces = [ax, yb, over(ax, by), over(yb, bx)]
        else:
            order = [0]
            for bit in self.line + self.plane:
                order = order + [chip ^ bit for chip in order]
            self.pieces = [order]
        self.order = sum(self.pieces, [])

    def places(self):
        return jnp.asarray(np.array(self.order, np.int32)) ^ self.me

    def spots(self):
        place = np.zeros(self.count, np.int32)
        place[self.order] = np.arange(self.count)
        return jnp.asarray(place)[jnp.arange(self.count, dtype=jnp.int32) ^ self.me]

    def cross(self, value, bit):
        if bit >= self.per:
            return swap(value, "seq", bit // self.per)
        return swap(value, "fsdp", bit * 2)

    def other_core(self, value):
        return swap(value, "fsdp", 1)

    def both(self, mine, other):
        first = self.core == 0
        return jnp.where(first, mine, other), jnp.where(first, other, mine)

    def pick(self, halves):
        first = self.core == 0
        return jnp.where(first, halves[0], halves[1]), jnp.where(first, halves[1], halves[0])


class Gather:
    def __init__(self, chips, shard):
        self.chips = chips
        self.parts = {"s": shard}

    def jobs(self, stage):
        chips, parts = self.chips, self.parts
        if not chips.cube:
            return []
        far, near = chips.line
        bx, by = chips.plane
        if stage == "near":
            parts["a"] = jnp.concatenate([parts["s"], parts["f"]], axis=0)
        if stage == "second":
            parts["ax"] = jnp.concatenate([parts["a"], parts["xa"]], axis=0)
            parts["by"] = jnp.concatenate([parts["b"], parts["yb"]], axis=0)
        return {
            "far": [("f", "s", far)],
            "near": [("b", "a", near)],
            "first": [("xa", "a", bx), ("yb", "b", by)],
            "second": [("yax", "ax", by), ("xby", "by", bx)],
        }[stage]

    def pieces(self):
        if not self.chips.cube:
            value = self.parts["s"]
            for bit in self.chips.line + self.chips.plane:
                value = jnp.concatenate([value, self.chips.cross(value, bit)], axis=0)
            return [value]
        return [self.parts[name] for name in ("ax", "by", "yax", "xby")]


class Scatter:
    def __init__(self, chips, pieces):
        self.chips = chips
        self.parts = dict(zip(("ax", "by", "yax", "xby"), pieces))

    def jobs(self, stage):
        chips, parts = self.chips, self.parts
        if not chips.cube:
            return []
        far, near = chips.line
        bx, by = chips.plane

        def total(name, *more):
            value = parts[name].astype(F32)
            for other in more:
                value = value + parts[other].astype(F32)
            return value

        half = parts["ax"].shape[0] // 2
        if stage == "second":
            value = total("ax", "r_yax")
            parts["a"], parts["xa"] = value[:half].astype(BF), value[half:].astype(BF)
            value = total("by", "r_xby")
            parts["b"], parts["yb"] = value[:half].astype(BF), value[half:].astype(BF)
        if stage == "near":
            parts["b"] = total("b", "r_yb").astype(BF)
        if stage == "far":
            value = total("a", "r_xa", "r_b")
            parts["keep"] = value[: half // 2]
            parts["send"] = value[half // 2 :].astype(BF)
        return {
            "first": [("r_yax", "yax", by), ("r_xby", "xby", bx)],
            "second": [("r_xa", "xa", bx), ("r_yb", "yb", by)],
            "near": [("r_b", "b", near)],
            "far": [("r_far", "send", far)],
        }[stage]

    def result(self):
        if not self.chips.cube:
            total = self.parts["ax"].astype(F32)
            for bit in reversed(self.chips.line + self.chips.plane):
                half = total.shape[0] // 2
                total = total[:half] + self.chips.cross(total[half:].astype(BF), bit).astype(F32)
            return total
        return self.parts["keep"] + self.parts["r_far"].astype(F32)


def cost(flops, bytes_accessed, transcendentals=0):
    return pl.CostEstimate(
        flops=flops, bytes_accessed=bytes_accessed, transcendentals=transcendentals
    )


def turn(value, cosine, forth, back):
    return (
        value * cosine
        + pltpu.roll(value, 128 - ROT // 2, 1) * forth
        + pltpu.roll(value, ROT // 2, 1) * back
    )


def tables_kernel(place_ref, speed_ref, forth_ref, back_ref, cos_ref, to_ref, from_ref):
    angle = place_ref[...].astype(F32) * speed_ref[...]
    cos_ref[...] = jnp.cos(angle)
    sine = jnp.sin(angle)
    to_ref[...] = sine * forth_ref[...]
    from_ref[...] = sine * back_ref[...]


def rope_tables(positions):
    half = ROT // 2
    inverse = 1.0 / 10000.0 ** (jnp.arange(0, ROT, 2, dtype=F32) / ROT)
    speed = jnp.concatenate([inverse, inverse, jnp.zeros((HD - ROT,), F32)])
    speed = jnp.concatenate([speed, speed]).reshape(1, 128)
    lanes = np.arange(128) % HD
    forth = -(lanes < half).astype(np.float32)[None, :]
    back = ((lanes >= half) & (lanes < ROT)).astype(np.float32)[None, :]
    rows = positions.shape[0]
    return pl.pallas_call(
        tables_kernel,
        out_shape=(jax.ShapeDtypeStruct((rows, 128), F32),) * 3,
        cost_estimate=cost(rows * 128 * 100, rows * 128 * 16),
        name="tables",
    )(positions.reshape(rows, 1), speed, jnp.asarray(forth), jnp.asarray(back))


def stack(refs):
    return jnp.concatenate([ref[...] for ref in refs], axis=0) if len(refs) > 1 else refs[0][...]


def project_kernel(count, normed_ref, bias_ref, cos_ref, forth_ref, back_ref, *refs):
    q_ref, kv_ref = refs[count:]
    value = dot(normed_ref[...], stack(refs[:count])) + bias_ref[...]
    tables = cos_ref[...], forth_ref[...], back_ref[...]
    q_ref[...] = turn(value[:, :128], *tables).astype(BF)
    kv_ref[:, :128] = turn(value[:, 128:256], *tables).astype(BF)
    kv_ref[:, 128:] = value[:, 256:].astype(BF)


def project(normed, pieces, bias, tables, group):
    rows = normed.shape[0]
    step = 512
    table = pl.BlockSpec((step, 128), lambda i: (i, 0))
    return pl.pallas_call(
        partial(project_kernel, len(pieces)),
        grid=(rows // step,),
        out_shape=(
            jax.ShapeDtypeStruct((rows, 128), BF),
            jax.ShapeDtypeStruct((rows, 256), BF),
        ),
        in_specs=[
            pl.BlockSpec((step, D), lambda i: (i, 0)),
            pl.BlockSpec((1, 384), lambda i: (0, group)),
            table,
            table,
            table,
        ]
        + [pl.BlockSpec((piece.shape[0], 384), lambda i: (0, group)) for piece in pieces],
        out_specs=(
            pl.BlockSpec((step, 128), lambda i: (i, 0)),
            pl.BlockSpec((step, 256), lambda i: (i, 0)),
        ),
        cost_estimate=cost(2 * rows * D * 384, 2 * (rows * D + D * 384 + rows * 384)),
        name="project",
    )(normed, bias, *tables, *pieces)


def attend_kernel(chunks, q_ref, do_ref, ql_ref, kl_ref, *refs):
    kv_refs = refs[:chunks]
    o_ref, dq_ref = refs[chunks : chunks + 2]
    dkv_refs = refs[chunks + 2 : 2 * chunks + 2]
    bias_ref = refs[-1]
    rows = q_ref.shape[0]
    for chunk in range(chunks):
        old = (chunks - 1 - chunk) * rows
        same = kl_ref[0, old : old + rows, :] == ql_ref[0]
        if chunk == 0:
            key = lax.broadcasted_iota(jnp.int32, (rows, rows), 0)
            query = lax.broadcasted_iota(jnp.int32, (rows, rows), 1)
            same = same & (key <= query)
        bias_ref[chunk * rows : (chunk + 1) * rows, :] = jnp.where(same, 0.0, -1e30)

    keys = jnp.concatenate([ref[:, :128] for ref in kv_refs], axis=0)
    values = jnp.concatenate([ref[:, 128:] for ref in kv_refs], axis=0)
    keys_t = keys.T
    values_t = values.T
    scaled = q_ref[...] * 0.125
    given = do_ref[...]
    lane = lax.broadcasted_iota(jnp.int32, (rows, 128), 1)
    out_t, dq_t, probs_all, ds_all, q_all, g_all = [], [], [], [], [], []
    for head in range(2):
        mine = (lane < HD) if head == 0 else (lane >= HD)
        query = jnp.where(mine, scaled, jnp.zeros_like(scaled))
        grad = jnp.where(mine, given, jnp.zeros_like(given))
        part = slice(head * HD, (head + 1) * HD)
        scores = times_transposed(keys, query) + bias_ref[...]
        top = jnp.max(scores, axis=0, keepdims=True)
        unscaled = jnp.exp(scores - top)
        total = jnp.sum(unscaled, axis=0, keepdims=True)
        probs = unscaled * (1.0 / total)
        rounded = probs.astype(BF)
        out_t.append(dot(values_t[part], rounded))
        prob_grad = times_transposed(values, grad)
        inner = jnp.sum(probs * prob_grad, axis=0, keepdims=True)
        score_grad = (probs * (prob_grad - inner)).astype(BF)
        dq_t.append(dot(keys_t[part], score_grad))
        probs_all.append(rounded)
        ds_all.append(score_grad)
        q_all.append(query)
        g_all.append(grad)
    o_ref[...] = jnp.concatenate(out_t, axis=0).T.astype(BF)
    dq_ref[...] = (jnp.concatenate(dq_t, axis=0).T * 0.125).astype(BF)
    dk = dot(jnp.concatenate(ds_all, axis=1), jnp.concatenate(q_all, axis=0))
    dv = dot(jnp.concatenate(probs_all, axis=1), jnp.concatenate(g_all, axis=0))
    for chunk, ref in enumerate(dkv_refs):
        ref[:, :128] = dk[chunk * rows : (chunk + 1) * rows].astype(ref.dtype)
        ref[:, 128:] = dv[chunk * rows : (chunk + 1) * rows].astype(ref.dtype)


def attend(group, seqs, query, grad, query_labels, key_labels, kvs):
    chunks = len(kvs)
    total, width = query.shape
    rows = total // seqs
    keys = rows * chunks
    narrow = pl.BlockSpec((rows, 128), lambda b: (b, 0))
    wide = pl.BlockSpec((rows, 256), lambda b: (b, 0))
    return pl.pallas_call(
        partial(attend_kernel, chunks),
        grid=(seqs,),
        out_shape=(
            jax.ShapeDtypeStruct((total, 128), BF),
            jax.ShapeDtypeStruct((total, 128), BF),
            jax.ShapeDtypeStruct((total, 256), F32),
        )
        + (jax.ShapeDtypeStruct((total, 256), BF),) * (chunks - 1),
        in_specs=[
            narrow,
            pl.BlockSpec((rows, 128), lambda b: (b, group)),
            pl.BlockSpec((1, 1, rows), lambda b: (b, 0, 0)),
            pl.BlockSpec((1, keys, 1), lambda b: (b, 0, 0)),
        ]
        + [
            pl.BlockSpec((rows, 256), lambda b, place=place: (b + place * seqs, 0))
            for _, place in kvs
        ],
        out_specs=(narrow, narrow) + (wide,) * chunks,
        scratch_shapes=[pltpu.VMEM((keys, rows), F32)],
        cost_estimate=cost(
            24 * seqs * rows * keys * 128, total * 256 * (3 + 5 * chunks), seqs * 2 * rows * keys
        ),
        name="attend",
    )(query, grad, query_labels, key_labels, *[array for array, _ in kvs])


def unturn_kernel(dq_ref, own_ref, more_ref, cos_ref, forth_ref, back_ref, out_ref):
    cosine, forth, back = cos_ref[...], -forth_ref[...], -back_ref[...]
    kv = (own_ref[...] + more_ref[...].astype(F32)).astype(BF)
    out_ref[:, :128] = turn(dq_ref[...].astype(F32), cosine, forth, back).astype(BF)
    out_ref[:, 128:256] = turn(kv[:, :128].astype(F32), cosine, forth, back).astype(BF)
    out_ref[:, 256:] = kv[:, 128:]


def unturn(dq, own, more, place, tables):
    rows = dq.shape[0]
    step = rows // 2

    def spec(columns, first=0):
        return pl.BlockSpec((step, columns), lambda i: (i + first, 0))

    return pl.pallas_call(
        unturn_kernel,
        grid=(rows // step,),
        out_shape=jax.ShapeDtypeStruct((rows, 384), BF),
        in_specs=[spec(128), spec(256), spec(256, place * 2)] + [spec(128)] * 3,
        out_specs=spec(384),
        cost_estimate=cost(rows * 128 * 20, rows * 128 * 26),
        name="unturn",
    )(dq, own, more, *tables)


ROOT_HALF = math.sqrt(0.5)
DENSITY = 1.0 / math.sqrt(2.0 * math.pi)


def gelu_and_slope(value):
    share = 0.5 + 0.5 * lax.erf(value * ROOT_HALF)
    return value * share, share + value * (DENSITY * jnp.exp(-0.5 * value * value))


def hidden_kernel(count, normed_ref, bias_ref, *refs):
    act_ref, act_t_ref, slope_ref = refs[count:]
    rows = 256
    weight = stack(refs[:count])

    def some(i, carry):
        here = pl.ds(pl.multiple_of(i * rows, rows), rows)
        value = dot(normed_ref[here, :], weight) + bias_ref[...]
        act, slope = gelu_and_slope(value)
        act = act.astype(BF)
        act_ref[here, :] = act
        act_t_ref[:, here] = act.T
        slope_ref[here, :] = slope
        return carry

    lax.fori_loop(0, normed_ref.shape[0] // rows, some, 0)


def hidden(normed, pieces, bias):
    rows, width = normed.shape[0], bias.shape[1]
    return pl.pallas_call(
        partial(hidden_kernel, len(pieces)),
        grid=(width // 256,),
        out_shape=(
            jax.ShapeDtypeStruct((rows, width), BF),
            jax.ShapeDtypeStruct((width, rows), BF),
            jax.ShapeDtypeStruct((rows, width), F32),
        ),
        in_specs=[
            pl.BlockSpec((rows, D), lambda j: (0, 0)),
            pl.BlockSpec((1, 256), lambda j: (0, j)),
        ]
        + [pl.BlockSpec((piece.shape[0], 256), lambda j: (0, j)) for piece in pieces],
        out_specs=(
            pl.BlockSpec((rows, 256), lambda j: (0, j)),
            pl.BlockSpec((256, rows), lambda j: (j, 0)),
            pl.BlockSpec((rows, 256), lambda j: (0, j)),
        ),
        cost_estimate=cost(2 * rows * D * width + 50 * rows * width, 9 * rows * width),
        name="hidden",
    )(normed, bias, *pieces)


def mlp_kernel(rels, me_ref, g_ref, act_ref, slope_ref, *refs):
    count = len(rels)
    hg_ref, sum_ref, out_ref, w_ref, sem = refs[count:]
    j = pl.program_id(0)
    rows = 256

    @pl.when(j == 0)
    def _():
        copies = []
        for piece, chips in zip(refs[:count], rels):
            for place, rel in enumerate(chips):
                first = pl.multiple_of((me_ref[0] ^ rel) * 128, 128)
                copies.append(
                    pltpu.make_async_copy(
                        piece.at[pl.ds(place * 128, 128), :], w_ref.at[pl.ds(first, 128), :], sem
                    )
                )
        for copy in copies:
            copy.start()
        out_ref[...] = jnp.zeros_like(out_ref)
        for copy in copies:
            copy.wait()

    w = w_ref[pl.ds(pl.multiple_of(j * 256, 256), 256), :]

    def some(i, total):
        here = pl.ds(pl.multiple_of(i * rows, rows), rows)
        grad = (times_transposed(g_ref[here, :], w) * slope_ref[here, :]).astype(BF)
        hg_ref[here, :] = grad
        out_ref[here, :] += dot(act_ref[here, :], w)
        return total + jnp.sum(grad.astype(F32), axis=0, keepdims=True)

    sum_ref[...] = lax.fori_loop(0, g_ref.shape[0] // rows, some, jnp.zeros((1, 256), F32))


def mlp(chips, grad, act, slope, pieces):
    rows, width = act.shape
    return pl.pallas_call(
        partial(mlp_kernel, chips.pieces),
        grid=(width // 256,),
        out_shape=(
            jax.ShapeDtypeStruct((rows, width), BF),
            jax.ShapeDtypeStruct((1, width), F32),
            jax.ShapeDtypeStruct((rows, D), F32),
        ),
        in_specs=[
            pl.BlockSpec(memory_space=pltpu.SMEM),
            pl.BlockSpec((rows, D), lambda j: (0, 0)),
            pl.BlockSpec((rows, 256), lambda j: (0, j)),
            pl.BlockSpec((rows, 256), lambda j: (0, j)),
        ]
        + [pl.BlockSpec(memory_space=pl.ANY)] * len(pieces),
        out_specs=(
            pl.BlockSpec((rows, 256), lambda j: (0, j)),
            pl.BlockSpec((1, 256), lambda j: (0, j)),
            pl.BlockSpec((rows, D), lambda j: (0, 0)),
        ),
        scratch_shapes=[pltpu.VMEM((width, D), BF), pltpu.SemaphoreType.DMA],
        cost_estimate=cost(4 * rows * D * width, 10 * rows * width),
        name="mlp",
    )(chips.me.reshape(1), grad, act, slope, *pieces)


def row_grads_kernel(heights, steps, left_ref, right_ref, *refs):
    out_refs = refs[-len(heights) :]
    more_refs = refs[: -len(heights)]

    @pl.when(pl.program_id(0) < steps)
    def _():
        value = dot(left_ref[...], right_ref[...])
        first = 0
        for height, ref in zip(heights, out_refs):
            ref[...] = value[first : first + height].astype(BF)
            first += height

    if more_refs:

        @pl.when(pl.program_id(0) >= steps)
        def _():
            first = 0
            for height, ref in zip(heights, out_refs):
                ref[...] = more_refs[0][first : first + height, :]
                first += height


def row_grads(chips, left, right, more=None):
    rows, tokens = left.shape
    heights = [rows // len(chips.pieces)] * len(chips.pieces)
    step = 256
    steps = right.shape[1] // step
    columns = right.shape[1] + (0 if more is None else more.shape[1])
    last = steps - 1
    return pl.pallas_call(
        partial(row_grads_kernel, heights, steps),
        grid=(columns // step,),
        out_shape=tuple(jax.ShapeDtypeStruct((height, columns), BF) for height in heights),
        in_specs=[
            pl.BlockSpec((rows, tokens), lambda j: (0, 0)),
            pl.BlockSpec((tokens, step), lambda j: (0, jnp.minimum(j, last))),
        ]
        + (
            []
            if more is None
            else [pl.BlockSpec((rows, step), lambda j: (0, jnp.maximum(j - steps, 0)))]
        ),
        out_specs=tuple(pl.BlockSpec((height, step), lambda j: (0, j)) for height in heights),
        cost_estimate=cost(2 * rows * tokens * columns, 2 * (rows * tokens + rows * columns)),
        name="row_grads",
    )(left, right, *([] if more is None else [more]))


def unit_grads_kernel(pieces, order_ref, *refs):
    lefts, right_ref, out_refs = refs[:4], refs[4], refs[5:]
    value = dot(stack(lefts), right_ref[...]).astype(BF)
    for piece in range(pieces):

        @pl.when(pl.program_id(0) == piece)
        def _(piece=piece):
            out_refs[piece][...] = value


def unit_grads(chips, left, right):
    tokens = left.shape[1]
    columns = right.shape[1]
    pieces = len(chips.pieces)

    def block(place):
        return pl.BlockSpec((128, tokens), lambda k, order: (order[4 * k + place], 0))

    return pl.pallas_call(
        partial(unit_grads_kernel, pieces),
        out_shape=tuple(jax.ShapeDtypeStruct((512, columns), BF) for _ in range(pieces)),
        grid_spec=pltpu.PrefetchScalarGridSpec(
            num_scalar_prefetch=1,
            grid=(pieces,),
            in_specs=[block(place) for place in range(4)]
            + [pl.BlockSpec((tokens, columns), lambda k, order: (0, 0))],
            out_specs=tuple(
                pl.BlockSpec((512, columns), lambda k, order: (0, 0)) for _ in range(pieces)
            ),
        ),
        cost_estimate=cost(2 * tokens * columns * 512 * pieces, 4 * 512 * pieces * columns),
        name="unit_grads",
    )(chips.places(), left, left, left, left, right)


def norm_grad_kernel(count, qkv_ref, hidden_ref, *refs):
    out_ref = refs[-1]
    first = 0
    wide, tall = qkv_ref.shape[1], hidden_ref.shape[1]
    for one, two in zip(refs[:count], refs[count : 2 * count]):
        rows = one.shape[0]
        out_ref[:, first : first + rows] = times_transposed(
            qkv_ref[...], one[:, :wide]
        ) + times_transposed(hidden_ref[...], two[:, :tall])
        first += rows


def norm_grad(projected_grad, hidden_grad, qkv_pieces, in_pieces):
    rows = projected_grad.shape[0]
    step = 256

    def whole(piece):
        return pl.BlockSpec(piece.shape, lambda i: (0, 0))

    return pl.pallas_call(
        partial(norm_grad_kernel, len(qkv_pieces)),
        grid=(rows // step,),
        out_shape=jax.ShapeDtypeStruct((rows, D), F32),
        in_specs=[
            pl.BlockSpec((step, projected_grad.shape[1]), lambda i: (i, 0)),
            pl.BlockSpec((step, hidden_grad.shape[1]), lambda i: (i, 0)),
        ]
        + [whole(piece) for piece in qkv_pieces + in_pieces],
        out_specs=pl.BlockSpec((step, D), lambda i: (i, 0)),
        cost_estimate=cost(7 * rows * D * D, 12 * rows * D),
        name="norm_grad",
    )(projected_grad, hidden_grad, *qkv_pieces, *in_pieces)


def local(
    hidden_in,
    document_labels,
    cotangent,
    ln_gain,
    ln_bias,
    qkv_weight,
    qkv_bias,
    out_weight,
    out_bias,
    fc_in_weight,
    fc_in_bias,
    fc_out_weight,
    fc_out_bias,
):
    chips = Chips()
    count, core, nz = chips.count, chips.core, chips.nz
    both, pick = chips.both, chips.pick
    local_seqs, tok_count = hidden_in.shape[:2]
    length = tok_count * nz
    row_count = local_seqs * tok_count
    seqs = 2 * local_seqs
    d_rows = qkv_weight.shape[0]
    f_rows = fc_out_weight.shape[0]
    units = fc_in_weight.shape[1] // 2
    pair = H // 2 // GROUPS
    reach = -(-(length // 2 - 1) // tok_count)
    smooth = chips.cube and f_rows == 128 and reach == 2

    x_own = hidden_in.reshape(row_count, D)
    g_own = cotangent.reshape(row_count, D)
    vectors = (ln_gain, ln_bias, qkv_bias, out_bias, fc_in_bias, fc_out_bias)
    marks = (document_labels + 1).astype(BF).reshape(-1)
    sides = [vector.reshape(-1, d_rows).T for vector in vectors + (marks,)]
    widths = [side.shape[1] for side in sides]
    side_width = 128 * (-(-sum(widths) // 128))
    side = jnp.pad(jnp.concatenate(sides, axis=1), ((0, 0), (0, side_width - sum(widths))))
    qkv_keep, qkv_give = pick(
        qkv_weight.reshape(d_rows, 2, GROUPS, pair, 3, HD)
        .transpose(1, 0, 2, 4, 3, 5)
        .reshape(2, d_rows, 3 * D // 2)
    )
    in_keep, in_give = pick(
        fc_in_weight.reshape(d_rows, count, 2, f_rows)
        .transpose(2, 0, 1, 3)
        .reshape(2, d_rows, units)
    )
    qkv_wide = 3 * D // 2
    clock = Clock(side[:1])
    box = {}

    def slot(jobs, work=None, *inputs):
        gated, given = clock.gate(tuple(job[2] for job in jobs), inputs)
        results = [job[3](value) for job, value in zip(jobs, gated)]
        made = work(*given) if work is not None else ()
        clock.tick(results, made)
        for job, value in zip(jobs, results):
            job[0][job[1]] = value
        return made

    def moves(line, stage):
        return [
            (line.parts, name, line.parts[source], partial(chips.cross, bit=bit))
            for name, source, bit in line.jobs(stage)
        ]

    def core_move(name, value):
        return (box, name, value, chips.other_core)

    block = 2 * d_rows
    wanted = jnp.repeat(chips.places(), block, total_repeat_length=D) * block + jnp.asarray(
        np.arange(D, dtype=np.int32) % block
    )

    def choice(wanted):
        return (jnp.arange(D, dtype=jnp.int32)[:, None] == wanted[None, :]).astype(BF)

    chosen = slot(
        [
            core_move("give", jnp.concatenate([qkv_give, side, in_give], axis=1)),
            core_move("x", x_own),
        ],
        choice,
        wanted,
    )
    keep = jnp.concatenate([qkv_keep, side, in_keep], axis=1)
    full = jnp.concatenate(both(keep, box["give"]), axis=0)
    folded = jnp.concatenate([out_weight[:, : D // 2], out_weight[:, D // 2 :]], axis=0)
    line_a = Gather(chips, full[:, : qkv_wide + side_width])
    line_b = Gather(chips, jnp.concatenate([full[:, qkv_wide + side_width :], folded], axis=1))
    line_c = Gather(chips, fc_out_weight)
    x_both = jnp.concatenate([x_own, box["x"]], axis=0)

    def prepare(x, chosen):
        x = dot(x, chosen)
        average = jnp.mean(x, axis=-1, keepdims=True)
        centered = x - average
        spread = jnp.mean(centered * centered, axis=-1, keepdims=True)
        inv_std = lax.rsqrt(spread + 1e-05)
        return centered * inv_std, inv_std

    xhat, inv_std = slot(
        moves(line_a, "far") + [core_move("g", g_own)], prepare, x_both, chosen
    )
    g_both = jnp.concatenate([g_own, box["g"]], axis=0)
    grad_sum = slot(
        moves(line_a, "near") + moves(line_b, "far"),
        lambda g: jnp.sum(g.astype(F32), axis=0),
        g_own,
    )

    def split_side(rows):
        values = rows[:, qkv_wide : qkv_wide + side_width]
        parts = []
        first = 0
        for width in widths:
            parts.append(values[:, first : first + width])
            first += width
        return parts

    def line_marks(*rows):
        if chips.cube:
            rows = jnp.concatenate(rows, axis=0)
            order = chips.pieces[0][:2] + chips.pieces[1][:2]
            spot = np.zeros(nz, np.int32)
            spot[[chip // chips.per for chip in order]] = np.arange(nz)
            place = lax.axis_index("seq")
            values = split_side(rows)[-1].reshape(nz, 2, d_rows, -1)
            values = values[jnp.asarray(spot)[jnp.arange(nz, dtype=jnp.int32) ^ place]]
            values = values.transpose(0, 1, 3, 2).reshape(nz, 2, local_seqs, tok_count)
        else:
            own = document_labels + 1
            values = jnp.stack(
                [
                    lax.all_gather(labels, "seq", axis=0)
                    for labels in both(own, chips.other_core(own))
                ],
                axis=1,
            )
        values = jnp.stack(pick(values.transpose(1, 0, 2, 3)), axis=0)
        values = values.transpose(0, 2, 1, 3).reshape(seqs, length).astype(jnp.int32)
        values = jnp.pad(values, ((0, 0), (reach * tok_count, 0)))
        seen = lax.dynamic_slice_in_dim(
            values, lax.axis_index("seq") * tok_count, (reach + 1) * tok_count, 1
        )
        mine = seen[:, reach * tok_count :]
        order_of = jnp.arange((reach + 1) * tok_count, dtype=jnp.int32) - reach * tok_count
        places = jnp.arange(tok_count, dtype=jnp.int32)
        earlier = (seen[:, None, :] == mine[:, :, None]) & (
            order_of[None, None, :] < places[None, :, None]
        )
        positions = jnp.sum(earlier.astype(jnp.int32), axis=-1).reshape(seqs * tok_count)
        return rope_tables(positions), seen[:, :, None], mine[:, None, :]

    tables, key_labels, query_labels = slot(
        moves(line_a, "first") + moves(line_b, "near") + moves(line_c, "far"),
        line_marks,
        *([line_a.parts["a"], line_a.parts["b"]] if chips.cube else []),
    )
    slot(moves(line_a, "second") + moves(line_c, "near"))
    qkv_pieces = line_a.pieces()

    def parameters(*pieces):
        rows = jnp.concatenate(
            [piece[:, qkv_wide : qkv_wide + side_width] for piece in pieces], axis=0
        ).T.astype(F32)
        spots = chips.spots()
        ours = rows[: sum(widths[:-1])].reshape(-1, count, 2, d_rows)[:, spots]
        values = []
        first = 0
        for width in widths[:-1]:
            value = ours[first : first + width]
            values.append(value.transpose(1, 2, 0, 3).reshape(count * block * width))
            first += width
        b_qkv, b_out, b_in, b_fc = values[2:]
        b_qkv = pick(
            b_qkv.reshape(2, GROUPS, pair, 3, HD).transpose(0, 1, 3, 2, 4).reshape(2, 1, qkv_wide)
        )[0]
        b_in = pick(b_in.reshape(count, 2, f_rows).transpose(1, 0, 2).reshape(2, 1, units))[0]
        return rows[0:1], rows[1:2], b_qkv, b_out + b_fc, b_in

    def start_work(xhat, pieces, tables):
        gain, norm_shift, b_qkv, b_rows, b_in = parameters(*pieces)
        normed = (xhat * gain + norm_shift).astype(BF)
        return gain, b_rows, b_in, b_qkv, normed, project(normed, pieces, b_qkv, tables, 0)

    gain, b_rows, b_in, b_qkv, normed, first_pair = slot(
        moves(line_b, "first"), start_work, xhat, qkv_pieces, tables
    )
    queries, own_kvs = {0: first_pair[0]}, {0: first_pair[1]}
    hops, backs, sent = {}, {}, {}
    total_rows = seqs * tok_count

    def hop(step):
        parts = []
        if step > 0:
            last = hops[step - 1]
            parts.append(last[-total_rows:])
        if step < GROUPS:
            parts.append(own_kvs[step])
        value = parts[0] if len(parts) == 1 else jnp.concatenate(parts, axis=0)
        return (hops, step, value, partial(shift, by=1))

    def seen_kvs(group):
        if not smooth:
            found = [(own_kvs[group], 0)]
            for _ in range(reach):
                found.append((shift(found[-1][0], 1), 0))
            return found
        return [
            (own_kvs[group], 0),
            (hops[group], 0 if group == 0 else 1),
            (hops[group + 1], 0),
        ]

    def hop_jobs(step):
        return [hop(step)] if smooth else []

    results = {}

    def back(step):
        parts = []
        if step > 0:
            last = backs[step - 1][-total_rows:]
            value = results[step - 1][3].astype(F32) + last.astype(F32)
            parts.append(value.astype(BF))
        if step < GROUPS:
            parts.append(results[step][4])
        value = parts[0] if len(parts) == 1 else jnp.concatenate(parts, axis=0)
        return (backs, step, value, partial(shift, by=-1))

    def back_jobs(step):
        return [back(step)] if smooth else []

    def returned(group):
        if smooth:
            return backs[group + 1], 0
        value = shift(results[group][-1], -1)
        for step in range(reach - 1, 0, -1):
            value = (results[group][2 + step].astype(F32) + value.astype(F32)).astype(BF)
            value = shift(value, -1)
        return value, 0

    def projections(groups):
        def work(normed, pieces, b_qkv, tables):
            return [project(normed, pieces, b_qkv, tables, group) for group in groups], normed.T

        return work

    made, normed_t = slot(
        moves(line_b, "second") + hop_jobs(0),
        projections((1, 2, 3)),
        normed,
        qkv_pieces,
        b_qkv,
        tables,
    )
    for group in (1, 2, 3):
        queries[group], own_kvs[group] = made[group - 1]
    in_pieces = line_b.pieces()

    def my_rows(*pieces):
        rows = jnp.concatenate([piece[:, units:] for piece in pieces], axis=0)
        rows = rows.reshape(count, 2, d_rows, D // 2).transpose(0, 2, 1, 3)
        return rows.reshape(count, d_rows, D)[chips.spots()]

    def units_of(normed, b_in, *pieces):
        if smooth:
            return hidden(normed, pieces, b_in)
        act, slope = gelu_and_slope(dot(normed, stack_arrays(pieces)[:, :units]) + b_in)
        act = act.astype(BF)
        return act, act.T, slope

    def stack_arrays(pieces):
        return jnp.concatenate(pieces, axis=0)

    out_mine = slot(moves(line_c, "first") + hop_jobs(1), my_rows, *in_pieces)
    act, act_t, slope = slot(
        [core_move("out", out_mine)] + hop_jobs(2), units_of, normed, b_in, *in_pieces
    )
    out_heads = pick(jnp.stack(both(out_mine, box["out"]), axis=1).reshape(2, D // 2, D))[0]

    def attention(group):
        def work(query, context_grad, query_labels, key_labels, *arrays):
            kvs = [(array, place) for array, (_, place) in zip(arrays, found)]
            return attend(group, seqs, query, context_grad, query_labels, key_labels, kvs)

        found = seen_kvs(group)
        return (work, queries[group], context_grad, query_labels, key_labels) + tuple(
            array for array, _ in found
        )

    def grad_of_context(g_both, out_heads):
        return times_transposed(g_both, out_heads).astype(BF)

    context_grad = grad_of_context(g_both, out_heads)
    results[0] = slot(moves(line_c, "second") + hop_jobs(3), *attention(0))
    fc_pieces = line_c.pieces()

    def fc_out_grad(act_t, g_both):
        if smooth:
            return unit_grads(chips, act_t, g_both)
        rows = act_t.reshape(count, f_rows, act_t.shape[1])[chips.places()]
        return [dot(rows.reshape(units, -1), g_both).astype(BF)]

    sum_fc = Scatter(
        chips, slot(hop_jobs(4) + back_jobs(0), fc_out_grad, act_t, g_both)
    )
    results[1] = slot(moves(sum_fc, "first"), *attention(1))

    def mlp_work(g_both, act, slope, *pieces):
        if smooth:
            return mlp(chips, g_both, act, slope, pieces)
        weight = stack_arrays(pieces).reshape(count, f_rows, D)[chips.spots()].reshape(units, D)
        grad = (times_transposed(g_both, weight) * slope).astype(BF)
        total = jnp.sum(grad.astype(F32), axis=0, keepdims=True)
        return grad, total, dot(act, weight)

    hidden_grad, hidden_sum, mlp_out = slot(
        moves(sum_fc, "second") + back_jobs(1), mlp_work, g_both, act, slope, *fc_pieces
    )

    def rows_of(normed_t, right, *more):
        return row_grads(chips, normed_t, right, *more)

    sum_in = Scatter(chips, slot(moves(sum_fc, "near"), rows_of, normed_t, hidden_grad))
    results[2] = slot(moves(sum_in, "first") + moves(sum_fc, "far"), *attention(2))
    results[3] = slot(moves(sum_in, "second") + back_jobs(2), *attention(3))
    context = jnp.concatenate([results[group][0] for group in range(GROUPS)], axis=1)

    def out_grad(context, g_both):
        value = outer_product(context, g_both).astype(BF).reshape(count // 2, 2, d_rows, D)
        return pick(value.transpose(1, 0, 2, 3))

    out_keep, out_give = slot(
        moves(sum_in, "near") + back_jobs(3), out_grad, context, g_both
    )
    out_side, = slot(
        [core_move("out_grad", out_give)] + back_jobs(4),
        lambda mlp_out, context, out_heads: (mlp_out + dot(context, out_heads),),
        mlp_out,
        context,
        out_heads,
    )
    out_rows = jnp.concatenate(both(out_keep, box["out_grad"]), axis=0)[chips.places()]
    out_rows = (
        out_rows.reshape(count, d_rows, 2, D // 2).transpose(0, 2, 1, 3).reshape(D, D // 2)
    )

    def undo(tables, *args):
        return jnp.concatenate(
            [
                unturn(*args[3 * group : 3 * group + 3], returned(group)[1], tables)
                for group in range(GROUPS)
            ],
            axis=1,
        )

    def last_grads(tables, normed_t, out_rows, *args):
        projected_grad = undo(tables, *args)
        return projected_grad, rows_of(normed_t, projected_grad, out_rows)

    projected_grad, parts = slot(
        moves(sum_in, "far") + [core_move("out_side", out_side[row_count:])],
        last_grads,
        tables,
        normed_t,
        out_rows,
        *[
            value
            for group in range(GROUPS)
            for value in (results[group][1], results[group][2], returned(group)[0])
        ],
    )
    sum_qkv = Scatter(chips, parts)

    def input_side(projected_grad, hidden_grad, qkv_pieces, in_pieces):
        return norm_grad(projected_grad, hidden_grad, qkv_pieces, in_pieces)

    norm_part = slot(
        moves(sum_qkv, "first"), input_side, projected_grad, hidden_grad, qkv_pieces, in_pieces
    )

    def finish_output(x_own, out_side, out_more, b_rows, projected_grad):
        output = (x_own.astype(F32) + out_side + out_more + b_rows).astype(BF)
        return output, jnp.sum(projected_grad.astype(F32), axis=0)

    in_keep, in_give = pick(sum_in.result().reshape(2, d_rows, units))
    output, qkv_bias_sum = slot(
        moves(sum_qkv, "second")
        + [core_move("norm", norm_part[row_count:]), core_move("in_rows", in_give)],
        finish_output,
        x_own,
        out_side[:row_count],
        box["out_side"],
        b_rows,
        projected_grad,
    )

    def norm_back(norm_part, norm_more, xhat, inv_std, gain, g_own, chosen):
        grad = norm_part + norm_more
        xhat = xhat[:row_count]
        scaled = grad * gain
        value = (
            scaled
            - jnp.mean(scaled, axis=-1, keepdims=True)
            - xhat * jnp.mean(scaled * xhat, axis=-1, keepdims=True)
        ) * inv_std[:row_count]
        high = value.astype(BF)
        low = (value - high.astype(F32)).astype(BF)
        value = times_transposed(high, chosen) + times_transposed(low, chosen)
        sums = jnp.stack([jnp.sum(grad * xhat, axis=0), jnp.sum(grad, axis=0)])
        return (g_own.astype(F32) + value).astype(BF), sums

    input_grad, norm_sums = slot(
        moves(sum_qkv, "near"),
        norm_back,
        norm_part[:row_count],
        box["norm"],
        xhat,
        inv_std,
        gain,
        g_own,
        chosen,
    )

    norm_sums = norm_sums.reshape(2, count, 2, d_rows)[:, chips.spots()].reshape(2, D)
    mine = (jnp.arange(2) == core)[:, None]
    qkv_full = (
        jnp.where(mine, qkv_bias_sum[None, :], 0.0)
        .reshape(2, GROUPS, 3, pair, HD)
        .transpose(0, 1, 3, 2, 4)
        .reshape(3 * D)
    )
    in_full = jnp.where(
        mine[None], hidden_sum.reshape(count, 1, f_rows), 0.0
    ).reshape(2 * units)
    packed = jnp.concatenate(
        [
            vector.reshape(2 * count, -1)
            for vector in (norm_sums[0], norm_sums[1], qkv_full, grad_sum, in_full)
        ],
        axis=1,
    ).reshape(count, -1)
    order = [0]
    bits = chips.line + chips.plane
    for bit in bits:
        order = order + [chip ^ bit for chip in order]
    packed = packed[jnp.asarray(np.array(order, np.int32)) ^ chips.me]

    def fold(bit):
        return (box, "fold", packed[packed.shape[0] // 2 :], partial(chips.cross, bit=bit))

    bits = bits[::-1]
    slot(moves(sum_qkv, "far") + [fold(bits[0])])
    packed = packed[: packed.shape[0] // 2] + box["fold"]
    for bit in bits[1:]:
        half = packed.shape[0] // 2
        packed = packed[:half] + chips.cross(packed[half:], bit)
    sums_keep, sums_give = pick(packed.reshape(2, -1))
    sums = sums_keep + chips.other_core(sums_give)
    parts = []
    first = 0
    for width in (d_rows, d_rows, 3 * d_rows, d_rows, f_rows):
        parts.append(sums[first : first + width])
        first += width

    last_rows = sum_qkv.result()
    out_weight_grad = last_rows[:, qkv_wide:].reshape(2, d_rows, D // 2)
    out_weight_grad = jnp.concatenate([out_weight_grad[0], out_weight_grad[1]], axis=1)
    qkv_keep, qkv_give = pick(last_rows[:, :qkv_wide].reshape(2, d_rows, qkv_wide))
    qkv_halves = jnp.stack(both(qkv_keep, chips.other_core(qkv_give)), axis=1)
    qkv_weight_grad = (
        qkv_halves.reshape(d_rows, 2, GROUPS, 3, pair, HD)
        .transpose(0, 1, 2, 4, 3, 5)
        .reshape(d_rows, 3 * D)
    )
    in_halves = [
        value.reshape(d_rows, count, 1, f_rows) for value in both(in_keep, box["in_rows"])
    ]
    fc_in_weight_grad = jnp.concatenate(in_halves, axis=2).reshape(d_rows, 2 * units)
    return (
        output.reshape(local_seqs, tok_count, D),
        input_grad.reshape(local_seqs, tok_count, D),
        parts[0],
        parts[1],
        qkv_weight_grad,
        parts[2],
        out_weight_grad,
        parts[3],
        fc_in_weight_grad,
        parts[4],
        sum_fc.result(),
        parts[3],
    )


def solution(mesh):
    rows = P(("seq", "fsdp"))
    wide = P(("seq", "fsdp"), None)
    act = P("fsdp", "seq", None)
    placed = (act, P("fsdp", "seq"), act) + (rows, rows) + (wide, rows) * 4
    return jax.shard_map(
        local,
        mesh=mesh,
        in_specs=placed,
        out_specs=(act, act, rows, rows) + (wide, rows) * 4,
        check_vma=False,
    )
```

```python
from functools import partial
import math

import jax
import jax.numpy as jnp
import numpy as np
from jax import lax
from jax.experimental import pallas as pl
from jax.experimental.pallas import tpu as pltpu
from jax.sharding import PartitionSpec as P

D = 1024
H = 16
HD = 64
ROT = 16
GROUPS = 4
BF = jnp.bfloat16
F32 = jnp.float32


def rotate(values, cosine, sine_part):
    half_rot = ROT // 2
    first_part = values[..., :half_rot]
    second_part = values[..., half_rot:ROT]
    return jnp.concatenate(
        [
            first_part * cosine - second_part * sine_part,
            second_part * cosine + first_part * sine_part,
            values[..., ROT:],
        ],
        axis=-1,
    )


def position_angles(segments):
    length = segments.shape[0]
    places = jnp.arange(length, dtype=jnp.int32)
    boundary = jnp.concatenate([jnp.ones((1,), dtype=jnp.bool_), segments[1:] != segments[:-1]])
    starts = lax.cummax(jnp.where(boundary, places, 0), axis=0)
    positions = (places - starts).astype(jnp.float32)
    inverse = 1.0 / 10000.0 ** (jnp.arange(0, ROT, 2, dtype=jnp.float32) / ROT)
    return positions[:, None] * inverse[None, :]


def make_mask(segments, first_row, block_rows):
    length = segments.shape[0]
    query_index = first_row + jnp.arange(block_rows, dtype=jnp.int32)
    key_index = jnp.arange(length, dtype=jnp.int32)
    query_segments = lax.dynamic_slice_in_dim(segments, first_row, block_rows, 0)
    return (key_index[None, :] <= query_index[:, None]) & (
        query_segments[:, None] == segments[None, :]
    )


def outer_product(left, right):
    return lax.dot_general(
        left, right, (((0,), (0,)), ((), ())), preferred_element_type=jnp.float32
    )


def times_transposed(left, right):
    return lax.dot_general(
        left, right, (((1,), (1,)), ((), ())), preferred_element_type=jnp.float32
    )


def local_plain(
    hidden_in,
    document_labels,
    cotangent,
    ln_gain,
    ln_bias,
    qkv_weight,
    qkv_bias,
    out_weight,
    out_bias,
    fc_in_weight,
    fc_in_bias,
    fc_out_weight,
    fc_out_bias,
):
    gathered = (
        lax.all_gather(ln_gain, ("seq", "fsdp"), axis=0, tiled=True),
        lax.all_gather(ln_bias, ("seq", "fsdp"), axis=0, tiled=True),
        lax.all_gather(qkv_weight, ("seq", "fsdp"), axis=0, tiled=True),
        lax.all_gather(qkv_bias, ("seq", "fsdp"), axis=0, tiled=True),
        lax.all_gather(out_weight, ("seq", "fsdp"), axis=0, tiled=True),
        lax.all_gather(out_bias, ("seq", "fsdp"), axis=0, tiled=True),
        lax.all_gather(fc_in_weight, ("seq", "fsdp"), axis=0, tiled=True),
        lax.all_gather(fc_in_bias, ("seq", "fsdp"), axis=0, tiled=True),
        lax.all_gather(fc_out_weight, ("seq", "fsdp"), axis=0, tiled=True),
        lax.all_gather(fc_out_bias, ("seq", "fsdp"), axis=0, tiled=True),
    )
    norm_multiplier, norm_shift, w_qkv, b_qkv, w_out, b_out, w_in, b_in, w_fc, b_fc = gathered
    norm_multiplier = norm_multiplier.astype(jnp.float32)
    norm_shift = norm_shift.astype(jnp.float32)
    groups = lax.axis_size("seq")
    per_group = H // groups
    local_seqs = hidden_in.shape[0]
    tok_count = hidden_in.shape[1]
    row_count = local_seqs * tok_count
    tokens = hidden_in.reshape(row_count, D).astype(jnp.float32)
    average = jnp.mean(tokens, axis=-1, keepdims=True)
    centered = tokens - average
    spread = jnp.mean(centered * centered, axis=-1, keepdims=True)
    inv_std = lax.rsqrt(spread + 1e-05)
    rescaled_rows = centered * inv_std
    normed = (rescaled_rows * norm_multiplier + norm_shift).astype(jnp.bfloat16)
    projected = jnp.dot(normed, w_qkv, preferred_element_type=jnp.float32) + b_qkv.astype(
        jnp.float32
    )
    segments_all = lax.all_gather(document_labels, "seq", axis=1, tiled=True)
    angles_all = jax.vmap(position_angles)(segments_all)
    angles = lax.dynamic_slice_in_dim(
        angles_all, lax.axis_index("seq") * tok_count, tok_count, 1
    ).reshape(row_count, ROT // 2)
    cosine = jnp.cos(angles)[:, None, None, :]
    sine_part = jnp.sin(angles)[:, None, None, :]
    head_parts = projected.reshape(row_count, H, 3, HD)
    turned = jnp.concatenate(
        [rotate(head_parts[:, :, :2], cosine, sine_part), head_parts[:, :, 2:]], axis=2
    ).astype(jnp.bfloat16)
    outgoing = turned.reshape(local_seqs, tok_count, groups, per_group * 3 * HD)
    arrived = lax.all_to_all(outgoing, "seq", split_axis=2, concat_axis=1, tiled=True)
    length = arrived.shape[1]
    local_heads = arrived.reshape(local_seqs, length, per_group, 3, HD)
    queries_seq = local_heads[:, :, :, 0]
    keys_seq = local_heads[:, :, :, 1]
    values_seq = local_heads[:, :, :, 2]
    block_rows = min(512, length)
    block_count = length // block_rows
    scale_factor = 1.0 / math.sqrt(HD)

    def attend_forward(inputs):
        query_all, key_everywhere, value_all, segments = inputs

        def forward_step(running, block_index):
            first_row = block_index * block_rows
            query_rows = lax.dynamic_slice_in_dim(query_all, first_row, block_rows, 0)
            allowed = make_mask(segments, first_row, block_rows)
            raw_scores = (
                jnp.einsum(
                    "qhd,khd->hqk", query_rows, key_everywhere, preferred_element_type=jnp.float32
                )
                * scale_factor
            )
            raw_scores = jnp.where(allowed[None], raw_scores, -1e30)
            row_max = jnp.max(raw_scores, axis=-1, keepdims=True)
            unscaled = jnp.exp(raw_scores - row_max)
            row_total = jnp.sum(unscaled, axis=-1, keepdims=True)
            probabilities = (unscaled / row_total).astype(jnp.bfloat16)
            context_rows = jnp.einsum(
                "hqk,khd->qhd", probabilities, value_all, preferred_element_type=jnp.float32
            )
            log_total = (row_max + jnp.log(row_total))[..., 0]
            return (running, (context_rows, log_total))

        _, (context_blocks, log_blocks) = lax.scan(
            forward_step, None, jnp.arange(block_count, dtype=jnp.int32)
        )
        return (context_blocks.reshape(length, per_group * HD).astype(jnp.bfloat16), log_blocks)

    context_seq, log_totals = lax.map(
        attend_forward, (queries_seq, keys_seq, values_seq, segments_all)
    )
    context_heads = context_seq.reshape(local_seqs, length, 1, per_group * HD)
    returned = lax.all_to_all(context_heads, "seq", split_axis=1, concat_axis=2, tiled=True)
    context = returned.reshape(row_count, D)
    attn_out = jnp.dot(context, w_out, preferred_element_type=jnp.float32) + b_out.astype(
        jnp.float32
    )
    hidden_pre = jnp.dot(normed, w_in, preferred_element_type=jnp.float32) + b_in.astype(
        jnp.float32
    )
    activated = jax.nn.gelu(hidden_pre, approximate=False).astype(jnp.bfloat16)
    mlp_out = jnp.dot(activated, w_fc, preferred_element_type=jnp.float32) + b_fc.astype(
        jnp.float32
    )
    output = (tokens + attn_out + mlp_out).astype(jnp.bfloat16).reshape(local_seqs, tok_count, D)
    grad_out = cotangent.reshape(row_count, D)
    grad_wide = grad_out.astype(jnp.float32)
    out_bias_grad = jnp.sum(grad_wide, axis=0)
    fc_out_bias_grad = jnp.sum(grad_wide, axis=0)
    out_weight_grad = outer_product(context, grad_out)
    fc_out_weight_grad = outer_product(activated, grad_out)
    act_grad = times_transposed(grad_out, w_fc)
    _, gelu_back = jax.vjp(partial(jax.nn.gelu, approximate=False), hidden_pre)
    hidden_grad = gelu_back(act_grad)[0].astype(jnp.bfloat16)
    fc_in_weight_grad = outer_product(normed, hidden_grad)
    fc_in_bias_grad = jnp.sum(hidden_grad.astype(jnp.float32), axis=0)
    context_grad = times_transposed(grad_out, w_out).astype(jnp.bfloat16)
    grad_outgoing = context_grad.reshape(local_seqs, tok_count, groups, per_group * HD)
    head_grad_seq = lax.all_to_all(
        grad_outgoing, "seq", split_axis=2, concat_axis=1, tiled=True
    ).reshape(local_seqs, length, per_group, HD)

    def attend_backward(inputs):
        query_all, key_everywhere, value_all, segments, head_grad, log_blocks = inputs

        def backward_step(running, block_index):
            key_acc, value_accumulator = running
            first_row = block_index * block_rows
            query_rows = lax.dynamic_slice_in_dim(query_all, first_row, block_rows, 0)
            grad_rows = lax.dynamic_slice_in_dim(head_grad, first_row, block_rows, 0)
            log_rows = log_blocks[block_index]
            allowed = make_mask(segments, first_row, block_rows)
            raw_scores = (
                jnp.einsum(
                    "qhd,khd->hqk", query_rows, key_everywhere, preferred_element_type=jnp.float32
                )
                * scale_factor
            )
            raw_scores = jnp.where(allowed[None], raw_scores, -1e30)
            probabilities = jnp.where(allowed[None], jnp.exp(raw_scores - log_rows[..., None]), 0.0)
            value_accumulator = value_accumulator + jnp.einsum(
                "hqk,qhd->khd",
                probabilities.astype(jnp.bfloat16),
                grad_rows,
                preferred_element_type=jnp.float32,
            )
            prob_grad = jnp.einsum(
                "qhd,khd->hqk", grad_rows, value_all, preferred_element_type=jnp.float32
            )
            inner_total = jnp.sum(probabilities * prob_grad, axis=-1, keepdims=True)
            score_grad = (probabilities * (prob_grad - inner_total)).astype(jnp.bfloat16)
            query_grad = (
                jnp.einsum(
                    "hqk,khd->qhd", score_grad, key_everywhere, preferred_element_type=jnp.float32
                )
                * scale_factor
            )
            key_acc = (
                key_acc
                + jnp.einsum(
                    "hqk,qhd->khd", score_grad, query_rows, preferred_element_type=jnp.float32
                )
                * scale_factor
            )
            return ((key_acc, value_accumulator), query_grad)

        empty_grad = jnp.zeros((length, per_group, HD), jnp.float32)
        (key_grad, value_grad), query_blocks = lax.scan(
            backward_step, (empty_grad, empty_grad), jnp.arange(block_count, dtype=jnp.int32)
        )
        query_grad = query_blocks.reshape(length, per_group, HD)
        return jnp.stack([query_grad, key_grad, value_grad], axis=2).astype(jnp.bfloat16)

    stacked = lax.map(
        attend_backward,
        (queries_seq, keys_seq, values_seq, segments_all, head_grad_seq, log_totals),
    )
    returned_grad = lax.all_to_all(
        stacked.reshape(local_seqs, length, 1, per_group * 3 * HD),
        "seq",
        split_axis=1,
        concat_axis=2,
        tiled=True,
    )
    back_heads = returned_grad.reshape(row_count, H, 3, HD).astype(jnp.float32)
    unturned = jnp.concatenate(
        [rotate(back_heads[:, :, :2], cosine, -sine_part), back_heads[:, :, 2:]], axis=2
    )
    projected_grad = unturned.reshape(row_count, 3 * D).astype(jnp.bfloat16)
    qkv_weight_grad = outer_product(normed, projected_grad)
    qkv_bias_grad = jnp.sum(projected_grad.astype(jnp.float32), axis=0)
    normalized_gradient = times_transposed(projected_grad, w_qkv) + times_transposed(
        hidden_grad, w_in
    )
    ln_gain_grad = jnp.sum(normalized_gradient * rescaled_rows, axis=0)
    ln_bias_grad = jnp.sum(normalized_gradient, axis=0)
    standardized_gradient = normalized_gradient * norm_multiplier
    norm_back = (
        standardized_gradient
        - jnp.mean(standardized_gradient, axis=-1, keepdims=True)
        - rescaled_rows * jnp.mean(standardized_gradient * rescaled_rows, axis=-1, keepdims=True)
    ) * inv_std
    input_grad = (grad_wide + norm_back).astype(jnp.bfloat16).reshape(local_seqs, tok_count, D)
    summed = (
        lax.psum_scatter(ln_gain_grad, ("seq", "fsdp"), scatter_dimension=0, tiled=True),
        lax.psum_scatter(ln_bias_grad, ("seq", "fsdp"), scatter_dimension=0, tiled=True),
        lax.psum_scatter(qkv_weight_grad, ("seq", "fsdp"), scatter_dimension=0, tiled=True),
        lax.psum_scatter(qkv_bias_grad, ("seq", "fsdp"), scatter_dimension=0, tiled=True),
        lax.psum_scatter(out_weight_grad, ("seq", "fsdp"), scatter_dimension=0, tiled=True),
        lax.psum_scatter(out_bias_grad, ("seq", "fsdp"), scatter_dimension=0, tiled=True),
        lax.psum_scatter(fc_in_weight_grad, ("seq", "fsdp"), scatter_dimension=0, tiled=True),
        lax.psum_scatter(fc_in_bias_grad, ("seq", "fsdp"), scatter_dimension=0, tiled=True),
        lax.psum_scatter(fc_out_weight_grad, ("seq", "fsdp"), scatter_dimension=0, tiled=True),
        lax.psum_scatter(fc_out_bias_grad, ("seq", "fsdp"), scatter_dimension=0, tiled=True),
    )
    return (
        output,
        input_grad,
        summed[0],
        summed[1],
        summed[2],
        summed[3],
        summed[4],
        summed[5],
        summed[6],
        summed[7],
        summed[8],
        summed[9],
    )


def dot(left, right):
    return jnp.dot(left, right, preferred_element_type=F32)


def swap(value, axis, bit):
    return lax.ppermute(value, axis, [(i, i ^ bit) for i in range(lax.axis_size(axis))])


def shift(value, by):
    count = lax.axis_size("seq")
    return lax.ppermute(
        value, "seq", [(i, i + by) for i in range(count) if 0 <= i + by < count]
    )


class Clock:
    def __init__(self, token):
        self.token = token

    def join(self, *values):
        values, self.token = lax.optimization_barrier((values, self.token))
        return values


X, Y, NEAR, FAR = 1, 2, 4, 8
CHIPS = 16
ORDER = [0, 8, 4, 12, 1, 9, 5, 13, 2, 10, 6, 14, 3, 11, 7, 15]
SUMS = {"ax": [0, 8, 1, 9], "by": [4, 12, 6, 14], "yax": [2, 10, 3, 11], "xby": [5, 13, 7, 15]}


def place_of(chip):
    return (chip // FAR) % 2 + (chip // NEAR) % 2 * 2 + chip % 2 * 4 + (chip // Y) % 2 * 8


def cross(value, bit):
    return swap(value, "seq", bit // 4) if bit >= 4 else swap(value, "fsdp", bit * 2)


def other_core(value):
    return swap(value, "fsdp", 1)


class Gather:
    def __init__(self, shard):
        self.parts = {"s": shard}

    def jobs(self, stage):
        parts = self.parts
        if stage == "near":
            parts["a"] = jnp.concatenate([parts["s"], parts["f"]], axis=0)
        if stage == "second":
            parts["ax"] = jnp.concatenate([parts["a"], parts["xa"]], axis=0)
            parts["by"] = jnp.concatenate([parts["b"], parts["yb"]], axis=0)
        return {
            "far": [("f", "s", FAR)],
            "near": [("b", "a", NEAR)],
            "first": [("xa", "a", X), ("yb", "b", Y)],
            "second": [("yax", "ax", Y), ("xby", "by", X)],
        }[stage]

    def pieces(self):
        return [self.parts[name] for name in SUMS]


LAY = [(0, 0), (1, 0), (0, 1), (3, 0), (2, 0), (1, 1), (2, 1), (3, 1)]


def gathered(refs, columns=slice(None), which=slice(None)):
    half = refs[0].shape[0] // 2
    return jnp.concatenate(
        [refs[array][part * half : part * half + half, columns] for array, part in LAY[which]],
        axis=0,
    )


BLOCKS = {
    "a": [0, 8],
    "xa": [1, 9],
    "b": [4, 12],
    "yb": [6, 14],
    "yax": [2, 10, 3, 11],
    "xby": [5, 13, 7, 15],
}


class Scatter:
    def __init__(self, blocks):
        self.parts = dict(zip(BLOCKS, blocks))

    def total(self, first, last, *names):
        return sum(self.parts[name][first:last].astype(F32) for name in names)

    def jobs(self, stage):
        parts = self.parts
        rows = parts["a"].shape[0]
        if stage == "second":
            for name, other in (("xa", "r_yax"), ("yb", "r_xby")):
                value = parts[name].astype(F32) + parts[other][rows:].astype(F32)
                parts[name] = value.astype(BF)
        if stage == "near":
            parts["b"] = self.total(0, rows, "b", "r_xby", "r_yb").astype(BF)
        if stage == "far":
            value = self.total(rows // 2, rows, "a", "r_yax", "r_xa", "r_b")
            parts["send"] = value.astype(BF)
        return {
            "first": [("r_yax", "yax", Y), ("r_xby", "xby", X)],
            "second": [("r_xa", "xa", X), ("r_yb", "yb", Y)],
            "near": [("r_b", "b", NEAR)],
            "far": [("r_far", "send", FAR)],
        }[stage]

    def result(self):
        rows = self.parts["a"].shape[0] // 2
        return self.total(0, rows, "a", "r_yax", "r_xa", "r_b", "r_far")


def cost(flops, bytes_accessed, transcendentals=0):
    return pl.CostEstimate(
        flops=flops, bytes_accessed=bytes_accessed, transcendentals=transcendentals
    )


SMEM = pl.BlockSpec(memory_space=pltpu.SMEM)
VMEM = pl.BlockSpec(memory_space=pltpu.VMEM)
ANY = pl.BlockSpec(memory_space=pl.ANY)


def whole(array):
    return pl.BlockSpec(array.shape, lambda *_: (0,) * len(array.shape))


def shaped(rows, columns, dtype):
    return jax.ShapeDtypeStruct((rows, columns), dtype)


def stack(refs):
    return jnp.concatenate([ref[...] for ref in refs], axis=0)


def lanes_low(rows):
    return lax.broadcasted_iota(jnp.int32, (rows, 128), 1) < HD


def cut_kernel(where_ref, qkv_ref, in_ref, out_w_ref, gain_ref, shift_ref, qb_ref, ob_ref, ib_ref, fb_ref, label_ref, *refs):
    keep1, give1, keep2, give2, in_keep, in_give, folded, columns_ref, line_ref = refs
    core = where_ref[1]
    rows = qkv_ref.shape[0]
    columns_ref[...] = jnp.zeros_like(columns_ref)
    for row, ref in enumerate((gain_ref, shift_ref, ob_ref, fb_ref)):
        columns_ref[row : row + 1, :rows] = ref[...].astype(F32)
    line_ref[...] = jnp.zeros_like(line_ref)
    line_ref[0:1, :96] = qb_ref[...].astype(F32)
    line_ref[1:2, :] = ib_ref[...].astype(F32)
    bias, units = line_ref[0:1, :], line_ref[1:2, :]
    lane = lax.broadcasted_iota(jnp.int32, (1, 128), 1)
    first = core == 0
    parts = []
    for seq in range(2):
        for part in range(2):
            labels = (label_ref[seq : seq + 1, 128 * part : 128 * part + 128] + 1).astype(F32)
            parts += [pltpu.roll(labels, HD, 1), labels]
    zero = jnp.zeros_like(bias)
    parts.append(jnp.where(first, pltpu.roll(bias, 64, 1), zero))
    parts.append(
        jnp.where(
            first,
            jnp.where(lane < 96, bias, zero),
            jnp.where(lane >= 96, pltpu.roll(bias, 96, 1), zero),
        )
    )
    parts.append(jnp.where(first, zero, pltpu.roll(bias, 32, 1)))
    parts += [pltpu.roll(units, HD, 1), units]
    for row, value in enumerate(parts):
        line_ref[row : row + 1, :] = value
    low = lanes_low(rows)
    side = jnp.where(low, columns_ref[...].T[:rows], line_ref[...]).astype(BF)
    for owner, out1, out2 in ((core, keep1, keep2), (1 - core, give1, give2)):
        for group in range(GROUPS):
            at = pl.multiple_of((owner * GROUPS + group) * 384, 128)
            b0, b1, b2 = (
                qkv_ref[:, pl.ds(at + 128 * part, 128)].astype(F32) for part in range(3)
            )
            out = out1 if group < 2 else out2
            place = (group % 2) * 384
            turned = pltpu.roll(b0, HD, 1), pltpu.roll(b2, HD, 1)
            out[:, place : place + 128] = jnp.where(low, b0, b1).astype(BF)
            out[:, place + 128 : place + 256] = jnp.where(low, *turned).astype(BF)
            out[:, place + 256 : place + 384] = jnp.where(low, b1, b2).astype(BF)
        out1[:, 768:] = side
    for owner, out in ((core, in_keep), (1 - core, in_give)):
        for block in range(CHIPS):
            at = pl.multiple_of((2 * block + owner) * 128, 128)
            out[:, block * 128 : block * 128 + 128] = in_ref[:, pl.ds(at, 128)]
    folded[:rows, :] = out_w_ref[:, : D // 2]
    folded[rows:, :] = out_w_ref[:, D // 2 :]


def cut(where, qkv_rows, in_rows, out_rows, vectors, labels):
    rows = qkv_rows.shape[0]
    widths = (896, 896, 768, 768, 2048, 2048)
    return pl.pallas_call(
        cut_kernel,
        out_shape=tuple(shaped(rows, width, BF) for width in widths)
        + (shaped(2 * rows, D // 2, BF),),
        in_specs=[SMEM] + [VMEM] * 10,
        out_specs=(VMEM,) * 7,
        scratch_shapes=[pltpu.VMEM((128, 128), F32), pltpu.VMEM((rows, 128), F32)],
        cost_estimate=cost(0, 8 * rows * 4 * D),
        name="cut",
    )(where, qkv_rows, in_rows, out_rows, *[vector.reshape(1, -1) for vector in vectors], labels)


def turn(value, cosine, forth, back):
    return (
        value * cosine
        + pltpu.roll(value, 128 - ROT // 2, 1) * forth
        + pltpu.roll(value, ROT // 2, 1) * back
    )


def marks_kernel(where_ref, a_ref, b_ref, speed_ref, forth_ref, back_ref, bias_ref, cos_ref, to_ref, from_ref, side_ref):
    seq = pl.program_id(0)
    line, core = where_ref[0] // 4, where_ref[1]

    @pl.when(seq == 0)
    def _():
        side_ref[:128, :] = a_ref[...].astype(F32)
        side_ref[128:, :] = b_ref[...].astype(F32)

    owner = jnp.where(seq < 2, core, 1 - core)
    low = lanes_low(1)
    chunks = []
    for back in range(3):
        other = line - back
        relative = jnp.where(other >= 0, other, 0) ^ line
        block = relative // 2 + 2 * (relative % 2)
        rows = side_ref[pl.ds(pl.multiple_of(block * 64 + owner * 32, 8), 8), :]
        rows = jnp.where(seq % 2 == 0, rows[:4], rows[4:])
        rows = jnp.where(other >= 0, rows, jnp.zeros_like(rows))
        chunks.append(
            [
                jnp.where(low, pltpu.roll(rows[i : i + 1], HD, 1), rows[i + 1 : i + 2])
                for i in (0, 2)
            ]
        )
    total = None
    query = lax.broadcasted_iota(jnp.int32, (128, 256), 1)
    key = lax.broadcasted_iota(jnp.int32, (128, 256), 0)
    mine = jnp.concatenate(chunks[0], axis=1)
    for back, halves in enumerate(chunks):
        for half, labels in enumerate(halves):
            column = jnp.broadcast_to(labels, (128, 128)).T
            column = jnp.concatenate([column, column], axis=1)
            same = column == mine
            if back == 0:
                same = same & (key + 128 * half <= query)
            at = back * 256 + half * 128
            bias_ref[0, at : at + 128, :] = jnp.where(same, 0.0, -1e30)
            count = jnp.sum(jnp.where(same, 1.0, 0.0), axis=0, keepdims=True)
            total = count if total is None else total + count
    for half in range(2):
        position = total[:, 128 * half : 128 * half + 128] - 1.0
        angle = jnp.broadcast_to(position, (128, 128)).T * speed_ref[...]
        here = slice(128 * half, 128 * half + 128)
        cos_ref[here, :] = jnp.cos(angle)
        sine = jnp.sin(angle)
        to_ref[here, :] = sine * forth_ref[...]
        from_ref[here, :] = sine * back_ref[...]


def marks(where, a, b):
    half = ROT // 2
    inverse = 1.0 / 10000.0 ** (jnp.arange(0, ROT, 2, dtype=F32) / ROT)
    speed = jnp.concatenate([inverse, inverse, jnp.zeros((HD - ROT,), F32)])
    speed = jnp.concatenate([speed, speed]).reshape(1, 128)
    lanes = np.arange(128) % HD
    forth = jnp.asarray(-(lanes < half).astype(np.float32)[None, :])
    back = jnp.asarray(((lanes >= half) & (lanes < ROT)).astype(np.float32)[None, :])
    side = pl.BlockSpec((128, 128), lambda i: (0, 6))
    table = pl.BlockSpec((256, 128), lambda i: (i, 0))
    return pl.pallas_call(
        marks_kernel,
        grid=(4,),
        out_shape=(jax.ShapeDtypeStruct((4, 768, 256), F32),) + (shaped(1024, 128, F32),) * 3,
        in_specs=[SMEM, side, side, whole(speed), whole(forth), whole(back)],
        out_specs=(pl.BlockSpec((1, 768, 256), lambda i: (i, 0, 0)), table, table, table),
        scratch_shapes=[pltpu.VMEM((256, 128), F32)],
        cost_estimate=cost(1024 * 128 * 100, 4 * 1024 * 1024),
        name="marks",
    )(where, a, b, speed, forth, back)


def choice_into(me, chosen_ref):
    step = 128
    column = lax.broadcasted_iota(jnp.int32, (1, D), 1)
    place = column // 64
    chip = place % 2 * FAR + (place // 2) % 2 * NEAR + (place // 4) % 2 * X + place // 8 * Y
    wanted = (chip ^ me) * 64 + column % 64

    def some(i, carry):
        here = pl.ds(pl.multiple_of(i * step, step), step)
        row = lax.broadcasted_iota(jnp.int32, (step, D), 0) + i * step
        chosen_ref[here, :] = jnp.where(row == wanted, 1.0, 0.0).astype(BF)
        return carry

    lax.fori_loop(0, D // step, some, 0)


def prepare_kernel(steps, where_ref, own_ref, other_ref, xhat_ref, inv_ref, chosen_ref):
    step = pl.program_id(0)

    @pl.when(step == 0)
    def _():
        choice_into(where_ref[0], chosen_ref)

    def work(rows):
        x = dot(rows, chosen_ref[...])
        average = jnp.mean(x, axis=-1, keepdims=True)
        centered = x - average
        spread = jnp.mean(centered * centered, axis=-1, keepdims=True)
        inv_std = lax.rsqrt(spread + 1e-05)
        xhat_ref[...] = centered * inv_std
        inv_ref[...] = inv_std

    @pl.when(step < steps)
    def _():
        work(own_ref[...])

    @pl.when(step >= steps)
    def _():
        work(other_ref[...])


def prepare(where, own, other):
    rows = own.shape[0]
    step = 256
    steps = rows // step
    return pl.pallas_call(
        partial(prepare_kernel, steps),
        grid=(2 * steps,),
        out_shape=(shaped(2 * rows, D, F32), shaped(2 * rows, 1, F32)),
        in_specs=[
            SMEM,
            pl.BlockSpec((step, D), lambda i: (jnp.minimum(i, steps - 1), 0)),
            pl.BlockSpec((step, D), lambda i: (jnp.maximum(i - steps, 0), 0)),
        ],
        out_specs=(
            pl.BlockSpec((step, D), lambda i: (i, 0)),
            pl.BlockSpec((step, 1), lambda i: (i, 0)),
        ),
        scratch_shapes=[pltpu.VMEM((D, D), BF)],
        cost_estimate=cost(4 * rows * D * D, 16 * rows * D),
        name="prepare",
    )(where, own, other)


def emit_heads(value, tables, outs):
    pairs = [
        (q_ref, kv_ref, pair)
        for q_ref, kv_ref in zip(outs[::2], outs[1::2])
        for pair in range(q_ref.shape[1] // 128)
    ]
    for index, (q_ref, kv_ref, pair) in enumerate(pairs):
        first, q, k = index * 384, pair * 128, pair * 256
        q_ref[:, q : q + 128] = turn(value[:, first : first + 128], *tables).astype(BF)
        kv_ref[:, k : k + 128] = turn(value[:, first + 128 : first + 256], *tables).astype(BF)
        kv_ref[:, k + 128 : k + 256] = value[:, first + 256 : first + 384].astype(BF)


def project_first_kernel(where_ref, xhat_ref, cos_ref, forth_ref, back_ref, *refs):
    pieces, outs = refs[:4], refs[4:8]
    normed_ref, normed_t_ref, more_ref, units_ref, rows_ref, gain_ref, side_ref, bias_ref, two_ref = refs[8:]
    me, core = where_ref[0], where_ref[1]

    @pl.when(pl.program_id(0) == 0)
    def _():
        side_ref[...] = gathered(pieces, slice(768, 896)).astype(F32)
        across = side_ref[...].T
        two_ref[...] = across[:8]
        gain_ref[...] = across[0:1]
        rows_ref[...] = across[2:3] + across[3:4]
        low = lanes_low(1)

        def block(chip, owner):
            start = place_of(chip ^ me) * 64 + owner * 32 + 8
            return side_ref[pl.ds(pl.multiple_of(start, 8), 8), :]

        def pair(one, two):
            return jnp.where(low, pltpu.roll(one, HD, 1), two)

        for group in range(GROUPS):
            heads = []
            for head in range(2):
                chip = core * 8 + 2 * group + head
                zero, one = block(chip, 0), block(chip, 1)
                heads.append((zero[0:1], zero[1:2] + one[1:2], one[2:3]))
            out = bias_ref if group < 2 else more_ref
            for part in range(3):
                at = (group % 2) * 384 + part * 128
                out[:, at : at + 128] = pair(heads[0][part], heads[1][part])
        for chip in range(CHIPS):
            found = block(chip, core)
            units_ref[:, chip * 128 : chip * 128 + 128] = pair(found[3:4], found[4:5])

    normed = (xhat_ref[...] * two_ref[0:1, :] + two_ref[1:2, :]).astype(BF)
    normed_ref[...] = normed
    normed_t_ref[...] = normed.T
    value = dot(normed, gathered(pieces, slice(0, 768))) + bias_ref[...]
    emit_heads(value, (cos_ref[...], forth_ref[...], back_ref[...]), outs)


TWO_PAIRS = (shaped(1024, 128, BF), shaped(1024, 256, BF)) * 2


def rows_spec(columns, step=256):
    return pl.BlockSpec((step, columns), lambda i: (i, 0))


def project_first(where, xhat, tables, pieces):
    small = (shaped(1, 768, F32), shaped(1, 2048, F32), shaped(1, D, F32), shaped(1, D, F32))
    return pl.pallas_call(
        project_first_kernel,
        grid=(4,),
        out_shape=TWO_PAIRS + (shaped(1024, D, BF), shaped(D, 1024, BF)) + small,
        in_specs=[SMEM, rows_spec(D)] + [rows_spec(128)] * 3 + [whole(piece) for piece in pieces],
        out_specs=tuple(rows_spec(shape.shape[1]) for shape in TWO_PAIRS)
        + (rows_spec(D), pl.BlockSpec((D, 256), lambda i: (0, i)))
        + tuple(whole(shape) for shape in small),
        scratch_shapes=[
            pltpu.VMEM((D, 128), F32),
            pltpu.VMEM((1, 768), F32),
            pltpu.VMEM((8, D), F32),
        ],
        cost_estimate=cost(2 * 1024 * D * 768, 12 * 1024 * D),
        name="project_first",
    )(where, xhat, *tables, *pieces)


def project_more_kernel(normed_ref, bias_ref, cos_ref, forth_ref, back_ref, *refs):
    value = dot(normed_ref[...], gathered(refs[:4], slice(512, 1280))) + bias_ref[...]
    emit_heads(value, (cos_ref[...], forth_ref[...], back_ref[...]), refs[4:])


def project_more(normed, bias, tables, pieces):
    return pl.pallas_call(
        project_more_kernel,
        grid=(4,),
        out_shape=TWO_PAIRS,
        in_specs=[rows_spec(D), whole(bias)]
        + [rows_spec(128)] * 3
        + [whole(piece) for piece in pieces],
        out_specs=tuple(rows_spec(shape.shape[1]) for shape in TWO_PAIRS),
        cost_estimate=cost(2 * 1024 * D * 768, 6 * 1024 * D),
        name="project_more",
    )(normed, bias, *tables, *pieces)


def head_rows_kernel(where_ref, *refs):
    keep_ref, give_ref, held_ref = refs[4:]
    me, core = where_ref[0], where_ref[1]
    for index, chip in enumerate(ORDER):
        array, part = LAY[index // 2]
        piece, at = refs[array], part * 128 + index % 2 * 64
        found = chip ^ me
        start = pl.multiple_of((((found // 8) ^ core) * 8 + found % 8) * 32, 32)
        held_ref[pl.ds(start, 32), : D // 2] = piece[at : at + 32, :]
        held_ref[pl.ds(start, 32), D // 2 :] = piece[at + 32 : at + 64, :]
    keep_ref[...] = held_ref[:256, :]
    give_ref[...] = held_ref[256:, :]


def head_rows(where, pieces):
    return pl.pallas_call(
        head_rows_kernel,
        out_shape=(shaped(256, D, BF),) * 2,
        grid=(1,),
        in_specs=[SMEM] + [pl.BlockSpec((256, D // 2), lambda i: (0, 0))] * 4,
        out_specs=(pl.BlockSpec((256, D), lambda i: (0, 0)),) * 2,
        scratch_shapes=[pltpu.VMEM((512, D), BF)],
        cost_estimate=cost(0, 4 * 512 * D),
        name="head_rows",
    )(where, *pieces)


def context_grad_kernel(where_ref, own_ref, other_ref, keep_ref, more_ref, grad_ref, heads_ref):
    core = where_ref[1]
    step = pl.program_id(0)

    @pl.when(step == 0)
    def _():
        for chip in range(8):
            rows = slice(chip * 32, chip * 32 + 32)
            heads_ref[pl.ds(pl.multiple_of(chip * 64 + core * 32, 32), 32), :] = keep_ref[rows, :]
            at = pl.multiple_of(chip * 64 + (1 - core) * 32, 32)
            heads_ref[pl.ds(at, 32), :] = more_ref[rows, :]

    @pl.when(step < 2)
    def _():
        grad_ref[...] = times_transposed(own_ref[...], heads_ref[...]).astype(BF)

    @pl.when(step >= 2)
    def _():
        grad_ref[...] = times_transposed(other_ref[...], heads_ref[...]).astype(BF)


def context_gradient(where, own, other, keep, more):
    return pl.pallas_call(
        context_grad_kernel,
        grid=(4,),
        out_shape=(shaped(1024, D // 2, BF), shaped(D // 2, D, BF)),
        in_specs=[
            SMEM,
            pl.BlockSpec((256, D), lambda i: (jnp.minimum(i, 1), 0)),
            pl.BlockSpec((256, D), lambda i: (jnp.maximum(i - 2, 0), 0)),
            whole(keep),
            whole(more),
        ],
        out_specs=(rows_spec(D // 2), pl.BlockSpec((D // 2, D), lambda i: (0, 0))),
        cost_estimate=cost(1024 * D * D, 6 * 1024 * D),
        name="context_grad",
    )(where, own, other, keep, more)


def attend_kernel(q_ref, do_ref, bias_ref, *refs):
    kv_refs, o_ref, dq_ref, dkv_refs = refs[:3], refs[3], refs[4], refs[5:]
    rows = q_ref.shape[0]
    keys = jnp.concatenate([ref[:, :128] for ref in kv_refs], axis=0)
    values = jnp.concatenate([ref[:, 128:] for ref in kv_refs], axis=0)
    keys_t = keys.T
    values_t = values.T
    scaled = q_ref[...] * 0.125
    given = do_ref[...]
    given_t = given.T.astype(F32)
    lane = lax.broadcasted_iota(jnp.int32, (rows, 128), 1)
    out_t, dq_t, probs_all, ds_all, q_all, g_all = [], [], [], [], [], []
    for head in range(2):
        mine = (lane < HD) if head == 0 else (lane >= HD)
        query = jnp.where(mine, scaled, jnp.zeros_like(scaled))
        grad = jnp.where(mine, given, jnp.zeros_like(given))
        part = slice(head * HD, (head + 1) * HD)
        scores = times_transposed(keys, query) + bias_ref[0]
        top = jnp.max(scores, axis=0, keepdims=True)
        unscaled = jnp.exp(scores - top)
        total = jnp.sum(unscaled, axis=0, keepdims=True)
        probs = unscaled * (1.0 / total)
        rounded = probs.astype(BF)
        out_t.append(dot(values_t[part], rounded))
        prob_grad = times_transposed(values, grad)
        inner = jnp.sum(out_t[head] * given_t[part], axis=0, keepdims=True)
        score_grad = (probs * (prob_grad - inner)).astype(BF)
        dq_t.append(dot(keys_t[part], score_grad))
        probs_all.append(rounded)
        ds_all.append(score_grad)
        q_all.append(query)
        g_all.append(grad)
    o_ref[...] = jnp.concatenate(out_t, axis=0).T.astype(BF)
    dq_ref[...] = (jnp.concatenate(dq_t, axis=0).T * 0.125).astype(BF)
    dk = dot(jnp.concatenate(ds_all, axis=1), jnp.concatenate(q_all, axis=0))
    dv = dot(jnp.concatenate(probs_all, axis=1), jnp.concatenate(g_all, axis=0))
    for chunk, ref in enumerate(dkv_refs):
        ref[:, :128] = dk[chunk * rows : (chunk + 1) * rows].astype(ref.dtype)
        ref[:, 128:] = dv[chunk * rows : (chunk + 1) * rows].astype(ref.dtype)


def attend(first, query, grad, bias, kvs):
    pairs = query.shape[1] // 128
    narrow = pl.BlockSpec((256, 128), lambda b, p: (b, p))
    wide = pl.BlockSpec((256, 256), lambda b, p: (b, p))
    return pl.pallas_call(
        attend_kernel,
        grid=(4, pairs),
        out_shape=(shaped(1024, 128 * pairs, BF),) * 2
        + (shaped(1024, 256 * pairs, F32),)
        + (shaped(1024, 256 * pairs, BF),) * 2,
        in_specs=[
            narrow,
            pl.BlockSpec((256, 128), lambda b, p: (b, first + p)),
            pl.BlockSpec((1, 768, 256), lambda b, p: (b, 0, 0)),
        ]
        + [wide] * 3,
        out_specs=(narrow, narrow) + (wide,) * 3,
        cost_estimate=cost(
            pairs * 24 * 4 * 256 * 768 * 128, pairs * 9 * 1024 * 1024, pairs * 8 * 256 * 768
        ),
        name="attend",
    )(query, grad, bias, *kvs)


def unturn_kernel(groups, cos_ref, forth_ref, back_ref, *refs):
    cosine, forth, back = cos_ref[...], -forth_ref[...], -back_ref[...]
    out_ref, sum_ref = refs[-2:]
    first = 0
    for group in range(groups):
        dq_ref, own_ref, more_ref = refs[3 * group : 3 * group + 3]
        for pair in range(dq_ref.shape[1] // 128):
            here = slice(pair * 256, pair * 256 + 256)
            kv = (own_ref[:, here] + more_ref[:, here].astype(F32)).astype(BF)
            key = kv[:, :128].astype(F32)
            query = dq_ref[:, pair * 128 : pair * 128 + 128].astype(F32)
            out_ref[:, first : first + 128] = turn(query, cosine, forth, back).astype(BF)
            out_ref[:, first + 128 : first + 256] = turn(key, cosine, forth, back).astype(BF)
            out_ref[:, first + 256 : first + 384] = kv[:, 128:]
            first += 384

    @pl.when(pl.program_id(0) == 0)
    def _():
        sum_ref[...] = jnp.zeros_like(sum_ref)

    sum_ref[...] += jnp.sum(out_ref[...].astype(F32), axis=0, keepdims=True)


def unturn(tables, triples):
    rows = triples[0][0].shape[0]
    step = 256
    width = 3 * sum(dq.shape[1] for dq, _, _ in triples)

    def spec(columns):
        return pl.BlockSpec((step, columns), lambda i: (i, 0))

    specs, arrays = [], []
    for dq, own, more in triples:
        specs += [spec(dq.shape[1]), spec(own.shape[1]), spec(more.shape[1])]
        arrays += [dq, own, more]
    return pl.pallas_call(
        partial(unturn_kernel, len(triples)),
        grid=(rows // step,),
        out_shape=(
            jax.ShapeDtypeStruct((rows, width), BF),
            jax.ShapeDtypeStruct((1, width), F32),
        ),
        in_specs=[spec(128)] * 3 + specs,
        out_specs=(spec(width), pl.BlockSpec((1, width), lambda i: (0, 0))),
        cost_estimate=cost(rows * width * 10, rows * width * 8),
        name="unturn",
    )(*tables, *arrays)


ROOT_HALF = math.sqrt(0.5)
DENSITY = 1.0 / math.sqrt(2.0 * math.pi)


def gelu_and_slope(value):
    share = 0.5 + 0.5 * lax.erf(value * ROOT_HALF)
    return value * share, share + value * (DENSITY * jnp.exp(-0.5 * value * value))


def hidden_kernel(normed_ref, bias_ref, *refs):
    act_ref, act_t_ref, slope_ref = refs[-3:]
    rows = 256
    weight = gathered(refs[:4])

    def some(i, carry):
        here = pl.ds(pl.multiple_of(i * rows, rows), rows)
        value = dot(normed_ref[here, :], weight) + bias_ref[...]
        act, slope = gelu_and_slope(value)
        act = act.astype(BF)
        act_ref[here, :] = act
        act_t_ref[:, here] = act.T
        slope_ref[here, :] = slope
        return carry

    lax.fori_loop(0, normed_ref.shape[0] // rows, some, 0)


def hidden(normed, pieces, bias):
    rows, width = normed.shape[0], bias.shape[1]
    column = pl.BlockSpec((rows, 256), lambda j: (0, j))
    return pl.pallas_call(
        hidden_kernel,
        grid=(width // 256,),
        out_shape=(shaped(rows, width, BF), shaped(width, rows, BF), shaped(rows, width, F32)),
        in_specs=[whole(normed), pl.BlockSpec((1, 256), lambda j: (0, j))]
        + [pl.BlockSpec((piece.shape[0], 256), lambda j: (0, j)) for piece in pieces],
        out_specs=(column, pl.BlockSpec((256, rows), lambda j: (j, 0)), column),
        cost_estimate=cost(2 * rows * D * width + 50 * rows * width, 9 * rows * width),
        name="hidden",
    )(normed, bias, *pieces)


def fetch_units(me, pieces, w_ref, sem):
    copies = []
    for index, chip in enumerate(ORDER):
        first = pl.multiple_of((me ^ chip) * 128, 128)
        array, part = LAY[index // 2]
        copies.append(
            pltpu.make_async_copy(
                pieces[array].at[pl.ds(part * 256 + index % 2 * 128, 128), :],
                w_ref.at[pl.ds(first, 128), :],
                sem,
            )
        )
    for copy in copies:
        copy.start()
    return copies


def unit_back_kernel(where_ref, own_ref, other_ref, slope_ref, *refs):
    hg_ref, sum_ref, w_ref, sem = refs[4:]
    j = pl.program_id(0)
    step = hg_ref.shape[1]

    @pl.when(j == 0)
    def _():
        for copy in fetch_units(where_ref[0], refs[:4], w_ref, sem):
            copy.wait()

    w = w_ref[pl.ds(pl.multiple_of(j * step, step), step), :]
    total = None
    rows = own_ref.shape[0]
    for half, g_ref in enumerate((own_ref, other_ref)):
        here = slice(half * rows, half * rows + rows)
        grad = (times_transposed(g_ref[...], w) * slope_ref[here, :]).astype(BF)
        hg_ref[here, :] = grad
        part = jnp.sum(grad.astype(F32), axis=0, keepdims=True)
        total = part if total is None else total + part
    sum_ref[...] = total


def unit_back(where, own, other, slope, pieces):
    rows, width = slope.shape
    step = 512
    column = pl.BlockSpec((rows, step), lambda j: (0, j))
    return pl.pallas_call(
        unit_back_kernel,
        grid=(width // step,),
        out_shape=(shaped(rows, width, BF), shaped(1, width, F32)),
        in_specs=[SMEM, whole(own), whole(other), column] + [ANY] * 4,
        out_specs=(column, pl.BlockSpec((1, step), lambda j: (0, j))),
        scratch_shapes=[pltpu.VMEM((width, D), BF), pltpu.SemaphoreType.DMA],
        cost_estimate=cost(2 * rows * D * width, 8 * rows * width),
        name="unit_back",
    )(where, own, other, slope, *pieces)


def unit_out_kernel(where_ref, act_ref, heads_ref, *refs):
    contexts, pieces = refs[:4], refs[4:8]
    mine_ref, theirs_ref, w_ref, sem = refs[8:]
    step = pl.program_id(0)

    @pl.when(step == 0)
    def _():
        for copy in fetch_units(where_ref[0], pieces, w_ref, sem):
            copy.wait()

    def term():
        context = jnp.concatenate([ref[...] for ref in contexts], axis=1)
        return dot(act_ref[...], w_ref[...]) + dot(context, heads_ref[...])

    @pl.when(step < 2)
    def _():
        mine_ref[...] = term()

    @pl.when(step >= 2)
    def _():
        theirs_ref[...] = term()


def unit_out(where, act, heads, contexts, pieces):
    rows, width = act.shape
    return pl.pallas_call(
        unit_out_kernel,
        grid=(4,),
        out_shape=(shaped(rows // 2, D, F32),) * 2,
        in_specs=[SMEM, rows_spec(width), whole(heads)] + [rows_spec(128)] * 4 + [ANY] * 4,
        out_specs=(
            pl.BlockSpec((256, D), lambda i: (jnp.minimum(i, 1), 0)),
            pl.BlockSpec((256, D), lambda i: (jnp.maximum(i - 2, 0), 0)),
        ),
        scratch_shapes=[pltpu.VMEM((width, D), BF), pltpu.SemaphoreType.DMA],
        cost_estimate=cost(3 * rows * D * width, 6 * rows * width),
        name="unit_out",
    )(where, act, heads, *contexts, *pieces)


def row_grads_kernel(steps, where_ref, left_ref, right_ref, *refs):
    out_refs = refs[-6:]
    spots = [[place_of(chip) for chip in chips] for chips in BLOCKS.values()]

    @pl.when(pl.program_id(0) < steps)
    def _():
        value = dot(left_ref[...], right_ref[...]).astype(BF)
        for places, ref in zip(spots, out_refs):
            for at, place in enumerate(places):
                ref[at * 64 : at * 64 + 64, :] = value[place * 64 : place * 64 + 64]

    if len(refs) == 7:
        held_ref = refs[0]
        me, core = where_ref[0], where_ref[1]

        @pl.when(pl.program_id(0) >= steps)
        def _():
            for chips, ref in zip(BLOCKS.values(), out_refs):
                for at, chip in enumerate(chips):
                    found = chip ^ me
                    start = (((found // 8) ^ core) * 8 + found % 8) * 32
                    rows = held_ref[pl.ds(pl.multiple_of(start, 32), 32), :]
                    ref[at * 64 : at * 64 + 32, :] = rows[:, : D // 2]
                    ref[at * 64 + 32 : at * 64 + 64, :] = rows[:, D // 2 :]


def row_grads(where, left, right, more=None):
    rows, tokens = left.shape
    step = 512
    steps = right.shape[1] // step
    columns = right.shape[1] + (0 if more is None else D // 2)
    heights = [64 * len(chips) for chips in BLOCKS.values()]
    return pl.pallas_call(
        partial(row_grads_kernel, steps),
        grid=(columns // step,),
        out_shape=tuple(shaped(height, columns, BF) for height in heights),
        in_specs=[
            SMEM,
            whole(left),
            pl.BlockSpec((tokens, step), lambda j: (0, jnp.minimum(j, steps - 1))),
        ]
        + ([] if more is None else [whole(more)]),
        out_specs=tuple(pl.BlockSpec((height, step), lambda j: (0, j)) for height in heights),
        cost_estimate=cost(2 * rows * tokens * columns, 2 * (rows * tokens + rows * columns)),
        name="row_grads",
    )(where, left, right, *([] if more is None else [more]))


def unit_grads_kernel(order_ref, *refs):
    lefts, own_ref, other_ref, out_refs = refs[:4], refs[4], refs[5], refs[6:]
    left = stack(lefts)
    tokens = own_ref.shape[0]
    value = dot(left[:, :tokens], own_ref[...]) + dot(left[:, tokens:], other_ref[...])
    value = value.astype(BF)
    a, xa, b, yb, yax, xby = out_refs
    for piece, outs in enumerate(((a, xa), (b, yb), (yax,), (xby,))):

        @pl.when(pl.program_id(0) == piece)
        def _(outs=outs):
            rows = 512 // len(outs)
            for at, ref in enumerate(outs):
                ref[...] = value[at * rows : at * rows + rows]


def unit_grads(me, left, own, other):
    tokens = left.shape[1]
    order = jnp.asarray(np.array(sum(SUMS.values(), []), np.int32)) ^ me

    def block(place):
        return pl.BlockSpec((128, tokens), lambda k, order: (order[4 * k + place], 0))

    return pl.pallas_call(
        unit_grads_kernel,
        out_shape=tuple(shaped(128 * len(chips), D, BF) for chips in BLOCKS.values()),
        grid_spec=pltpu.PrefetchScalarGridSpec(
            num_scalar_prefetch=1,
            grid=(4,),
            in_specs=[block(place) for place in range(4)] + [whole(own), whole(other)],
            out_specs=tuple(
                pl.BlockSpec((128 * len(chips), D), lambda k, order: (0, 0))
                for chips in BLOCKS.values()
            ),
        ),
        cost_estimate=cost(2 * tokens * D * 2048, 4 * 2048 * D),
        name="unit_grads",
    )(order, left, left, left, left, own, other)


def out_grad_kernel(where_ref, own_ref, other_ref, *refs):
    contexts, keep_ref, give_ref = refs[:4], refs[4], refs[5]
    first = where_ref[1] == 0
    tokens = own_ref.shape[0]
    for group in range(4):

        @pl.when(pl.program_id(0) == group)
        def _(group=group):
            across = contexts[group][...].T
            value = dot(across[:, :tokens], own_ref[...]) + dot(across[:, tokens:], other_ref[...])
            value = value.astype(BF)
            for head in range(2):
                zero, one = value[head * 64 : head * 64 + 32], value[head * 64 + 32 : head * 64 + 64]
                rows = slice(head * 32, head * 32 + 32)
                keep_ref[rows, :] = jnp.where(first, zero, one)
                give_ref[rows, :] = jnp.where(first, one, zero)


def out_grad(where, own, other, contexts):
    block = pl.BlockSpec((64, D), lambda i: (i, 0))
    return pl.pallas_call(
        out_grad_kernel,
        grid=(4,),
        out_shape=(shaped(256, D, BF),) * 2,
        in_specs=[SMEM, whole(own), whole(other)] + [whole(context) for context in contexts],
        out_specs=(block, block),
        cost_estimate=cost(1024 * D * D, 6 * 1024 * D),
        name="out_grad",
    )(where, own, other, *contexts)


def norm_grad_kernel(spans, qkv_ref, hidden_ref, *refs):
    mine_ref, theirs_ref = refs[-2:]
    width = qkv_ref.shape[1] // 2
    lefts = (qkv_ref[:, :width], qkv_ref[:, width:], hidden_ref[...])
    for step, out_ref in ((0, mine_ref), (1, theirs_ref)):

        @pl.when(pl.program_id(0) // 2 == step)
        def _(out_ref=out_ref):
            for pair in range(4):
                total = None
                for line, (left, span) in enumerate(zip(lefts, spans)):
                    right = gathered(
                        refs[4 * line : 4 * line + 4], slice(*span), slice(2 * pair, 2 * pair + 2)
                    )
                    part = times_transposed(left, right)
                    total = part if total is None else total + part
                out_ref[:, 256 * pair : 256 * pair + 256] = total


def norm_grad(projected_grad, hidden_grad, lines, spans):
    rows = projected_grad.shape[0]
    flat = [piece for line in lines for piece in line]
    return pl.pallas_call(
        partial(norm_grad_kernel, spans),
        grid=(4,),
        out_shape=(shaped(rows // 2, D, F32),) * 2,
        in_specs=[rows_spec(projected_grad.shape[1]), rows_spec(hidden_grad.shape[1])]
        + [whole(piece) for piece in flat],
        out_specs=(
            pl.BlockSpec((256, D), lambda i: (jnp.minimum(i, 1), 0)),
            pl.BlockSpec((256, D), lambda i: (jnp.maximum(i - 2, 0), 0)),
        ),
        cost_estimate=cost(7 * rows * D * D, 12 * rows * D),
        name="norm_grad",
    )(projected_grad, hidden_grad, *flat)


def norm_back_kernel(
    where_ref, part_ref, more_ref, xhat_ref, inv_ref, gain_ref, g_ref, out_ref, sum_ref, chosen_ref
):
    @pl.when(pl.program_id(0) == 0)
    def _():
        choice_into(where_ref[0], chosen_ref)
        sum_ref[...] = jnp.zeros_like(sum_ref)

    grad = part_ref[...] + more_ref[...]
    xhat = xhat_ref[...]
    scaled = grad * gain_ref[...]
    value = (
        scaled
        - jnp.mean(scaled, axis=-1, keepdims=True)
        - xhat * jnp.mean(scaled * xhat, axis=-1, keepdims=True)
    ) * inv_ref[...]
    high = value.astype(BF)
    low = (value - high.astype(F32)).astype(BF)
    value = times_transposed(high, chosen_ref[...]) + times_transposed(low, chosen_ref[...])
    out_ref[...] = (g_ref[...].astype(F32) + value).astype(BF)
    sum_ref[0:1, :] += jnp.sum(grad * xhat, axis=0, keepdims=True)
    sum_ref[1:2, :] += jnp.sum(grad, axis=0, keepdims=True)


def norm_back(where, part, more, xhat, inv_std, gain, grad):
    rows = grad.shape[0]
    one = pl.BlockSpec((1, D), lambda i: (0, 0))
    return pl.pallas_call(
        norm_back_kernel,
        grid=(rows // 256,),
        out_shape=(shaped(rows, D, BF), shaped(8, D, F32)),
        in_specs=[SMEM] + [rows_spec(D)] * 3 + [rows_spec(1), one, rows_spec(D)],
        out_specs=(rows_spec(D), pl.BlockSpec((8, D), lambda i: (0, 0))),
        scratch_shapes=[pltpu.VMEM((D, D), BF)],
        cost_estimate=cost(4 * rows * D * D, 16 * rows * D),
        name="norm_back",
    )(where, part, more, xhat, inv_std, gain, grad)


def paste_in_kernel(where_ref, mine_ref, other_ref, out_ref):
    core = where_ref[1]
    for owner, ref in ((core, mine_ref), (1 - core, other_ref)):
        for block in range(CHIPS):
            at = pl.multiple_of((2 * block + owner) * 128, 128)
            out_ref[:, pl.ds(at, 128)] = ref[:, block * 128 : block * 128 + 128]


def paste_qkv_kernel(where_ref, mine_ref, other_ref, out_ref):
    core = where_ref[1]
    low = lanes_low(mine_ref.shape[0])
    for owner, ref in ((core, mine_ref), (1 - core, other_ref)):
        for group in range(GROUPS):
            q, k, v = (
                ref[:, group * 384 + part * 128 : group * 384 + part * 128 + 128]
                for part in range(3)
            )
            turned = pltpu.roll(k, HD, 1)
            blocks = (jnp.where(low, q, turned), jnp.where(low, v, q), jnp.where(low, turned, v))
            for part, value in enumerate(blocks):
                at = (owner * GROUPS + group) * 384 + part * 128
                out_ref[:, pl.ds(pl.multiple_of(at, 128), 128)] = value


def paste(kernel, where, mine, other):
    return pl.pallas_call(
        kernel,
        out_shape=shaped(mine.shape[0], 2 * mine.shape[1], F32),
        in_specs=[SMEM, VMEM, VMEM],
        out_specs=VMEM,
        cost_estimate=cost(0, 16 * mine.shape[0] * mine.shape[1]),
        name="paste",
    )(where, mine, other)


def local_fast(
    hidden_in,
    document_labels,
    cotangent,
    ln_gain,
    ln_bias,
    qkv_weight,
    qkv_bias,
    out_weight,
    out_bias,
    fc_in_weight,
    fc_in_bias,
    fc_out_weight,
    fc_out_bias,
):
    local_seqs, tok_count = hidden_in.shape[:2]
    row_count = local_seqs * tok_count
    d_rows = qkv_weight.shape[0]
    f_rows = fc_out_weight.shape[0]
    units = fc_in_weight.shape[1] // 2
    pair = 2
    core = lax.axis_index("fsdp") % 2
    me = lax.axis_index("seq") * 4 + lax.axis_index("fsdp") // 2
    clock = Clock(jnp.stack([me, core]).astype(jnp.int32))
    box = {}

    waiting = []

    def slot(jobs, work=None, *inputs, chain=None, late=()):
        nonlocal waiting
        jobs, late = list(jobs), list(late)
        name, follow, more = chain if chain is not None else (None, None, ())
        gated, given, more = clock.join(tuple(job[2] for job in jobs + late), inputs, tuple(more))
        values = [job[3](value) for job, value in zip(jobs + late, gated)]
        made = work(*given) if work is not None else ()
        after = ()
        for job, value in zip(jobs, values):
            if chain is not None and job[1] == name:
                after = follow(value, *more)
        ended, values, older = waiting, values[: len(jobs)], values[len(jobs) :]
        found = values + [value for _, value in ended]
        found, made, after = clock.join(tuple(found), made, after)
        for job, value in zip(jobs + [job for job, _ in ended], found):
            job[0][job[1]] = value
        waiting = list(zip(late, older))
        return made if chain is None else (made, after)

    def moves(line, stage):
        return [
            (line.parts, name, line.parts[source], partial(cross, bit=bit))
            for name, source, bit in line.jobs(stage)
        ]

    def core_move(name, value):
        return (box, name, value, other_core)

    def pick(halves):
        first = core == 0
        return jnp.where(first, halves[0], halves[1]), jnp.where(first, halves[1], halves[0])

    def joined(mine, other):
        first = core == 0
        return jnp.concatenate(
            [jnp.where(first, mine, other), jnp.where(first, other, mine)], axis=0
        )

    x_own = hidden_in.reshape(row_count, D)
    g_own = cotangent.reshape(row_count, D)
    vectors = (ln_gain, ln_bias, qkv_bias, out_bias, fc_in_bias, fc_out_bias)
    keep1, give1, keep2, give2, in_keep, in_give, folded = cut(
        clock.token, qkv_weight, fc_in_weight, out_weight, vectors, document_labels
    )
    slot([core_move("give1", give1)])
    line_a = Gather(joined(keep1, box["give1"]))
    slot(moves(line_a, "far") + [core_move("x", x_own), core_move("give2", give2)])
    line_b = Gather(jnp.concatenate([folded, joined(keep2, box["give2"])], axis=1))
    line_d = Gather(fc_out_weight)
    slot(moves(line_a, "near") + moves(line_b, "far") + [core_move("in", in_give), core_move("g", g_own)])
    g_more = box["g"]
    bias, *tables = slot(
        moves(line_a, "first") + moves(line_b, "near"),
        lambda a, b: marks(clock.token, a, b),
        line_a.parts["a"],
        line_a.parts["b"],
    )
    line_c = Gather(joined(in_keep, box["in"]))
    (xhat, inv_std), grad_sum = slot(
        moves(line_a, "second") + moves(line_c, "far"),
        lambda own, other, g: (
            prepare(clock.token, own, other),
            jnp.sum(g.astype(F32), axis=0),
        ),
        x_own,
        box["x"],
        g_own,
    )
    a_pieces = line_a.pieces()
    made = slot(
        moves(line_b, "first") + moves(line_c, "near"),
        lambda xhat, tables, pieces: project_first(clock.token, xhat, tables, pieces),
        xhat,
        tables,
        a_pieces,
    )
    queries, kvs = [made[0], made[2]], [[made[1]], [made[3]]]
    normed, normed_t, b_more, b_in, b_rows, gain = made[4:]
    moved, results, backs = {}, {}, {}

    def up(group, hop):
        return (moved, (group, hop), kvs[group][hop], partial(shift, by=1))

    def landed(*found):
        for group, hop in found:
            kvs[group].append(moved[group, hop])

    def down(group, hop):
        value = results[group][4]
        if hop == 1:
            value = (results[group][3].astype(F32) + backs[group, 0].astype(F32)).astype(BF)
        return (backs, (group, hop), value, partial(shift, by=-1))

    def attention(*groups):
        def work(*given):
            return [attend(group, *args) for group, args in zip(groups, given)]

        return work, *[
            (queries[group], context_grad, bias, tuple(kvs[group])) for group in groups
        ]

    def attended(groups, found):
        for group, result in zip(groups, found):
            results[group] = result

    slot(moves(line_b, "second") + [up(0, 0)], late=moves(line_d, "far"))
    landed((0, 0))
    b_pieces = line_b.pieces()
    made, (out_keep, out_give) = slot(
        moves(line_c, "first") + [up(0, 1)],
        lambda normed, bias, tables, pieces: (
            project_more(normed, bias, tables, pieces),
            head_rows(clock.token, pieces),
        ),
        normed,
        b_more,
        tables,
        b_pieces,
    )
    landed((0, 1))
    queries += [made[0], made[2]]
    kvs += [[made[1]], [made[3]]]

    def first_attention(out_more, g_own, g_more, out_keep, query, bias, kvs):
        grad, heads = context_gradient(clock.token, g_own, g_more, out_keep, out_more)
        return grad, heads, attend(0, query, grad, bias, kvs)

    _, (context_grad, out_heads, found) = slot(
        moves(line_c, "second") + moves(line_d, "near") + [up(1, 0), core_move("out", out_give)],
        chain=(
            "out",
            first_attention,
            (g_own, g_more, out_keep, queries[0], bias, tuple(kvs[0])),
        ),
    )
    results[0] = found
    landed((1, 0))
    c_pieces = line_c.pieces()
    act, act_t, slope = slot(
        moves(line_d, "first") + [up(1, 1), up(2, 0), down(0, 0)],
        lambda normed, b_in, pieces: hidden(normed, pieces, b_in),
        normed,
        b_in,
        c_pieces,
    )
    landed((1, 1), (2, 0))
    work, *given = attention(1)

    def with_units(given, act_t, own, other):
        return work(given), unit_grads(clock.token[0], act_t, own, other)

    found, fc_parts = slot(
        moves(line_d, "second") + [up(2, 1), up(3, 0), down(0, 1)],
        with_units,
        *given,
        act_t,
        g_own,
        g_more,
    )
    attended([1], found)
    landed((2, 1), (3, 0))
    d_pieces = line_d.pieces()
    sum_fc = Scatter(fc_parts)
    work2, *given = attention(2)
    attended([2], slot([up(3, 1), down(1, 0)], work2, *given, late=moves(sum_fc, "first")))
    landed((3, 1))
    work3, *given = attention(3)

    def last_attention(given, earlier, own, other):
        found = work3(given)
        contexts = earlier + [found[0][0]]
        return found, contexts, out_grad(clock.token, own, other, contexts)

    found, contexts, (out_keep, out_give) = slot(
        [down(1, 1)],
        last_attention,
        *given,
        [results[group][0] for group in range(3)],
        g_own,
        g_more,
    )
    attended([3], found)

    def units_back(out_more, out_keep, normed_t, own, other, slope, pieces):
        hidden_grad, hidden_sum = unit_back(clock.token, own, other, slope, pieces)
        more = jnp.concatenate([out_keep, out_more], axis=0)
        return hidden_grad, hidden_sum, row_grads(clock.token, normed_t, hidden_grad, more)

    _, (hidden_grad, hidden_sum, in_parts) = slot(
        moves(sum_fc, "second") + [down(2, 0), down(3, 0), core_move("out_grad", out_give)],
        chain=("out_grad", units_back, (out_keep, normed_t, g_own, g_more, slope, d_pieces)),
    )
    sum_in = Scatter(in_parts)
    out_mine, out_theirs = slot(
        moves(sum_in, "first") + [down(2, 1), down(3, 1)],
        lambda act, heads, contexts, pieces: unit_out(clock.token, act, heads, contexts, pieces),
        act,
        out_heads,
        contexts,
        d_pieces,
    )

    def last_grads(normed_t, tables, triples):
        projected_grad, total = unturn(tables, triples)
        return projected_grad, total, row_grads(clock.token, normed_t, projected_grad)

    projected_grad, qkv_bias_sum, parts = slot(
        moves(sum_in, "second") + moves(sum_fc, "near") + [core_move("out_side", out_theirs)],
        last_grads,
        normed_t,
        tables,
        [(results[group][1], results[group][2], backs[group, 1]) for group in range(GROUPS)],
    )
    sum_qkv = Scatter(parts)
    norm_mine, norm_theirs = slot(
        moves(sum_qkv, "first") + moves(sum_in, "near") + moves(sum_fc, "far"),
        lambda projected_grad, hidden_grad, *lines: norm_grad(
            projected_grad, hidden_grad, lines, ((0, 768), (512, 1280), (0, units))
        ),
        projected_grad,
        hidden_grad,
        a_pieces,
        b_pieces,
        c_pieces,
    )

    def finish_output(x_own, out_mine, out_more, b_rows):
        order = jnp.asarray(np.array(ORDER, np.int32)) ^ me
        spots = place_of(jnp.arange(CHIPS, dtype=jnp.int32) ^ me)
        b_rows = b_rows.reshape(CHIPS, 2 * d_rows)[spots].reshape(1, D)
        return (x_own.astype(F32) + out_mine + out_more + b_rows).astype(BF)

    def small_rows(norm_sums, qkv_bias_sum, hidden_sum, grad_sum):
        spots = place_of(jnp.arange(CHIPS, dtype=jnp.int32) ^ me)
        norm_sums = norm_sums[:2].reshape(2, CHIPS, 2, d_rows)[:, spots].reshape(2, D)
        mine = (jnp.arange(2) == core)[:, None]
        qkv_full = (
            jnp.where(mine, qkv_bias_sum, 0.0)
            .reshape(2, GROUPS, 3, pair, HD)
            .transpose(0, 1, 3, 2, 4)
            .reshape(3 * D)
        )
        in_full = jnp.where(mine[None], hidden_sum.reshape(CHIPS, 1, f_rows), 0.0)
        packed = jnp.concatenate(
            [
                vector.reshape(2 * CHIPS, -1)
                for vector in (norm_sums[0], norm_sums[1], qkv_full, grad_sum, in_full)
            ],
            axis=1,
        ).reshape(CHIPS, -1)
        return packed[jnp.asarray(np.array(ORDER, np.int32)) ^ me]

    def back_work(norm_more, norm_mine, xhat, inv_std, gain, g_own, *sums):
        input_grad, norm_sums = norm_back(
            clock.token, norm_mine, norm_more, xhat, inv_std, gain, g_own
        )
        return input_grad, small_rows(norm_sums, *sums)

    output, (input_grad, packed) = slot(
        moves(sum_qkv, "second") + moves(sum_in, "far") + [core_move("norm", norm_theirs)],
        finish_output,
        x_own,
        out_mine,
        box["out_side"],
        b_rows,
        chain=(
            "norm",
            back_work,
            (norm_mine, xhat, inv_std, gain, g_own, qkv_bias_sum, hidden_sum, grad_sum),
        ),
    )

    def fold(bit):
        return (box, "fold", packed[packed.shape[0] // 2 :], partial(cross, bit=bit))

    def half_sum():
        return packed[: packed.shape[0] // 2] + box["fold"]

    def two_folds(value, rows):
        half = rows[: rows.shape[0] // 2] + value
        give = half[half.shape[0] // 2 :]
        return half[: half.shape[0] // 2] + cross(give, X)

    in_rows = sum_in.result()
    in_keep, in_give = pick(in_rows[:, :units].reshape(2, d_rows, units))
    out_weight_grad = in_rows[:, units:].reshape(2, d_rows, D // 2)
    _, packed = slot(
        moves(sum_qkv, "near") + [fold(Y), core_move("in_rows", in_give)],
        chain=("fold", two_folds, (packed,)),
    )
    fc_in_weight_grad = slot(
        moves(sum_qkv, "far") + [fold(NEAR)],
        lambda mine, other: paste(paste_in_kernel, clock.token, mine, other),
        in_keep,
        box["in_rows"],
    )
    packed = half_sum()
    qkv_keep, qkv_give = pick(sum_qkv.result().reshape(2, d_rows, -1))
    slot([core_move("qkv_rows", qkv_give), fold(FAR)])
    sums_keep, sums_give = pick(half_sum().reshape(2, -1))
    sums = sums_keep + other_core(sums_give)
    parts = []
    first = 0
    for width in (d_rows, d_rows, 3 * d_rows, d_rows, f_rows):
        parts.append(sums[first : first + width])
        first += width
    return (
        output.reshape(local_seqs, tok_count, D),
        input_grad.reshape(local_seqs, tok_count, D),
        parts[0],
        parts[1],
        paste(paste_qkv_kernel, clock.token, qkv_keep, box["qkv_rows"]),
        parts[2],
        jnp.concatenate([out_weight_grad[0], out_weight_grad[1]], axis=1),
        parts[3],
        fc_in_weight_grad,
        parts[4],
        sum_fc.result(),
        parts[3],
    )


def solution(mesh):
    rows = P(("seq", "fsdp"))
    wide = P(("seq", "fsdp"), None)
    act = P("fsdp", "seq", None)
    placed = (act, P("fsdp", "seq"), act) + (rows, rows) + (wide, rows) * 4
    small = dict(mesh.shape) == {"seq": 4, "fsdp": 8}
    return jax.shard_map(
        local_fast if small else local_plain,
        mesh=mesh,
        in_specs=placed,
        out_specs=(act, act, rows, rows) + (wide, rows) * 4,
        check_vma=False,
    )
```

```python
from functools import partial
import math

import jax
import jax.numpy as jnp
import numpy as np
from jax import lax
from jax.experimental import pallas as pl
from jax.experimental.pallas import tpu as pltpu
from jax.sharding import PartitionSpec as P

D = 1024
H = 16
HD = 64
ROT = 16
GROUPS = 4
BF = jnp.bfloat16
F32 = jnp.float32


def rotate(values, cosine, sine_part):
    half_rot = ROT // 2
    first_part = values[..., :half_rot]
    second_part = values[..., half_rot:ROT]
    return jnp.concatenate(
        [
            first_part * cosine - second_part * sine_part,
            second_part * cosine + first_part * sine_part,
            values[..., ROT:],
        ],
        axis=-1,
    )


def position_angles(segments):
    length = segments.shape[0]
    places = jnp.arange(length, dtype=jnp.int32)
    boundary = jnp.concatenate([jnp.ones((1,), dtype=jnp.bool_), segments[1:] != segments[:-1]])
    starts = lax.cummax(jnp.where(boundary, places, 0), axis=0)
    positions = (places - starts).astype(jnp.float32)
    inverse = 1.0 / 10000.0 ** (jnp.arange(0, ROT, 2, dtype=jnp.float32) / ROT)
    return positions[:, None] * inverse[None, :]


def make_mask(segments, first_row, block_rows):
    length = segments.shape[0]
    query_index = first_row + jnp.arange(block_rows, dtype=jnp.int32)
    key_index = jnp.arange(length, dtype=jnp.int32)
    query_segments = lax.dynamic_slice_in_dim(segments, first_row, block_rows, 0)
    return (key_index[None, :] <= query_index[:, None]) & (
        query_segments[:, None] == segments[None, :]
    )


def outer_product(left, right):
    return lax.dot_general(
        left, right, (((0,), (0,)), ((), ())), preferred_element_type=jnp.float32
    )


def times_transposed(left, right):
    return lax.dot_general(
        left, right, (((1,), (1,)), ((), ())), preferred_element_type=jnp.float32
    )


def local_plain(
    hidden_in,
    document_labels,
    cotangent,
    ln_gain,
    ln_bias,
    qkv_weight,
    qkv_bias,
    out_weight,
    out_bias,
    fc_in_weight,
    fc_in_bias,
    fc_out_weight,
    fc_out_bias,
):
    gathered = (
        lax.all_gather(ln_gain, ("seq", "fsdp"), axis=0, tiled=True),
        lax.all_gather(ln_bias, ("seq", "fsdp"), axis=0, tiled=True),
        lax.all_gather(qkv_weight, ("seq", "fsdp"), axis=0, tiled=True),
        lax.all_gather(qkv_bias, ("seq", "fsdp"), axis=0, tiled=True),
        lax.all_gather(out_weight, ("seq", "fsdp"), axis=0, tiled=True),
        lax.all_gather(out_bias, ("seq", "fsdp"), axis=0, tiled=True),
        lax.all_gather(fc_in_weight, ("seq", "fsdp"), axis=0, tiled=True),
        lax.all_gather(fc_in_bias, ("seq", "fsdp"), axis=0, tiled=True),
        lax.all_gather(fc_out_weight, ("seq", "fsdp"), axis=0, tiled=True),
        lax.all_gather(fc_out_bias, ("seq", "fsdp"), axis=0, tiled=True),
    )
    norm_multiplier, norm_shift, w_qkv, b_qkv, w_out, b_out, w_in, b_in, w_fc, b_fc = gathered
    norm_multiplier = norm_multiplier.astype(jnp.float32)
    norm_shift = norm_shift.astype(jnp.float32)
    groups = lax.axis_size("seq")
    per_group = H // groups
    local_seqs = hidden_in.shape[0]
    tok_count = hidden_in.shape[1]
    row_count = local_seqs * tok_count
    tokens = hidden_in.reshape(row_count, D).astype(jnp.float32)
    average = jnp.mean(tokens, axis=-1, keepdims=True)
    centered = tokens - average
    spread = jnp.mean(centered * centered, axis=-1, keepdims=True)
    inv_std = lax.rsqrt(spread + 1e-05)
    rescaled_rows = centered * inv_std
    normed = (rescaled_rows * norm_multiplier + norm_shift).astype(jnp.bfloat16)
    projected = jnp.dot(normed, w_qkv, preferred_element_type=jnp.float32) + b_qkv.astype(
        jnp.float32
    )
    segments_all = lax.all_gather(document_labels, "seq", axis=1, tiled=True)
    angles_all = jax.vmap(position_angles)(segments_all)
    angles = lax.dynamic_slice_in_dim(
        angles_all, lax.axis_index("seq") * tok_count, tok_count, 1
    ).reshape(row_count, ROT // 2)
    cosine = jnp.cos(angles)[:, None, None, :]
    sine_part = jnp.sin(angles)[:, None, None, :]
    head_parts = projected.reshape(row_count, H, 3, HD)
    turned = jnp.concatenate(
        [rotate(head_parts[:, :, :2], cosine, sine_part), head_parts[:, :, 2:]], axis=2
    ).astype(jnp.bfloat16)
    outgoing = turned.reshape(local_seqs, tok_count, groups, per_group * 3 * HD)
    arrived = lax.all_to_all(outgoing, "seq", split_axis=2, concat_axis=1, tiled=True)
    length = arrived.shape[1]
    local_heads = arrived.reshape(local_seqs, length, per_group, 3, HD)
    queries_seq = local_heads[:, :, :, 0]
    keys_seq = local_heads[:, :, :, 1]
    values_seq = local_heads[:, :, :, 2]
    block_rows = min(512, length)
    block_count = length // block_rows
    scale_factor = 1.0 / math.sqrt(HD)

    def attend_forward(inputs):
        query_all, key_everywhere, value_all, segments = inputs

        def forward_step(running, block_index):
            first_row = block_index * block_rows
            query_rows = lax.dynamic_slice_in_dim(query_all, first_row, block_rows, 0)
            allowed = make_mask(segments, first_row, block_rows)
            raw_scores = (
                jnp.einsum(
                    "qhd,khd->hqk", query_rows, key_everywhere, preferred_element_type=jnp.float32
                )
                * scale_factor
            )
            raw_scores = jnp.where(allowed[None], raw_scores, -1e30)
            row_max = jnp.max(raw_scores, axis=-1, keepdims=True)
            unscaled = jnp.exp(raw_scores - row_max)
            row_total = jnp.sum(unscaled, axis=-1, keepdims=True)
            probabilities = (unscaled / row_total).astype(jnp.bfloat16)
            context_rows = jnp.einsum(
                "hqk,khd->qhd", probabilities, value_all, preferred_element_type=jnp.float32
            )
            log_total = (row_max + jnp.log(row_total))[..., 0]
            return (running, (context_rows, log_total))

        _, (context_blocks, log_blocks) = lax.scan(
            forward_step, None, jnp.arange(block_count, dtype=jnp.int32)
        )
        return (context_blocks.reshape(length, per_group * HD).astype(jnp.bfloat16), log_blocks)

    context_seq, log_totals = lax.map(
        attend_forward, (queries_seq, keys_seq, values_seq, segments_all)
    )
    context_heads = context_seq.reshape(local_seqs, length, 1, per_group * HD)
    returned = lax.all_to_all(context_heads, "seq", split_axis=1, concat_axis=2, tiled=True)
    context = returned.reshape(row_count, D)
    attn_out = jnp.dot(context, w_out, preferred_element_type=jnp.float32) + b_out.astype(
        jnp.float32
    )
    hidden_pre = jnp.dot(normed, w_in, preferred_element_type=jnp.float32) + b_in.astype(
        jnp.float32
    )
    activated = jax.nn.gelu(hidden_pre, approximate=False).astype(jnp.bfloat16)
    mlp_out = jnp.dot(activated, w_fc, preferred_element_type=jnp.float32) + b_fc.astype(
        jnp.float32
    )
    output = (tokens + attn_out + mlp_out).astype(jnp.bfloat16).reshape(local_seqs, tok_count, D)
    grad_out = cotangent.reshape(row_count, D)
    grad_wide = grad_out.astype(jnp.float32)
    out_bias_grad = jnp.sum(grad_wide, axis=0)
    fc_out_bias_grad = jnp.sum(grad_wide, axis=0)
    out_weight_grad = outer_product(context, grad_out)
    fc_out_weight_grad = outer_product(activated, grad_out)
    act_grad = times_transposed(grad_out, w_fc)
    _, gelu_back = jax.vjp(partial(jax.nn.gelu, approximate=False), hidden_pre)
    hidden_grad = gelu_back(act_grad)[0].astype(jnp.bfloat16)
    fc_in_weight_grad = outer_product(normed, hidden_grad)
    fc_in_bias_grad = jnp.sum(hidden_grad.astype(jnp.float32), axis=0)
    context_grad = times_transposed(grad_out, w_out).astype(jnp.bfloat16)
    grad_outgoing = context_grad.reshape(local_seqs, tok_count, groups, per_group * HD)
    head_grad_seq = lax.all_to_all(
        grad_outgoing, "seq", split_axis=2, concat_axis=1, tiled=True
    ).reshape(local_seqs, length, per_group, HD)

    def attend_backward(inputs):
        query_all, key_everywhere, value_all, segments, head_grad, log_blocks = inputs

        def backward_step(running, block_index):
            key_acc, value_accumulator = running
            first_row = block_index * block_rows
            query_rows = lax.dynamic_slice_in_dim(query_all, first_row, block_rows, 0)
            grad_rows = lax.dynamic_slice_in_dim(head_grad, first_row, block_rows, 0)
            log_rows = log_blocks[block_index]
            allowed = make_mask(segments, first_row, block_rows)
            raw_scores = (
                jnp.einsum(
                    "qhd,khd->hqk", query_rows, key_everywhere, preferred_element_type=jnp.float32
                )
                * scale_factor
            )
            raw_scores = jnp.where(allowed[None], raw_scores, -1e30)
            probabilities = jnp.where(allowed[None], jnp.exp(raw_scores - log_rows[..., None]), 0.0)
            value_accumulator = value_accumulator + jnp.einsum(
                "hqk,qhd->khd",
                probabilities.astype(jnp.bfloat16),
                grad_rows,
                preferred_element_type=jnp.float32,
            )
            prob_grad = jnp.einsum(
                "qhd,khd->hqk", grad_rows, value_all, preferred_element_type=jnp.float32
            )
            inner_total = jnp.sum(probabilities * prob_grad, axis=-1, keepdims=True)
            score_grad = (probabilities * (prob_grad - inner_total)).astype(jnp.bfloat16)
            query_grad = (
                jnp.einsum(
                    "hqk,khd->qhd", score_grad, key_everywhere, preferred_element_type=jnp.float32
                )
                * scale_factor
            )
            key_acc = (
                key_acc
                + jnp.einsum(
                    "hqk,qhd->khd", score_grad, query_rows, preferred_element_type=jnp.float32
                )
                * scale_factor
            )
            return ((key_acc, value_accumulator), query_grad)

        empty_grad = jnp.zeros((length, per_group, HD), jnp.float32)
        (key_grad, value_grad), query_blocks = lax.scan(
            backward_step, (empty_grad, empty_grad), jnp.arange(block_count, dtype=jnp.int32)
        )
        query_grad = query_blocks.reshape(length, per_group, HD)
        return jnp.stack([query_grad, key_grad, value_grad], axis=2).astype(jnp.bfloat16)

    stacked = lax.map(
        attend_backward,
        (queries_seq, keys_seq, values_seq, segments_all, head_grad_seq, log_totals),
    )
    returned_grad = lax.all_to_all(
        stacked.reshape(local_seqs, length, 1, per_group * 3 * HD),
        "seq",
        split_axis=1,
        concat_axis=2,
        tiled=True,
    )
    back_heads = returned_grad.reshape(row_count, H, 3, HD).astype(jnp.float32)
    unturned = jnp.concatenate(
        [rotate(back_heads[:, :, :2], cosine, -sine_part), back_heads[:, :, 2:]], axis=2
    )
    projected_grad = unturned.reshape(row_count, 3 * D).astype(jnp.bfloat16)
    qkv_weight_grad = outer_product(normed, projected_grad)
    qkv_bias_grad = jnp.sum(projected_grad.astype(jnp.float32), axis=0)
    normalized_gradient = times_transposed(projected_grad, w_qkv) + times_transposed(
        hidden_grad, w_in
    )
    ln_gain_grad = jnp.sum(normalized_gradient * rescaled_rows, axis=0)
    ln_bias_grad = jnp.sum(normalized_gradient, axis=0)
    standardized_gradient = normalized_gradient * norm_multiplier
    norm_back = (
        standardized_gradient
        - jnp.mean(standardized_gradient, axis=-1, keepdims=True)
        - rescaled_rows * jnp.mean(standardized_gradient * rescaled_rows, axis=-1, keepdims=True)
    ) * inv_std
    input_grad = (grad_wide + norm_back).astype(jnp.bfloat16).reshape(local_seqs, tok_count, D)
    summed = (
        lax.psum_scatter(ln_gain_grad, ("seq", "fsdp"), scatter_dimension=0, tiled=True),
        lax.psum_scatter(ln_bias_grad, ("seq", "fsdp"), scatter_dimension=0, tiled=True),
        lax.psum_scatter(qkv_weight_grad, ("seq", "fsdp"), scatter_dimension=0, tiled=True),
        lax.psum_scatter(qkv_bias_grad, ("seq", "fsdp"), scatter_dimension=0, tiled=True),
        lax.psum_scatter(out_weight_grad, ("seq", "fsdp"), scatter_dimension=0, tiled=True),
        lax.psum_scatter(out_bias_grad, ("seq", "fsdp"), scatter_dimension=0, tiled=True),
        lax.psum_scatter(fc_in_weight_grad, ("seq", "fsdp"), scatter_dimension=0, tiled=True),
        lax.psum_scatter(fc_in_bias_grad, ("seq", "fsdp"), scatter_dimension=0, tiled=True),
        lax.psum_scatter(fc_out_weight_grad, ("seq", "fsdp"), scatter_dimension=0, tiled=True),
        lax.psum_scatter(fc_out_bias_grad, ("seq", "fsdp"), scatter_dimension=0, tiled=True),
    )
    return (
        output,
        input_grad,
        summed[0],
        summed[1],
        summed[2],
        summed[3],
        summed[4],
        summed[5],
        summed[6],
        summed[7],
        summed[8],
        summed[9],
    )


def dot(left, right):
    return jnp.dot(left, right, preferred_element_type=F32)


def swap(value, axis, bit):
    return lax.ppermute(value, axis, [(i, i ^ bit) for i in range(lax.axis_size(axis))])


def shift(value, by):
    count = lax.axis_size("seq")
    return lax.ppermute(
        value, "seq", [(i, i + by) for i in range(count) if 0 <= i + by < count]
    )


class Clock:
    def __init__(self, token):
        self.token = token

    def join(self, *values):
        values, self.token = lax.optimization_barrier((values, self.token))
        return values


X, Y, NEAR, FAR = 1, 2, 4, 8
CHIPS = 16
ORDER = [0, 8, 4, 12, 1, 9, 5, 13, 2, 10, 6, 14, 3, 11, 7, 15]
SUMS = {"ax": [0, 8, 1, 9], "by": [4, 12, 6, 14], "yax": [2, 10, 3, 11], "xby": [5, 13, 7, 15]}


def place_of(chip):
    return (chip // FAR) % 2 + (chip // NEAR) % 2 * 2 + chip % 2 * 4 + (chip // Y) % 2 * 8


def cross(value, bit):
    return swap(value, "seq", bit // 4) if bit >= 4 else swap(value, "fsdp", bit * 2)


def other_core(value):
    return swap(value, "fsdp", 1)


class Gather:
    def __init__(self, shard):
        self.parts = {"s": shard}

    def jobs(self, stage):
        parts = self.parts
        if stage == "near":
            parts["a"] = jnp.concatenate([parts["s"], parts["f"]], axis=0)
        if stage == "second":
            parts["ax"] = jnp.concatenate([parts["a"], parts["xa"]], axis=0)
            parts["by"] = jnp.concatenate([parts["b"], parts["yb"]], axis=0)
        return {
            "far": [("f", "s", FAR)],
            "near": [("b", "a", NEAR)],
            "first": [("xa", "a", X), ("yb", "b", Y)],
            "second": [("yax", "ax", Y), ("xby", "by", X)],
        }[stage]

    def pieces(self):
        return [self.parts[name] for name in SUMS]


LAY = [(0, 0), (1, 0), (0, 1), (3, 0), (2, 0), (1, 1), (2, 1), (3, 1)]


def gathered(refs, columns=slice(None), which=slice(None)):
    half = refs[0].shape[0] // 2
    return jnp.concatenate(
        [refs[array][part * half : part * half + half, columns] for array, part in LAY[which]],
        axis=0,
    )


BLOCKS = {
    "a": [0, 8],
    "xa": [1, 9],
    "b": [4, 12],
    "yb": [6, 14],
    "yax": [2, 10, 3, 11],
    "xby": [5, 13, 7, 15],
}


class Scatter:
    def __init__(self, blocks):
        self.parts = dict(zip(BLOCKS, blocks))

    def total(self, first, last, *names):
        return sum(self.parts[name][first:last].astype(F32) for name in names)

    def jobs(self, stage):
        parts = self.parts
        rows = parts["a"].shape[0]
        if stage == "second":
            for name, other in (("xa", "r_yax"), ("yb", "r_xby")):
                value = parts[name].astype(F32) + parts[other][rows:].astype(F32)
                parts[name] = value.astype(BF)
        if stage == "near":
            parts["b"] = self.total(0, rows, "b", "r_xby", "r_yb").astype(BF)
        if stage == "far":
            value = self.total(rows // 2, rows, "a", "r_yax", "r_xa", "r_b")
            parts["send"] = value.astype(BF)
        return {
            "first": [("r_yax", "yax", Y), ("r_xby", "xby", X)],
            "second": [("r_xa", "xa", X), ("r_yb", "yb", Y)],
            "near": [("r_b", "b", NEAR)],
            "far": [("r_far", "send", FAR)],
        }[stage]

    def result(self):
        rows = self.parts["a"].shape[0] // 2
        return self.total(0, rows, "a", "r_yax", "r_xa", "r_b", "r_far")


def cost(flops, bytes_accessed, transcendentals=0):
    return pl.CostEstimate(
        flops=flops, bytes_accessed=bytes_accessed, transcendentals=transcendentals
    )


SMEM = pl.BlockSpec(memory_space=pltpu.SMEM)
VMEM = pl.BlockSpec(memory_space=pltpu.VMEM)
ANY = pl.BlockSpec(memory_space=pl.ANY)


def whole(array):
    return pl.BlockSpec(array.shape, lambda *_: (0,) * len(array.shape))


def shaped(rows, columns, dtype):
    return jax.ShapeDtypeStruct((rows, columns), dtype)


def stack(refs):
    return jnp.concatenate([ref[...] for ref in refs], axis=0)


def lanes_low(rows):
    return lax.broadcasted_iota(jnp.int32, (rows, 128), 1) < HD


def cut_kernel(where_ref, qkv_ref, in_ref, out_w_ref, gain_ref, shift_ref, qb_ref, ob_ref, ib_ref, fb_ref, label_ref, *refs):
    keep1, give1, keep2, give2, in_keep, in_give, folded, columns_ref, line_ref = refs
    core = where_ref[1]
    rows = qkv_ref.shape[0]
    columns_ref[...] = jnp.zeros_like(columns_ref)
    for row, ref in enumerate((gain_ref, shift_ref, ob_ref, fb_ref)):
        columns_ref[row : row + 1, :rows] = ref[...].astype(F32)
    line_ref[...] = jnp.zeros_like(line_ref)
    line_ref[0:1, :96] = qb_ref[...].astype(F32)
    line_ref[1:2, :] = ib_ref[...].astype(F32)
    bias, units = line_ref[0:1, :], line_ref[1:2, :]
    lane = lax.broadcasted_iota(jnp.int32, (1, 128), 1)
    first = core == 0
    parts = []
    for seq in range(2):
        for part in range(2):
            labels = (label_ref[seq : seq + 1, 128 * part : 128 * part + 128] + 1).astype(F32)
            parts += [pltpu.roll(labels, HD, 1), labels]
    zero = jnp.zeros_like(bias)
    parts.append(jnp.where(first, pltpu.roll(bias, 64, 1), zero))
    parts.append(
        jnp.where(
            first,
            jnp.where(lane < 96, bias, zero),
            jnp.where(lane >= 96, pltpu.roll(bias, 96, 1), zero),
        )
    )
    parts.append(jnp.where(first, zero, pltpu.roll(bias, 32, 1)))
    parts += [pltpu.roll(units, HD, 1), units]
    for row, value in enumerate(parts):
        line_ref[row : row + 1, :] = value
    low = lanes_low(rows)
    side = jnp.where(low, columns_ref[...].T[:rows], line_ref[...]).astype(BF)
    for owner, out1, out2 in ((core, keep1, keep2), (1 - core, give1, give2)):
        for group in range(GROUPS):
            at = pl.multiple_of((owner * GROUPS + group) * 384, 128)
            b0, b1, b2 = (
                qkv_ref[:, pl.ds(at + 128 * part, 128)].astype(F32) for part in range(3)
            )
            out = out1 if group < 2 else out2
            place = (group % 2) * 384
            turned = pltpu.roll(b0, HD, 1), pltpu.roll(b2, HD, 1)
            out[:, place : place + 128] = jnp.where(low, b0, b1).astype(BF)
            out[:, place + 128 : place + 256] = jnp.where(low, *turned).astype(BF)
            out[:, place + 256 : place + 384] = jnp.where(low, b1, b2).astype(BF)
        out1[:, 768:] = side
    for owner, out in ((core, in_keep), (1 - core, in_give)):
        for block in range(CHIPS):
            at = pl.multiple_of((2 * block + owner) * 128, 128)
            out[:, block * 128 : block * 128 + 128] = in_ref[:, pl.ds(at, 128)]
    folded[:rows, :] = out_w_ref[:, : D // 2]
    folded[rows:, :] = out_w_ref[:, D // 2 :]


def cut(where, qkv_rows, in_rows, out_rows, vectors, labels):
    rows = qkv_rows.shape[0]
    widths = (896, 896, 768, 768, 2048, 2048)
    return pl.pallas_call(
        cut_kernel,
        out_shape=tuple(shaped(rows, width, BF) for width in widths)
        + (shaped(2 * rows, D // 2, BF),),
        in_specs=[SMEM] + [VMEM] * 10,
        out_specs=(VMEM,) * 7,
        scratch_shapes=[pltpu.VMEM((128, 128), F32), pltpu.VMEM((rows, 128), F32)],
        cost_estimate=cost(0, 8 * rows * 4 * D),
        name="cut",
    )(where, qkv_rows, in_rows, out_rows, *[vector.reshape(1, -1) for vector in vectors], labels)


def turn(value, cosine, forth, back):
    return (
        value * cosine
        + pltpu.roll(value, 128 - ROT // 2, 1) * forth
        + pltpu.roll(value, ROT // 2, 1) * back
    )


def marks_kernel(where_ref, a_ref, b_ref, speed_ref, forth_ref, back_ref, bias_ref, cos_ref, to_ref, from_ref, side_ref):
    seq = pl.program_id(0)
    line, core = where_ref[0] // 4, where_ref[1]

    @pl.when(seq == 0)
    def _():
        side_ref[:128, :] = a_ref[...].astype(F32)
        side_ref[128:, :] = b_ref[...].astype(F32)

    owner = jnp.where(seq < 2, core, 1 - core)
    low = lanes_low(1)
    chunks = []
    for back in range(3):
        other = line - back
        relative = jnp.where(other >= 0, other, 0) ^ line
        block = relative // 2 + 2 * (relative % 2)
        rows = side_ref[pl.ds(pl.multiple_of(block * 64 + owner * 32, 8), 8), :]
        rows = jnp.where(seq % 2 == 0, rows[:4], rows[4:])
        rows = jnp.where(other >= 0, rows, jnp.zeros_like(rows))
        chunks.append(
            [
                jnp.where(low, pltpu.roll(rows[i : i + 1], HD, 1), rows[i + 1 : i + 2])
                for i in (0, 2)
            ]
        )
    total = None
    query = lax.broadcasted_iota(jnp.int32, (128, 256), 1)
    key = lax.broadcasted_iota(jnp.int32, (128, 256), 0)
    mine = jnp.concatenate(chunks[0], axis=1)
    for back, halves in enumerate(chunks):
        for half, labels in enumerate(halves):
            column = jnp.broadcast_to(labels, (128, 128)).T
            column = jnp.concatenate([column, column], axis=1)
            same = column == mine
            if back == 0:
                same = same & (key + 128 * half <= query)
            at = back * 256 + half * 128
            bias_ref[0, at : at + 128, :] = jnp.where(same, 0.0, -1e30)
            count = jnp.sum(jnp.where(same, 1.0, 0.0), axis=0, keepdims=True)
            total = count if total is None else total + count
    for half in range(2):
        position = total[:, 128 * half : 128 * half + 128] - 1.0
        angle = jnp.broadcast_to(position, (128, 128)).T * speed_ref[...]
        here = slice(128 * half, 128 * half + 128)
        cos_ref[here, :] = jnp.cos(angle)
        sine = jnp.sin(angle)
        to_ref[here, :] = sine * forth_ref[...]
        from_ref[here, :] = sine * back_ref[...]


def marks(where, a, b):
    half = ROT // 2
    inverse = 1.0 / 10000.0 ** (jnp.arange(0, ROT, 2, dtype=F32) / ROT)
    speed = jnp.concatenate([inverse, inverse, jnp.zeros((HD - ROT,), F32)])
    speed = jnp.concatenate([speed, speed]).reshape(1, 128)
    lanes = np.arange(128) % HD
    forth = jnp.asarray(-(lanes < half).astype(np.float32)[None, :])
    back = jnp.asarray(((lanes >= half) & (lanes < ROT)).astype(np.float32)[None, :])
    side = pl.BlockSpec((128, 128), lambda i: (0, 6))
    table = pl.BlockSpec((256, 128), lambda i: (i, 0))
    return pl.pallas_call(
        marks_kernel,
        grid=(4,),
        out_shape=(jax.ShapeDtypeStruct((4, 768, 256), F32),) + (shaped(1024, 128, F32),) * 3,
        in_specs=[SMEM, side, side, whole(speed), whole(forth), whole(back)],
        out_specs=(pl.BlockSpec((1, 768, 256), lambda i: (i, 0, 0)), table, table, table),
        scratch_shapes=[pltpu.VMEM((256, 128), F32)],
        cost_estimate=cost(1024 * 128 * 100, 4 * 1024 * 1024),
        name="marks",
    )(where, a, b, speed, forth, back)


def choice_into(me, chosen_ref):
    step = 128
    column = lax.broadcasted_iota(jnp.int32, (1, D), 1)
    place = column // 64
    chip = place % 2 * FAR + (place // 2) % 2 * NEAR + (place // 4) % 2 * X + place // 8 * Y
    wanted = (chip ^ me) * 64 + column % 64

    def some(i, carry):
        here = pl.ds(pl.multiple_of(i * step, step), step)
        row = lax.broadcasted_iota(jnp.int32, (step, D), 0) + i * step
        chosen_ref[here, :] = jnp.where(row == wanted, 1.0, 0.0).astype(BF)
        return carry

    lax.fori_loop(0, D // step, some, 0)


def prepare_kernel(
    steps, where_ref, own_ref, other_ref, xhat_ref, inv_ref, chosen_ref, rows_ref
):
    step = pl.program_id(0)

    @pl.when(step == 0)
    def _():
        choice_into(where_ref[0], chosen_ref)

    @pl.when(step < steps)
    def _():
        rows_ref[...] = own_ref[...]

    @pl.when(step >= steps)
    def _():
        rows_ref[...] = other_ref[...]

    x = dot(rows_ref[...], chosen_ref[...])
    average = jnp.mean(x, axis=-1, keepdims=True)
    centered = x - average
    spread = jnp.mean(centered * centered, axis=-1, keepdims=True)
    inv_std = lax.rsqrt(spread + 1e-05)
    xhat_ref[...] = centered * inv_std
    inv_ref[...] = inv_std


def prepare(where, own, other):
    rows = own.shape[0]
    step = 128
    steps = rows // step
    return pl.pallas_call(
        partial(prepare_kernel, steps),
        grid=(2 * steps,),
        out_shape=(shaped(2 * rows, D, F32), shaped(2 * rows, 1, F32)),
        in_specs=[
            SMEM,
            pl.BlockSpec((step, D), lambda i: (jnp.minimum(i, steps - 1), 0)),
            pl.BlockSpec((step, D), lambda i: (jnp.maximum(i - steps, 0), 0)),
        ],
        out_specs=(
            pl.BlockSpec((step, D), lambda i: (i, 0)),
            pl.BlockSpec((step, 1), lambda i: (i, 0)),
        ),
        scratch_shapes=[pltpu.VMEM((D, D), BF), pltpu.VMEM((step, D), BF)],
        cost_estimate=cost(4 * rows * D * D, 16 * rows * D),
        name="prepare",
    )(where, own, other)


def emit_heads(value, tables, outs):
    pairs = [
        (q_ref, kv_ref, pair)
        for q_ref, kv_ref in zip(outs[::2], outs[1::2])
        for pair in range(q_ref.shape[1] // 128)
    ]
    for index, (q_ref, kv_ref, pair) in enumerate(pairs):
        first, q, k = index * 384, pair * 128, pair * 256
        q_ref[:, q : q + 128] = turn(value[:, first : first + 128], *tables).astype(BF)
        kv_ref[:, k : k + 128] = turn(value[:, first + 128 : first + 256], *tables).astype(BF)
        kv_ref[:, k + 128 : k + 256] = value[:, first + 256 : first + 384].astype(BF)


def project_first_kernel(where_ref, xhat_ref, cos_ref, forth_ref, back_ref, *refs):
    pieces, outs = refs[:4], refs[4:8]
    normed_ref, normed_t_ref, more_ref, units_ref, rows_ref, gain_ref, side_ref, bias_ref, two_ref = refs[8:]
    me, core = where_ref[0], where_ref[1]

    @pl.when(pl.program_id(0) == 0)
    def _():
        side_ref[...] = gathered(pieces, slice(768, 896)).astype(F32)
        across = side_ref[...].T
        two_ref[...] = across[:8]
        gain_ref[...] = across[0:1]
        rows_ref[...] = across[2:3] + across[3:4]
        low = lanes_low(1)

        def block(chip, owner):
            start = place_of(chip ^ me) * 64 + owner * 32 + 8
            return side_ref[pl.ds(pl.multiple_of(start, 8), 8), :]

        def pair(one, two):
            return jnp.where(low, pltpu.roll(one, HD, 1), two)

        for group in range(GROUPS):
            heads = []
            for head in range(2):
                chip = core * 8 + 2 * group + head
                zero, one = block(chip, 0), block(chip, 1)
                heads.append((zero[0:1], zero[1:2] + one[1:2], one[2:3]))
            out = bias_ref if group < 2 else more_ref
            for part in range(3):
                at = (group % 2) * 384 + part * 128
                out[:, at : at + 128] = pair(heads[0][part], heads[1][part])
        for chip in range(CHIPS):
            found = block(chip, core)
            units_ref[:, chip * 128 : chip * 128 + 128] = pair(found[3:4], found[4:5])

    normed = (xhat_ref[...] * two_ref[0:1, :] + two_ref[1:2, :]).astype(BF)
    normed_ref[...] = normed
    normed_t_ref[...] = normed.T
    value = dot(normed, gathered(pieces, slice(0, 768))) + bias_ref[...]
    emit_heads(value, (cos_ref[...], forth_ref[...], back_ref[...]), outs)


TWO_PAIRS = (shaped(1024, 128, BF), shaped(1024, 256, BF)) * 2
ONE_GROUP = (shaped(1024, 256, BF), shaped(1024, 512, BF))


def rows_spec(columns, step=256):
    return pl.BlockSpec((step, columns), lambda i: (i, 0))


def project_first(where, xhat, tables, pieces):
    small = (shaped(1, 768, F32), shaped(1, 2048, F32), shaped(1, D, F32), shaped(1, D, F32))
    return pl.pallas_call(
        project_first_kernel,
        grid=(4,),
        out_shape=TWO_PAIRS + (shaped(1024, D, BF), shaped(D, 1024, BF)) + small,
        in_specs=[SMEM, rows_spec(D)] + [rows_spec(128)] * 3 + [whole(piece) for piece in pieces],
        out_specs=tuple(rows_spec(shape.shape[1]) for shape in TWO_PAIRS)
        + (rows_spec(D), pl.BlockSpec((D, 256), lambda i: (0, i)))
        + tuple(whole(shape) for shape in small),
        scratch_shapes=[
            pltpu.VMEM((D, 128), F32),
            pltpu.VMEM((1, 768), F32),
            pltpu.VMEM((8, D), F32),
        ],
        cost_estimate=cost(2 * 1024 * D * 768, 12 * 1024 * D),
        name="project_first",
    )(where, xhat, *tables, *pieces)


def project_more_kernel(normed_ref, bias_ref, cos_ref, forth_ref, back_ref, *refs):
    value = dot(normed_ref[...], gathered(refs[:4], slice(512, 1280))) + bias_ref[...]
    emit_heads(value, (cos_ref[...], forth_ref[...], back_ref[...]), refs[4:])


def project_more(normed, bias, tables, pieces):
    return pl.pallas_call(
        project_more_kernel,
        grid=(4,),
        out_shape=ONE_GROUP,
        in_specs=[rows_spec(D), whole(bias)]
        + [rows_spec(128)] * 3
        + [whole(piece) for piece in pieces],
        out_specs=tuple(rows_spec(shape.shape[1]) for shape in ONE_GROUP),
        cost_estimate=cost(2 * 1024 * D * 768, 6 * 1024 * D),
        name="project_more",
    )(normed, bias, *tables, *pieces)


def head_rows_kernel(where_ref, *refs):
    keep_ref, give_ref, held_ref = refs[4:]
    me, core = where_ref[0], where_ref[1]
    for index, chip in enumerate(ORDER):
        array, part = LAY[index // 2]
        piece, at = refs[array], part * 128 + index % 2 * 64
        found = chip ^ me
        start = pl.multiple_of((((found // 8) ^ core) * 8 + found % 8) * 32, 32)
        held_ref[pl.ds(start, 32), : D // 2] = piece[at : at + 32, :]
        held_ref[pl.ds(start, 32), D // 2 :] = piece[at + 32 : at + 64, :]
    keep_ref[...] = held_ref[:256, :]
    give_ref[...] = held_ref[256:, :]


def head_rows(where, pieces):
    return pl.pallas_call(
        head_rows_kernel,
        out_shape=(shaped(256, D, BF),) * 2,
        grid=(1,),
        in_specs=[SMEM] + [pl.BlockSpec((256, D // 2), lambda i: (0, 0))] * 4,
        out_specs=(pl.BlockSpec((256, D), lambda i: (0, 0)),) * 2,
        scratch_shapes=[pltpu.VMEM((512, D), BF)],
        cost_estimate=cost(0, 4 * 512 * D),
        name="head_rows",
    )(where, *pieces)


def context_grad_kernel(
    where_ref, own_ref, other_ref, keep_ref, more_ref, grad_ref, heads_ref, rows_ref
):
    core = where_ref[1]
    step = pl.program_id(0)

    @pl.when(step == 0)
    def _():
        for chip in range(8):
            rows = slice(chip * 32, chip * 32 + 32)
            heads_ref[pl.ds(pl.multiple_of(chip * 64 + core * 32, 32), 32), :] = keep_ref[rows, :]
            at = pl.multiple_of(chip * 64 + (1 - core) * 32, 32)
            heads_ref[pl.ds(at, 32), :] = more_ref[rows, :]

    @pl.when(step < 2)
    def _():
        rows_ref[...] = own_ref[...]

    @pl.when(step >= 2)
    def _():
        rows_ref[...] = other_ref[...]

    grad_ref[...] = times_transposed(rows_ref[...], heads_ref[...]).astype(BF)


def context_gradient(where, own, other, keep, more):
    return pl.pallas_call(
        context_grad_kernel,
        grid=(4,),
        out_shape=(shaped(1024, D // 2, BF), shaped(D // 2, D, BF)),
        in_specs=[
            SMEM,
            pl.BlockSpec((256, D), lambda i: (jnp.minimum(i, 1), 0)),
            pl.BlockSpec((256, D), lambda i: (jnp.maximum(i - 2, 0), 0)),
            whole(keep),
            whole(more),
        ],
        out_specs=(rows_spec(D // 2), pl.BlockSpec((D // 2, D), lambda i: (0, 0))),
        scratch_shapes=[pltpu.VMEM((256, D), BF)],
        cost_estimate=cost(1024 * D * D, 6 * 1024 * D),
        name="context_grad",
    )(where, own, other, keep, more)


def attend_kernel(q_ref, do_ref, bias_ref, *refs):
    kv_refs, o_ref, dq_ref, dkv_refs = refs[:3], refs[3], refs[4], refs[5:8]
    weight_ref, probs_ref, grad_ref = refs[8:]
    rows = q_ref.shape[0]
    scaled = q_ref[...] * 0.125
    given = do_ref[...]
    given_t = given.T.astype(F32)
    low = lanes_low(rows)
    zero = jnp.zeros_like(given)

    def heads(value):
        return jnp.concatenate([jnp.where(low, value, zero), jnp.where(low, zero, value)], axis=0)

    queries, grads = heads(scaled), heads(given)
    spans = [slice(chunk * rows, chunk * rows + rows) for chunk in range(3)]
    top = None
    for here, ref in zip(spans, kv_refs):
        bias = bias_ref[0, here, :]
        scores = times_transposed(ref[:, :128], queries) + jnp.concatenate([bias, bias], axis=1)
        weight_ref[here, :] = scores
        most = jnp.max(scores, axis=0, keepdims=True)
        top = most if top is None else jnp.maximum(top, most)
    total = jnp.zeros_like(top)
    for here in spans:
        unscaled = jnp.exp(weight_ref[here, :] - top)
        weight_ref[here, :] = unscaled
        total = total + jnp.sum(unscaled, axis=0, keepdims=True)
    inverse = 1.0 / total
    for here in spans:
        probs = weight_ref[here, :] * inverse
        weight_ref[here, :] = probs
        probs_ref[here, :] = probs.astype(BF)

    def both_heads(across, right_ref):
        return jnp.concatenate(
            [dot(across[:HD], right_ref[:, :rows]), dot(across[HD:], right_ref[:, rows:])], axis=0
        )

    values_t = jnp.concatenate([ref[:, 128:] for ref in kv_refs], axis=0).T
    keys_t = jnp.concatenate([ref[:, :128] for ref in kv_refs], axis=0).T
    out_t = both_heads(values_t, probs_ref)
    product = out_t * given_t
    inner = jnp.concatenate(
        [
            jnp.sum(product[:HD], axis=0, keepdims=True),
            jnp.sum(product[HD:], axis=0, keepdims=True),
        ],
        axis=1,
    )
    for here, ref in zip(spans, kv_refs):
        prob_grad = times_transposed(ref[:, 128:], grads)
        grad_ref[here, :] = (weight_ref[here, :] * (prob_grad - inner)).astype(BF)
    dq_t = both_heads(keys_t, grad_ref)
    o_ref[...] = out_t.T.astype(BF)
    dq_ref[...] = (dq_t.T * 0.125).astype(BF)
    for here, ref in zip(spans, dkv_refs):
        ref[:, :128] = dot(grad_ref[here, :], queries).astype(ref.dtype)
        ref[:, 128:] = dot(probs_ref[here, :], grads).astype(ref.dtype)


def attend(first, query, grad, bias, kvs):
    pairs = query.shape[1] // 128
    narrow = pl.BlockSpec((256, 128), lambda b, p: (b, p))
    wide = pl.BlockSpec((256, 256), lambda b, p: (b, p))
    return pl.pallas_call(
        attend_kernel,
        grid=(4, pairs),
        out_shape=(shaped(1024, 128 * pairs, BF),) * 2
        + (shaped(1024, 256 * pairs, F32),)
        + (shaped(1024, 256 * pairs, BF),) * 2,
        in_specs=[
            narrow,
            pl.BlockSpec((256, 128), lambda b, p: (b, first + p)),
            pl.BlockSpec((1, 768, 256), lambda b, p: (b, 0, 0)),
        ]
        + [wide] * 3,
        out_specs=(narrow, narrow) + (wide,) * 3,
        scratch_shapes=[pltpu.VMEM((768, 512), dtype) for dtype in (F32, BF, BF)],
        cost_estimate=cost(
            pairs * 24 * 4 * 256 * 768 * 128, pairs * 9 * 1024 * 1024, pairs * 8 * 256 * 768
        ),
        name="attend",
    )(query, grad, bias, *kvs)


def unturn_kernel(groups, cos_ref, forth_ref, back_ref, *refs):
    cosine, forth, back = cos_ref[...], -forth_ref[...], -back_ref[...]
    out_ref, sum_ref = refs[-2:]
    first = 0
    for group in range(groups):
        dq_ref, own_ref, more_ref = refs[3 * group : 3 * group + 3]
        for pair in range(dq_ref.shape[1] // 128):
            here = slice(pair * 256, pair * 256 + 256)
            kv = (own_ref[:, here] + more_ref[:, here].astype(F32)).astype(BF)
            key = kv[:, :128].astype(F32)
            query = dq_ref[:, pair * 128 : pair * 128 + 128].astype(F32)
            out_ref[:, first : first + 128] = turn(query, cosine, forth, back).astype(BF)
            out_ref[:, first + 128 : first + 256] = turn(key, cosine, forth, back).astype(BF)
            out_ref[:, first + 256 : first + 384] = kv[:, 128:]
            first += 384

    @pl.when(pl.program_id(0) == 0)
    def _():
        sum_ref[...] = jnp.zeros_like(sum_ref)

    sum_ref[...] += jnp.sum(out_ref[...].astype(F32), axis=0, keepdims=True)


def unturn(tables, triples):
    rows = triples[0][0].shape[0]
    step = 256
    width = 3 * sum(dq.shape[1] for dq, _, _ in triples)

    def spec(columns):
        return pl.BlockSpec((step, columns), lambda i: (i, 0))

    specs, arrays = [], []
    for dq, own, more in triples:
        specs += [spec(dq.shape[1]), spec(own.shape[1]), spec(more.shape[1])]
        arrays += [dq, own, more]
    return pl.pallas_call(
        partial(unturn_kernel, len(triples)),
        grid=(rows // step,),
        out_shape=(
            jax.ShapeDtypeStruct((rows, width), BF),
            jax.ShapeDtypeStruct((1, width), F32),
        ),
        in_specs=[spec(128)] * 3 + specs,
        out_specs=(spec(width), pl.BlockSpec((1, width), lambda i: (0, 0))),
        cost_estimate=cost(rows * width * 10, rows * width * 8),
        name="unturn",
    )(*tables, *arrays)


ROOT_HALF = math.sqrt(0.5)
DENSITY = 1.0 / math.sqrt(2.0 * math.pi)


def gelu_and_slope(value):
    share = 0.5 + 0.5 * lax.erf(value * ROOT_HALF)
    return value * share, share + value * (DENSITY * jnp.exp(-0.5 * value * value))


def hidden_kernel(normed_ref, bias_ref, *refs):
    act_ref, act_t_ref, slope_ref, value_ref = refs[-4:]
    rows = 128
    value_ref[...] = dot(normed_ref[...], gathered(refs[:4])) + bias_ref[...]

    def some(i, carry):
        here = pl.ds(pl.multiple_of(i * rows, rows), rows)
        act, slope = gelu_and_slope(value_ref[here, :])
        act = act.astype(BF)
        act_ref[here, :] = act
        act_t_ref[:, here] = act.T
        slope_ref[here, :] = slope
        return carry

    lax.fori_loop(0, normed_ref.shape[0] // rows, some, 0)


def hidden(normed, pieces, bias):
    rows, width = normed.shape[0], bias.shape[1]
    step = 512
    column = pl.BlockSpec((rows, step), lambda j: (0, j))
    return pl.pallas_call(
        hidden_kernel,
        grid=(width // step,),
        out_shape=(shaped(rows, width, BF), shaped(width, rows, BF), shaped(rows, width, F32)),
        in_specs=[whole(normed), pl.BlockSpec((1, step), lambda j: (0, j))]
        + [pl.BlockSpec((piece.shape[0], step), lambda j: (0, j)) for piece in pieces],
        out_specs=(column, pl.BlockSpec((step, rows), lambda j: (j, 0)), column),
        scratch_shapes=[pltpu.VMEM((rows, step), F32)],
        cost_estimate=cost(2 * rows * D * width + 50 * rows * width, 9 * rows * width),
        name="hidden",
    )(normed, bias, *pieces)


def fetch_units(me, pieces, w_ref, sem):
    copies = []
    for index, chip in enumerate(ORDER):
        first = pl.multiple_of((me ^ chip) * 128, 128)
        array, part = LAY[index // 2]
        copies.append(
            pltpu.make_async_copy(
                pieces[array].at[pl.ds(part * 256 + index % 2 * 128, 128), :],
                w_ref.at[pl.ds(first, 128), :],
                sem,
            )
        )
    for copy in copies:
        copy.start()
    return copies


def unit_back_kernel(where_ref, own_ref, other_ref, slope_ref, *refs):
    hg_ref, sum_ref, w_ref, sem = refs[4:]
    j = pl.program_id(0)
    step = hg_ref.shape[1]

    @pl.when(j == 0)
    def _():
        for copy in fetch_units(where_ref[0], refs[:4], w_ref, sem):
            copy.wait()

    w = w_ref[pl.ds(pl.multiple_of(j * step, step), step), :]
    total = None
    rows = own_ref.shape[0]
    for half, g_ref in enumerate((own_ref, other_ref)):
        here = slice(half * rows, half * rows + rows)
        grad = (times_transposed(g_ref[...], w) * slope_ref[here, :]).astype(BF)
        hg_ref[here, :] = grad
        part = jnp.sum(grad.astype(F32), axis=0, keepdims=True)
        total = part if total is None else total + part
    sum_ref[...] = total


def unit_back(where, own, other, slope, pieces):
    rows, width = slope.shape
    step = 512
    column = pl.BlockSpec((rows, step), lambda j: (0, j))
    return pl.pallas_call(
        unit_back_kernel,
        grid=(width // step,),
        out_shape=(shaped(rows, width, BF), shaped(1, width, F32)),
        in_specs=[SMEM, whole(own), whole(other), column] + [ANY] * 4,
        out_specs=(column, pl.BlockSpec((1, step), lambda j: (0, j))),
        scratch_shapes=[pltpu.VMEM((width, D), BF), pltpu.SemaphoreType.DMA],
        cost_estimate=cost(2 * rows * D * width, 8 * rows * width),
        name="unit_back",
    )(where, own, other, slope, *pieces)


def unit_out_kernel(where_ref, act_ref, heads_ref, *refs):
    contexts, pieces = refs[:3], refs[3:7]
    mine_ref, theirs_ref, w_ref, total_ref, sem = refs[7:]
    step = pl.program_id(0)

    @pl.when(step == 0)
    def _():
        for copy in fetch_units(where_ref[0], pieces, w_ref, sem):
            copy.wait()

    context = jnp.concatenate([ref[...] for ref in contexts], axis=1)
    total_ref[...] = dot(act_ref[...], w_ref[...]) + dot(context, heads_ref[...])

    @pl.when(step < 2)
    def _():
        mine_ref[...] = total_ref[...]

    @pl.when(step >= 2)
    def _():
        theirs_ref[...] = total_ref[...]


def unit_out(where, act, heads, contexts, pieces):
    rows, width = act.shape
    return pl.pallas_call(
        unit_out_kernel,
        grid=(4,),
        out_shape=(shaped(rows // 2, D, F32),) * 2,
        in_specs=[SMEM, rows_spec(width), whole(heads)]
        + [rows_spec(context.shape[1]) for context in contexts]
        + [ANY] * 4,
        out_specs=(
            pl.BlockSpec((256, D), lambda i: (jnp.minimum(i, 1), 0)),
            pl.BlockSpec((256, D), lambda i: (jnp.maximum(i - 2, 0), 0)),
        ),
        scratch_shapes=[
            pltpu.VMEM((width, D), BF),
            pltpu.VMEM((256, D), F32),
            pltpu.SemaphoreType.DMA,
        ],
        cost_estimate=cost(3 * rows * D * width, 6 * rows * width),
        name="unit_out",
    )(where, act, heads, *contexts, *pieces)


def row_grads_kernel(steps, where_ref, left_ref, right_ref, *refs):
    out_refs = refs[-6:]
    spots = [[place_of(chip) for chip in chips] for chips in BLOCKS.values()]

    @pl.when(pl.program_id(0) < steps)
    def _():
        value = dot(left_ref[...], right_ref[...]).astype(BF)
        for places, ref in zip(spots, out_refs):
            for at, place in enumerate(places):
                ref[at * 64 : at * 64 + 64, :] = value[place * 64 : place * 64 + 64]

    if len(refs) == 7:
        held_ref = refs[0]
        me, core = where_ref[0], where_ref[1]

        @pl.when(pl.program_id(0) >= steps)
        def _():
            for chips, ref in zip(BLOCKS.values(), out_refs):
                for at, chip in enumerate(chips):
                    found = chip ^ me
                    start = (((found // 8) ^ core) * 8 + found % 8) * 32
                    rows = held_ref[pl.ds(pl.multiple_of(start, 32), 32), :]
                    ref[at * 64 : at * 64 + 32, :] = rows[:, : D // 2]
                    ref[at * 64 + 32 : at * 64 + 64, :] = rows[:, D // 2 :]


def row_grads(where, left, right, more=None):
    rows, tokens = left.shape
    step = 512
    steps = right.shape[1] // step
    columns = right.shape[1] + (0 if more is None else D // 2)
    heights = [64 * len(chips) for chips in BLOCKS.values()]
    return pl.pallas_call(
        partial(row_grads_kernel, steps),
        grid=(columns // step,),
        out_shape=tuple(shaped(height, columns, BF) for height in heights),
        in_specs=[
            SMEM,
            whole(left),
            pl.BlockSpec((tokens, step), lambda j: (0, jnp.minimum(j, steps - 1))),
        ]
        + ([] if more is None else [whole(more)]),
        out_specs=tuple(pl.BlockSpec((height, step), lambda j: (0, j)) for height in heights),
        cost_estimate=cost(2 * rows * tokens * columns, 2 * (rows * tokens + rows * columns)),
        name="row_grads",
    )(where, left, right, *([] if more is None else [more]))


def unit_grads_kernel(order_ref, *refs):
    lefts, own_ref, other_ref, out_refs = refs[:4], refs[4], refs[5], refs[6:]
    left = stack(lefts)
    tokens = own_ref.shape[0]
    a, xa, b, yb, yax, xby = out_refs
    columns = 512

    def some(i, carry):
        here = pl.ds(pl.multiple_of(i * columns, columns), columns)
        value = dot(left[:, :tokens], own_ref[:, here]) + dot(left[:, tokens:], other_ref[:, here])
        value = value.astype(BF)
        for piece, outs in enumerate(((a, xa), (b, yb), (yax,), (xby,))):

            @pl.when(pl.program_id(0) == piece)
            def _(outs=outs):
                rows = 512 // len(outs)
                for at, ref in enumerate(outs):
                    ref[:, here] = value[at * rows : at * rows + rows]

        return carry

    lax.fori_loop(0, D // columns, some, 0)


def unit_grads(me, left, own, other):
    tokens = left.shape[1]
    order = jnp.asarray(np.array(sum(SUMS.values(), []), np.int32)) ^ me

    def block(place):
        return pl.BlockSpec((128, tokens), lambda k, order: (order[4 * k + place], 0))

    return pl.pallas_call(
        unit_grads_kernel,
        out_shape=tuple(shaped(128 * len(chips), D, BF) for chips in BLOCKS.values()),
        grid_spec=pltpu.PrefetchScalarGridSpec(
            num_scalar_prefetch=1,
            grid=(4,),
            in_specs=[block(place) for place in range(4)] + [whole(own), whole(other)],
            out_specs=tuple(
                pl.BlockSpec((128 * len(chips), D), lambda k, order: (0, 0))
                for chips in BLOCKS.values()
            ),
        ),
        cost_estimate=cost(2 * tokens * D * 2048, 4 * 2048 * D),
        name="unit_grads",
    )(order, left, left, left, left, own, other)


def out_grad_kernel(where_ref, own_ref, other_ref, *refs):
    contexts, keep_ref, give_ref, across_ref = refs[:3], refs[3], refs[4], refs[5]
    first = where_ref[1] == 0
    tokens = own_ref.shape[0]
    group = pl.program_id(0)

    @pl.when(group == 0)
    def _():
        lane = 0
        for ref in contexts:
            across_ref[lane : lane + ref.shape[1], :] = ref[...].T
            lane += ref.shape[1]

    across = across_ref[pl.ds(pl.multiple_of(group * 128, 128), 128), :]
    value = dot(across[:, :tokens], own_ref[...]) + dot(across[:, tokens:], other_ref[...])
    value = value.astype(BF)
    for head in range(2):
        zero, one = value[head * 64 : head * 64 + 32], value[head * 64 + 32 : head * 64 + 64]
        rows = slice(head * 32, head * 32 + 32)
        keep_ref[rows, :] = jnp.where(first, zero, one)
        give_ref[rows, :] = jnp.where(first, one, zero)


def out_grad(where, own, other, contexts):
    block = pl.BlockSpec((64, D), lambda i: (i, 0))
    return pl.pallas_call(
        out_grad_kernel,
        grid=(4,),
        out_shape=(shaped(256, D, BF),) * 2,
        in_specs=[SMEM, whole(own), whole(other)] + [whole(context) for context in contexts],
        out_specs=(block, block),
        scratch_shapes=[pltpu.VMEM((D // 2, 1024), BF)],
        cost_estimate=cost(1024 * D * D, 6 * 1024 * D),
        name="out_grad",
    )(where, own, other, *contexts)


def norm_grad_kernel(spans, left_ref, *refs):
    count = 4 * len(spans)
    mine_ref, theirs_ref, total_ref = refs[-3:]
    earlier = refs[count:-3]
    step = pl.program_id(0)
    first = 0
    lefts = []
    for start, end in spans:
        lefts.append(left_ref[:, first : first + end - start])
        first += end - start
    for pair in range(4):
        total = None
        for line, (left, span) in enumerate(zip(lefts, spans)):
            right = gathered(
                refs[4 * line : 4 * line + 4], slice(*span), slice(2 * pair, 2 * pair + 2)
            )
            part = times_transposed(left, right)
            total = part if total is None else total + part
        total_ref[:, 256 * pair : 256 * pair + 256] = total

    for half, out_ref in enumerate((mine_ref, theirs_ref)):

        @pl.when(step // 2 == half)
        def _(half=half, out_ref=out_ref):
            if earlier:
                out_ref[...] = total_ref[...] + earlier[half][...]
            else:
                out_ref[...] = total_ref[...]


def norm_grad(left, lines, spans, earlier=()):
    rows = left.shape[0]
    flat = [piece for line in lines for piece in line]
    halves = (
        pl.BlockSpec((256, D), lambda i: (jnp.minimum(i, 1), 0)),
        pl.BlockSpec((256, D), lambda i: (jnp.maximum(i - 2, 0), 0)),
    )
    return pl.pallas_call(
        partial(norm_grad_kernel, spans),
        grid=(4,),
        out_shape=(shaped(rows // 2, D, F32),) * 2,
        in_specs=[rows_spec(left.shape[1])]
        + [whole(piece) for piece in flat]
        + list(halves[: len(earlier)]),
        out_specs=halves,
        scratch_shapes=[pltpu.VMEM((256, D), F32)],
        cost_estimate=cost(2 * rows * D * left.shape[1], 12 * rows * D),
        name="norm_grad",
    )(left, *flat, *earlier)


def norm_back_kernel(
    where_ref, part_ref, more_ref, xhat_ref, inv_ref, gain_ref, g_ref, out_ref, sum_ref, chosen_ref
):
    @pl.when(pl.program_id(0) == 0)
    def _():
        choice_into(where_ref[0], chosen_ref)
        sum_ref[...] = jnp.zeros_like(sum_ref)

    grad = part_ref[...] + more_ref[...]
    xhat = xhat_ref[...]
    scaled = grad * gain_ref[...]
    value = (
        scaled
        - jnp.mean(scaled, axis=-1, keepdims=True)
        - xhat * jnp.mean(scaled * xhat, axis=-1, keepdims=True)
    ) * inv_ref[...]
    high = value.astype(BF)
    low = (value - high.astype(F32)).astype(BF)
    value = times_transposed(high, chosen_ref[...]) + times_transposed(low, chosen_ref[...])
    out_ref[...] = (g_ref[...].astype(F32) + value).astype(BF)
    sum_ref[0:1, :] += jnp.sum(grad * xhat, axis=0, keepdims=True)
    sum_ref[1:2, :] += jnp.sum(grad, axis=0, keepdims=True)


def norm_back(where, part, more, xhat, inv_std, gain, grad):
    rows = grad.shape[0]
    one = pl.BlockSpec((1, D), lambda i: (0, 0))
    return pl.pallas_call(
        norm_back_kernel,
        grid=(rows // 256,),
        out_shape=(shaped(rows, D, BF), shaped(8, D, F32)),
        in_specs=[SMEM] + [rows_spec(D)] * 3 + [rows_spec(1), one, rows_spec(D)],
        out_specs=(rows_spec(D), pl.BlockSpec((8, D), lambda i: (0, 0))),
        scratch_shapes=[pltpu.VMEM((D, D), BF)],
        cost_estimate=cost(4 * rows * D * D, 16 * rows * D),
        name="norm_back",
    )(where, part, more, xhat, inv_std, gain, grad)


def paste_in_kernel(where_ref, mine_ref, other_ref, out_ref):
    core = where_ref[1]
    for owner, ref in ((core, mine_ref), (1 - core, other_ref)):
        for block in range(CHIPS):
            at = pl.multiple_of((2 * block + owner) * 128, 128)
            out_ref[:, pl.ds(at, 128)] = ref[:, block * 128 : block * 128 + 128]


def paste_qkv_kernel(where_ref, mine_ref, other_ref, out_ref):
    core = where_ref[1]
    low = lanes_low(mine_ref.shape[0])
    for owner, ref in ((core, mine_ref), (1 - core, other_ref)):
        for group in range(GROUPS):
            q, k, v = (
                ref[:, group * 384 + part * 128 : group * 384 + part * 128 + 128]
                for part in range(3)
            )
            turned = pltpu.roll(k, HD, 1)
            blocks = (jnp.where(low, q, turned), jnp.where(low, v, q), jnp.where(low, turned, v))
            for part, value in enumerate(blocks):
                at = (owner * GROUPS + group) * 384 + part * 128
                out_ref[:, pl.ds(pl.multiple_of(at, 128), 128)] = value


def paste(kernel, where, mine, other):
    return pl.pallas_call(
        kernel,
        out_shape=shaped(mine.shape[0], 2 * mine.shape[1], F32),
        in_specs=[SMEM, VMEM, VMEM],
        out_specs=VMEM,
        cost_estimate=cost(0, 16 * mine.shape[0] * mine.shape[1]),
        name="paste",
    )(where, mine, other)


def local_fast(
    hidden_in,
    document_labels,
    cotangent,
    ln_gain,
    ln_bias,
    qkv_weight,
    qkv_bias,
    out_weight,
    out_bias,
    fc_in_weight,
    fc_in_bias,
    fc_out_weight,
    fc_out_bias,
):
    local_seqs, tok_count = hidden_in.shape[:2]
    row_count = local_seqs * tok_count
    d_rows = qkv_weight.shape[0]
    f_rows = fc_out_weight.shape[0]
    units = fc_in_weight.shape[1] // 2
    pair = 2
    core = lax.axis_index("fsdp") % 2
    me = lax.axis_index("seq") * 4 + lax.axis_index("fsdp") // 2
    clock = Clock(jnp.stack([me, core]).astype(jnp.int32))
    box = {}

    waiting = []

    def slot(jobs, work=None, *inputs, chain=None, late=(), then=None):
        nonlocal waiting
        jobs, late = list(jobs), list(late)
        name, follow, more = chain if chain is not None else (None, None, ())
        gated, given, more = clock.join(tuple(job[2] for job in jobs + late), inputs, tuple(more))
        values = [job[3](value) for job, value in zip(jobs + late, gated)]
        made = work(*given) if work is not None else ()
        after = ()
        for job, value in list(zip(jobs, values)) + waiting:
            if chain is not None and job[1] == name:
                after = follow(value, *more)
        if then is not None:
            started = then(made)
            late = late + started
            values = values + [job[3](job[2]) for job in started]
        ended, values, older = waiting, values[: len(jobs)], values[len(jobs) :]
        found = values + [value for _, value in ended]
        found, made, after = clock.join(tuple(found), made, after)
        for job, value in zip(jobs + [job for job, _ in ended], found):
            job[0][job[1]] = value
        waiting = list(zip(late, older))
        return made if chain is None else (made, after)

    def moves(line, stage):
        return [
            (line.parts, name, line.parts[source], partial(cross, bit=bit))
            for name, source, bit in line.jobs(stage)
        ]

    def core_move(name, value):
        return (box, name, value, other_core)

    def pick(halves):
        first = core == 0
        return jnp.where(first, halves[0], halves[1]), jnp.where(first, halves[1], halves[0])

    def joined(mine, other):
        first = core == 0
        return jnp.concatenate(
            [jnp.where(first, mine, other), jnp.where(first, other, mine)], axis=0
        )

    x_own = hidden_in.reshape(row_count, D)
    g_own = cotangent.reshape(row_count, D)
    vectors = (ln_gain, ln_bias, qkv_bias, out_bias, fc_in_bias, fc_out_bias)
    keep1, give1, keep2, give2, in_keep, in_give, folded = cut(
        clock.token, qkv_weight, fc_in_weight, out_weight, vectors, document_labels
    )
    slot([core_move("give1", give1)])
    line_a = Gather(joined(keep1, box["give1"]))
    slot(moves(line_a, "far") + [core_move("x", x_own), core_move("give2", give2)])
    line_b = Gather(jnp.concatenate([folded, joined(keep2, box["give2"])], axis=1))
    line_d = Gather(fc_out_weight)
    slot(moves(line_a, "near") + moves(line_b, "far") + [core_move("in", in_give), core_move("g", g_own)])
    g_more = box["g"]
    bias, *tables = slot(
        moves(line_a, "first") + moves(line_b, "near"),
        lambda a, b: marks(clock.token, a, b),
        line_a.parts["a"],
        line_a.parts["b"],
    )
    line_c = Gather(joined(in_keep, box["in"]))
    (xhat, inv_std), grad_sum = slot(
        moves(line_a, "second") + moves(line_c, "far"),
        lambda own, other, g: (
            prepare(clock.token, own, other),
            jnp.sum(g.astype(F32), axis=0),
        ),
        x_own,
        box["x"],
        g_own,
    )
    a_pieces = line_a.pieces()
    made = slot(
        moves(line_b, "first") + moves(line_c, "near"),
        lambda xhat, tables, pieces: project_first(clock.token, xhat, tables, pieces),
        xhat,
        tables,
        a_pieces,
    )
    queries, kvs = [made[0], made[2]], [[made[1]], [made[3]]]
    normed, normed_t, b_more, b_in, b_rows, gain = made[4:]
    moved, results, backs = {}, {}, {}

    def up(group, hop):
        return (moved, (group, hop), kvs[group][hop], partial(shift, by=1))

    def landed(*found):
        for group, hop in found:
            kvs[group].append(moved[group, hop])

    def down(group, hop):
        value = results[group][4]
        if hop == 1:
            value = (results[group][3].astype(F32) + backs[group, 0].astype(F32)).astype(BF)
        return (backs, (group, hop), value, partial(shift, by=-1))

    def attention(*groups):
        def work(*given):
            return [attend(group, *args) for group, args in zip(groups, given)]

        return work, *[
            (queries[group], context_grad, bias, tuple(kvs[group])) for group in groups
        ]

    def attended(groups, found):
        for group, result in zip(groups, found):
            results[group] = result

    slot(moves(line_b, "second") + [up(0, 0)], late=moves(line_d, "far"))
    landed((0, 0))
    b_pieces = line_b.pieces()
    made, (out_keep, out_give) = slot(
        moves(line_c, "first") + [up(0, 1)],
        lambda normed, bias, tables, pieces: (
            project_more(normed, bias, tables, pieces),
            head_rows(clock.token, pieces),
        ),
        normed,
        b_more,
        tables,
        b_pieces,
    )
    landed((0, 1))
    queries.append(made[0])
    kvs.append([made[1]])

    def first_attention(out_more, g_own, g_more, out_keep, query, bias, kvs):
        grad, heads = context_gradient(clock.token, g_own, g_more, out_keep, out_more)
        return grad, heads, attend(0, query, grad, bias, kvs)

    _, (context_grad, out_heads, found) = slot(
        moves(line_c, "second") + moves(line_d, "near") + [up(1, 0), core_move("out", out_give)],
        chain=(
            "out",
            first_attention,
            (g_own, g_more, out_keep, queries[0], bias, tuple(kvs[0])),
        ),
    )
    results[0] = found
    landed((1, 0))
    c_pieces = line_c.pieces()
    act, act_t, slope = slot(
        moves(line_d, "first") + [up(1, 1), down(0, 0)],
        lambda normed, b_in, pieces: hidden(normed, pieces, b_in),
        normed,
        b_in,
        c_pieces,
        late=[up(2, 0)],
    )
    landed((1, 1))
    work, *given = attention(1)

    def with_units(given, act_t, own, other):
        found = work(given)
        return found, unit_grads(clock.token[0], act_t, own, other), shift(found[0][4], -1)

    (found, fc_parts, backs[1, 0]), moved[2, 1] = slot(
        moves(line_d, "second") + [down(0, 1)],
        with_units,
        *given,
        act_t,
        g_own,
        g_more,
        chain=((2, 0), lambda value: shift(value, 1), ()),
    )
    attended([1], found)
    landed((2, 0), (2, 1))
    d_pieces = line_d.pieces()
    sum_fc = Scatter(fc_parts)
    work2, *given = attention(2)

    def last_attention(given, earlier, own, other):
        found = work2(given)
        contexts = earlier + [found[0][0]]
        return found, contexts, out_grad(clock.token, own, other, contexts)

    found, contexts, (out_keep, out_give) = slot(
        moves(sum_fc, "first") + [down(1, 1)],
        last_attention,
        *given,
        [results[group][0] for group in range(2)],
        g_own,
        g_more,
        then=lambda made: [(backs, (2, 0), made[0][0][4], partial(shift, by=-1))],
    )
    attended([2], found)

    def units_back(out_more, out_keep, normed_t, own, other, slope, pieces):
        hidden_grad, hidden_sum = unit_back(clock.token, own, other, slope, pieces)
        more = jnp.concatenate([out_keep, out_more], axis=0)
        return hidden_grad, hidden_sum, row_grads(clock.token, normed_t, hidden_grad, more)

    _, (hidden_grad, hidden_sum, in_parts) = slot(
        moves(sum_fc, "second") + [core_move("out_grad", out_give)],
        chain=("out_grad", units_back, (out_keep, normed_t, g_own, g_more, slope, d_pieces)),
    )
    sum_in = Scatter(in_parts)
    (out_mine, out_theirs), earlier = slot(
        moves(sum_in, "first") + [down(2, 1)],
        lambda act, heads, contexts, pieces, grad, c_pieces: (
            unit_out(clock.token, act, heads, contexts, pieces),
            norm_grad(grad, [c_pieces], [(0, units)]),
        ),
        act,
        out_heads,
        contexts,
        d_pieces,
        hidden_grad,
        c_pieces,
    )

    def last_grads(normed_t, tables, triples):
        projected_grad, total = unturn(tables, triples)
        return projected_grad, total, row_grads(clock.token, normed_t, projected_grad)

    projected_grad, qkv_bias_sum, parts = slot(
        moves(sum_in, "second") + moves(sum_fc, "near") + [core_move("out_side", out_theirs)],
        last_grads,
        normed_t,
        tables,
        [(results[group][1], results[group][2], backs[group, 1]) for group in range(3)],
    )
    sum_qkv = Scatter(parts)
    norm_mine, norm_theirs = slot(
        moves(sum_qkv, "first") + moves(sum_in, "near") + moves(sum_fc, "far"),
        lambda projected_grad, earlier, *lines: norm_grad(
            projected_grad, lines, [(0, 768), (512, 1280)], earlier
        ),
        projected_grad,
        earlier,
        a_pieces,
        b_pieces,
    )

    def finish_output(x_own, out_mine, out_more, b_rows):
        order = jnp.asarray(np.array(ORDER, np.int32)) ^ me
        spots = place_of(jnp.arange(CHIPS, dtype=jnp.int32) ^ me)
        b_rows = b_rows.reshape(CHIPS, 2 * d_rows)[spots].reshape(1, D)
        return (x_own.astype(F32) + out_mine + out_more + b_rows).astype(BF)

    def small_rows(norm_sums, qkv_bias_sum, hidden_sum, grad_sum):
        spots = place_of(jnp.arange(CHIPS, dtype=jnp.int32) ^ me)
        norm_sums = norm_sums[:2].reshape(2, CHIPS, 2, d_rows)[:, spots].reshape(2, D)
        mine = (jnp.arange(2) == core)[:, None]
        qkv_full = (
            jnp.where(mine, qkv_bias_sum, 0.0)
            .reshape(2, GROUPS, 3, pair, HD)
            .transpose(0, 1, 3, 2, 4)
            .reshape(3 * D)
        )
        in_full = jnp.where(mine[None], hidden_sum.reshape(CHIPS, 1, f_rows), 0.0)
        packed = jnp.concatenate(
            [
                vector.reshape(2 * CHIPS, -1)
                for vector in (norm_sums[0], norm_sums[1], qkv_full, grad_sum, in_full)
            ],
            axis=1,
        ).reshape(CHIPS, -1)
        return packed[jnp.asarray(np.array(ORDER, np.int32)) ^ me]

    def back_work(norm_more, norm_mine, xhat, inv_std, gain, g_own, *sums):
        input_grad, norm_sums = norm_back(
            clock.token, norm_mine, norm_more, xhat, inv_std, gain, g_own
        )
        return input_grad, small_rows(norm_sums, *sums)

    _, (input_grad, packed) = slot(
        moves(sum_qkv, "second") + moves(sum_in, "far") + [core_move("norm", norm_theirs)],
        chain=(
            "norm",
            back_work,
            (norm_mine, xhat, inv_std, gain, g_own, qkv_bias_sum, hidden_sum, grad_sum),
        ),
    )

    def fold(bit):
        return (box, "fold", packed[packed.shape[0] // 2 :], partial(cross, bit=bit))

    def half_sum():
        return packed[: packed.shape[0] // 2] + box["fold"]

    def two_folds(value, rows):
        half = rows[: rows.shape[0] // 2] + value
        give = half[half.shape[0] // 2 :]
        return half[: half.shape[0] // 2] + cross(give, X)

    in_rows = sum_in.result()
    in_keep, in_give = pick(in_rows[:, :units].reshape(2, d_rows, units))
    out_weight_grad = in_rows[:, units:].reshape(2, d_rows, D // 2)
    output, packed = slot(
        moves(sum_qkv, "near") + [fold(Y), core_move("in_rows", in_give)],
        finish_output,
        x_own,
        out_mine,
        box["out_side"],
        b_rows,
        chain=("fold", two_folds, (packed,)),
    )
    fc_in_weight_grad = slot(
        moves(sum_qkv, "far") + [fold(NEAR)],
        lambda mine, other: paste(paste_in_kernel, clock.token, mine, other),
        in_keep,
        box["in_rows"],
    )
    packed = half_sum()
    qkv_keep, qkv_give = pick(sum_qkv.result().reshape(2, d_rows, -1))
    slot([core_move("qkv_rows", qkv_give), fold(FAR)])
    sums_keep, sums_give = pick(half_sum().reshape(2, -1))
    sums = sums_keep + other_core(sums_give)
    parts = []
    first = 0
    for width in (d_rows, d_rows, 3 * d_rows, d_rows, f_rows):
        parts.append(sums[first : first + width])
        first += width
    return (
        output.reshape(local_seqs, tok_count, D),
        input_grad.reshape(local_seqs, tok_count, D),
        parts[0],
        parts[1],
        paste(paste_qkv_kernel, clock.token, qkv_keep, box["qkv_rows"]),
        parts[2],
        jnp.concatenate([out_weight_grad[0], out_weight_grad[1]], axis=1),
        parts[3],
        fc_in_weight_grad,
        parts[4],
        sum_fc.result(),
        parts[3],
    )


def solution(mesh):
    rows = P(("seq", "fsdp"))
    wide = P(("seq", "fsdp"), None)
    act = P("fsdp", "seq", None)
    placed = (act, P("fsdp", "seq"), act) + (rows, rows) + (wide, rows) * 4
    small = dict(mesh.shape) == {"seq": 4, "fsdp": 8}
    return jax.shard_map(
        local_fast if small else local_plain,
        mesh=mesh,
        in_specs=placed,
        out_specs=(act, act, rows, rows) + (wide, rows) * 4,
        check_vma=False,
    )
```

```python
from functools import partial
import math

import jax
import jax.numpy as jnp
import numpy as np
from jax import lax
from jax.experimental import pallas as pl
from jax.experimental.pallas import tpu as pltpu
from jax.sharding import PartitionSpec as P

D = 1024
H = 16
HD = 64
ROT = 16
GROUPS = 4
BF = jnp.bfloat16
F32 = jnp.float32


def rotate(values, cosine, sine_part):
    half_rot = ROT // 2
    first_part = values[..., :half_rot]
    second_part = values[..., half_rot:ROT]
    return jnp.concatenate(
        [
            first_part * cosine - second_part * sine_part,
            second_part * cosine + first_part * sine_part,
            values[..., ROT:],
        ],
        axis=-1,
    )


def position_angles(segments):
    length = segments.shape[0]
    places = jnp.arange(length, dtype=jnp.int32)
    boundary = jnp.concatenate([jnp.ones((1,), dtype=jnp.bool_), segments[1:] != segments[:-1]])
    starts = lax.cummax(jnp.where(boundary, places, 0), axis=0)
    positions = (places - starts).astype(jnp.float32)
    inverse = 1.0 / 10000.0 ** (jnp.arange(0, ROT, 2, dtype=jnp.float32) / ROT)
    return positions[:, None] * inverse[None, :]


def make_mask(segments, first_row, block_rows):
    length = segments.shape[0]
    query_index = first_row + jnp.arange(block_rows, dtype=jnp.int32)
    key_index = jnp.arange(length, dtype=jnp.int32)
    query_segments = lax.dynamic_slice_in_dim(segments, first_row, block_rows, 0)
    return (key_index[None, :] <= query_index[:, None]) & (
        query_segments[:, None] == segments[None, :]
    )


def outer_product(left, right):
    return lax.dot_general(
        left, right, (((0,), (0,)), ((), ())), preferred_element_type=jnp.float32
    )


def times_transposed(left, right):
    return lax.dot_general(
        left, right, (((1,), (1,)), ((), ())), preferred_element_type=jnp.float32
    )


def local_plain(
    hidden_in,
    document_labels,
    cotangent,
    ln_gain,
    ln_bias,
    qkv_weight,
    qkv_bias,
    out_weight,
    out_bias,
    fc_in_weight,
    fc_in_bias,
    fc_out_weight,
    fc_out_bias,
):
    gathered = (
        lax.all_gather(ln_gain, ("seq", "fsdp"), axis=0, tiled=True),
        lax.all_gather(ln_bias, ("seq", "fsdp"), axis=0, tiled=True),
        lax.all_gather(qkv_weight, ("seq", "fsdp"), axis=0, tiled=True),
        lax.all_gather(qkv_bias, ("seq", "fsdp"), axis=0, tiled=True),
        lax.all_gather(out_weight, ("seq", "fsdp"), axis=0, tiled=True),
        lax.all_gather(out_bias, ("seq", "fsdp"), axis=0, tiled=True),
        lax.all_gather(fc_in_weight, ("seq", "fsdp"), axis=0, tiled=True),
        lax.all_gather(fc_in_bias, ("seq", "fsdp"), axis=0, tiled=True),
        lax.all_gather(fc_out_weight, ("seq", "fsdp"), axis=0, tiled=True),
        lax.all_gather(fc_out_bias, ("seq", "fsdp"), axis=0, tiled=True),
    )
    norm_multiplier, norm_shift, w_qkv, b_qkv, w_out, b_out, w_in, b_in, w_fc, b_fc = gathered
    norm_multiplier = norm_multiplier.astype(jnp.float32)
    norm_shift = norm_shift.astype(jnp.float32)
    groups = lax.axis_size("seq")
    per_group = H // groups
    local_seqs = hidden_in.shape[0]
    tok_count = hidden_in.shape[1]
    row_count = local_seqs * tok_count
    tokens = hidden_in.reshape(row_count, D).astype(jnp.float32)
    average = jnp.mean(tokens, axis=-1, keepdims=True)
    centered = tokens - average
    spread = jnp.mean(centered * centered, axis=-1, keepdims=True)
    inv_std = lax.rsqrt(spread + 1e-05)
    rescaled_rows = centered * inv_std
    normed = (rescaled_rows * norm_multiplier + norm_shift).astype(jnp.bfloat16)
    projected = jnp.dot(normed, w_qkv, preferred_element_type=jnp.float32) + b_qkv.astype(
        jnp.float32
    )
    segments_all = lax.all_gather(document_labels, "seq", axis=1, tiled=True)
    angles_all = jax.vmap(position_angles)(segments_all)
    angles = lax.dynamic_slice_in_dim(
        angles_all, lax.axis_index("seq") * tok_count, tok_count, 1
    ).reshape(row_count, ROT // 2)
    cosine = jnp.cos(angles)[:, None, None, :]
    sine_part = jnp.sin(angles)[:, None, None, :]
    head_parts = projected.reshape(row_count, H, 3, HD)
    turned = jnp.concatenate(
        [rotate(head_parts[:, :, :2], cosine, sine_part), head_parts[:, :, 2:]], axis=2
    ).astype(jnp.bfloat16)
    outgoing = turned.reshape(local_seqs, tok_count, groups, per_group * 3 * HD)
    arrived = lax.all_to_all(outgoing, "seq", split_axis=2, concat_axis=1, tiled=True)
    length = arrived.shape[1]
    local_heads = arrived.reshape(local_seqs, length, per_group, 3, HD)
    queries_seq = local_heads[:, :, :, 0]
    keys_seq = local_heads[:, :, :, 1]
    values_seq = local_heads[:, :, :, 2]
    block_rows = min(512, length)
    block_count = length // block_rows
    scale_factor = 1.0 / math.sqrt(HD)

    def attend_forward(inputs):
        query_all, key_everywhere, value_all, segments = inputs

        def forward_step(running, block_index):
            first_row = block_index * block_rows
            query_rows = lax.dynamic_slice_in_dim(query_all, first_row, block_rows, 0)
            allowed = make_mask(segments, first_row, block_rows)
            raw_scores = (
                jnp.einsum(
                    "qhd,khd->hqk", query_rows, key_everywhere, preferred_element_type=jnp.float32
                )
                * scale_factor
            )
            raw_scores = jnp.where(allowed[None], raw_scores, -1e30)
            row_max = jnp.max(raw_scores, axis=-1, keepdims=True)
            unscaled = jnp.exp(raw_scores - row_max)
            row_total = jnp.sum(unscaled, axis=-1, keepdims=True)
            probabilities = (unscaled / row_total).astype(jnp.bfloat16)
            context_rows = jnp.einsum(
                "hqk,khd->qhd", probabilities, value_all, preferred_element_type=jnp.float32
            )
            log_total = (row_max + jnp.log(row_total))[..., 0]
            return (running, (context_rows, log_total))

        _, (context_blocks, log_blocks) = lax.scan(
            forward_step, None, jnp.arange(block_count, dtype=jnp.int32)
        )
        return (context_blocks.reshape(length, per_group * HD).astype(jnp.bfloat16), log_blocks)

    context_seq, log_totals = lax.map(
        attend_forward, (queries_seq, keys_seq, values_seq, segments_all)
    )
    context_heads = context_seq.reshape(local_seqs, length, 1, per_group * HD)
    returned = lax.all_to_all(context_heads, "seq", split_axis=1, concat_axis=2, tiled=True)
    context = returned.reshape(row_count, D)
    attn_out = jnp.dot(context, w_out, preferred_element_type=jnp.float32) + b_out.astype(
        jnp.float32
    )
    hidden_pre = jnp.dot(normed, w_in, preferred_element_type=jnp.float32) + b_in.astype(
        jnp.float32
    )
    activated = jax.nn.gelu(hidden_pre, approximate=False).astype(jnp.bfloat16)
    mlp_out = jnp.dot(activated, w_fc, preferred_element_type=jnp.float32) + b_fc.astype(
        jnp.float32
    )
    output = (tokens + attn_out + mlp_out).astype(jnp.bfloat16).reshape(local_seqs, tok_count, D)
    grad_out = cotangent.reshape(row_count, D)
    grad_wide = grad_out.astype(jnp.float32)
    out_bias_grad = jnp.sum(grad_wide, axis=0)
    fc_out_bias_grad = jnp.sum(grad_wide, axis=0)
    out_weight_grad = outer_product(context, grad_out)
    fc_out_weight_grad = outer_product(activated, grad_out)
    act_grad = times_transposed(grad_out, w_fc)
    _, gelu_back = jax.vjp(partial(jax.nn.gelu, approximate=False), hidden_pre)
    hidden_grad = gelu_back(act_grad)[0].astype(jnp.bfloat16)
    fc_in_weight_grad = outer_product(normed, hidden_grad)
    fc_in_bias_grad = jnp.sum(hidden_grad.astype(jnp.float32), axis=0)
    context_grad = times_transposed(grad_out, w_out).astype(jnp.bfloat16)
    grad_outgoing = context_grad.reshape(local_seqs, tok_count, groups, per_group * HD)
    head_grad_seq = lax.all_to_all(
        grad_outgoing, "seq", split_axis=2, concat_axis=1, tiled=True
    ).reshape(local_seqs, length, per_group, HD)

    def attend_backward(inputs):
        query_all, key_everywhere, value_all, segments, head_grad, log_blocks = inputs

        def backward_step(running, block_index):
            key_acc, value_accumulator = running
            first_row = block_index * block_rows
            query_rows = lax.dynamic_slice_in_dim(query_all, first_row, block_rows, 0)
            grad_rows = lax.dynamic_slice_in_dim(head_grad, first_row, block_rows, 0)
            log_rows = log_blocks[block_index]
            allowed = make_mask(segments, first_row, block_rows)
            raw_scores = (
                jnp.einsum(
                    "qhd,khd->hqk", query_rows, key_everywhere, preferred_element_type=jnp.float32
                )
                * scale_factor
            )
            raw_scores = jnp.where(allowed[None], raw_scores, -1e30)
            probabilities = jnp.where(allowed[None], jnp.exp(raw_scores - log_rows[..., None]), 0.0)
            value_accumulator = value_accumulator + jnp.einsum(
                "hqk,qhd->khd",
                probabilities.astype(jnp.bfloat16),
                grad_rows,
                preferred_element_type=jnp.float32,
            )
            prob_grad = jnp.einsum(
                "qhd,khd->hqk", grad_rows, value_all, preferred_element_type=jnp.float32
            )
            inner_total = jnp.sum(probabilities * prob_grad, axis=-1, keepdims=True)
            score_grad = (probabilities * (prob_grad - inner_total)).astype(jnp.bfloat16)
            query_grad = (
                jnp.einsum(
                    "hqk,khd->qhd", score_grad, key_everywhere, preferred_element_type=jnp.float32
                )
                * scale_factor
            )
            key_acc = (
                key_acc
                + jnp.einsum(
                    "hqk,qhd->khd", score_grad, query_rows, preferred_element_type=jnp.float32
                )
                * scale_factor
            )
            return ((key_acc, value_accumulator), query_grad)

        empty_grad = jnp.zeros((length, per_group, HD), jnp.float32)
        (key_grad, value_grad), query_blocks = lax.scan(
            backward_step, (empty_grad, empty_grad), jnp.arange(block_count, dtype=jnp.int32)
        )
        query_grad = query_blocks.reshape(length, per_group, HD)
        return jnp.stack([query_grad, key_grad, value_grad], axis=2).astype(jnp.bfloat16)

    stacked = lax.map(
        attend_backward,
        (queries_seq, keys_seq, values_seq, segments_all, head_grad_seq, log_totals),
    )
    returned_grad = lax.all_to_all(
        stacked.reshape(local_seqs, length, 1, per_group * 3 * HD),
        "seq",
        split_axis=1,
        concat_axis=2,
        tiled=True,
    )
    back_heads = returned_grad.reshape(row_count, H, 3, HD).astype(jnp.float32)
    unturned = jnp.concatenate(
        [rotate(back_heads[:, :, :2], cosine, -sine_part), back_heads[:, :, 2:]], axis=2
    )
    projected_grad = unturned.reshape(row_count, 3 * D).astype(jnp.bfloat16)
    qkv_weight_grad = outer_product(normed, projected_grad)
    qkv_bias_grad = jnp.sum(projected_grad.astype(jnp.float32), axis=0)
    normalized_gradient = times_transposed(projected_grad, w_qkv) + times_transposed(
        hidden_grad, w_in
    )
    ln_gain_grad = jnp.sum(normalized_gradient * rescaled_rows, axis=0)
    ln_bias_grad = jnp.sum(normalized_gradient, axis=0)
    standardized_gradient = normalized_gradient * norm_multiplier
    norm_back = (
        standardized_gradient
        - jnp.mean(standardized_gradient, axis=-1, keepdims=True)
        - rescaled_rows * jnp.mean(standardized_gradient * rescaled_rows, axis=-1, keepdims=True)
    ) * inv_std
    input_grad = (grad_wide + norm_back).astype(jnp.bfloat16).reshape(local_seqs, tok_count, D)
    summed = (
        lax.psum_scatter(ln_gain_grad, ("seq", "fsdp"), scatter_dimension=0, tiled=True),
        lax.psum_scatter(ln_bias_grad, ("seq", "fsdp"), scatter_dimension=0, tiled=True),
        lax.psum_scatter(qkv_weight_grad, ("seq", "fsdp"), scatter_dimension=0, tiled=True),
        lax.psum_scatter(qkv_bias_grad, ("seq", "fsdp"), scatter_dimension=0, tiled=True),
        lax.psum_scatter(out_weight_grad, ("seq", "fsdp"), scatter_dimension=0, tiled=True),
        lax.psum_scatter(out_bias_grad, ("seq", "fsdp"), scatter_dimension=0, tiled=True),
        lax.psum_scatter(fc_in_weight_grad, ("seq", "fsdp"), scatter_dimension=0, tiled=True),
        lax.psum_scatter(fc_in_bias_grad, ("seq", "fsdp"), scatter_dimension=0, tiled=True),
        lax.psum_scatter(fc_out_weight_grad, ("seq", "fsdp"), scatter_dimension=0, tiled=True),
        lax.psum_scatter(fc_out_bias_grad, ("seq", "fsdp"), scatter_dimension=0, tiled=True),
    )
    return (
        output,
        input_grad,
        summed[0],
        summed[1],
        summed[2],
        summed[3],
        summed[4],
        summed[5],
        summed[6],
        summed[7],
        summed[8],
        summed[9],
    )


def dot(left, right):
    return jnp.dot(left, right, preferred_element_type=F32)


def swap(value, axis, bit):
    return lax.ppermute(value, axis, [(i, i ^ bit) for i in range(lax.axis_size(axis))])


def shift(value, by):
    count = lax.axis_size("seq")
    return lax.ppermute(
        value, "seq", [(i, i + by) for i in range(count) if 0 <= i + by < count]
    )


class Clock:
    def __init__(self, token):
        self.token = token

    def join(self, *values):
        values, self.token = lax.optimization_barrier((values, self.token))
        return values


X, Y, NEAR, FAR = 1, 2, 4, 8
CHIPS = 16
ORDER = [0, 8, 4, 12, 1, 9, 5, 13, 2, 10, 6, 14, 3, 11, 7, 15]
SUMS = {"ax": [0, 8, 1, 9], "by": [4, 12, 6, 14], "yax": [2, 10, 3, 11], "xby": [5, 13, 7, 15]}


def place_of(chip):
    return (chip // FAR) % 2 + (chip // NEAR) % 2 * 2 + chip % 2 * 4 + (chip // Y) % 2 * 8


def cross(value, bit):
    return swap(value, "seq", bit // 4) if bit >= 4 else swap(value, "fsdp", bit * 2)


def other_core(value):
    return swap(value, "fsdp", 1)


class Gather:
    def __init__(self, shard):
        self.parts = {"s": shard}

    def jobs(self, stage):
        parts = self.parts
        if stage == "near":
            parts["a"] = jnp.concatenate([parts["s"], parts["f"]], axis=0)
        if stage == "second":
            parts["ax"] = jnp.concatenate([parts["a"], parts["xa"]], axis=0)
            parts["by"] = jnp.concatenate([parts["b"], parts["yb"]], axis=0)
        return {
            "far": [("f", "s", FAR)],
            "near": [("b", "a", NEAR)],
            "first": [("xa", "a", X), ("yb", "b", Y)],
            "second": [("yax", "ax", Y), ("xby", "by", X)],
        }[stage]

    def pieces(self):
        return [self.parts[name] for name in SUMS]


LAY = [(0, 0), (1, 0), (0, 1), (3, 0), (2, 0), (1, 1), (2, 1), (3, 1)]


def gathered(refs, columns=slice(None), which=slice(None)):
    half = refs[0].shape[0] // 2
    return jnp.concatenate(
        [refs[array][part * half : part * half + half, columns] for array, part in LAY[which]],
        axis=0,
    )


BLOCKS = {
    "a": [0, 8],
    "xa": [1, 9],
    "b": [4, 12],
    "yb": [6, 14],
    "yax": [2, 10, 3, 11],
    "xby": [5, 13, 7, 15],
}


class Scatter:
    def __init__(self, blocks):
        self.parts = dict(zip(BLOCKS, blocks))

    def total(self, first, last, *names):
        return sum(self.parts[name][first:last].astype(F32) for name in names)

    def jobs(self, stage):
        parts = self.parts
        rows = parts["a"].shape[0]
        if stage == "second":
            for name, other in (("xa", "r_yax"), ("yb", "r_xby")):
                value = parts[name].astype(F32) + parts[other][rows:].astype(F32)
                parts[name] = value.astype(BF)
        if stage == "near":
            parts["b"] = self.total(0, rows, "b", "r_xby", "r_yb").astype(BF)
        if stage == "far":
            value = self.total(rows // 2, rows, "a", "r_yax", "r_xa", "r_b")
            parts["send"] = value.astype(BF)
        return {
            "first": [("r_yax", "yax", Y), ("r_xby", "xby", X)],
            "second": [("r_xa", "xa", X), ("r_yb", "yb", Y)],
            "near": [("r_b", "b", NEAR)],
            "far": [("r_far", "send", FAR)],
        }[stage]

    def result(self):
        rows = self.parts["a"].shape[0] // 2
        return self.total(0, rows, "a", "r_yax", "r_xa", "r_b", "r_far")


def cost(flops, bytes_accessed, transcendentals=0):
    return pl.CostEstimate(
        flops=flops, bytes_accessed=bytes_accessed, transcendentals=transcendentals
    )


SMEM = pl.BlockSpec(memory_space=pltpu.SMEM)
VMEM = pl.BlockSpec(memory_space=pltpu.VMEM)
ANY = pl.BlockSpec(memory_space=pl.ANY)


def whole(array):
    return pl.BlockSpec(array.shape, lambda *_: (0,) * len(array.shape))


def shaped(rows, columns, dtype):
    return jax.ShapeDtypeStruct((rows, columns), dtype)


def stack(refs):
    return jnp.concatenate([ref[...] for ref in refs], axis=0)


def lanes_low(rows):
    return lax.broadcasted_iota(jnp.int32, (rows, 128), 1) < HD


def cut_kernel(where_ref, qkv_ref, in_ref, out_w_ref, gain_ref, shift_ref, qb_ref, ob_ref, ib_ref, fb_ref, label_ref, *refs):
    keep1, give1, keep2, give2, in_keep, in_give, folded, columns_ref, line_ref = refs
    core = where_ref[1]
    rows = qkv_ref.shape[0]
    columns_ref[...] = jnp.zeros_like(columns_ref)
    for row, ref in enumerate((gain_ref, shift_ref, ob_ref, fb_ref)):
        columns_ref[row : row + 1, :rows] = ref[...].astype(F32)
    line_ref[...] = jnp.zeros_like(line_ref)
    line_ref[0:1, :96] = qb_ref[...].astype(F32)
    line_ref[1:2, :] = ib_ref[...].astype(F32)
    bias, units = line_ref[0:1, :], line_ref[1:2, :]
    lane = lax.broadcasted_iota(jnp.int32, (1, 128), 1)
    first = core == 0
    parts = []
    for seq in range(2):
        for part in range(2):
            labels = (label_ref[seq : seq + 1, 128 * part : 128 * part + 128] + 1).astype(F32)
            parts += [pltpu.roll(labels, HD, 1), labels]
    zero = jnp.zeros_like(bias)
    parts.append(jnp.where(first, pltpu.roll(bias, 64, 1), zero))
    parts.append(
        jnp.where(
            first,
            jnp.where(lane < 96, bias, zero),
            jnp.where(lane >= 96, pltpu.roll(bias, 96, 1), zero),
        )
    )
    parts.append(jnp.where(first, zero, pltpu.roll(bias, 32, 1)))
    parts += [pltpu.roll(units, HD, 1), units]
    for row, value in enumerate(parts):
        line_ref[row : row + 1, :] = value
    low = lanes_low(rows)
    side = jnp.where(low, columns_ref[...].T[:rows], line_ref[...]).astype(BF)
    for owner, out1, out2 in ((core, keep1, keep2), (1 - core, give1, give2)):
        for group in range(GROUPS):
            at = pl.multiple_of((owner * GROUPS + group) * 384, 128)
            b0, b1, b2 = (
                qkv_ref[:, pl.ds(at + 128 * part, 128)].astype(F32) for part in range(3)
            )
            out = out1 if group < 2 else out2
            place = (group % 2) * 384
            turned = pltpu.roll(b0, HD, 1), pltpu.roll(b2, HD, 1)
            out[:, place : place + 128] = jnp.where(low, b0, b1).astype(BF)
            out[:, place + 128 : place + 256] = jnp.where(low, *turned).astype(BF)
            out[:, place + 256 : place + 384] = jnp.where(low, b1, b2).astype(BF)
        out1[:, 768:] = side
    for owner, out in ((core, in_keep), (1 - core, in_give)):
        for block in range(CHIPS):
            at = pl.multiple_of((2 * block + owner) * 128, 128)
            out[:, block * 128 : block * 128 + 128] = in_ref[:, pl.ds(at, 128)]
    folded[:rows, :] = out_w_ref[:, : D // 2]
    folded[rows:, :] = out_w_ref[:, D // 2 :]


def cut(where, qkv_rows, in_rows, out_rows, vectors, labels):
    rows = qkv_rows.shape[0]
    widths = (896, 896, 768, 768, 2048, 2048)
    return pl.pallas_call(
        cut_kernel,
        out_shape=tuple(shaped(rows, width, BF) for width in widths)
        + (shaped(2 * rows, D // 2, BF),),
        in_specs=[SMEM] + [VMEM] * 10,
        out_specs=(VMEM,) * 7,
        scratch_shapes=[pltpu.VMEM((128, 128), F32), pltpu.VMEM((rows, 128), F32)],
        cost_estimate=cost(0, 8 * rows * 4 * D),
        name="cut",
    )(where, qkv_rows, in_rows, out_rows, *[vector.reshape(1, -1) for vector in vectors], labels)


def turn(value, cosine, forth, back):
    return (
        value * cosine
        + pltpu.roll(value, 128 - ROT // 2, 1) * forth
        + pltpu.roll(value, ROT // 2, 1) * back
    )


def marks_kernel(where_ref, a_ref, b_ref, speed_ref, forth_ref, back_ref, bias_ref, cos_ref, to_ref, from_ref, side_ref):
    seq = pl.program_id(0)
    line, core = where_ref[0] // 4, where_ref[1]

    @pl.when(seq == 0)
    def _():
        side_ref[:128, :] = a_ref[...].astype(F32)
        side_ref[128:, :] = b_ref[...].astype(F32)

    owner = jnp.where(seq < 2, core, 1 - core)
    low = lanes_low(1)
    chunks = []
    for back in range(3):
        other = line - back
        relative = jnp.where(other >= 0, other, 0) ^ line
        block = relative // 2 + 2 * (relative % 2)
        rows = side_ref[pl.ds(pl.multiple_of(block * 64 + owner * 32, 8), 8), :]
        rows = jnp.where(seq % 2 == 0, rows[:4], rows[4:])
        rows = jnp.where(other >= 0, rows, jnp.zeros_like(rows))
        chunks.append(
            [
                jnp.where(low, pltpu.roll(rows[i : i + 1], HD, 1), rows[i + 1 : i + 2])
                for i in (0, 2)
            ]
        )
    total = None
    query = lax.broadcasted_iota(jnp.int32, (128, 256), 1)
    key = lax.broadcasted_iota(jnp.int32, (128, 256), 0)
    mine = jnp.concatenate(chunks[0], axis=1)
    for back, halves in enumerate(chunks):
        for half, labels in enumerate(halves):
            column = jnp.broadcast_to(labels, (128, 128)).T
            column = jnp.concatenate([column, column], axis=1)
            same = column == mine
            if back == 0:
                same = same & (key + 128 * half <= query)
            at = back * 256 + half * 128
            bias_ref[0, at : at + 128, :] = jnp.where(same, 0.0, -1e30)
            count = jnp.sum(jnp.where(same, 1.0, 0.0), axis=0, keepdims=True)
            total = count if total is None else total + count
    for half in range(2):
        position = total[:, 128 * half : 128 * half + 128] - 1.0
        angle = jnp.broadcast_to(position, (128, 128)).T * speed_ref[...]
        here = slice(128 * half, 128 * half + 128)
        cos_ref[here, :] = jnp.cos(angle)
        sine = jnp.sin(angle)
        to_ref[here, :] = sine * forth_ref[...]
        from_ref[here, :] = sine * back_ref[...]


def marks(where, a, b):
    half = ROT // 2
    inverse = 1.0 / 10000.0 ** (jnp.arange(0, ROT, 2, dtype=F32) / ROT)
    speed = jnp.concatenate([inverse, inverse, jnp.zeros((HD - ROT,), F32)])
    speed = jnp.concatenate([speed, speed]).reshape(1, 128)
    lanes = np.arange(128) % HD
    forth = jnp.asarray(-(lanes < half).astype(np.float32)[None, :])
    back = jnp.asarray(((lanes >= half) & (lanes < ROT)).astype(np.float32)[None, :])
    side = pl.BlockSpec((128, 128), lambda i: (0, 6))
    table = pl.BlockSpec((256, 128), lambda i: (i, 0))
    return pl.pallas_call(
        marks_kernel,
        grid=(4,),
        out_shape=(jax.ShapeDtypeStruct((4, 768, 256), F32),) + (shaped(1024, 128, F32),) * 3,
        in_specs=[SMEM, side, side, whole(speed), whole(forth), whole(back)],
        out_specs=(pl.BlockSpec((1, 768, 256), lambda i: (i, 0, 0)), table, table, table),
        scratch_shapes=[pltpu.VMEM((256, 128), F32)],
        cost_estimate=cost(1024 * 128 * 100, 4 * 1024 * 1024),
        name="marks",
    )(where, a, b, speed, forth, back)


def choice_into(me, chosen_ref):
    step = 128
    column = lax.broadcasted_iota(jnp.int32, (1, D), 1)
    place = column // 64
    chip = place % 2 * FAR + (place // 2) % 2 * NEAR + (place // 4) % 2 * X + place // 8 * Y
    wanted = (chip ^ me) * 64 + column % 64

    def some(i, carry):
        here = pl.ds(pl.multiple_of(i * step, step), step)
        row = lax.broadcasted_iota(jnp.int32, (step, D), 0) + i * step
        chosen_ref[here, :] = jnp.where(row == wanted, 1.0, 0.0).astype(BF)
        return carry

    lax.fori_loop(0, D // step, some, 0)


def prepare_kernel(
    steps, where_ref, own_ref, other_ref, xhat_ref, inv_ref, chosen_ref, rows_ref
):
    step = pl.program_id(0)

    @pl.when(step == 0)
    def _():
        choice_into(where_ref[0], chosen_ref)

    @pl.when(step < steps)
    def _():
        rows_ref[...] = own_ref[...]

    @pl.when(step >= steps)
    def _():
        rows_ref[...] = other_ref[...]

    x = dot(rows_ref[...], chosen_ref[...])
    average = jnp.mean(x, axis=-1, keepdims=True)
    centered = x - average
    spread = jnp.mean(centered * centered, axis=-1, keepdims=True)
    inv_std = lax.rsqrt(spread + 1e-05)
    xhat_ref[...] = centered * inv_std
    inv_ref[...] = inv_std


def prepare(where, own, other):
    rows = own.shape[0]
    step = 256
    steps = rows // step
    return pl.pallas_call(
        partial(prepare_kernel, steps),
        grid=(2 * steps,),
        out_shape=(shaped(2 * rows, D, F32), shaped(2 * rows, 1, F32)),
        in_specs=[
            SMEM,
            pl.BlockSpec((step, D), lambda i: (jnp.minimum(i, steps - 1), 0)),
            pl.BlockSpec((step, D), lambda i: (jnp.maximum(i - steps, 0), 0)),
        ],
        out_specs=(
            pl.BlockSpec((step, D), lambda i: (i, 0)),
            pl.BlockSpec((step, 1), lambda i: (i, 0)),
        ),
        scratch_shapes=[pltpu.VMEM((D, D), BF), pltpu.VMEM((step, D), BF)],
        cost_estimate=cost(4 * rows * D * D, 16 * rows * D),
        name="prepare",
    )(where, own, other)


def emit_heads(value, tables, outs):
    pairs = [
        (q_ref, kv_ref, pair)
        for q_ref, kv_ref in zip(outs[::2], outs[1::2])
        for pair in range(q_ref.shape[1] // 128)
    ]
    for index, (q_ref, kv_ref, pair) in enumerate(pairs):
        first, q, k = index * 384, pair * 128, pair * 256
        q_ref[:, q : q + 128] = turn(value[:, first : first + 128], *tables).astype(BF)
        kv_ref[:, k : k + 128] = turn(value[:, first + 128 : first + 256], *tables).astype(BF)
        kv_ref[:, k + 128 : k + 256] = value[:, first + 256 : first + 384].astype(BF)


def project_first_kernel(where_ref, xhat_ref, cos_ref, forth_ref, back_ref, *refs):
    pieces, outs = refs[:4], refs[4:8]
    normed_ref, normed_t_ref, more_ref, units_ref, rows_ref, gain_ref, side_ref, bias_ref, two_ref = refs[8:]
    me, core = where_ref[0], where_ref[1]

    @pl.when(pl.program_id(0) == 0)
    def _():
        side_ref[...] = gathered(pieces, slice(768, 896)).astype(F32)
        across = side_ref[...].T
        two_ref[...] = across[:8]
        gain_ref[...] = across[0:1]
        rows_ref[...] = across[2:3] + across[3:4]
        low = lanes_low(1)

        def block(chip, owner):
            start = place_of(chip ^ me) * 64 + owner * 32 + 8
            return side_ref[pl.ds(pl.multiple_of(start, 8), 8), :]

        def pair(one, two):
            return jnp.where(low, pltpu.roll(one, HD, 1), two)

        for group in range(GROUPS):
            heads = []
            for head in range(2):
                chip = core * 8 + 2 * group + head
                zero, one = block(chip, 0), block(chip, 1)
                heads.append((zero[0:1], zero[1:2] + one[1:2], one[2:3]))
            out = bias_ref if group < 2 else more_ref
            for part in range(3):
                at = (group % 2) * 384 + part * 128
                out[:, at : at + 128] = pair(heads[0][part], heads[1][part])
        for chip in range(CHIPS):
            found = block(chip, core)
            units_ref[:, chip * 128 : chip * 128 + 128] = pair(found[3:4], found[4:5])

    normed = (xhat_ref[...] * two_ref[0:1, :] + two_ref[1:2, :]).astype(BF)
    normed_ref[...] = normed
    normed_t_ref[...] = normed.T
    value = dot(normed, gathered(pieces, slice(0, 768))) + bias_ref[...]
    emit_heads(value, (cos_ref[...], forth_ref[...], back_ref[...]), outs)


TWO_PAIRS = (shaped(1024, 128, BF), shaped(1024, 256, BF)) * 2
ONE_GROUP = (shaped(1024, 256, BF), shaped(1024, 512, BF))


def rows_spec(columns, step=256):
    return pl.BlockSpec((step, columns), lambda i: (i, 0))


def project_first(where, xhat, tables, pieces):
    small = (shaped(1, 768, F32), shaped(1, 2048, F32), shaped(1, D, F32), shaped(1, D, F32))
    return pl.pallas_call(
        project_first_kernel,
        grid=(4,),
        out_shape=TWO_PAIRS + (shaped(1024, D, BF), shaped(D, 1024, BF)) + small,
        in_specs=[SMEM, rows_spec(D)] + [rows_spec(128)] * 3 + [whole(piece) for piece in pieces],
        out_specs=tuple(rows_spec(shape.shape[1]) for shape in TWO_PAIRS)
        + (rows_spec(D), pl.BlockSpec((D, 256), lambda i: (0, i)))
        + tuple(whole(shape) for shape in small),
        scratch_shapes=[
            pltpu.VMEM((D, 128), F32),
            pltpu.VMEM((1, 768), F32),
            pltpu.VMEM((8, D), F32),
        ],
        cost_estimate=cost(2 * 1024 * D * 768, 12 * 1024 * D),
        name="project_first",
    )(where, xhat, *tables, *pieces)


def project_more_kernel(normed_ref, bias_ref, cos_ref, forth_ref, back_ref, *refs):
    value = dot(normed_ref[...], gathered(refs[:4], slice(512, 1280))) + bias_ref[...]
    emit_heads(value, (cos_ref[...], forth_ref[...], back_ref[...]), refs[4:])


def project_more(normed, bias, tables, pieces):
    return pl.pallas_call(
        project_more_kernel,
        grid=(4,),
        out_shape=ONE_GROUP,
        in_specs=[rows_spec(D), whole(bias)]
        + [rows_spec(128)] * 3
        + [whole(piece) for piece in pieces],
        out_specs=tuple(rows_spec(shape.shape[1]) for shape in ONE_GROUP),
        cost_estimate=cost(2 * 1024 * D * 768, 6 * 1024 * D),
        name="project_more",
    )(normed, bias, *tables, *pieces)


def head_rows_kernel(where_ref, *refs):
    keep_ref, give_ref, held_ref = refs[4:]
    me, core = where_ref[0], where_ref[1]
    for index, chip in enumerate(ORDER):
        array, part = LAY[index // 2]
        piece, at = refs[array], part * 128 + index % 2 * 64
        found = chip ^ me
        start = pl.multiple_of((((found // 8) ^ core) * 8 + found % 8) * 32, 32)
        held_ref[pl.ds(start, 32), : D // 2] = piece[at : at + 32, :]
        held_ref[pl.ds(start, 32), D // 2 :] = piece[at + 32 : at + 64, :]
    keep_ref[...] = held_ref[:256, :]
    give_ref[...] = held_ref[256:, :]


def head_rows(where, pieces):
    return pl.pallas_call(
        head_rows_kernel,
        out_shape=(shaped(256, D, BF),) * 2,
        grid=(1,),
        in_specs=[SMEM] + [pl.BlockSpec((256, D // 2), lambda i: (0, 0))] * 4,
        out_specs=(pl.BlockSpec((256, D), lambda i: (0, 0)),) * 2,
        scratch_shapes=[pltpu.VMEM((512, D), BF)],
        cost_estimate=cost(0, 4 * 512 * D),
        name="head_rows",
    )(where, *pieces)


def context_grad_kernel(
    where_ref, own_ref, other_ref, keep_ref, more_ref, grad_ref, heads_ref, rows_ref
):
    core = where_ref[1]
    step = pl.program_id(0)

    @pl.when(step == 0)
    def _():
        for chip in range(8):
            rows = slice(chip * 32, chip * 32 + 32)
            heads_ref[pl.ds(pl.multiple_of(chip * 64 + core * 32, 32), 32), :] = keep_ref[rows, :]
            at = pl.multiple_of(chip * 64 + (1 - core) * 32, 32)
            heads_ref[pl.ds(at, 32), :] = more_ref[rows, :]

    @pl.when(step < 2)
    def _():
        rows_ref[...] = own_ref[...]

    @pl.when(step >= 2)
    def _():
        rows_ref[...] = other_ref[...]

    grad_ref[...] = times_transposed(rows_ref[...], heads_ref[...]).astype(BF)


def context_gradient(where, own, other, keep, more):
    return pl.pallas_call(
        context_grad_kernel,
        grid=(4,),
        out_shape=(shaped(1024, D // 2, BF), shaped(D // 2, D, BF)),
        in_specs=[
            SMEM,
            pl.BlockSpec((256, D), lambda i: (jnp.minimum(i, 1), 0)),
            pl.BlockSpec((256, D), lambda i: (jnp.maximum(i - 2, 0), 0)),
            whole(keep),
            whole(more),
        ],
        out_specs=(rows_spec(D // 2), pl.BlockSpec((D // 2, D), lambda i: (0, 0))),
        scratch_shapes=[pltpu.VMEM((256, D), BF)],
        cost_estimate=cost(1024 * D * D, 6 * 1024 * D),
        name="context_grad",
    )(where, own, other, keep, more)


def attend_kernel(q_ref, do_ref, bias_ref, *refs):
    kv_refs, o_ref, dq_ref, dkv_refs = refs[:3], refs[3], refs[4], refs[5:8]
    weight_ref, probs_ref, grad_ref = refs[8:]
    rows = q_ref.shape[0]
    scaled = q_ref[...] * 0.125
    given = do_ref[...]
    given_t = given.T.astype(F32)
    low = lanes_low(rows)
    zero = jnp.zeros_like(given)

    def heads(value):
        return jnp.concatenate([jnp.where(low, value, zero), jnp.where(low, zero, value)], axis=0)

    queries, grads = heads(scaled), heads(given)
    spans = [slice(chunk * rows, chunk * rows + rows) for chunk in range(3)]
    top = None
    for here, ref in zip(spans, kv_refs):
        bias = bias_ref[0, here, :]
        scores = times_transposed(ref[:, :128], queries) + jnp.concatenate([bias, bias], axis=1)
        weight_ref[here, :] = scores
        most = jnp.max(scores, axis=0, keepdims=True)
        top = most if top is None else jnp.maximum(top, most)
    total = jnp.zeros_like(top)
    for here in spans:
        unscaled = jnp.exp(weight_ref[here, :] - top)
        weight_ref[here, :] = unscaled
        total = total + jnp.sum(unscaled, axis=0, keepdims=True)
    inverse = 1.0 / total
    for here in spans:
        probs = weight_ref[here, :] * inverse
        weight_ref[here, :] = probs
        probs_ref[here, :] = probs.astype(BF)

    def both_heads(across, right_ref):
        return jnp.concatenate(
            [dot(across[:HD], right_ref[:, :rows]), dot(across[HD:], right_ref[:, rows:])], axis=0
        )

    values_t = jnp.concatenate([ref[:, 128:] for ref in kv_refs], axis=0).T
    keys_t = jnp.concatenate([ref[:, :128] for ref in kv_refs], axis=0).T
    out_t = both_heads(values_t, probs_ref)
    product = out_t * given_t
    inner = jnp.concatenate(
        [
            jnp.sum(product[:HD], axis=0, keepdims=True),
            jnp.sum(product[HD:], axis=0, keepdims=True),
        ],
        axis=1,
    )
    for here, ref in zip(spans, kv_refs):
        prob_grad = times_transposed(ref[:, 128:], grads)
        grad_ref[here, :] = (weight_ref[here, :] * (prob_grad - inner)).astype(BF)
    dq_t = both_heads(keys_t, grad_ref)
    o_ref[...] = out_t.T.astype(BF)
    dq_ref[...] = (dq_t.T * 0.125).astype(BF)
    for here, ref in zip(spans, dkv_refs):
        ref[:, :128] = dot(grad_ref[here, :], queries).astype(ref.dtype)
        ref[:, 128:] = dot(probs_ref[here, :], grads).astype(ref.dtype)


def attend(first, query, grad, bias, kvs):
    pairs = query.shape[1] // 128
    narrow = pl.BlockSpec((256, 128), lambda b, p: (b, p))
    wide = pl.BlockSpec((256, 256), lambda b, p: (b, p))
    return pl.pallas_call(
        attend_kernel,
        grid=(4, pairs),
        out_shape=(shaped(1024, 128 * pairs, BF),) * 2
        + (shaped(1024, 256 * pairs, F32),)
        + (shaped(1024, 256 * pairs, BF),) * 2,
        in_specs=[
            narrow,
            pl.BlockSpec((256, 128), lambda b, p: (b, first + p)),
            pl.BlockSpec((1, 768, 256), lambda b, p: (b, 0, 0)),
        ]
        + [wide] * 3,
        out_specs=(narrow, narrow) + (wide,) * 3,
        scratch_shapes=[pltpu.VMEM((768, 512), dtype) for dtype in (F32, BF, BF)],
        cost_estimate=cost(
            pairs * 24 * 4 * 256 * 768 * 128, pairs * 9 * 1024 * 1024, pairs * 8 * 256 * 768
        ),
        name="attend",
    )(query, grad, bias, *kvs)


def unturn_kernel(groups, cos_ref, forth_ref, back_ref, *refs):
    cosine, forth, back = cos_ref[...], -forth_ref[...], -back_ref[...]
    out_ref, sum_ref = refs[-2:]
    first = 0
    for group in range(groups):
        dq_ref, own_ref, more_ref = refs[3 * group : 3 * group + 3]
        for pair in range(dq_ref.shape[1] // 128):
            here = slice(pair * 256, pair * 256 + 256)
            kv = (own_ref[:, here] + more_ref[:, here].astype(F32)).astype(BF)
            key = kv[:, :128].astype(F32)
            query = dq_ref[:, pair * 128 : pair * 128 + 128].astype(F32)
            out_ref[:, first : first + 128] = turn(query, cosine, forth, back).astype(BF)
            out_ref[:, first + 128 : first + 256] = turn(key, cosine, forth, back).astype(BF)
            out_ref[:, first + 256 : first + 384] = kv[:, 128:]
            first += 384

    @pl.when(pl.program_id(0) == 0)
    def _():
        sum_ref[...] = jnp.zeros_like(sum_ref)

    sum_ref[...] += jnp.sum(out_ref[...].astype(F32), axis=0, keepdims=True)


def unturn(tables, triples):
    rows = triples[0][0].shape[0]
    step = 256
    width = 3 * sum(dq.shape[1] for dq, _, _ in triples)

    def spec(columns):
        return pl.BlockSpec((step, columns), lambda i: (i, 0))

    specs, arrays = [], []
    for dq, own, more in triples:
        specs += [spec(dq.shape[1]), spec(own.shape[1]), spec(more.shape[1])]
        arrays += [dq, own, more]
    return pl.pallas_call(
        partial(unturn_kernel, len(triples)),
        grid=(rows // step,),
        out_shape=(
            jax.ShapeDtypeStruct((rows, width), BF),
            jax.ShapeDtypeStruct((1, width), F32),
        ),
        in_specs=[spec(128)] * 3 + specs,
        out_specs=(spec(width), pl.BlockSpec((1, width), lambda i: (0, 0))),
        cost_estimate=cost(rows * width * 10, rows * width * 8),
        name="unturn",
    )(*tables, *arrays)


ROOT_HALF = math.sqrt(0.5)
DENSITY = 1.0 / math.sqrt(2.0 * math.pi)


def gelu_and_slope(value):
    share = 0.5 + 0.5 * lax.erf(value * ROOT_HALF)
    return value * share, share + value * (DENSITY * jnp.exp(-0.5 * value * value))


def hidden_kernel(normed_ref, bias_ref, *refs):
    act_ref, act_t_ref, slope_ref, value_ref = refs[-4:]
    rows = 128
    value_ref[...] = dot(normed_ref[...], gathered(refs[:4])) + bias_ref[...]

    def some(i, carry):
        here = pl.ds(pl.multiple_of(i * rows, rows), rows)
        act, slope = gelu_and_slope(value_ref[here, :])
        act = act.astype(BF)
        act_ref[here, :] = act
        act_t_ref[:, here] = act.T
        slope_ref[here, :] = slope
        return carry

    lax.fori_loop(0, normed_ref.shape[0] // rows, some, 0)


def hidden(normed, pieces, bias):
    rows, width = normed.shape[0], bias.shape[1]
    step = 512
    column = pl.BlockSpec((rows, step), lambda j: (0, j))
    return pl.pallas_call(
        hidden_kernel,
        grid=(width // step,),
        out_shape=(shaped(rows, width, BF), shaped(width, rows, BF), shaped(rows, width, F32)),
        in_specs=[whole(normed), pl.BlockSpec((1, step), lambda j: (0, j))]
        + [pl.BlockSpec((piece.shape[0], step), lambda j: (0, j)) for piece in pieces],
        out_specs=(column, pl.BlockSpec((step, rows), lambda j: (j, 0)), column),
        scratch_shapes=[pltpu.VMEM((rows, step), F32)],
        cost_estimate=cost(2 * rows * D * width + 50 * rows * width, 9 * rows * width),
        name="hidden",
    )(normed, bias, *pieces)


def fetch_units(me, pieces, w_ref, sem):
    copies = []
    for index, chip in enumerate(ORDER):
        first = pl.multiple_of((me ^ chip) * 128, 128)
        array, part = LAY[index // 2]
        copies.append(
            pltpu.make_async_copy(
                pieces[array].at[pl.ds(part * 256 + index % 2 * 128, 128), :],
                w_ref.at[pl.ds(first, 128), :],
                sem,
            )
        )
    for copy in copies:
        copy.start()
    return copies


def unit_back_kernel(where_ref, own_ref, other_ref, slope_ref, *refs):
    hg_ref, sum_ref, w_ref, sem = refs[4:]
    j = pl.program_id(0)
    step = hg_ref.shape[1]

    @pl.when(j == 0)
    def _():
        for copy in fetch_units(where_ref[0], refs[:4], w_ref, sem):
            copy.wait()

    w = w_ref[pl.ds(pl.multiple_of(j * step, step), step), :]
    total = None
    rows = own_ref.shape[0]
    for half, g_ref in enumerate((own_ref, other_ref)):
        here = slice(half * rows, half * rows + rows)
        grad = (times_transposed(g_ref[...], w) * slope_ref[here, :]).astype(BF)
        hg_ref[here, :] = grad
        part = jnp.sum(grad.astype(F32), axis=0, keepdims=True)
        total = part if total is None else total + part
    sum_ref[...] = total


def unit_back(where, own, other, slope, pieces):
    rows, width = slope.shape
    step = 512
    column = pl.BlockSpec((rows, step), lambda j: (0, j))
    return pl.pallas_call(
        unit_back_kernel,
        grid=(width // step,),
        out_shape=(shaped(rows, width, BF), shaped(1, width, F32)),
        in_specs=[SMEM, whole(own), whole(other), column] + [ANY] * 4,
        out_specs=(column, pl.BlockSpec((1, step), lambda j: (0, j))),
        scratch_shapes=[pltpu.VMEM((width, D), BF), pltpu.SemaphoreType.DMA],
        cost_estimate=cost(2 * rows * D * width, 8 * rows * width),
        name="unit_back",
    )(where, own, other, slope, *pieces)


def unit_out_kernel(where_ref, act_ref, heads_ref, *refs):
    contexts, pieces = refs[:3], refs[3:7]
    mine_ref, theirs_ref, w_ref, total_ref, sem = refs[7:]
    step = pl.program_id(0)

    @pl.when(step == 0)
    def _():
        for copy in fetch_units(where_ref[0], pieces, w_ref, sem):
            copy.wait()

    context = jnp.concatenate([ref[...] for ref in contexts], axis=1)
    total_ref[...] = dot(act_ref[...], w_ref[...]) + dot(context, heads_ref[...])

    @pl.when(step < 2)
    def _():
        mine_ref[...] = total_ref[...]

    @pl.when(step >= 2)
    def _():
        theirs_ref[...] = total_ref[...]


def unit_out(where, act, heads, contexts, pieces):
    rows, width = act.shape
    return pl.pallas_call(
        unit_out_kernel,
        grid=(4,),
        out_shape=(shaped(rows // 2, D, F32),) * 2,
        in_specs=[SMEM, rows_spec(width), whole(heads)]
        + [rows_spec(context.shape[1]) for context in contexts]
        + [ANY] * 4,
        out_specs=(
            pl.BlockSpec((256, D), lambda i: (jnp.minimum(i, 1), 0)),
            pl.BlockSpec((256, D), lambda i: (jnp.maximum(i - 2, 0), 0)),
        ),
        scratch_shapes=[
            pltpu.VMEM((width, D), BF),
            pltpu.VMEM((256, D), F32),
            pltpu.SemaphoreType.DMA,
        ],
        cost_estimate=cost(3 * rows * D * width, 6 * rows * width),
        name="unit_out",
    )(where, act, heads, *contexts, *pieces)


def row_grads_kernel(steps, where_ref, left_ref, right_ref, *refs):
    out_refs = refs[-6:]
    spots = [[place_of(chip) for chip in chips] for chips in BLOCKS.values()]

    @pl.when(pl.program_id(0) < steps)
    def _():
        value = dot(left_ref[...], right_ref[...]).astype(BF)
        for places, ref in zip(spots, out_refs):
            for at, place in enumerate(places):
                ref[at * 64 : at * 64 + 64, :] = value[place * 64 : place * 64 + 64]

    if len(refs) == 7:
        held_ref = refs[0]
        me, core = where_ref[0], where_ref[1]

        @pl.when(pl.program_id(0) >= steps)
        def _():
            for chips, ref in zip(BLOCKS.values(), out_refs):
                for at, chip in enumerate(chips):
                    found = chip ^ me
                    start = (((found // 8) ^ core) * 8 + found % 8) * 32
                    rows = held_ref[pl.ds(pl.multiple_of(start, 32), 32), :]
                    ref[at * 64 : at * 64 + 32, :] = rows[:, : D // 2]
                    ref[at * 64 + 32 : at * 64 + 64, :] = rows[:, D // 2 :]


def row_grads(where, left, right, more=None):
    rows, tokens = left.shape
    step = 512
    steps = right.shape[1] // step
    columns = right.shape[1] + (0 if more is None else D // 2)
    heights = [64 * len(chips) for chips in BLOCKS.values()]
    return pl.pallas_call(
        partial(row_grads_kernel, steps),
        grid=(columns // step,),
        out_shape=tuple(shaped(height, columns, BF) for height in heights),
        in_specs=[
            SMEM,
            whole(left),
            pl.BlockSpec((tokens, step), lambda j: (0, jnp.minimum(j, steps - 1))),
        ]
        + ([] if more is None else [whole(more)]),
        out_specs=tuple(pl.BlockSpec((height, step), lambda j: (0, j)) for height in heights),
        cost_estimate=cost(2 * rows * tokens * columns, 2 * (rows * tokens + rows * columns)),
        name="row_grads",
    )(where, left, right, *([] if more is None else [more]))


def unit_grads_kernel(order_ref, *refs):
    lefts, own_ref, other_ref, out_refs = refs[:4], refs[4], refs[5], refs[6:]
    left = stack(lefts)
    tokens = own_ref.shape[0]
    a, xa, b, yb, yax, xby = out_refs
    columns = 512

    def some(i, carry):
        here = pl.ds(pl.multiple_of(i * columns, columns), columns)
        value = dot(left[:, :tokens], own_ref[:, here]) + dot(left[:, tokens:], other_ref[:, here])
        value = value.astype(BF)
        for piece, outs in enumerate(((a, xa), (b, yb), (yax,), (xby,))):

            @pl.when(pl.program_id(0) == piece)
            def _(outs=outs):
                rows = 512 // len(outs)
                for at, ref in enumerate(outs):
                    ref[:, here] = value[at * rows : at * rows + rows]

        return carry

    lax.fori_loop(0, D // columns, some, 0)


def unit_grads(me, left, own, other):
    tokens = left.shape[1]
    order = jnp.asarray(np.array(sum(SUMS.values(), []), np.int32)) ^ me

    def block(place):
        return pl.BlockSpec((128, tokens), lambda k, order: (order[4 * k + place], 0))

    return pl.pallas_call(
        unit_grads_kernel,
        out_shape=tuple(shaped(128 * len(chips), D, BF) for chips in BLOCKS.values()),
        grid_spec=pltpu.PrefetchScalarGridSpec(
            num_scalar_prefetch=1,
            grid=(4,),
            in_specs=[block(place) for place in range(4)] + [whole(own), whole(other)],
            out_specs=tuple(
                pl.BlockSpec((128 * len(chips), D), lambda k, order: (0, 0))
                for chips in BLOCKS.values()
            ),
        ),
        cost_estimate=cost(2 * tokens * D * 2048, 4 * 2048 * D),
        name="unit_grads",
    )(order, left, left, left, left, own, other)


def out_grad_kernel(where_ref, own_ref, other_ref, *refs):
    contexts, keep_ref, give_ref, across_ref = refs[:3], refs[3], refs[4], refs[5]
    first = where_ref[1] == 0
    tokens = own_ref.shape[0]
    group = pl.program_id(0)

    @pl.when(group == 0)
    def _():
        lane = 0
        for ref in contexts:
            across_ref[lane : lane + ref.shape[1], :] = ref[...].T
            lane += ref.shape[1]

    across = across_ref[pl.ds(pl.multiple_of(group * 128, 128), 128), :]
    value = dot(across[:, :tokens], own_ref[...]) + dot(across[:, tokens:], other_ref[...])
    value = value.astype(BF)
    for head in range(2):
        zero, one = value[head * 64 : head * 64 + 32], value[head * 64 + 32 : head * 64 + 64]
        rows = slice(head * 32, head * 32 + 32)
        keep_ref[rows, :] = jnp.where(first, zero, one)
        give_ref[rows, :] = jnp.where(first, one, zero)


def out_grad(where, own, other, contexts):
    block = pl.BlockSpec((64, D), lambda i: (i, 0))
    return pl.pallas_call(
        out_grad_kernel,
        grid=(4,),
        out_shape=(shaped(256, D, BF),) * 2,
        in_specs=[SMEM, whole(own), whole(other)] + [whole(context) for context in contexts],
        out_specs=(block, block),
        scratch_shapes=[pltpu.VMEM((D // 2, 1024), BF)],
        cost_estimate=cost(1024 * D * D, 6 * 1024 * D),
        name="out_grad",
    )(where, own, other, *contexts)


def norm_grad_kernel(spans, left_ref, *refs):
    count = 4 * len(spans)
    mine_ref, theirs_ref, total_ref = refs[-3:]
    earlier = refs[count:-3]
    step = pl.program_id(0)
    first = 0
    lefts = []
    for start, end in spans:
        lefts.append(left_ref[:, first : first + end - start])
        first += end - start
    for pair in range(4):
        total = None
        for line, (left, span) in enumerate(zip(lefts, spans)):
            right = gathered(
                refs[4 * line : 4 * line + 4], slice(*span), slice(2 * pair, 2 * pair + 2)
            )
            part = times_transposed(left, right)
            total = part if total is None else total + part
        total_ref[:, 256 * pair : 256 * pair + 256] = total

    for half, out_ref in enumerate((mine_ref, theirs_ref)):

        @pl.when(step // 2 == half)
        def _(half=half, out_ref=out_ref):
            if earlier:
                out_ref[...] = total_ref[...] + earlier[half][...]
            else:
                out_ref[...] = total_ref[...]


def norm_grad(left, lines, spans, earlier=()):
    rows = left.shape[0]
    flat = [piece for line in lines for piece in line]
    halves = (
        pl.BlockSpec((256, D), lambda i: (jnp.minimum(i, 1), 0)),
        pl.BlockSpec((256, D), lambda i: (jnp.maximum(i - 2, 0), 0)),
    )
    return pl.pallas_call(
        partial(norm_grad_kernel, spans),
        grid=(4,),
        out_shape=(shaped(rows // 2, D, F32),) * 2,
        in_specs=[rows_spec(left.shape[1])]
        + [whole(piece) for piece in flat]
        + list(halves[: len(earlier)]),
        out_specs=halves,
        scratch_shapes=[pltpu.VMEM((256, D), F32)],
        cost_estimate=cost(2 * rows * D * left.shape[1], 12 * rows * D),
        name="norm_grad",
    )(left, *flat, *earlier)


def norm_back_kernel(
    where_ref, part_ref, more_ref, xhat_ref, inv_ref, gain_ref, g_ref, out_ref, sum_ref, chosen_ref
):
    @pl.when(pl.program_id(0) == 0)
    def _():
        choice_into(where_ref[0], chosen_ref)
        sum_ref[...] = jnp.zeros_like(sum_ref)

    grad = part_ref[...] + more_ref[...]
    xhat = xhat_ref[...]
    scaled = grad * gain_ref[...]
    value = (
        scaled
        - jnp.mean(scaled, axis=-1, keepdims=True)
        - xhat * jnp.mean(scaled * xhat, axis=-1, keepdims=True)
    ) * inv_ref[...]
    high = value.astype(BF)
    low = (value - high.astype(F32)).astype(BF)
    value = times_transposed(high, chosen_ref[...]) + times_transposed(low, chosen_ref[...])
    out_ref[...] = (g_ref[...].astype(F32) + value).astype(BF)
    sum_ref[0:1, :] += jnp.sum(grad * xhat, axis=0, keepdims=True)
    sum_ref[1:2, :] += jnp.sum(grad, axis=0, keepdims=True)


def norm_back(where, part, more, xhat, inv_std, gain, grad):
    rows = grad.shape[0]
    one = pl.BlockSpec((1, D), lambda i: (0, 0))
    return pl.pallas_call(
        norm_back_kernel,
        grid=(rows // 256,),
        out_shape=(shaped(rows, D, BF), shaped(8, D, F32)),
        in_specs=[SMEM] + [rows_spec(D)] * 3 + [rows_spec(1), one, rows_spec(D)],
        out_specs=(rows_spec(D), pl.BlockSpec((8, D), lambda i: (0, 0))),
        scratch_shapes=[pltpu.VMEM((D, D), BF)],
        cost_estimate=cost(4 * rows * D * D, 16 * rows * D),
        name="norm_back",
    )(where, part, more, xhat, inv_std, gain, grad)


def paste_in_kernel(where_ref, mine_ref, other_ref, out_ref):
    core = where_ref[1]
    for owner, ref in ((core, mine_ref), (1 - core, other_ref)):
        for block in range(CHIPS):
            at = pl.multiple_of((2 * block + owner) * 128, 128)
            out_ref[:, pl.ds(at, 128)] = ref[:, block * 128 : block * 128 + 128]


def paste_qkv_kernel(where_ref, mine_ref, other_ref, out_ref):
    core = where_ref[1]
    low = lanes_low(mine_ref.shape[0])
    for owner, ref in ((core, mine_ref), (1 - core, other_ref)):
        for group in range(GROUPS):
            q, k, v = (
                ref[:, group * 384 + part * 128 : group * 384 + part * 128 + 128]
                for part in range(3)
            )
            turned = pltpu.roll(k, HD, 1)
            blocks = (jnp.where(low, q, turned), jnp.where(low, v, q), jnp.where(low, turned, v))
            for part, value in enumerate(blocks):
                at = (owner * GROUPS + group) * 384 + part * 128
                out_ref[:, pl.ds(pl.multiple_of(at, 128), 128)] = value


def paste(kernel, where, mine, other):
    return pl.pallas_call(
        kernel,
        out_shape=shaped(mine.shape[0], 2 * mine.shape[1], F32),
        in_specs=[SMEM, VMEM, VMEM],
        out_specs=VMEM,
        cost_estimate=cost(0, 16 * mine.shape[0] * mine.shape[1]),
        name="paste",
    )(where, mine, other)


def local_fast(
    hidden_in,
    document_labels,
    cotangent,
    ln_gain,
    ln_bias,
    qkv_weight,
    qkv_bias,
    out_weight,
    out_bias,
    fc_in_weight,
    fc_in_bias,
    fc_out_weight,
    fc_out_bias,
):
    local_seqs, tok_count = hidden_in.shape[:2]
    row_count = local_seqs * tok_count
    d_rows = qkv_weight.shape[0]
    f_rows = fc_out_weight.shape[0]
    units = fc_in_weight.shape[1] // 2
    pair = 2
    core = lax.axis_index("fsdp") % 2
    me = lax.axis_index("seq") * 4 + lax.axis_index("fsdp") // 2
    clock = Clock(jnp.stack([me, core]).astype(jnp.int32))
    box = {}

    waiting = []

    def slot(jobs, work=None, *inputs, chain=None, late=(), then=None):
        nonlocal waiting
        jobs, late = list(jobs), list(late)
        chains = chain if isinstance(chain, list) else [chain] if chain is not None else []
        gated, given, more = clock.join(
            tuple(job[2] for job in jobs + late), inputs, tuple(tuple(link[2]) for link in chains)
        )
        values = [job[3](value) for job, value in zip(jobs + late, gated)]
        made = work(*given) if work is not None else ()
        after = []
        for (name, follow, _), inputs in zip(chains, more):
            for job, value in list(zip(jobs, values)) + waiting:
                if job[1] == name:
                    after.append(follow(value, *inputs))
        if then is not None:
            started = then(made)
            late = late + started
            values = values + [job[3](job[2]) for job in started]
        ended, values, older = waiting, values[: len(jobs)], values[len(jobs) :]
        found = values + [value for _, value in ended]
        found, made, after = clock.join(tuple(found), made, after)
        for job, value in zip(jobs + [job for job, _ in ended], found):
            job[0][job[1]] = value
        waiting = list(zip(late, older))
        if chain is None:
            return made
        return made, after if isinstance(chain, list) else after[0]

    def moves(line, stage):
        return [
            (line.parts, name, line.parts[source], partial(cross, bit=bit))
            for name, source, bit in line.jobs(stage)
        ]

    def core_move(name, value):
        return (box, name, value, other_core)

    def pick(halves):
        first = core == 0
        return jnp.where(first, halves[0], halves[1]), jnp.where(first, halves[1], halves[0])

    def joined(mine, other):
        first = core == 0
        return jnp.concatenate(
            [jnp.where(first, mine, other), jnp.where(first, other, mine)], axis=0
        )

    x_own = hidden_in.reshape(row_count, D)
    g_own = cotangent.reshape(row_count, D)
    vectors = (ln_gain, ln_bias, qkv_bias, out_bias, fc_in_bias, fc_out_bias)
    keep1, give1, keep2, give2, in_keep, in_give, folded = cut(
        clock.token, qkv_weight, fc_in_weight, out_weight, vectors, document_labels
    )
    slot([core_move("give1", give1)])
    line_a = Gather(joined(keep1, box["give1"]))
    slot(moves(line_a, "far") + [core_move("x", x_own), core_move("give2", give2)])
    line_b = Gather(jnp.concatenate([folded, joined(keep2, box["give2"])], axis=1))
    line_d = Gather(fc_out_weight)
    slot(moves(line_a, "near") + moves(line_b, "far") + [core_move("in", in_give), core_move("g", g_own)])
    g_more = box["g"]
    bias, *tables = slot(
        moves(line_a, "first") + moves(line_b, "near"),
        lambda a, b: marks(clock.token, a, b),
        line_a.parts["a"],
        line_a.parts["b"],
    )
    line_c = Gather(joined(in_keep, box["in"]))
    (xhat, inv_std), grad_sum = slot(
        moves(line_a, "second") + moves(line_c, "far"),
        lambda own, other, g: (
            prepare(clock.token, own, other),
            jnp.sum(g.astype(F32), axis=0),
        ),
        x_own,
        box["x"],
        g_own,
    )
    a_pieces = line_a.pieces()
    made = slot(
        moves(line_b, "first") + moves(line_c, "near") + moves(line_d, "far"),
        lambda xhat, tables, pieces: project_first(clock.token, xhat, tables, pieces),
        xhat,
        tables,
        a_pieces,
    )
    queries, kvs = [made[0], made[2]], [[made[1]], [made[3]]]
    normed, normed_t, b_more, b_in, b_rows, gain = made[4:]
    moved, results, backs = {}, {}, {}

    def up(group, hop):
        return (moved, (group, hop), kvs[group][hop], partial(shift, by=1))

    def landed(*found):
        for group, hop in found:
            kvs[group].append(moved[group, hop])

    def down(group, hop):
        value = results[group][4]
        if hop == 1:
            value = (results[group][3].astype(F32) + backs[group, 0].astype(F32)).astype(BF)
        return (backs, (group, hop), value, partial(shift, by=-1))

    def attention(*groups):
        def work(*given):
            return [attend(group, *args) for group, args in zip(groups, given)]

        return work, *[
            (queries[group], context_grad, bias, tuple(kvs[group])) for group in groups
        ]

    def attended(groups, found):
        for group, result in zip(groups, found):
            results[group] = result

    slot(moves(line_b, "second") + [up(0, 0)])
    landed((0, 0))
    b_pieces = line_b.pieces()
    made, (out_keep, out_give) = slot(
        moves(line_c, "first") + [up(0, 1), up(1, 0)],
        lambda normed, bias, tables, pieces: (
            project_more(normed, bias, tables, pieces),
            head_rows(clock.token, pieces),
        ),
        normed,
        b_more,
        tables,
        b_pieces,
    )
    landed((0, 1), (1, 0))
    queries.append(made[0])
    kvs.append([made[1]])

    def first_attention(out_more, g_own, g_more, out_keep, query, bias, kvs):
        grad, heads = context_gradient(clock.token, g_own, g_more, out_keep, out_more)
        return grad, heads, attend(0, query, grad, bias, kvs)

    _, (context_grad, out_heads, found) = slot(
        moves(line_c, "second") + moves(line_d, "near") + [up(1, 1), core_move("out", out_give)],
        chain=(
            "out",
            first_attention,
            (g_own, g_more, out_keep, queries[0], bias, tuple(kvs[0])),
        ),
    )
    results[0] = found
    landed((1, 1))
    c_pieces = line_c.pieces()
    act, act_t, slope = slot(
        moves(line_d, "first") + [up(2, 0), down(0, 0)],
        lambda normed, b_in, pieces: hidden(normed, pieces, b_in),
        normed,
        b_in,
        c_pieces,
    )
    landed((2, 0))
    work, *given = attention(1)

    def with_units(given, act_t, own, other):
        found = work(given)
        return found, unit_grads(clock.token[0], act_t, own, other), shift(found[0][4], -1)

    found, fc_parts, backs[1, 0] = slot(
        moves(line_d, "second") + [up(2, 1)],
        with_units,
        *given,
        act_t,
        g_own,
        g_more,
        late=[down(0, 1)],
    )
    attended([1], found)
    landed((2, 1))
    d_pieces = line_d.pieces()
    sum_fc = Scatter(fc_parts)
    work2, *given = attention(2)

    def last_attention(given, earlier, own, other):
        found = work2(given)
        contexts = earlier + [found[0][0]]
        return found, contexts, out_grad(clock.token, own, other, contexts)

    found, contexts, (out_keep, out_give) = slot(
        moves(sum_fc, "first") + [down(1, 1)],
        last_attention,
        *given,
        [results[group][0] for group in range(2)],
        g_own,
        g_more,
        then=lambda made: [(backs, (2, 0), made[0][0][4], partial(shift, by=-1))],
    )
    attended([2], found)

    def units_back(out_more, out_keep, normed_t, own, other, slope, pieces):
        hidden_grad, hidden_sum = unit_back(clock.token, own, other, slope, pieces)
        more = jnp.concatenate([out_keep, out_more], axis=0)
        return hidden_grad, hidden_sum, row_grads(clock.token, normed_t, hidden_grad, more)

    def near_now(last, own, earlier):
        rows = own.shape[0]
        total = own.astype(F32) + earlier[:rows].astype(F32) + last.astype(F32)
        return cross(total.astype(BF), NEAR)

    _, ((hidden_grad, hidden_sum, in_parts), sum_fc.parts["r_b"]) = slot(
        moves(sum_fc, "second") + [core_move("out_grad", out_give)],
        chain=[
            ("out_grad", units_back, (out_keep, normed_t, g_own, g_more, slope, d_pieces)),
            ("r_yb", near_now, (sum_fc.parts["b"], sum_fc.parts["r_xby"])),
        ],
    )
    sum_in = Scatter(in_parts)
    (out_mine, out_theirs), earlier = slot(
        moves(sum_in, "first") + [down(2, 1)],
        lambda act, heads, contexts, pieces, grad, c_pieces: (
            unit_out(clock.token, act, heads, contexts, pieces),
            norm_grad(grad, [c_pieces], [(0, units)]),
        ),
        act,
        out_heads,
        contexts,
        d_pieces,
        hidden_grad,
        c_pieces,
    )

    def last_grads(normed_t, tables, triples):
        projected_grad, total = unturn(tables, triples)
        return projected_grad, total, row_grads(clock.token, normed_t, projected_grad)

    projected_grad, qkv_bias_sum, parts = slot(
        moves(sum_in, "second") + moves(sum_fc, "far") + [core_move("out_side", out_theirs)],
        last_grads,
        normed_t,
        tables,
        [(results[group][1], results[group][2], backs[group, 1]) for group in range(3)],
    )
    sum_qkv = Scatter(parts)
    (norm_mine, norm_theirs), sum_in.parts["r_b"] = slot(
        moves(sum_qkv, "first"),
        lambda projected_grad, earlier, terms, *lines: (
            norm_grad(projected_grad, lines, [(0, 768), (512, 1280)], earlier),
            near_now(*terms),
        ),
        projected_grad,
        earlier,
        tuple(sum_in.parts[name] for name in ("r_yb", "b", "r_xby")),
        a_pieces,
        b_pieces,
    )

    def finish_output(x_own, out_mine, out_more, b_rows):
        order = jnp.asarray(np.array(ORDER, np.int32)) ^ me
        spots = place_of(jnp.arange(CHIPS, dtype=jnp.int32) ^ me)
        b_rows = b_rows.reshape(CHIPS, 2 * d_rows)[spots].reshape(1, D)
        return (x_own.astype(F32) + out_mine + out_more + b_rows).astype(BF)

    def small_rows(norm_sums, qkv_bias_sum, hidden_sum, grad_sum):
        spots = place_of(jnp.arange(CHIPS, dtype=jnp.int32) ^ me)
        norm_sums = norm_sums[:2].reshape(2, CHIPS, 2, d_rows)[:, spots].reshape(2, D)
        mine = (jnp.arange(2) == core)[:, None]
        qkv_full = (
            jnp.where(mine, qkv_bias_sum, 0.0)
            .reshape(2, GROUPS, 3, pair, HD)
            .transpose(0, 1, 3, 2, 4)
            .reshape(3 * D)
        )
        in_full = jnp.where(mine[None], hidden_sum.reshape(CHIPS, 1, f_rows), 0.0)
        packed = jnp.concatenate(
            [
                vector.reshape(2 * CHIPS, -1)
                for vector in (norm_sums[0], norm_sums[1], qkv_full, grad_sum, in_full)
            ],
            axis=1,
        ).reshape(CHIPS, -1)
        return packed[jnp.asarray(np.array(ORDER, np.int32)) ^ me]

    def back_work(norm_more, norm_mine, xhat, inv_std, gain, g_own, *sums):
        input_grad, norm_sums = norm_back(
            clock.token, norm_mine, norm_more, xhat, inv_std, gain, g_own
        )
        return input_grad, small_rows(norm_sums, *sums)

    _, (input_grad, packed) = slot(
        moves(sum_qkv, "second") + moves(sum_in, "far") + [core_move("norm", norm_theirs)],
        chain=(
            "norm",
            back_work,
            (norm_mine, xhat, inv_std, gain, g_own, qkv_bias_sum, hidden_sum, grad_sum),
        ),
    )

    def fold(bit):
        return (box, "fold", packed[packed.shape[0] // 2 :], partial(cross, bit=bit))

    def half_sum():
        return packed[: packed.shape[0] // 2] + box["fold"]

    def two_folds(value, rows):
        half = rows[: rows.shape[0] // 2] + value
        give = half[half.shape[0] // 2 :]
        return half[: half.shape[0] // 2] + cross(give, X)

    in_rows = sum_in.result()
    in_keep, in_give = pick(in_rows[:, :units].reshape(2, d_rows, units))
    out_weight_grad = in_rows[:, units:].reshape(2, d_rows, D // 2)
    output, packed = slot(
        moves(sum_qkv, "near") + [fold(Y), core_move("in_rows", in_give)],
        finish_output,
        x_own,
        out_mine,
        box["out_side"],
        b_rows,
        chain=("fold", two_folds, (packed,)),
    )
    fc_in_weight_grad = slot(
        moves(sum_qkv, "far") + [fold(NEAR)],
        lambda mine, other: paste(paste_in_kernel, clock.token, mine, other),
        in_keep,
        box["in_rows"],
    )
    packed = half_sum()
    qkv_keep, qkv_give = pick(sum_qkv.result().reshape(2, d_rows, -1))
    slot([core_move("qkv_rows", qkv_give), fold(FAR)])
    sums_keep, sums_give = pick(half_sum().reshape(2, -1))
    sums = sums_keep + other_core(sums_give)
    parts = []
    first = 0
    for width in (d_rows, d_rows, 3 * d_rows, d_rows, f_rows):
        parts.append(sums[first : first + width])
        first += width
    return (
        output.reshape(local_seqs, tok_count, D),
        input_grad.reshape(local_seqs, tok_count, D),
        parts[0],
        parts[1],
        paste(paste_qkv_kernel, clock.token, qkv_keep, box["qkv_rows"]),
        parts[2],
        jnp.concatenate([out_weight_grad[0], out_weight_grad[1]], axis=1),
        parts[3],
        fc_in_weight_grad,
        parts[4],
        sum_fc.result(),
        parts[3],
    )


def solution(mesh):
    rows = P(("seq", "fsdp"))
    wide = P(("seq", "fsdp"), None)
    act = P("fsdp", "seq", None)
    placed = (act, P("fsdp", "seq"), act) + (rows, rows) + (wide, rows) * 4
    small = dict(mesh.shape) == {"seq": 4, "fsdp": 8}
    return jax.shard_map(
        local_fast if small else local_plain,
        mesh=mesh,
        in_specs=placed,
        out_specs=(act, act, rows, rows) + (wide, rows) * 4,
        check_vma=False,
    )
```

```python
from functools import partial
import math

import jax
import jax.numpy as jnp
import numpy as np
from jax import lax
from jax.experimental import pallas as pl
from jax.experimental.pallas import tpu as pltpu
from jax.sharding import PartitionSpec as P

D = 1024
H = 16
HD = 64
ROT = 16
GROUPS = 4
BF = jnp.bfloat16
F32 = jnp.float32


def rotate(values, cosine, sine_part):
    half_rot = ROT // 2
    first_part = values[..., :half_rot]
    second_part = values[..., half_rot:ROT]
    return jnp.concatenate(
        [
            first_part * cosine - second_part * sine_part,
            second_part * cosine + first_part * sine_part,
            values[..., ROT:],
        ],
        axis=-1,
    )


def position_angles(segments):
    length = segments.shape[0]
    places = jnp.arange(length, dtype=jnp.int32)
    boundary = jnp.concatenate([jnp.ones((1,), dtype=jnp.bool_), segments[1:] != segments[:-1]])
    starts = lax.cummax(jnp.where(boundary, places, 0), axis=0)
    positions = (places - starts).astype(jnp.float32)
    inverse = 1.0 / 10000.0 ** (jnp.arange(0, ROT, 2, dtype=jnp.float32) / ROT)
    return positions[:, None] * inverse[None, :]


def make_mask(segments, first_row, block_rows):
    length = segments.shape[0]
    query_index = first_row + jnp.arange(block_rows, dtype=jnp.int32)
    key_index = jnp.arange(length, dtype=jnp.int32)
    query_segments = lax.dynamic_slice_in_dim(segments, first_row, block_rows, 0)
    return (key_index[None, :] <= query_index[:, None]) & (
        query_segments[:, None] == segments[None, :]
    )


def outer_product(left, right):
    return lax.dot_general(
        left, right, (((0,), (0,)), ((), ())), preferred_element_type=jnp.float32
    )


def times_transposed(left, right):
    return lax.dot_general(
        left, right, (((1,), (1,)), ((), ())), preferred_element_type=jnp.float32
    )


def local_plain(
    hidden_in,
    document_labels,
    cotangent,
    ln_gain,
    ln_bias,
    qkv_weight,
    qkv_bias,
    out_weight,
    out_bias,
    fc_in_weight,
    fc_in_bias,
    fc_out_weight,
    fc_out_bias,
):
    gathered = (
        lax.all_gather(ln_gain, ("seq", "fsdp"), axis=0, tiled=True),
        lax.all_gather(ln_bias, ("seq", "fsdp"), axis=0, tiled=True),
        lax.all_gather(qkv_weight, ("seq", "fsdp"), axis=0, tiled=True),
        lax.all_gather(qkv_bias, ("seq", "fsdp"), axis=0, tiled=True),
        lax.all_gather(out_weight, ("seq", "fsdp"), axis=0, tiled=True),
        lax.all_gather(out_bias, ("seq", "fsdp"), axis=0, tiled=True),
        lax.all_gather(fc_in_weight, ("seq", "fsdp"), axis=0, tiled=True),
        lax.all_gather(fc_in_bias, ("seq", "fsdp"), axis=0, tiled=True),
        lax.all_gather(fc_out_weight, ("seq", "fsdp"), axis=0, tiled=True),
        lax.all_gather(fc_out_bias, ("seq", "fsdp"), axis=0, tiled=True),
    )
    norm_multiplier, norm_shift, w_qkv, b_qkv, w_out, b_out, w_in, b_in, w_fc, b_fc = gathered
    norm_multiplier = norm_multiplier.astype(jnp.float32)
    norm_shift = norm_shift.astype(jnp.float32)
    groups = lax.axis_size("seq")
    per_group = H // groups
    local_seqs = hidden_in.shape[0]
    tok_count = hidden_in.shape[1]
    row_count = local_seqs * tok_count
    tokens = hidden_in.reshape(row_count, D).astype(jnp.float32)
    average = jnp.mean(tokens, axis=-1, keepdims=True)
    centered = tokens - average
    spread = jnp.mean(centered * centered, axis=-1, keepdims=True)
    inv_std = lax.rsqrt(spread + 1e-05)
    rescaled_rows = centered * inv_std
    normed = (rescaled_rows * norm_multiplier + norm_shift).astype(jnp.bfloat16)
    projected = jnp.dot(normed, w_qkv, preferred_element_type=jnp.float32) + b_qkv.astype(
        jnp.float32
    )
    segments_all = lax.all_gather(document_labels, "seq", axis=1, tiled=True)
    angles_all = jax.vmap(position_angles)(segments_all)
    angles = lax.dynamic_slice_in_dim(
        angles_all, lax.axis_index("seq") * tok_count, tok_count, 1
    ).reshape(row_count, ROT // 2)
    cosine = jnp.cos(angles)[:, None, None, :]
    sine_part = jnp.sin(angles)[:, None, None, :]
    head_parts = projected.reshape(row_count, H, 3, HD)
    turned = jnp.concatenate(
        [rotate(head_parts[:, :, :2], cosine, sine_part), head_parts[:, :, 2:]], axis=2
    ).astype(jnp.bfloat16)
    outgoing = turned.reshape(local_seqs, tok_count, groups, per_group * 3 * HD)
    arrived = lax.all_to_all(outgoing, "seq", split_axis=2, concat_axis=1, tiled=True)
    length = arrived.shape[1]
    local_heads = arrived.reshape(local_seqs, length, per_group, 3, HD)
    queries_seq = local_heads[:, :, :, 0]
    keys_seq = local_heads[:, :, :, 1]
    values_seq = local_heads[:, :, :, 2]
    block_rows = min(512, length)
    block_count = length // block_rows
    scale_factor = 1.0 / math.sqrt(HD)

    def attend_forward(inputs):
        query_all, key_everywhere, value_all, segments = inputs

        def forward_step(running, block_index):
            first_row = block_index * block_rows
            query_rows = lax.dynamic_slice_in_dim(query_all, first_row, block_rows, 0)
            allowed = make_mask(segments, first_row, block_rows)
            raw_scores = (
                jnp.einsum(
                    "qhd,khd->hqk", query_rows, key_everywhere, preferred_element_type=jnp.float32
                )
                * scale_factor
            )
            raw_scores = jnp.where(allowed[None], raw_scores, -1e30)
            row_max = jnp.max(raw_scores, axis=-1, keepdims=True)
            unscaled = jnp.exp(raw_scores - row_max)
            row_total = jnp.sum(unscaled, axis=-1, keepdims=True)
            probabilities = (unscaled / row_total).astype(jnp.bfloat16)
            context_rows = jnp.einsum(
                "hqk,khd->qhd", probabilities, value_all, preferred_element_type=jnp.float32
            )
            log_total = (row_max + jnp.log(row_total))[..., 0]
            return (running, (context_rows, log_total))

        _, (context_blocks, log_blocks) = lax.scan(
            forward_step, None, jnp.arange(block_count, dtype=jnp.int32)
        )
        return (context_blocks.reshape(length, per_group * HD).astype(jnp.bfloat16), log_blocks)

    context_seq, log_totals = lax.map(
        attend_forward, (queries_seq, keys_seq, values_seq, segments_all)
    )
    context_heads = context_seq.reshape(local_seqs, length, 1, per_group * HD)
    returned = lax.all_to_all(context_heads, "seq", split_axis=1, concat_axis=2, tiled=True)
    context = returned.reshape(row_count, D)
    attn_out = jnp.dot(context, w_out, preferred_element_type=jnp.float32) + b_out.astype(
        jnp.float32
    )
    hidden_pre = jnp.dot(normed, w_in, preferred_element_type=jnp.float32) + b_in.astype(
        jnp.float32
    )
    activated = jax.nn.gelu(hidden_pre, approximate=False).astype(jnp.bfloat16)
    mlp_out = jnp.dot(activated, w_fc, preferred_element_type=jnp.float32) + b_fc.astype(
        jnp.float32
    )
    output = (tokens + attn_out + mlp_out).astype(jnp.bfloat16).reshape(local_seqs, tok_count, D)
    grad_out = cotangent.reshape(row_count, D)
    grad_wide = grad_out.astype(jnp.float32)
    out_bias_grad = jnp.sum(grad_wide, axis=0)
    fc_out_bias_grad = jnp.sum(grad_wide, axis=0)
    out_weight_grad = outer_product(context, grad_out)
    fc_out_weight_grad = outer_product(activated, grad_out)
    act_grad = times_transposed(grad_out, w_fc)
    _, gelu_back = jax.vjp(partial(jax.nn.gelu, approximate=False), hidden_pre)
    hidden_grad = gelu_back(act_grad)[0].astype(jnp.bfloat16)
    fc_in_weight_grad = outer_product(normed, hidden_grad)
    fc_in_bias_grad = jnp.sum(hidden_grad.astype(jnp.float32), axis=0)
    context_grad = times_transposed(grad_out, w_out).astype(jnp.bfloat16)
    grad_outgoing = context_grad.reshape(local_seqs, tok_count, groups, per_group * HD)
    head_grad_seq = lax.all_to_all(
        grad_outgoing, "seq", split_axis=2, concat_axis=1, tiled=True
    ).reshape(local_seqs, length, per_group, HD)

    def attend_backward(inputs):
        query_all, key_everywhere, value_all, segments, head_grad, log_blocks = inputs

        def backward_step(running, block_index):
            key_acc, value_accumulator = running
            first_row = block_index * block_rows
            query_rows = lax.dynamic_slice_in_dim(query_all, first_row, block_rows, 0)
            grad_rows = lax.dynamic_slice_in_dim(head_grad, first_row, block_rows, 0)
            log_rows = log_blocks[block_index]
            allowed = make_mask(segments, first_row, block_rows)
            raw_scores = (
                jnp.einsum(
                    "qhd,khd->hqk", query_rows, key_everywhere, preferred_element_type=jnp.float32
                )
                * scale_factor
            )
            raw_scores = jnp.where(allowed[None], raw_scores, -1e30)
            probabilities = jnp.where(allowed[None], jnp.exp(raw_scores - log_rows[..., None]), 0.0)
            value_accumulator = value_accumulator + jnp.einsum(
                "hqk,qhd->khd",
                probabilities.astype(jnp.bfloat16),
                grad_rows,
                preferred_element_type=jnp.float32,
            )
            prob_grad = jnp.einsum(
                "qhd,khd->hqk", grad_rows, value_all, preferred_element_type=jnp.float32
            )
            inner_total = jnp.sum(probabilities * prob_grad, axis=-1, keepdims=True)
            score_grad = (probabilities * (prob_grad - inner_total)).astype(jnp.bfloat16)
            query_grad = (
                jnp.einsum(
                    "hqk,khd->qhd", score_grad, key_everywhere, preferred_element_type=jnp.float32
                )
                * scale_factor
            )
            key_acc = (
                key_acc
                + jnp.einsum(
                    "hqk,qhd->khd", score_grad, query_rows, preferred_element_type=jnp.float32
                )
                * scale_factor
            )
            return ((key_acc, value_accumulator), query_grad)

        empty_grad = jnp.zeros((length, per_group, HD), jnp.float32)
        (key_grad, value_grad), query_blocks = lax.scan(
            backward_step, (empty_grad, empty_grad), jnp.arange(block_count, dtype=jnp.int32)
        )
        query_grad = query_blocks.reshape(length, per_group, HD)
        return jnp.stack([query_grad, key_grad, value_grad], axis=2).astype(jnp.bfloat16)

    stacked = lax.map(
        attend_backward,
        (queries_seq, keys_seq, values_seq, segments_all, head_grad_seq, log_totals),
    )
    returned_grad = lax.all_to_all(
        stacked.reshape(local_seqs, length, 1, per_group * 3 * HD),
        "seq",
        split_axis=1,
        concat_axis=2,
        tiled=True,
    )
    back_heads = returned_grad.reshape(row_count, H, 3, HD).astype(jnp.float32)
    unturned = jnp.concatenate(
        [rotate(back_heads[:, :, :2], cosine, -sine_part), back_heads[:, :, 2:]], axis=2
    )
    projected_grad = unturned.reshape(row_count, 3 * D).astype(jnp.bfloat16)
    qkv_weight_grad = outer_product(normed, projected_grad)
    qkv_bias_grad = jnp.sum(projected_grad.astype(jnp.float32), axis=0)
    normalized_gradient = times_transposed(projected_grad, w_qkv) + times_transposed(
        hidden_grad, w_in
    )
    ln_gain_grad = jnp.sum(normalized_gradient * rescaled_rows, axis=0)
    ln_bias_grad = jnp.sum(normalized_gradient, axis=0)
    standardized_gradient = normalized_gradient * norm_multiplier
    norm_back = (
        standardized_gradient
        - jnp.mean(standardized_gradient, axis=-1, keepdims=True)
        - rescaled_rows * jnp.mean(standardized_gradient * rescaled_rows, axis=-1, keepdims=True)
    ) * inv_std
    input_grad = (grad_wide + norm_back).astype(jnp.bfloat16).reshape(local_seqs, tok_count, D)
    summed = (
        lax.psum_scatter(ln_gain_grad, ("seq", "fsdp"), scatter_dimension=0, tiled=True),
        lax.psum_scatter(ln_bias_grad, ("seq", "fsdp"), scatter_dimension=0, tiled=True),
        lax.psum_scatter(qkv_weight_grad, ("seq", "fsdp"), scatter_dimension=0, tiled=True),
        lax.psum_scatter(qkv_bias_grad, ("seq", "fsdp"), scatter_dimension=0, tiled=True),
        lax.psum_scatter(out_weight_grad, ("seq", "fsdp"), scatter_dimension=0, tiled=True),
        lax.psum_scatter(out_bias_grad, ("seq", "fsdp"), scatter_dimension=0, tiled=True),
        lax.psum_scatter(fc_in_weight_grad, ("seq", "fsdp"), scatter_dimension=0, tiled=True),
        lax.psum_scatter(fc_in_bias_grad, ("seq", "fsdp"), scatter_dimension=0, tiled=True),
        lax.psum_scatter(fc_out_weight_grad, ("seq", "fsdp"), scatter_dimension=0, tiled=True),
        lax.psum_scatter(fc_out_bias_grad, ("seq", "fsdp"), scatter_dimension=0, tiled=True),
    )
    return (
        output,
        input_grad,
        summed[0],
        summed[1],
        summed[2],
        summed[3],
        summed[4],
        summed[5],
        summed[6],
        summed[7],
        summed[8],
        summed[9],
    )


def dot(left, right):
    return jnp.dot(left, right, preferred_element_type=F32)


def swap(value, axis, bit):
    return lax.ppermute(value, axis, [(i, i ^ bit) for i in range(lax.axis_size(axis))])


def shift(value, by):
    count = lax.axis_size("seq")
    return lax.ppermute(
        value, "seq", [(i, i + by) for i in range(count) if 0 <= i + by < count]
    )


class Clock:
    def __init__(self, token):
        self.token = token

    def join(self, *values):
        values, self.token = lax.optimization_barrier((values, self.token))
        return values


X, Y, NEAR, FAR = 1, 2, 4, 8
CHIPS = 16
ORDER = [0, 8, 4, 12, 1, 9, 5, 13, 2, 10, 6, 14, 3, 11, 7, 15]
SUMS = {"ax": [0, 8, 1, 9], "by": [4, 12, 6, 14], "yax": [2, 10, 3, 11], "xby": [5, 13, 7, 15]}


def place_of(chip):
    return (chip // FAR) % 2 + (chip // NEAR) % 2 * 2 + chip % 2 * 4 + (chip // Y) % 2 * 8


def cross(value, bit):
    return swap(value, "seq", bit // 4) if bit >= 4 else swap(value, "fsdp", bit * 2)


def other_core(value):
    return swap(value, "fsdp", 1)


class Gather:
    def __init__(self, shard):
        self.parts = {"s": shard}

    def jobs(self, stage):
        parts = self.parts
        if stage == "near":
            parts["a"] = jnp.concatenate([parts["s"], parts["f"]], axis=0)
        if stage == "second":
            parts["ax"] = jnp.concatenate([parts["a"], parts["xa"]], axis=0)
            parts["by"] = jnp.concatenate([parts["b"], parts["yb"]], axis=0)
        return {
            "far": [("f", "s", FAR)],
            "near": [("b", "a", NEAR)],
            "first": [("xa", "a", X), ("yb", "b", Y)],
            "second": [("yax", "ax", Y), ("xby", "by", X)],
        }[stage]

    def pieces(self):
        return [self.parts[name] for name in SUMS]


LAY = [(0, 0), (1, 0), (0, 1), (3, 0), (2, 0), (1, 1), (2, 1), (3, 1)]


def gathered(refs, columns=slice(None), which=slice(None)):
    half = refs[0].shape[0] // 2
    return jnp.concatenate(
        [refs[array][part * half : part * half + half, columns] for array, part in LAY[which]],
        axis=0,
    )


BLOCKS = {
    "a": [0, 8],
    "xa": [1, 9],
    "b": [4, 12],
    "yb": [6, 14],
    "yax": [2, 10, 3, 11],
    "xby": [5, 13, 7, 15],
}


class Scatter:
    def __init__(self, blocks):
        self.parts = dict(zip(BLOCKS, blocks))

    def total(self, first, last, *names):
        return sum(self.parts[name][first:last].astype(F32) for name in names)

    def jobs(self, stage):
        parts = self.parts
        rows = parts["a"].shape[0]
        if stage == "second":
            for name, other in (("xa", "r_yax"), ("yb", "r_xby")):
                value = parts[name].astype(F32) + parts[other][rows:].astype(F32)
                parts[name] = value.astype(BF)
        if stage == "near":
            parts["b"] = self.total(0, rows, "b", "r_xby", "r_yb").astype(BF)
        if stage == "far":
            value = self.total(rows // 2, rows, "a", "r_yax", "r_xa", "r_b")
            parts["send"] = value.astype(BF)
        return {
            "first": [("r_yax", "yax", Y), ("r_xby", "xby", X)],
            "second": [("r_xa", "xa", X), ("r_yb", "yb", Y)],
            "near": [("r_b", "b", NEAR)],
            "far": [("r_far", "send", FAR)],
        }[stage]

    def result(self):
        rows = self.parts["a"].shape[0] // 2
        return self.total(0, rows, "a", "r_yax", "r_xa", "r_b", "r_far")


def cost(flops, bytes_accessed, transcendentals=0):
    return pl.CostEstimate(
        flops=flops, bytes_accessed=bytes_accessed, transcendentals=transcendentals
    )


SMEM = pl.BlockSpec(memory_space=pltpu.SMEM)
VMEM = pl.BlockSpec(memory_space=pltpu.VMEM)
ANY = pl.BlockSpec(memory_space=pl.ANY)


def whole(array):
    return pl.BlockSpec(array.shape, lambda *_: (0,) * len(array.shape))


def shaped(rows, columns, dtype):
    return jax.ShapeDtypeStruct((rows, columns), dtype)


def stack(refs):
    return jnp.concatenate([ref[...] for ref in refs], axis=0)


def lanes_low(rows):
    return lax.broadcasted_iota(jnp.int32, (rows, 128), 1) < HD


def cut_kernel(where_ref, qkv_ref, in_ref, out_w_ref, gain_ref, shift_ref, qb_ref, ob_ref, ib_ref, fb_ref, label_ref, *refs):
    keep1, give1, keep2, give2, in_keep, in_give, folded, columns_ref, line_ref = refs
    core = where_ref[1]
    rows = qkv_ref.shape[0]
    columns_ref[...] = jnp.zeros_like(columns_ref)
    for row, ref in enumerate((gain_ref, shift_ref, ob_ref, fb_ref)):
        columns_ref[row : row + 1, :rows] = ref[...].astype(F32)
    line_ref[...] = jnp.zeros_like(line_ref)
    line_ref[0:1, :96] = qb_ref[...].astype(F32)
    line_ref[1:2, :] = ib_ref[...].astype(F32)
    bias, units = line_ref[0:1, :], line_ref[1:2, :]
    lane = lax.broadcasted_iota(jnp.int32, (1, 128), 1)
    first = core == 0
    parts = []
    for seq in range(2):
        for part in range(2):
            labels = (label_ref[seq : seq + 1, 128 * part : 128 * part + 128] + 1).astype(F32)
            parts += [pltpu.roll(labels, HD, 1), labels]
    zero = jnp.zeros_like(bias)
    parts.append(jnp.where(first, pltpu.roll(bias, 64, 1), zero))
    parts.append(
        jnp.where(
            first,
            jnp.where(lane < 96, bias, zero),
            jnp.where(lane >= 96, pltpu.roll(bias, 96, 1), zero),
        )
    )
    parts.append(jnp.where(first, zero, pltpu.roll(bias, 32, 1)))
    parts += [pltpu.roll(units, HD, 1), units]
    for row, value in enumerate(parts):
        line_ref[row : row + 1, :] = value
    low = lanes_low(rows)
    side = jnp.where(low, columns_ref[...].T[:rows], line_ref[...]).astype(BF)
    for owner, out1, out2 in ((core, keep1, keep2), (1 - core, give1, give2)):
        for group in range(GROUPS):
            at = pl.multiple_of((owner * GROUPS + group) * 384, 128)
            b0, b1, b2 = (
                qkv_ref[:, pl.ds(at + 128 * part, 128)].astype(F32) for part in range(3)
            )
            out = out1 if group < 2 else out2
            place = (group % 2) * 384
            turned = pltpu.roll(b0, HD, 1), pltpu.roll(b2, HD, 1)
            out[:, place : place + 128] = jnp.where(low, b0, b1).astype(BF)
            out[:, place + 128 : place + 256] = jnp.where(low, *turned).astype(BF)
            out[:, place + 256 : place + 384] = jnp.where(low, b1, b2).astype(BF)
        out1[:, 768:] = side
    for owner, out in ((core, in_keep), (1 - core, in_give)):
        for block in range(CHIPS):
            at = pl.multiple_of((2 * block + owner) * 128, 128)
            out[:, block * 128 : block * 128 + 128] = in_ref[:, pl.ds(at, 128)]
    folded[:rows, :] = out_w_ref[:, : D // 2]
    folded[rows:, :] = out_w_ref[:, D // 2 :]


def cut(where, qkv_rows, in_rows, out_rows, vectors, labels):
    rows = qkv_rows.shape[0]
    widths = (896, 896, 768, 768, 2048, 2048)
    return pl.pallas_call(
        cut_kernel,
        out_shape=tuple(shaped(rows, width, BF) for width in widths)
        + (shaped(2 * rows, D // 2, BF),),
        in_specs=[SMEM] + [VMEM] * 10,
        out_specs=(VMEM,) * 7,
        scratch_shapes=[pltpu.VMEM((128, 128), F32), pltpu.VMEM((rows, 128), F32)],
        cost_estimate=cost(0, 8 * rows * 4 * D),
        name="cut",
    )(where, qkv_rows, in_rows, out_rows, *[vector.reshape(1, -1) for vector in vectors], labels)


def turn(value, cosine, forth, back):
    return (
        value * cosine
        + pltpu.roll(value, 128 - ROT // 2, 1) * forth
        + pltpu.roll(value, ROT // 2, 1) * back
    )


def marks_kernel(where_ref, a_ref, b_ref, speed_ref, forth_ref, back_ref, bias_ref, cos_ref, to_ref, from_ref, side_ref):
    seq = pl.program_id(0)
    line, core = where_ref[0] // 4, where_ref[1]

    @pl.when(seq == 0)
    def _():
        side_ref[:128, :] = a_ref[...].astype(F32)
        side_ref[128:, :] = b_ref[...].astype(F32)

    owner = jnp.where(seq < 2, core, 1 - core)
    low = lanes_low(1)
    chunks = []
    for back in range(3):
        other = line - back
        relative = jnp.where(other >= 0, other, 0) ^ line
        block = relative // 2 + 2 * (relative % 2)
        rows = side_ref[pl.ds(pl.multiple_of(block * 64 + owner * 32, 8), 8), :]
        rows = jnp.where(seq % 2 == 0, rows[:4], rows[4:])
        rows = jnp.where(other >= 0, rows, jnp.zeros_like(rows))
        chunks.append(
            [
                jnp.where(low, pltpu.roll(rows[i : i + 1], HD, 1), rows[i + 1 : i + 2])
                for i in (0, 2)
            ]
        )
    total = None
    query = lax.broadcasted_iota(jnp.int32, (128, 256), 1)
    key = lax.broadcasted_iota(jnp.int32, (128, 256), 0)
    mine = jnp.concatenate(chunks[0], axis=1)
    for back, halves in enumerate(chunks):
        for half, labels in enumerate(halves):
            column = jnp.broadcast_to(labels, (128, 128)).T
            column = jnp.concatenate([column, column], axis=1)
            same = column == mine
            if back == 0:
                same = same & (key + 128 * half <= query)
            at = back * 256 + half * 128
            bias_ref[0, at : at + 128, :] = jnp.where(same, 0.0, -1e30)
            count = jnp.sum(jnp.where(same, 1.0, 0.0), axis=0, keepdims=True)
            total = count if total is None else total + count
    for half in range(2):
        position = total[:, 128 * half : 128 * half + 128] - 1.0
        angle = jnp.broadcast_to(position, (128, 128)).T * speed_ref[...]
        here = slice(128 * half, 128 * half + 128)
        cos_ref[here, :] = jnp.cos(angle)
        sine = jnp.sin(angle)
        to_ref[here, :] = sine * forth_ref[...]
        from_ref[here, :] = sine * back_ref[...]


def marks(where, a, b):
    half = ROT // 2
    inverse = 1.0 / 10000.0 ** (jnp.arange(0, ROT, 2, dtype=F32) / ROT)
    speed = jnp.concatenate([inverse, inverse, jnp.zeros((HD - ROT,), F32)])
    speed = jnp.concatenate([speed, speed]).reshape(1, 128)
    lanes = np.arange(128) % HD
    forth = jnp.asarray(-(lanes < half).astype(np.float32)[None, :])
    back = jnp.asarray(((lanes >= half) & (lanes < ROT)).astype(np.float32)[None, :])
    side = pl.BlockSpec((128, 128), lambda i: (0, 6))
    table = pl.BlockSpec((256, 128), lambda i: (i, 0))
    return pl.pallas_call(
        marks_kernel,
        grid=(4,),
        out_shape=(jax.ShapeDtypeStruct((4, 768, 256), F32),) + (shaped(1024, 128, F32),) * 3,
        in_specs=[SMEM, side, side, whole(speed), whole(forth), whole(back)],
        out_specs=(pl.BlockSpec((1, 768, 256), lambda i: (i, 0, 0)), table, table, table),
        scratch_shapes=[pltpu.VMEM((256, 128), F32)],
        cost_estimate=cost(1024 * 128 * 100, 4 * 1024 * 1024),
        name="marks",
    )(where, a, b, speed, forth, back)


def choice_into(me, chosen_ref):
    step = 128
    column = lax.broadcasted_iota(jnp.int32, (1, D), 1)
    place = column // 64
    chip = place % 2 * FAR + (place // 2) % 2 * NEAR + (place // 4) % 2 * X + place // 8 * Y
    wanted = (chip ^ me) * 64 + column % 64

    def some(i, carry):
        here = pl.ds(pl.multiple_of(i * step, step), step)
        row = lax.broadcasted_iota(jnp.int32, (step, D), 0) + i * step
        chosen_ref[here, :] = jnp.where(row == wanted, 1.0, 0.0).astype(BF)
        return carry

    lax.fori_loop(0, D // step, some, 0)


def prepare_kernel(
    steps, where_ref, own_ref, other_ref, xhat_ref, inv_ref, chosen_ref, rows_ref
):
    step = pl.program_id(0)

    @pl.when(step == 0)
    def _():
        choice_into(where_ref[0], chosen_ref)

    @pl.when(step < steps)
    def _():
        rows_ref[...] = own_ref[...]

    @pl.when(step >= steps)
    def _():
        rows_ref[...] = other_ref[...]

    x = dot(rows_ref[...], chosen_ref[...])
    average = jnp.mean(x, axis=-1, keepdims=True)
    centered = x - average
    spread = jnp.mean(centered * centered, axis=-1, keepdims=True)
    inv_std = lax.rsqrt(spread + 1e-05)
    xhat_ref[...] = centered * inv_std
    inv_ref[...] = inv_std


def prepare(where, own, other):
    rows = own.shape[0]
    step = 256
    steps = rows // step
    return pl.pallas_call(
        partial(prepare_kernel, steps),
        grid=(2 * steps,),
        out_shape=(shaped(2 * rows, D, F32), shaped(2 * rows, 1, F32)),
        in_specs=[
            SMEM,
            pl.BlockSpec((step, D), lambda i: (jnp.minimum(i, steps - 1), 0)),
            pl.BlockSpec((step, D), lambda i: (jnp.maximum(i - steps, 0), 0)),
        ],
        out_specs=(
            pl.BlockSpec((step, D), lambda i: (i, 0)),
            pl.BlockSpec((step, 1), lambda i: (i, 0)),
        ),
        scratch_shapes=[pltpu.VMEM((D, D), BF), pltpu.VMEM((step, D), BF)],
        cost_estimate=cost(4 * rows * D * D, 16 * rows * D),
        name="prepare",
    )(where, own, other)


def emit_heads(value, tables, outs):
    pairs = [
        (q_ref, kv_ref, pair)
        for q_ref, kv_ref in zip(outs[::2], outs[1::2])
        for pair in range(q_ref.shape[1] // 128)
    ]
    for index, (q_ref, kv_ref, pair) in enumerate(pairs):
        first, q, k = index * 384, pair * 128, pair * 256
        q_ref[:, q : q + 128] = turn(value[:, first : first + 128], *tables).astype(BF)
        kv_ref[:, k : k + 128] = turn(value[:, first + 128 : first + 256], *tables).astype(BF)
        kv_ref[:, k + 128 : k + 256] = value[:, first + 256 : first + 384].astype(BF)


def project_first_kernel(where_ref, xhat_ref, cos_ref, forth_ref, back_ref, *refs):
    pieces, outs = refs[:4], refs[4:8]
    normed_ref, normed_t_ref, more_ref, units_ref, rows_ref, gain_ref, side_ref, bias_ref, two_ref = refs[8:]
    me, core = where_ref[0], where_ref[1]

    @pl.when(pl.program_id(0) == 0)
    def _():
        side_ref[...] = gathered(pieces, slice(768, 896)).astype(F32)
        across = side_ref[...].T
        two_ref[...] = across[:8]
        gain_ref[...] = across[0:1]
        rows_ref[...] = across[2:3] + across[3:4]
        low = lanes_low(1)

        def block(chip, owner):
            start = place_of(chip ^ me) * 64 + owner * 32 + 8
            return side_ref[pl.ds(pl.multiple_of(start, 8), 8), :]

        def pair(one, two):
            return jnp.where(low, pltpu.roll(one, HD, 1), two)

        for group in range(GROUPS):
            heads = []
            for head in range(2):
                chip = core * 8 + 2 * group + head
                zero, one = block(chip, 0), block(chip, 1)
                heads.append((zero[0:1], zero[1:2] + one[1:2], one[2:3]))
            out = bias_ref if group < 2 else more_ref
            for part in range(3):
                at = (group % 2) * 384 + part * 128
                out[:, at : at + 128] = pair(heads[0][part], heads[1][part])
        for chip in range(CHIPS):
            found = block(chip, core)
            units_ref[:, chip * 128 : chip * 128 + 128] = pair(found[3:4], found[4:5])

    normed = (xhat_ref[...] * two_ref[0:1, :] + two_ref[1:2, :]).astype(BF)
    normed_ref[...] = normed
    normed_t_ref[...] = normed.T
    value = dot(normed, gathered(pieces, slice(0, 768))) + bias_ref[...]
    emit_heads(value, (cos_ref[...], forth_ref[...], back_ref[...]), outs)


TWO_PAIRS = (shaped(1024, 128, BF), shaped(1024, 256, BF)) * 2
ONE_GROUP = (shaped(1024, 256, BF), shaped(1024, 512, BF))


def rows_spec(columns, step=256):
    return pl.BlockSpec((step, columns), lambda i: (i, 0))


def project_first(where, xhat, tables, pieces):
    small = (shaped(1, 768, F32), shaped(1, 2048, F32), shaped(1, D, F32), shaped(1, D, F32))
    return pl.pallas_call(
        project_first_kernel,
        grid=(4,),
        out_shape=TWO_PAIRS + (shaped(1024, D, BF), shaped(D, 1024, BF)) + small,
        in_specs=[SMEM, rows_spec(D)] + [rows_spec(128)] * 3 + [whole(piece) for piece in pieces],
        out_specs=tuple(rows_spec(shape.shape[1]) for shape in TWO_PAIRS)
        + (rows_spec(D), pl.BlockSpec((D, 256), lambda i: (0, i)))
        + tuple(whole(shape) for shape in small),
        scratch_shapes=[
            pltpu.VMEM((D, 128), F32),
            pltpu.VMEM((1, 768), F32),
            pltpu.VMEM((8, D), F32),
        ],
        cost_estimate=cost(2 * 1024 * D * 768, 12 * 1024 * D),
        name="project_first",
    )(where, xhat, *tables, *pieces)


def project_more_kernel(normed_ref, bias_ref, cos_ref, forth_ref, back_ref, *refs):
    value = dot(normed_ref[...], gathered(refs[:4], slice(512, 1280))) + bias_ref[...]
    emit_heads(value, (cos_ref[...], forth_ref[...], back_ref[...]), refs[4:])


def project_more(normed, bias, tables, pieces):
    return pl.pallas_call(
        project_more_kernel,
        grid=(4,),
        out_shape=ONE_GROUP,
        in_specs=[rows_spec(D), whole(bias)]
        + [rows_spec(128)] * 3
        + [whole(piece) for piece in pieces],
        out_specs=tuple(rows_spec(shape.shape[1]) for shape in ONE_GROUP),
        cost_estimate=cost(2 * 1024 * D * 768, 6 * 1024 * D),
        name="project_more",
    )(normed, bias, *tables, *pieces)


def head_rows_kernel(where_ref, *refs):
    keep_ref, give_ref, held_ref = refs[4:]
    me, core = where_ref[0], where_ref[1]
    for index, chip in enumerate(ORDER):
        array, part = LAY[index // 2]
        piece, at = refs[array], part * 128 + index % 2 * 64
        found = chip ^ me
        start = pl.multiple_of((((found // 8) ^ core) * 8 + found % 8) * 32, 32)
        held_ref[pl.ds(start, 32), : D // 2] = piece[at : at + 32, :]
        held_ref[pl.ds(start, 32), D // 2 :] = piece[at + 32 : at + 64, :]
    keep_ref[...] = held_ref[:256, :]
    give_ref[...] = held_ref[256:, :]


def head_rows(where, pieces):
    return pl.pallas_call(
        head_rows_kernel,
        out_shape=(shaped(256, D, BF),) * 2,
        grid=(1,),
        in_specs=[SMEM] + [pl.BlockSpec((256, D // 2), lambda i: (0, 0))] * 4,
        out_specs=(pl.BlockSpec((256, D), lambda i: (0, 0)),) * 2,
        scratch_shapes=[pltpu.VMEM((512, D), BF)],
        cost_estimate=cost(0, 4 * 512 * D),
        name="head_rows",
    )(where, *pieces)


def context_grad_kernel(
    where_ref, own_ref, other_ref, keep_ref, more_ref, grad_ref, heads_ref, rows_ref
):
    core = where_ref[1]
    step = pl.program_id(0)

    @pl.when(step == 0)
    def _():
        for chip in range(8):
            rows = slice(chip * 32, chip * 32 + 32)
            heads_ref[pl.ds(pl.multiple_of(chip * 64 + core * 32, 32), 32), :] = keep_ref[rows, :]
            at = pl.multiple_of(chip * 64 + (1 - core) * 32, 32)
            heads_ref[pl.ds(at, 32), :] = more_ref[rows, :]

    @pl.when(step < 2)
    def _():
        rows_ref[...] = own_ref[...]

    @pl.when(step >= 2)
    def _():
        rows_ref[...] = other_ref[...]

    grad_ref[...] = times_transposed(rows_ref[...], heads_ref[...]).astype(BF)


def context_gradient(where, own, other, keep, more):
    return pl.pallas_call(
        context_grad_kernel,
        grid=(4,),
        out_shape=(shaped(1024, D // 2, BF), shaped(D // 2, D, BF)),
        in_specs=[
            SMEM,
            pl.BlockSpec((256, D), lambda i: (jnp.minimum(i, 1), 0)),
            pl.BlockSpec((256, D), lambda i: (jnp.maximum(i - 2, 0), 0)),
            whole(keep),
            whole(more),
        ],
        out_specs=(rows_spec(D // 2), pl.BlockSpec((D // 2, D), lambda i: (0, 0))),
        scratch_shapes=[pltpu.VMEM((256, D), BF)],
        cost_estimate=cost(1024 * D * D, 6 * 1024 * D),
        name="context_grad",
    )(where, own, other, keep, more)


def attend_kernel(q_ref, do_ref, bias_ref, *refs):
    kv_refs, o_ref, dq_ref, dkv_refs = refs[:3], refs[3], refs[4], refs[5:8]
    weight_ref, probs_ref, grad_ref = refs[8:]
    rows = q_ref.shape[0]
    scaled = q_ref[...] * 0.125
    given = do_ref[...]
    given_t = given.T.astype(F32)
    low = lanes_low(rows)
    zero = jnp.zeros_like(given)

    def heads(value):
        return jnp.concatenate([jnp.where(low, value, zero), jnp.where(low, zero, value)], axis=0)

    queries, grads = heads(scaled), heads(given)
    spans = [slice(chunk * rows, chunk * rows + rows) for chunk in range(3)]
    top = None
    for here, ref in zip(spans, kv_refs):
        bias = bias_ref[0, here, :]
        scores = times_transposed(ref[:, :128], queries) + jnp.concatenate([bias, bias], axis=1)
        weight_ref[here, :] = scores
        most = jnp.max(scores, axis=0, keepdims=True)
        top = most if top is None else jnp.maximum(top, most)
    total = jnp.zeros_like(top)
    for here in spans:
        unscaled = jnp.exp(weight_ref[here, :] - top)
        weight_ref[here, :] = unscaled
        total = total + jnp.sum(unscaled, axis=0, keepdims=True)
    inverse = 1.0 / total
    for here in spans:
        probs = weight_ref[here, :] * inverse
        weight_ref[here, :] = probs
        probs_ref[here, :] = probs.astype(BF)

    def both_heads(across, right_ref):
        return jnp.concatenate(
            [dot(across[:HD], right_ref[:, :rows]), dot(across[HD:], right_ref[:, rows:])], axis=0
        )

    values_t = jnp.concatenate([ref[:, 128:] for ref in kv_refs], axis=0).T
    keys_t = jnp.concatenate([ref[:, :128] for ref in kv_refs], axis=0).T
    out_t = both_heads(values_t, probs_ref)
    product = out_t * given_t
    inner = jnp.concatenate(
        [
            jnp.sum(product[:HD], axis=0, keepdims=True),
            jnp.sum(product[HD:], axis=0, keepdims=True),
        ],
        axis=1,
    )
    for here, ref in zip(spans, kv_refs):
        prob_grad = times_transposed(ref[:, 128:], grads)
        grad_ref[here, :] = (weight_ref[here, :] * (prob_grad - inner)).astype(BF)
    dq_t = both_heads(keys_t, grad_ref)
    o_ref[...] = out_t.T.astype(BF)
    dq_ref[...] = (dq_t.T * 0.125).astype(BF)
    for here, ref in zip(spans, dkv_refs):
        ref[:, :128] = dot(grad_ref[here, :], queries).astype(ref.dtype)
        ref[:, 128:] = dot(probs_ref[here, :], grads).astype(ref.dtype)


def attend(first, query, grad, bias, kvs):
    pairs = query.shape[1] // 128
    narrow = pl.BlockSpec((256, 128), lambda b, p: (b, p))
    wide = pl.BlockSpec((256, 256), lambda b, p: (b, p))
    return pl.pallas_call(
        attend_kernel,
        grid=(4, pairs),
        out_shape=(shaped(1024, 128 * pairs, BF),) * 2
        + (shaped(1024, 256 * pairs, F32),)
        + (shaped(1024, 256 * pairs, BF),) * 2,
        in_specs=[
            narrow,
            pl.BlockSpec((256, 128), lambda b, p: (b, first + p)),
            pl.BlockSpec((1, 768, 256), lambda b, p: (b, 0, 0)),
        ]
        + [wide] * 3,
        out_specs=(narrow, narrow) + (wide,) * 3,
        scratch_shapes=[pltpu.VMEM((768, 512), dtype) for dtype in (F32, BF, BF)],
        cost_estimate=cost(
            pairs * 24 * 4 * 256 * 768 * 128, pairs * 9 * 1024 * 1024, pairs * 8 * 256 * 768
        ),
        name="attend",
    )(query, grad, bias, *kvs)


def unturn_kernel(groups, cos_ref, forth_ref, back_ref, *refs):
    cosine, forth, back = cos_ref[...], -forth_ref[...], -back_ref[...]
    out_ref, sum_ref = refs[-2:]
    first = 0
    for group in range(groups):
        dq_ref, own_ref, more_ref = refs[3 * group : 3 * group + 3]
        for pair in range(dq_ref.shape[1] // 128):
            here = slice(pair * 256, pair * 256 + 256)
            kv = (own_ref[:, here] + more_ref[:, here].astype(F32)).astype(BF)
            key = kv[:, :128].astype(F32)
            query = dq_ref[:, pair * 128 : pair * 128 + 128].astype(F32)
            out_ref[:, first : first + 128] = turn(query, cosine, forth, back).astype(BF)
            out_ref[:, first + 128 : first + 256] = turn(key, cosine, forth, back).astype(BF)
            out_ref[:, first + 256 : first + 384] = kv[:, 128:]
            first += 384

    @pl.when(pl.program_id(0) == 0)
    def _():
        sum_ref[...] = jnp.zeros_like(sum_ref)

    sum_ref[...] += jnp.sum(out_ref[...].astype(F32), axis=0, keepdims=True)


def unturn(tables, triples):
    rows = triples[0][0].shape[0]
    step = 256
    width = 3 * sum(dq.shape[1] for dq, _, _ in triples)

    def spec(columns):
        return pl.BlockSpec((step, columns), lambda i: (i, 0))

    specs, arrays = [], []
    for dq, own, more in triples:
        specs += [spec(dq.shape[1]), spec(own.shape[1]), spec(more.shape[1])]
        arrays += [dq, own, more]
    return pl.pallas_call(
        partial(unturn_kernel, len(triples)),
        grid=(rows // step,),
        out_shape=(
            jax.ShapeDtypeStruct((rows, width), BF),
            jax.ShapeDtypeStruct((1, width), F32),
        ),
        in_specs=[spec(128)] * 3 + specs,
        out_specs=(spec(width), pl.BlockSpec((1, width), lambda i: (0, 0))),
        cost_estimate=cost(rows * width * 10, rows * width * 8),
        name="unturn",
    )(*tables, *arrays)


ROOT_HALF = math.sqrt(0.5)
DENSITY = 1.0 / math.sqrt(2.0 * math.pi)


def gelu_and_slope(value):
    share = 0.5 + 0.5 * lax.erf(value * ROOT_HALF)
    return value * share, share + value * (DENSITY * jnp.exp(-0.5 * value * value))


def hidden_kernel(normed_ref, bias_ref, *refs):
    act_ref, act_t_ref, slope_ref, value_ref = refs[-4:]
    rows = 128
    value_ref[...] = dot(normed_ref[...], gathered(refs[:4])) + bias_ref[...]

    def some(i, carry):
        here = pl.ds(pl.multiple_of(i * rows, rows), rows)
        act, slope = gelu_and_slope(value_ref[here, :])
        act = act.astype(BF)
        act_ref[here, :] = act
        act_t_ref[:, here] = act.T
        slope_ref[here, :] = slope
        return carry

    lax.fori_loop(0, normed_ref.shape[0] // rows, some, 0)


def hidden(normed, pieces, bias):
    rows, width = normed.shape[0], bias.shape[1]
    step = 512
    column = pl.BlockSpec((rows, step), lambda j: (0, j))
    return pl.pallas_call(
        hidden_kernel,
        grid=(width // step,),
        out_shape=(shaped(rows, width, BF), shaped(width, rows, BF), shaped(rows, width, F32)),
        in_specs=[whole(normed), pl.BlockSpec((1, step), lambda j: (0, j))]
        + [pl.BlockSpec((piece.shape[0], step), lambda j: (0, j)) for piece in pieces],
        out_specs=(column, pl.BlockSpec((step, rows), lambda j: (j, 0)), column),
        scratch_shapes=[pltpu.VMEM((rows, step), F32)],
        cost_estimate=cost(2 * rows * D * width + 50 * rows * width, 9 * rows * width),
        name="hidden",
    )(normed, bias, *pieces)


def fetch_units(me, pieces, w_ref, sem):
    copies = []
    for index, chip in enumerate(ORDER):
        first = pl.multiple_of((me ^ chip) * 128, 128)
        array, part = LAY[index // 2]
        copies.append(
            pltpu.make_async_copy(
                pieces[array].at[pl.ds(part * 256 + index % 2 * 128, 128), :],
                w_ref.at[pl.ds(first, 128), :],
                sem,
            )
        )
    for copy in copies:
        copy.start()
    return copies


def unit_back_kernel(where_ref, own_ref, other_ref, slope_ref, *refs):
    hg_ref, sum_ref, w_ref, sem = refs[4:]
    j = pl.program_id(0)
    step = hg_ref.shape[1]

    @pl.when(j == 0)
    def _():
        for copy in fetch_units(where_ref[0], refs[:4], w_ref, sem):
            copy.wait()

    w = w_ref[pl.ds(pl.multiple_of(j * step, step), step), :]
    total = None
    rows = own_ref.shape[0]
    for half, g_ref in enumerate((own_ref, other_ref)):
        here = slice(half * rows, half * rows + rows)
        grad = (times_transposed(g_ref[...], w) * slope_ref[here, :]).astype(BF)
        hg_ref[here, :] = grad
        part = jnp.sum(grad.astype(F32), axis=0, keepdims=True)
        total = part if total is None else total + part
    sum_ref[...] = total


def unit_back(where, own, other, slope, pieces):
    rows, width = slope.shape
    step = 512
    column = pl.BlockSpec((rows, step), lambda j: (0, j))
    return pl.pallas_call(
        unit_back_kernel,
        grid=(width // step,),
        out_shape=(shaped(rows, width, BF), shaped(1, width, F32)),
        in_specs=[SMEM, whole(own), whole(other), column] + [ANY] * 4,
        out_specs=(column, pl.BlockSpec((1, step), lambda j: (0, j))),
        scratch_shapes=[pltpu.VMEM((width, D), BF), pltpu.SemaphoreType.DMA],
        cost_estimate=cost(2 * rows * D * width, 8 * rows * width),
        name="unit_back",
    )(where, own, other, slope, *pieces)


def unit_out_kernel(where_ref, act_ref, heads_ref, *refs):
    contexts, pieces = refs[:3], refs[3:7]
    mine_ref, theirs_ref, w_ref, total_ref, sem = refs[7:]
    step = pl.program_id(0)

    @pl.when(step == 0)
    def _():
        for copy in fetch_units(where_ref[0], pieces, w_ref, sem):
            copy.wait()

    context = jnp.concatenate([ref[...] for ref in contexts], axis=1)
    total_ref[...] = dot(act_ref[...], w_ref[...]) + dot(context, heads_ref[...])

    @pl.when(step < 2)
    def _():
        mine_ref[...] = total_ref[...]

    @pl.when(step >= 2)
    def _():
        theirs_ref[...] = total_ref[...]


def unit_out(where, act, heads, contexts, pieces):
    rows, width = act.shape
    return pl.pallas_call(
        unit_out_kernel,
        grid=(4,),
        out_shape=(shaped(rows // 2, D, F32),) * 2,
        in_specs=[SMEM, rows_spec(width), whole(heads)]
        + [rows_spec(context.shape[1]) for context in contexts]
        + [ANY] * 4,
        out_specs=(
            pl.BlockSpec((256, D), lambda i: (jnp.minimum(i, 1), 0)),
            pl.BlockSpec((256, D), lambda i: (jnp.maximum(i - 2, 0), 0)),
        ),
        scratch_shapes=[
            pltpu.VMEM((width, D), BF),
            pltpu.VMEM((256, D), F32),
            pltpu.SemaphoreType.DMA,
        ],
        cost_estimate=cost(3 * rows * D * width, 6 * rows * width),
        name="unit_out",
    )(where, act, heads, *contexts, *pieces)


def row_grads_kernel(steps, where_ref, left_ref, right_ref, *refs):
    out_refs = refs[-6:]
    spots = [[place_of(chip) for chip in chips] for chips in BLOCKS.values()]

    @pl.when(pl.program_id(0) < steps)
    def _():
        value = dot(left_ref[...], right_ref[...]).astype(BF)
        for places, ref in zip(spots, out_refs):
            for at, place in enumerate(places):
                ref[at * 64 : at * 64 + 64, :] = value[place * 64 : place * 64 + 64]

    if len(refs) == 7:
        held_ref = refs[0]
        me, core = where_ref[0], where_ref[1]

        @pl.when(pl.program_id(0) >= steps)
        def _():
            for chips, ref in zip(BLOCKS.values(), out_refs):
                for at, chip in enumerate(chips):
                    found = chip ^ me
                    start = (((found // 8) ^ core) * 8 + found % 8) * 32
                    rows = held_ref[pl.ds(pl.multiple_of(start, 32), 32), :]
                    ref[at * 64 : at * 64 + 32, :] = rows[:, : D // 2]
                    ref[at * 64 + 32 : at * 64 + 64, :] = rows[:, D // 2 :]


def row_grads(where, left, right, more=None):
    rows, tokens = left.shape
    step = 512
    steps = right.shape[1] // step
    columns = right.shape[1] + (0 if more is None else D // 2)
    heights = [64 * len(chips) for chips in BLOCKS.values()]
    return pl.pallas_call(
        partial(row_grads_kernel, steps),
        grid=(columns // step,),
        out_shape=tuple(shaped(height, columns, BF) for height in heights),
        in_specs=[
            SMEM,
            whole(left),
            pl.BlockSpec((tokens, step), lambda j: (0, jnp.minimum(j, steps - 1))),
        ]
        + ([] if more is None else [whole(more)]),
        out_specs=tuple(pl.BlockSpec((height, step), lambda j: (0, j)) for height in heights),
        cost_estimate=cost(2 * rows * tokens * columns, 2 * (rows * tokens + rows * columns)),
        name="row_grads",
    )(where, left, right, *([] if more is None else [more]))


def unit_grads_kernel(order_ref, *refs):
    lefts, own_ref, other_ref, out_refs = refs[:4], refs[4], refs[5], refs[6:]
    left = stack(lefts)
    tokens = own_ref.shape[0]
    a, xa, b, yb, yax, xby = out_refs
    columns = 512

    def some(i, carry):
        here = pl.ds(pl.multiple_of(i * columns, columns), columns)
        value = dot(left[:, :tokens], own_ref[:, here]) + dot(left[:, tokens:], other_ref[:, here])
        value = value.astype(BF)
        for piece, outs in enumerate(((a, xa), (b, yb), (yax,), (xby,))):

            @pl.when(pl.program_id(0) == piece)
            def _(outs=outs):
                rows = 512 // len(outs)
                for at, ref in enumerate(outs):
                    ref[:, here] = value[at * rows : at * rows + rows]

        return carry

    lax.fori_loop(0, D // columns, some, 0)


def unit_grads(me, left, own, other):
    tokens = left.shape[1]
    order = jnp.asarray(np.array(sum(SUMS.values(), []), np.int32)) ^ me

    def block(place):
        return pl.BlockSpec((128, tokens), lambda k, order: (order[4 * k + place], 0))

    return pl.pallas_call(
        unit_grads_kernel,
        out_shape=tuple(shaped(128 * len(chips), D, BF) for chips in BLOCKS.values()),
        grid_spec=pltpu.PrefetchScalarGridSpec(
            num_scalar_prefetch=1,
            grid=(4,),
            in_specs=[block(place) for place in range(4)] + [whole(own), whole(other)],
            out_specs=tuple(
                pl.BlockSpec((128 * len(chips), D), lambda k, order: (0, 0))
                for chips in BLOCKS.values()
            ),
        ),
        cost_estimate=cost(2 * tokens * D * 2048, 4 * 2048 * D),
        name="unit_grads",
    )(order, left, left, left, left, own, other)


def out_grad_kernel(where_ref, own_ref, other_ref, *refs):
    contexts, keep_ref, give_ref, across_ref = refs[:3], refs[3], refs[4], refs[5]
    first = where_ref[1] == 0
    tokens = own_ref.shape[0]
    group = pl.program_id(0)

    @pl.when(group == 0)
    def _():
        lane = 0
        for ref in contexts:
            across_ref[lane : lane + ref.shape[1], :] = ref[...].T
            lane += ref.shape[1]

    across = across_ref[pl.ds(pl.multiple_of(group * 128, 128), 128), :]
    value = dot(across[:, :tokens], own_ref[...]) + dot(across[:, tokens:], other_ref[...])
    value = value.astype(BF)
    for head in range(2):
        zero, one = value[head * 64 : head * 64 + 32], value[head * 64 + 32 : head * 64 + 64]
        rows = slice(head * 32, head * 32 + 32)
        keep_ref[rows, :] = jnp.where(first, zero, one)
        give_ref[rows, :] = jnp.where(first, one, zero)


def out_grad(where, own, other, contexts):
    block = pl.BlockSpec((64, D), lambda i: (i, 0))
    return pl.pallas_call(
        out_grad_kernel,
        grid=(4,),
        out_shape=(shaped(256, D, BF),) * 2,
        in_specs=[SMEM, whole(own), whole(other)] + [whole(context) for context in contexts],
        out_specs=(block, block),
        scratch_shapes=[pltpu.VMEM((D // 2, 1024), BF)],
        cost_estimate=cost(1024 * D * D, 6 * 1024 * D),
        name="out_grad",
    )(where, own, other, *contexts)


def norm_grad_kernel(spans, left_ref, *refs):
    count = 4 * len(spans)
    mine_ref, theirs_ref, total_ref = refs[-3:]
    earlier = refs[count:-3]
    step = pl.program_id(0)
    first = 0
    lefts = []
    for start, end in spans:
        lefts.append(left_ref[:, first : first + end - start])
        first += end - start
    for pair in range(4):
        total = None
        for line, (left, span) in enumerate(zip(lefts, spans)):
            right = gathered(
                refs[4 * line : 4 * line + 4], slice(*span), slice(2 * pair, 2 * pair + 2)
            )
            part = times_transposed(left, right)
            total = part if total is None else total + part
        total_ref[:, 256 * pair : 256 * pair + 256] = total

    for half, out_ref in enumerate((mine_ref, theirs_ref)):

        @pl.when(step // 2 == half)
        def _(half=half, out_ref=out_ref):
            if earlier:
                out_ref[...] = total_ref[...] + earlier[half][...]
            else:
                out_ref[...] = total_ref[...]


def norm_grad(left, lines, spans, earlier=()):
    rows = left.shape[0]
    flat = [piece for line in lines for piece in line]
    halves = (
        pl.BlockSpec((256, D), lambda i: (jnp.minimum(i, 1), 0)),
        pl.BlockSpec((256, D), lambda i: (jnp.maximum(i - 2, 0), 0)),
    )
    return pl.pallas_call(
        partial(norm_grad_kernel, spans),
        grid=(4,),
        out_shape=(shaped(rows // 2, D, F32),) * 2,
        in_specs=[rows_spec(left.shape[1])]
        + [whole(piece) for piece in flat]
        + list(halves[: len(earlier)]),
        out_specs=halves,
        scratch_shapes=[pltpu.VMEM((256, D), F32)],
        cost_estimate=cost(2 * rows * D * left.shape[1], 12 * rows * D),
        name="norm_grad",
    )(left, *flat, *earlier)


def norm_back_kernel(
    where_ref, part_ref, more_ref, xhat_ref, inv_ref, gain_ref, g_ref, out_ref, sum_ref, chosen_ref
):
    @pl.when(pl.program_id(0) == 0)
    def _():
        choice_into(where_ref[0], chosen_ref)
        sum_ref[...] = jnp.zeros_like(sum_ref)

    grad = part_ref[...] + more_ref[...]
    xhat = xhat_ref[...]
    scaled = grad * gain_ref[...]
    value = (
        scaled
        - jnp.mean(scaled, axis=-1, keepdims=True)
        - xhat * jnp.mean(scaled * xhat, axis=-1, keepdims=True)
    ) * inv_ref[...]
    high = value.astype(BF)
    low = (value - high.astype(F32)).astype(BF)
    value = times_transposed(high, chosen_ref[...]) + times_transposed(low, chosen_ref[...])
    out_ref[...] = (g_ref[...].astype(F32) + value).astype(BF)
    sum_ref[0:1, :] += jnp.sum(grad * xhat, axis=0, keepdims=True)
    sum_ref[1:2, :] += jnp.sum(grad, axis=0, keepdims=True)


def norm_back(where, part, more, xhat, inv_std, gain, grad):
    rows = grad.shape[0]
    one = pl.BlockSpec((1, D), lambda i: (0, 0))
    return pl.pallas_call(
        norm_back_kernel,
        grid=(rows // 256,),
        out_shape=(shaped(rows, D, BF), shaped(8, D, F32)),
        in_specs=[SMEM] + [rows_spec(D)] * 3 + [rows_spec(1), one, rows_spec(D)],
        out_specs=(rows_spec(D), pl.BlockSpec((8, D), lambda i: (0, 0))),
        scratch_shapes=[pltpu.VMEM((D, D), BF)],
        cost_estimate=cost(4 * rows * D * D, 16 * rows * D),
        name="norm_back",
    )(where, part, more, xhat, inv_std, gain, grad)


def paste_in_kernel(where_ref, mine_ref, other_ref, out_ref):
    core = where_ref[1]
    for owner, ref in ((core, mine_ref), (1 - core, other_ref)):
        for block in range(CHIPS):
            at = pl.multiple_of((2 * block + owner) * 128, 128)
            out_ref[:, pl.ds(at, 128)] = ref[:, block * 128 : block * 128 + 128]


def paste_qkv_kernel(where_ref, mine_ref, other_ref, out_ref):
    core = where_ref[1]
    low = lanes_low(mine_ref.shape[0])
    for owner, ref in ((core, mine_ref), (1 - core, other_ref)):
        for group in range(GROUPS):
            q, k, v = (
                ref[:, group * 384 + part * 128 : group * 384 + part * 128 + 128]
                for part in range(3)
            )
            turned = pltpu.roll(k, HD, 1)
            blocks = (jnp.where(low, q, turned), jnp.where(low, v, q), jnp.where(low, turned, v))
            for part, value in enumerate(blocks):
                at = (owner * GROUPS + group) * 384 + part * 128
                out_ref[:, pl.ds(pl.multiple_of(at, 128), 128)] = value


def paste(kernel, where, mine, other):
    return pl.pallas_call(
        kernel,
        out_shape=shaped(mine.shape[0], 2 * mine.shape[1], F32),
        in_specs=[SMEM, VMEM, VMEM],
        out_specs=VMEM,
        cost_estimate=cost(0, 16 * mine.shape[0] * mine.shape[1]),
        name="paste",
    )(where, mine, other)


def local_fast(
    hidden_in,
    document_labels,
    cotangent,
    ln_gain,
    ln_bias,
    qkv_weight,
    qkv_bias,
    out_weight,
    out_bias,
    fc_in_weight,
    fc_in_bias,
    fc_out_weight,
    fc_out_bias,
):
    local_seqs, tok_count = hidden_in.shape[:2]
    row_count = local_seqs * tok_count
    d_rows = qkv_weight.shape[0]
    f_rows = fc_out_weight.shape[0]
    units = fc_in_weight.shape[1] // 2
    pair = 2
    core = lax.axis_index("fsdp") % 2
    me = lax.axis_index("seq") * 4 + lax.axis_index("fsdp") // 2
    clock = Clock(jnp.stack([me, core]).astype(jnp.int32))
    box = {}

    waiting, deferred = [], []

    def slot(jobs, work=None, *inputs, chain=None, late=(), then=None):
        nonlocal waiting
        jobs, late = list(jobs), list(late)
        chains = chain if isinstance(chain, list) else [chain] if chain is not None else []
        gated, given, more = clock.join(
            tuple(job[2] for job in jobs + late), inputs, tuple(tuple(link[2]) for link in chains)
        )
        values = [job[3](value) for job, value in zip(jobs + late, gated)]
        made = work(*given) if work is not None else ()
        after = []
        for (name, follow, _), inputs in zip(chains, more):
            for job, value in list(zip(jobs, values)) + waiting:
                if job[1] == name:
                    after.append(follow(value, *inputs))
        for job, value in deferred:
            late.append(job)
            values.append(value)
        deferred.clear()
        if then is not None:
            started = then(made)
            late = late + started
            values = values + [job[3](job[2]) for job in started]
        ended, values, older = waiting, values[: len(jobs)], values[len(jobs) :]
        found = values + [value for _, value in ended]
        found, made, after = clock.join(tuple(found), made, after)
        for job, value in zip(jobs + [job for job, _ in ended], found):
            job[0][job[1]] = value
        waiting = list(zip(late, older))
        if chain is None:
            return made
        return made, after if isinstance(chain, list) else after[0]

    def moves(line, stage):
        return [
            (line.parts, name, line.parts[source], partial(cross, bit=bit))
            for name, source, bit in line.jobs(stage)
        ]

    def core_move(name, value):
        return (box, name, value, other_core)

    def pick(halves):
        first = core == 0
        return jnp.where(first, halves[0], halves[1]), jnp.where(first, halves[1], halves[0])

    def joined(mine, other):
        first = core == 0
        return jnp.concatenate(
            [jnp.where(first, mine, other), jnp.where(first, other, mine)], axis=0
        )

    x_own = hidden_in.reshape(row_count, D)
    g_own = cotangent.reshape(row_count, D)
    vectors = (ln_gain, ln_bias, qkv_bias, out_bias, fc_in_bias, fc_out_bias)
    keep1, give1, keep2, give2, in_keep, in_give, folded = cut(
        clock.token, qkv_weight, fc_in_weight, out_weight, vectors, document_labels
    )
    slot([core_move("give1", give1)])
    line_a = Gather(joined(keep1, box["give1"]))
    slot(moves(line_a, "far") + [core_move("x", x_own), core_move("give2", give2)])
    line_b = Gather(jnp.concatenate([folded, joined(keep2, box["give2"])], axis=1))
    line_d = Gather(fc_out_weight)
    slot(moves(line_a, "near") + moves(line_b, "far") + [core_move("in", in_give), core_move("g", g_own)])
    g_more = box["g"]
    slot(moves(line_a, "first") + moves(line_b, "near"))
    line_c = Gather(joined(in_keep, box["in"]))
    (xhat, inv_std), grad_sum, (bias, *tables) = slot(
        moves(line_a, "second") + moves(line_c, "far"),
        lambda own, other, g, a, b: (
            prepare(clock.token, own, other),
            jnp.sum(g.astype(F32), axis=0),
            marks(clock.token, a, b),
        ),
        x_own,
        box["x"],
        g_own,
        line_a.parts["a"],
        line_a.parts["b"],
    )
    a_pieces = line_a.pieces()
    made = slot(
        moves(line_b, "first") + moves(line_c, "near") + moves(line_d, "far"),
        lambda xhat, tables, pieces: project_first(clock.token, xhat, tables, pieces),
        xhat,
        tables,
        a_pieces,
    )
    queries, kvs = [made[0], made[2]], [[made[1]], [made[3]]]
    normed, normed_t, b_more, b_in, b_rows, gain = made[4:]
    moved, results, backs = {}, {}, {}

    def up(group, hop):
        return (moved, (group, hop), kvs[group][hop], partial(shift, by=1))

    def landed(*found):
        for group, hop in found:
            kvs[group].append(moved[group, hop])

    def down(group, hop):
        value = results[group][4]
        if hop == 1:
            value = (results[group][3].astype(F32) + backs[group, 0].astype(F32)).astype(BF)
        return (backs, (group, hop), value, partial(shift, by=-1))

    def attention(*groups):
        def work(*given):
            return [attend(group, *args) for group, args in zip(groups, given)]

        return work, *[
            (queries[group], context_grad, bias, tuple(kvs[group])) for group in groups
        ]

    def attended(groups, found):
        for group, result in zip(groups, found):
            results[group] = result

    slot(moves(line_b, "second") + [up(0, 0)])
    landed((0, 0))
    b_pieces = line_b.pieces()
    made, (out_keep, out_give) = slot(
        moves(line_c, "first") + [up(0, 1), up(1, 0)],
        lambda normed, bias, tables, pieces: (
            project_more(normed, bias, tables, pieces),
            head_rows(clock.token, pieces),
        ),
        normed,
        b_more,
        tables,
        b_pieces,
    )
    landed((0, 1), (1, 0))
    queries.append(made[0])
    kvs.append([made[1]])

    def first_attention(out_more, g_own, g_more, out_keep, query, bias, kvs):
        grad, heads = context_gradient(clock.token, g_own, g_more, out_keep, out_more)
        return grad, heads, attend(0, query, grad, bias, kvs)

    _, (context_grad, out_heads, found) = slot(
        moves(line_c, "second") + moves(line_d, "near") + [up(1, 1), core_move("out", out_give)],
        chain=(
            "out",
            first_attention,
            (g_own, g_more, out_keep, queries[0], bias, tuple(kvs[0])),
        ),
    )
    results[0] = found
    landed((1, 1))
    c_pieces = line_c.pieces()
    act, act_t, slope = slot(
        moves(line_d, "first") + [up(2, 0), down(0, 0)],
        lambda normed, b_in, pieces: hidden(normed, pieces, b_in),
        normed,
        b_in,
        c_pieces,
    )
    landed((2, 0))
    work, *given = attention(1)

    def with_units(given, act_t, own, other):
        found = work(given)
        return found, unit_grads(clock.token[0], act_t, own, other), shift(found[0][4], -1)

    found, fc_parts, backs[1, 0] = slot(
        moves(line_d, "second") + [up(2, 1)],
        with_units,
        *given,
        act_t,
        g_own,
        g_more,
        late=[down(0, 1)],
    )
    attended([1], found)
    landed((2, 1))
    d_pieces = line_d.pieces()
    sum_fc = Scatter(fc_parts)
    work2, *given = attention(2)

    def last_attention(given, earlier, own, other):
        found = work2(given)
        contexts = earlier + [found[0][0]]
        return found, contexts, out_grad(clock.token, own, other, contexts)

    found, contexts, (out_keep, out_give) = slot(
        moves(sum_fc, "first") + [down(1, 1)],
        last_attention,
        *given,
        [results[group][0] for group in range(2)],
        g_own,
        g_more,
        then=lambda made: [(backs, (2, 0), made[0][0][4], partial(shift, by=-1))],
    )
    attended([2], found)

    def units_back(out_more, out_keep, normed_t, own, other, slope, pieces):
        hidden_grad, hidden_sum = unit_back(clock.token, own, other, slope, pieces)
        more = jnp.concatenate([out_keep, out_more], axis=0)
        return hidden_grad, hidden_sum, row_grads(clock.token, normed_t, hidden_grad, more)

    def near_now(last, own, earlier):
        rows = own.shape[0]
        total = own.astype(F32) + earlier[:rows].astype(F32) + last.astype(F32)
        return cross(total.astype(BF), NEAR)

    _, ((hidden_grad, hidden_sum, in_parts), sum_fc.parts["r_b"]) = slot(
        moves(sum_fc, "second") + [core_move("out_grad", out_give)],
        chain=[
            ("out_grad", units_back, (out_keep, normed_t, g_own, g_more, slope, d_pieces)),
            ("r_yb", near_now, (sum_fc.parts["b"], sum_fc.parts["r_xby"])),
        ],
    )
    sum_in = Scatter(in_parts)
    (out_mine, out_theirs), earlier = slot(
        moves(sum_in, "first") + [down(2, 1)],
        lambda act, heads, contexts, pieces, grad, c_pieces: (
            unit_out(clock.token, act, heads, contexts, pieces),
            norm_grad(grad, [c_pieces], [(0, units)]),
        ),
        act,
        out_heads,
        contexts,
        d_pieces,
        hidden_grad,
        c_pieces,
    )

    def last_grads(normed_t, tables, triples):
        projected_grad, total = unturn(tables, triples)
        return projected_grad, total, row_grads(clock.token, normed_t, projected_grad)

    def near_soon(*terms):
        deferred.append(((sum_in.parts, "r_b"), near_now(*terms)))
        return ()

    def far_soon(last, *terms):
        rows = last.shape[0]
        total = sum(term[rows // 2 : rows].astype(F32) for term in terms + (last,))
        deferred.append(((sum_in.parts, "r_far"), cross(total.astype(BF), FAR)))
        return ()

    (projected_grad, qkv_bias_sum, parts), _ = slot(
        moves(sum_in, "second") + moves(sum_fc, "far") + [core_move("out_side", out_theirs)],
        last_grads,
        normed_t,
        tables,
        [(results[group][1], results[group][2], backs[group, 1]) for group in range(3)],
        chain=[("r_yb", near_soon, (sum_in.parts["b"], sum_in.parts["r_xby"]))],
    )
    sum_qkv = Scatter(parts)
    (norm_mine, norm_theirs), _ = slot(
        moves(sum_qkv, "first"),
        lambda projected_grad, earlier, *lines: norm_grad(
            projected_grad, lines, [(0, 768), (512, 1280)], earlier
        ),
        projected_grad,
        earlier,
        a_pieces,
        b_pieces,
        chain=[("r_b", far_soon, [sum_in.parts[name] for name in ("a", "r_yax", "r_xa")])],
    )

    def finish_output(x_own, out_mine, out_more, b_rows):
        order = jnp.asarray(np.array(ORDER, np.int32)) ^ me
        spots = place_of(jnp.arange(CHIPS, dtype=jnp.int32) ^ me)
        b_rows = b_rows.reshape(CHIPS, 2 * d_rows)[spots].reshape(1, D)
        return (x_own.astype(F32) + out_mine + out_more + b_rows).astype(BF)

    def small_rows(norm_sums, qkv_bias_sum, hidden_sum, grad_sum):
        spots = place_of(jnp.arange(CHIPS, dtype=jnp.int32) ^ me)
        norm_sums = norm_sums[:2].reshape(2, CHIPS, 2, d_rows)[:, spots].reshape(2, D)
        mine = (jnp.arange(2) == core)[:, None]
        qkv_full = (
            jnp.where(mine, qkv_bias_sum, 0.0)
            .reshape(2, GROUPS, 3, pair, HD)
            .transpose(0, 1, 3, 2, 4)
            .reshape(3 * D)
        )
        in_full = jnp.where(mine[None], hidden_sum.reshape(CHIPS, 1, f_rows), 0.0)
        packed = jnp.concatenate(
            [
                vector.reshape(2 * CHIPS, -1)
                for vector in (norm_sums[0], norm_sums[1], qkv_full, grad_sum, in_full)
            ],
            axis=1,
        ).reshape(CHIPS, -1)
        order = [NEAR * (i % 2) + FAR * (i // 2 % 2) + i // 4 % 2 + Y * (i // 8) for i in range(CHIPS)]
        return packed[jnp.asarray(np.array(order, np.int32)) ^ me]

    def back_work(norm_more, norm_mine, xhat, inv_std, gain, g_own, *sums):
        input_grad, norm_sums = norm_back(
            clock.token, norm_mine, norm_more, xhat, inv_std, gain, g_own
        )
        return input_grad, small_rows(norm_sums, *sums)

    _, (input_grad, packed) = slot(
        moves(sum_qkv, "second") + [core_move("norm", norm_theirs)],
        chain=(
            "norm",
            back_work,
            (norm_mine, xhat, inv_std, gain, g_own, qkv_bias_sum, hidden_sum, grad_sum),
        ),
    )

    def fold(bit):
        return (box, "fold", packed[packed.shape[0] // 2 :], partial(cross, bit=bit))

    def half_sum():
        return packed[: packed.shape[0] // 2] + box["fold"]

    def two_folds(value, rows):
        half = rows[: rows.shape[0] // 2] + value
        give = half[half.shape[0] // 2 :]
        return half[: half.shape[0] // 2] + cross(give, X)

    in_rows = sum_in.result()
    in_keep, in_give = pick(in_rows[:, :units].reshape(2, d_rows, units))
    out_weight_grad = in_rows[:, units:].reshape(2, d_rows, D // 2)
    output, packed = slot(
        moves(sum_qkv, "near") + [fold(Y), core_move("in_rows", in_give)],
        finish_output,
        x_own,
        out_mine,
        box["out_side"],
        b_rows,
        chain=("fold", two_folds, (packed,)),
    )
    fc_in_weight_grad = slot(
        moves(sum_qkv, "far") + [fold(FAR)],
        lambda mine, other: paste(paste_in_kernel, clock.token, mine, other),
        in_keep,
        box["in_rows"],
    )
    packed = half_sum()
    qkv_keep, qkv_give = pick(sum_qkv.result().reshape(2, d_rows, -1))
    slot([core_move("qkv_rows", qkv_give), fold(NEAR)])
    sums_keep, sums_give = pick(half_sum().reshape(2, -1))
    sums = sums_keep + other_core(sums_give)
    parts = []
    first = 0
    for width in (d_rows, d_rows, 3 * d_rows, d_rows, f_rows):
        parts.append(sums[first : first + width])
        first += width
    return (
        output.reshape(local_seqs, tok_count, D),
        input_grad.reshape(local_seqs, tok_count, D),
        parts[0],
        parts[1],
        paste(paste_qkv_kernel, clock.token, qkv_keep, box["qkv_rows"]),
        parts[2],
        jnp.concatenate([out_weight_grad[0], out_weight_grad[1]], axis=1),
        parts[3],
        fc_in_weight_grad,
        parts[4],
        sum_fc.result(),
        parts[3],
    )


def solution(mesh):
    rows = P(("seq", "fsdp"))
    wide = P(("seq", "fsdp"), None)
    act = P("fsdp", "seq", None)
    placed = (act, P("fsdp", "seq"), act) + (rows, rows) + (wide, rows) * 4
    small = dict(mesh.shape) == {"seq": 4, "fsdp": 8}
    return jax.shard_map(
        local_fast if small else local_plain,
        mesh=mesh,
        in_specs=placed,
        out_specs=(act, act, rows, rows) + (wide, rows) * 4,
        check_vma=False,
    )
```

```python
from functools import partial
import math

import jax
import jax.numpy as jnp
import numpy as np
from jax import lax
from jax.experimental import pallas as pl
from jax.experimental.pallas import tpu as pltpu
from jax.sharding import PartitionSpec as P

D = 1024
H = 16
HD = 64
ROT = 16
GROUPS = 4
BF = jnp.bfloat16
F32 = jnp.float32


def rotate(values, cosine, sine_part):
    half_rot = ROT // 2
    first_part = values[..., :half_rot]
    second_part = values[..., half_rot:ROT]
    return jnp.concatenate(
        [
            first_part * cosine - second_part * sine_part,
            second_part * cosine + first_part * sine_part,
            values[..., ROT:],
        ],
        axis=-1,
    )


def position_angles(segments):
    length = segments.shape[0]
    places = jnp.arange(length, dtype=jnp.int32)
    boundary = jnp.concatenate([jnp.ones((1,), dtype=jnp.bool_), segments[1:] != segments[:-1]])
    starts = lax.cummax(jnp.where(boundary, places, 0), axis=0)
    positions = (places - starts).astype(jnp.float32)
    inverse = 1.0 / 10000.0 ** (jnp.arange(0, ROT, 2, dtype=jnp.float32) / ROT)
    return positions[:, None] * inverse[None, :]


def make_mask(segments, first_row, block_rows):
    length = segments.shape[0]
    query_index = first_row + jnp.arange(block_rows, dtype=jnp.int32)
    key_index = jnp.arange(length, dtype=jnp.int32)
    query_segments = lax.dynamic_slice_in_dim(segments, first_row, block_rows, 0)
    return (key_index[None, :] <= query_index[:, None]) & (
        query_segments[:, None] == segments[None, :]
    )


def outer_product(left, right):
    return lax.dot_general(
        left, right, (((0,), (0,)), ((), ())), preferred_element_type=jnp.float32
    )


def times_transposed(left, right):
    return lax.dot_general(
        left, right, (((1,), (1,)), ((), ())), preferred_element_type=jnp.float32
    )


def local_plain(
    hidden_in,
    document_labels,
    cotangent,
    ln_gain,
    ln_bias,
    qkv_weight,
    qkv_bias,
    out_weight,
    out_bias,
    fc_in_weight,
    fc_in_bias,
    fc_out_weight,
    fc_out_bias,
):
    gathered = (
        lax.all_gather(ln_gain, ("seq", "fsdp"), axis=0, tiled=True),
        lax.all_gather(ln_bias, ("seq", "fsdp"), axis=0, tiled=True),
        lax.all_gather(qkv_weight, ("seq", "fsdp"), axis=0, tiled=True),
        lax.all_gather(qkv_bias, ("seq", "fsdp"), axis=0, tiled=True),
        lax.all_gather(out_weight, ("seq", "fsdp"), axis=0, tiled=True),
        lax.all_gather(out_bias, ("seq", "fsdp"), axis=0, tiled=True),
        lax.all_gather(fc_in_weight, ("seq", "fsdp"), axis=0, tiled=True),
        lax.all_gather(fc_in_bias, ("seq", "fsdp"), axis=0, tiled=True),
        lax.all_gather(fc_out_weight, ("seq", "fsdp"), axis=0, tiled=True),
        lax.all_gather(fc_out_bias, ("seq", "fsdp"), axis=0, tiled=True),
    )
    norm_multiplier, norm_shift, w_qkv, b_qkv, w_out, b_out, w_in, b_in, w_fc, b_fc = gathered
    norm_multiplier = norm_multiplier.astype(jnp.float32)
    norm_shift = norm_shift.astype(jnp.float32)
    groups = lax.axis_size("seq")
    per_group = H // groups
    local_seqs = hidden_in.shape[0]
    tok_count = hidden_in.shape[1]
    row_count = local_seqs * tok_count
    tokens = hidden_in.reshape(row_count, D).astype(jnp.float32)
    average = jnp.mean(tokens, axis=-1, keepdims=True)
    centered = tokens - average
    spread = jnp.mean(centered * centered, axis=-1, keepdims=True)
    inv_std = lax.rsqrt(spread + 1e-05)
    rescaled_rows = centered * inv_std
    normed = (rescaled_rows * norm_multiplier + norm_shift).astype(jnp.bfloat16)
    projected = jnp.dot(normed, w_qkv, preferred_element_type=jnp.float32) + b_qkv.astype(
        jnp.float32
    )
    segments_all = lax.all_gather(document_labels, "seq", axis=1, tiled=True)
    angles_all = jax.vmap(position_angles)(segments_all)
    angles = lax.dynamic_slice_in_dim(
        angles_all, lax.axis_index("seq") * tok_count, tok_count, 1
    ).reshape(row_count, ROT // 2)
    cosine = jnp.cos(angles)[:, None, None, :]
    sine_part = jnp.sin(angles)[:, None, None, :]
    head_parts = projected.reshape(row_count, H, 3, HD)
    turned = jnp.concatenate(
        [rotate(head_parts[:, :, :2], cosine, sine_part), head_parts[:, :, 2:]], axis=2
    ).astype(jnp.bfloat16)
    outgoing = turned.reshape(local_seqs, tok_count, groups, per_group * 3 * HD)
    arrived = lax.all_to_all(outgoing, "seq", split_axis=2, concat_axis=1, tiled=True)
    length = arrived.shape[1]
    local_heads = arrived.reshape(local_seqs, length, per_group, 3, HD)
    queries_seq = local_heads[:, :, :, 0]
    keys_seq = local_heads[:, :, :, 1]
    values_seq = local_heads[:, :, :, 2]
    block_rows = min(512, length)
    block_count = length // block_rows
    scale_factor = 1.0 / math.sqrt(HD)

    def attend_forward(inputs):
        query_all, key_everywhere, value_all, segments = inputs

        def forward_step(running, block_index):
            first_row = block_index * block_rows
            query_rows = lax.dynamic_slice_in_dim(query_all, first_row, block_rows, 0)
            allowed = make_mask(segments, first_row, block_rows)
            raw_scores = (
                jnp.einsum(
                    "qhd,khd->hqk", query_rows, key_everywhere, preferred_element_type=jnp.float32
                )
                * scale_factor
            )
            raw_scores = jnp.where(allowed[None], raw_scores, -1e30)
            row_max = jnp.max(raw_scores, axis=-1, keepdims=True)
            unscaled = jnp.exp(raw_scores - row_max)
            row_total = jnp.sum(unscaled, axis=-1, keepdims=True)
            probabilities = (unscaled / row_total).astype(jnp.bfloat16)
            context_rows = jnp.einsum(
                "hqk,khd->qhd", probabilities, value_all, preferred_element_type=jnp.float32
            )
            log_total = (row_max + jnp.log(row_total))[..., 0]
            return (running, (context_rows, log_total))

        _, (context_blocks, log_blocks) = lax.scan(
            forward_step, None, jnp.arange(block_count, dtype=jnp.int32)
        )
        return (context_blocks.reshape(length, per_group * HD).astype(jnp.bfloat16), log_blocks)

    context_seq, log_totals = lax.map(
        attend_forward, (queries_seq, keys_seq, values_seq, segments_all)
    )
    context_heads = context_seq.reshape(local_seqs, length, 1, per_group * HD)
    returned = lax.all_to_all(context_heads, "seq", split_axis=1, concat_axis=2, tiled=True)
    context = returned.reshape(row_count, D)
    attn_out = jnp.dot(context, w_out, preferred_element_type=jnp.float32) + b_out.astype(
        jnp.float32
    )
    hidden_pre = jnp.dot(normed, w_in, preferred_element_type=jnp.float32) + b_in.astype(
        jnp.float32
    )
    activated = jax.nn.gelu(hidden_pre, approximate=False).astype(jnp.bfloat16)
    mlp_out = jnp.dot(activated, w_fc, preferred_element_type=jnp.float32) + b_fc.astype(
        jnp.float32
    )
    output = (tokens + attn_out + mlp_out).astype(jnp.bfloat16).reshape(local_seqs, tok_count, D)
    grad_out = cotangent.reshape(row_count, D)
    grad_wide = grad_out.astype(jnp.float32)
    out_bias_grad = jnp.sum(grad_wide, axis=0)
    fc_out_bias_grad = jnp.sum(grad_wide, axis=0)
    out_weight_grad = outer_product(context, grad_out)
    fc_out_weight_grad = outer_product(activated, grad_out)
    act_grad = times_transposed(grad_out, w_fc)
    _, gelu_back = jax.vjp(partial(jax.nn.gelu, approximate=False), hidden_pre)
    hidden_grad = gelu_back(act_grad)[0].astype(jnp.bfloat16)
    fc_in_weight_grad = outer_product(normed, hidden_grad)
    fc_in_bias_grad = jnp.sum(hidden_grad.astype(jnp.float32), axis=0)
    context_grad = times_transposed(grad_out, w_out).astype(jnp.bfloat16)
    grad_outgoing = context_grad.reshape(local_seqs, tok_count, groups, per_group * HD)
    head_grad_seq = lax.all_to_all(
        grad_outgoing, "seq", split_axis=2, concat_axis=1, tiled=True
    ).reshape(local_seqs, length, per_group, HD)

    def attend_backward(inputs):
        query_all, key_everywhere, value_all, segments, head_grad, log_blocks = inputs

        def backward_step(running, block_index):
            key_acc, value_accumulator = running
            first_row = block_index * block_rows
            query_rows = lax.dynamic_slice_in_dim(query_all, first_row, block_rows, 0)
            grad_rows = lax.dynamic_slice_in_dim(head_grad, first_row, block_rows, 0)
            log_rows = log_blocks[block_index]
            allowed = make_mask(segments, first_row, block_rows)
            raw_scores = (
                jnp.einsum(
                    "qhd,khd->hqk", query_rows, key_everywhere, preferred_element_type=jnp.float32
                )
                * scale_factor
            )
            raw_scores = jnp.where(allowed[None], raw_scores, -1e30)
            probabilities = jnp.where(allowed[None], jnp.exp(raw_scores - log_rows[..., None]), 0.0)
            value_accumulator = value_accumulator + jnp.einsum(
                "hqk,qhd->khd",
                probabilities.astype(jnp.bfloat16),
                grad_rows,
                preferred_element_type=jnp.float32,
            )
            prob_grad = jnp.einsum(
                "qhd,khd->hqk", grad_rows, value_all, preferred_element_type=jnp.float32
            )
            inner_total = jnp.sum(probabilities * prob_grad, axis=-1, keepdims=True)
            score_grad = (probabilities * (prob_grad - inner_total)).astype(jnp.bfloat16)
            query_grad = (
                jnp.einsum(
                    "hqk,khd->qhd", score_grad, key_everywhere, preferred_element_type=jnp.float32
                )
                * scale_factor
            )
            key_acc = (
                key_acc
                + jnp.einsum(
                    "hqk,qhd->khd", score_grad, query_rows, preferred_element_type=jnp.float32
                )
                * scale_factor
            )
            return ((key_acc, value_accumulator), query_grad)

        empty_grad = jnp.zeros((length, per_group, HD), jnp.float32)
        (key_grad, value_grad), query_blocks = lax.scan(
            backward_step, (empty_grad, empty_grad), jnp.arange(block_count, dtype=jnp.int32)
        )
        query_grad = query_blocks.reshape(length, per_group, HD)
        return jnp.stack([query_grad, key_grad, value_grad], axis=2).astype(jnp.bfloat16)

    stacked = lax.map(
        attend_backward,
        (queries_seq, keys_seq, values_seq, segments_all, head_grad_seq, log_totals),
    )
    returned_grad = lax.all_to_all(
        stacked.reshape(local_seqs, length, 1, per_group * 3 * HD),
        "seq",
        split_axis=1,
        concat_axis=2,
        tiled=True,
    )
    back_heads = returned_grad.reshape(row_count, H, 3, HD).astype(jnp.float32)
    unturned = jnp.concatenate(
        [rotate(back_heads[:, :, :2], cosine, -sine_part), back_heads[:, :, 2:]], axis=2
    )
    projected_grad = unturned.reshape(row_count, 3 * D).astype(jnp.bfloat16)
    qkv_weight_grad = outer_product(normed, projected_grad)
    qkv_bias_grad = jnp.sum(projected_grad.astype(jnp.float32), axis=0)
    normalized_gradient = times_transposed(projected_grad, w_qkv) + times_transposed(
        hidden_grad, w_in
    )
    ln_gain_grad = jnp.sum(normalized_gradient * rescaled_rows, axis=0)
    ln_bias_grad = jnp.sum(normalized_gradient, axis=0)
    standardized_gradient = normalized_gradient * norm_multiplier
    norm_back = (
        standardized_gradient
        - jnp.mean(standardized_gradient, axis=-1, keepdims=True)
        - rescaled_rows * jnp.mean(standardized_gradient * rescaled_rows, axis=-1, keepdims=True)
    ) * inv_std
    input_grad = (grad_wide + norm_back).astype(jnp.bfloat16).reshape(local_seqs, tok_count, D)
    summed = (
        lax.psum_scatter(ln_gain_grad, ("seq", "fsdp"), scatter_dimension=0, tiled=True),
        lax.psum_scatter(ln_bias_grad, ("seq", "fsdp"), scatter_dimension=0, tiled=True),
        lax.psum_scatter(qkv_weight_grad, ("seq", "fsdp"), scatter_dimension=0, tiled=True),
        lax.psum_scatter(qkv_bias_grad, ("seq", "fsdp"), scatter_dimension=0, tiled=True),
        lax.psum_scatter(out_weight_grad, ("seq", "fsdp"), scatter_dimension=0, tiled=True),
        lax.psum_scatter(out_bias_grad, ("seq", "fsdp"), scatter_dimension=0, tiled=True),
        lax.psum_scatter(fc_in_weight_grad, ("seq", "fsdp"), scatter_dimension=0, tiled=True),
        lax.psum_scatter(fc_in_bias_grad, ("seq", "fsdp"), scatter_dimension=0, tiled=True),
        lax.psum_scatter(fc_out_weight_grad, ("seq", "fsdp"), scatter_dimension=0, tiled=True),
        lax.psum_scatter(fc_out_bias_grad, ("seq", "fsdp"), scatter_dimension=0, tiled=True),
    )
    return (
        output,
        input_grad,
        summed[0],
        summed[1],
        summed[2],
        summed[3],
        summed[4],
        summed[5],
        summed[6],
        summed[7],
        summed[8],
        summed[9],
    )


def dot(left, right):
    return jnp.dot(left, right, preferred_element_type=F32)


def swap(value, axis, bit):
    return lax.ppermute(value, axis, [(i, i ^ bit) for i in range(lax.axis_size(axis))])


def shift(value, by):
    count = lax.axis_size("seq")
    return lax.ppermute(
        value, "seq", [(i, i + by) for i in range(count) if 0 <= i + by < count]
    )


class Clock:
    def __init__(self, token):
        self.token = token

    def join(self, *values):
        values, self.token = lax.optimization_barrier((values, self.token))
        return values


X, Y, NEAR, FAR = 1, 2, 4, 8
CHIPS = 16
ORDER = [0, 8, 4, 12, 1, 9, 5, 13, 2, 10, 6, 14, 3, 11, 7, 15]
SUMS = {"ax": [0, 8, 1, 9], "by": [4, 12, 6, 14], "yax": [2, 10, 3, 11], "xby": [5, 13, 7, 15]}


def place_of(chip):
    return (chip // FAR) % 2 + (chip // NEAR) % 2 * 2 + chip % 2 * 4 + (chip // Y) % 2 * 8


def cross(value, bit):
    return swap(value, "seq", bit // 4) if bit >= 4 else swap(value, "fsdp", bit * 2)


def other_core(value):
    return swap(value, "fsdp", 1)


class Gather:
    def __init__(self, shard):
        self.parts = {"s": shard}

    def jobs(self, stage):
        parts = self.parts
        if stage == "near" and "a" not in parts:
            parts["a"] = jnp.concatenate([parts["s"], parts["f"]], axis=0)
        if stage == "second":
            parts["ax"] = jnp.concatenate([parts["a"], parts["xa"]], axis=0)
            parts["by"] = jnp.concatenate([parts["b"], parts["yb"]], axis=0)
        return {
            "far": [("f", "s", FAR)],
            "near": [("b", "a", NEAR)],
            "first": [("xa", "a", X), ("yb", "b", Y)],
            "second": [("yax", "ax", Y), ("xby", "by", X)],
        }[stage]

    def pieces(self):
        return [self.parts[name] for name in SUMS]


LAY = [(0, 0), (1, 0), (0, 1), (3, 0), (2, 0), (1, 1), (2, 1), (3, 1)]


def gathered(refs, columns=slice(None), which=slice(None)):
    half = refs[0].shape[0] // 2
    return jnp.concatenate(
        [refs[array][part * half : part * half + half, columns] for array, part in LAY[which]],
        axis=0,
    )


BLOCKS = {
    "a": [0, 8],
    "xa": [1, 9],
    "b": [4, 12],
    "yb": [6, 14],
    "yax": [2, 10, 3, 11],
    "xby": [5, 13, 7, 15],
}


class Scatter:
    def __init__(self, blocks):
        self.parts = dict(zip(BLOCKS, blocks))

    def total(self, first, last, *names):
        return sum(self.parts[name][first:last].astype(F32) for name in names)

    def jobs(self, stage):
        parts = self.parts
        rows = parts["a"].shape[0]
        if stage == "second":
            for name, other in (("xa", "r_yax"), ("yb", "r_xby")):
                value = parts[name].astype(F32) + parts[other][rows:].astype(F32)
                parts[name] = value.astype(BF)
        if stage == "near":
            parts["b"] = self.total(0, rows, "b", "r_xby", "r_yb").astype(BF)
        if stage == "far":
            value = self.total(rows // 2, rows, "a", "r_yax", "r_xa", "r_b")
            parts["send"] = value.astype(BF)
        return {
            "first": [("r_yax", "yax", Y), ("r_xby", "xby", X)],
            "second": [("r_xa", "xa", X), ("r_yb", "yb", Y)],
            "near": [("r_b", "b", NEAR)],
            "far": [("r_far", "send", FAR)],
        }[stage]

    def result(self):
        rows = self.parts["a"].shape[0] // 2
        return self.total(0, rows, "a", "r_yax", "r_xa", "r_b", "r_far")


def cost(flops, bytes_accessed, transcendentals=0):
    return pl.CostEstimate(
        flops=flops, bytes_accessed=bytes_accessed, transcendentals=transcendentals
    )


SMEM = pl.BlockSpec(memory_space=pltpu.SMEM)
VMEM = pl.BlockSpec(memory_space=pltpu.VMEM)
ANY = pl.BlockSpec(memory_space=pl.ANY)


def whole(array):
    return pl.BlockSpec(array.shape, lambda *_: (0,) * len(array.shape))


def shaped(rows, columns, dtype):
    return jax.ShapeDtypeStruct((rows, columns), dtype)


def stack(refs):
    return jnp.concatenate([ref[...] for ref in refs], axis=0)


def lanes_low(rows):
    return lax.broadcasted_iota(jnp.int32, (rows, 128), 1) < HD


def cut_kernel(where_ref, qkv_ref, in_ref, out_w_ref, gain_ref, shift_ref, qb_ref, ob_ref, ib_ref, fb_ref, label_ref, *refs):
    keep1, give1, keep2, give2, in_keep, in_give, folded, columns_ref, line_ref = refs
    core = where_ref[1]
    rows = qkv_ref.shape[0]
    columns_ref[...] = jnp.zeros_like(columns_ref)
    for row, ref in enumerate((gain_ref, shift_ref, ob_ref, fb_ref)):
        columns_ref[row : row + 1, :rows] = ref[...].astype(F32)
    line_ref[...] = jnp.zeros_like(line_ref)
    line_ref[0:1, :96] = qb_ref[...].astype(F32)
    line_ref[1:2, :] = ib_ref[...].astype(F32)
    bias, units = line_ref[0:1, :], line_ref[1:2, :]
    lane = lax.broadcasted_iota(jnp.int32, (1, 128), 1)
    first = core == 0
    parts = []
    for seq in range(2):
        for part in range(2):
            labels = (label_ref[seq : seq + 1, 128 * part : 128 * part + 128] + 1).astype(F32)
            parts += [pltpu.roll(labels, HD, 1), labels]
    zero = jnp.zeros_like(bias)
    parts.append(jnp.where(first, pltpu.roll(bias, 64, 1), zero))
    parts.append(
        jnp.where(
            first,
            jnp.where(lane < 96, bias, zero),
            jnp.where(lane >= 96, pltpu.roll(bias, 96, 1), zero),
        )
    )
    parts.append(jnp.where(first, zero, pltpu.roll(bias, 32, 1)))
    parts += [pltpu.roll(units, HD, 1), units]
    for row, value in enumerate(parts):
        line_ref[row : row + 1, :] = value
    low = lanes_low(rows)
    side = jnp.where(low, columns_ref[...].T[:rows], line_ref[...]).astype(BF)
    for owner, out1, out2 in ((core, keep1, keep2), (1 - core, give1, give2)):
        for group in range(GROUPS):
            at = pl.multiple_of((owner * GROUPS + group) * 384, 128)
            b0, b1, b2 = (
                qkv_ref[:, pl.ds(at + 128 * part, 128)].astype(F32) for part in range(3)
            )
            out = out1 if group < 2 else out2
            place = (group % 2) * 384
            turned = pltpu.roll(b0, HD, 1), pltpu.roll(b2, HD, 1)
            out[:, place : place + 128] = jnp.where(low, b0, b1).astype(BF)
            out[:, place + 128 : place + 256] = jnp.where(low, *turned).astype(BF)
            out[:, place + 256 : place + 384] = jnp.where(low, b1, b2).astype(BF)
        out1[:, 768:] = side
    for owner, out in ((core, in_keep), (1 - core, in_give)):
        for block in range(CHIPS):
            at = pl.multiple_of((2 * block + owner) * 128, 128)
            out[:, block * 128 : block * 128 + 128] = in_ref[:, pl.ds(at, 128)]
    folded[:rows, :] = out_w_ref[:, : D // 2]
    folded[rows:, :] = out_w_ref[:, D // 2 :]


def cut(where, qkv_rows, in_rows, out_rows, vectors, labels):
    rows = qkv_rows.shape[0]
    widths = (896, 896, 768, 768, 2048, 2048)
    return pl.pallas_call(
        cut_kernel,
        out_shape=tuple(shaped(rows, width, BF) for width in widths)
        + (shaped(2 * rows, D // 2, BF),),
        in_specs=[SMEM] + [VMEM] * 10,
        out_specs=(VMEM,) * 7,
        scratch_shapes=[pltpu.VMEM((128, 128), F32), pltpu.VMEM((rows, 128), F32)],
        cost_estimate=cost(0, 8 * rows * 4 * D),
        name="cut",
    )(where, qkv_rows, in_rows, out_rows, *[vector.reshape(1, -1) for vector in vectors], labels)


def turn(value, cosine, forth, back):
    return (
        value * cosine
        + pltpu.roll(value, 128 - ROT // 2, 1) * forth
        + pltpu.roll(value, ROT // 2, 1) * back
    )


def marks_kernel(where_ref, a_ref, b_ref, speed_ref, forth_ref, back_ref, bias_ref, cos_ref, to_ref, from_ref, side_ref):
    seq = pl.program_id(0)
    line, core = where_ref[0] // 4, where_ref[1]

    @pl.when(seq == 0)
    def _():
        side_ref[:128, :] = a_ref[...].astype(F32)
        side_ref[128:, :] = b_ref[...].astype(F32)

    owner = jnp.where(seq < 2, core, 1 - core)
    low = lanes_low(1)
    chunks = []
    for back in range(3):
        other = line - back
        relative = jnp.where(other >= 0, other, 0) ^ line
        block = relative // 2 + 2 * (relative % 2)
        rows = side_ref[pl.ds(pl.multiple_of(block * 64 + owner * 32, 8), 8), :]
        rows = jnp.where(seq % 2 == 0, rows[:4], rows[4:])
        rows = jnp.where(other >= 0, rows, jnp.zeros_like(rows))
        chunks.append(
            [
                jnp.where(low, pltpu.roll(rows[i : i + 1], HD, 1), rows[i + 1 : i + 2])
                for i in (0, 2)
            ]
        )
    total = None
    query = lax.broadcasted_iota(jnp.int32, (128, 256), 1)
    key = lax.broadcasted_iota(jnp.int32, (128, 256), 0)
    mine = jnp.concatenate(chunks[0], axis=1)
    for back, halves in enumerate(chunks):
        for half, labels in enumerate(halves):
            column = jnp.broadcast_to(labels, (128, 128)).T
            column = jnp.concatenate([column, column], axis=1)
            same = column == mine
            if back == 0:
                same = same & (key + 128 * half <= query)
            at = back * 256 + half * 128
            bias_ref[0, at : at + 128, :] = jnp.where(same, 0.0, -1e30)
            count = jnp.sum(jnp.where(same, 1.0, 0.0), axis=0, keepdims=True)
            total = count if total is None else total + count
    for half in range(2):
        position = total[:, 128 * half : 128 * half + 128] - 1.0
        angle = jnp.broadcast_to(position, (128, 128)).T * speed_ref[...]
        here = slice(128 * half, 128 * half + 128)
        cos_ref[here, :] = jnp.cos(angle)
        sine = jnp.sin(angle)
        to_ref[here, :] = sine * forth_ref[...]
        from_ref[here, :] = sine * back_ref[...]


def marks(where, a, b):
    half = ROT // 2
    inverse = 1.0 / 10000.0 ** (jnp.arange(0, ROT, 2, dtype=F32) / ROT)
    speed = jnp.concatenate([inverse, inverse, jnp.zeros((HD - ROT,), F32)])
    speed = jnp.concatenate([speed, speed]).reshape(1, 128)
    lanes = np.arange(128) % HD
    forth = jnp.asarray(-(lanes < half).astype(np.float32)[None, :])
    back = jnp.asarray(((lanes >= half) & (lanes < ROT)).astype(np.float32)[None, :])
    side = pl.BlockSpec((128, 128), lambda i: (0, 6))
    table = pl.BlockSpec((256, 128), lambda i: (i, 0))
    return pl.pallas_call(
        marks_kernel,
        grid=(4,),
        out_shape=(jax.ShapeDtypeStruct((4, 768, 256), F32),) + (shaped(1024, 128, F32),) * 3,
        in_specs=[SMEM, side, side, whole(speed), whole(forth), whole(back)],
        out_specs=(pl.BlockSpec((1, 768, 256), lambda i: (i, 0, 0)), table, table, table),
        scratch_shapes=[pltpu.VMEM((256, 128), F32)],
        cost_estimate=cost(1024 * 128 * 100, 4 * 1024 * 1024),
        name="marks",
    )(where, a, b, speed, forth, back)


def choice_into(me, chosen_ref):
    step = 128
    column = lax.broadcasted_iota(jnp.int32, (1, D), 1)
    place = column // 64
    chip = place % 2 * FAR + (place // 2) % 2 * NEAR + (place // 4) % 2 * X + place // 8 * Y
    wanted = (chip ^ me) * 64 + column % 64

    def some(i, carry):
        here = pl.ds(pl.multiple_of(i * step, step), step)
        row = lax.broadcasted_iota(jnp.int32, (step, D), 0) + i * step
        chosen_ref[here, :] = jnp.where(row == wanted, 1.0, 0.0).astype(BF)
        return carry

    lax.fori_loop(0, D // step, some, 0)


def prepare_kernel(
    steps, where_ref, own_ref, other_ref, xhat_ref, inv_ref, chosen_ref, rows_ref
):
    step = pl.program_id(0)

    @pl.when(step == 0)
    def _():
        choice_into(where_ref[0], chosen_ref)

    @pl.when(step < steps)
    def _():
        rows_ref[...] = own_ref[...]

    @pl.when(step >= steps)
    def _():
        rows_ref[...] = other_ref[...]

    x = dot(rows_ref[...], chosen_ref[...])
    average = jnp.mean(x, axis=-1, keepdims=True)
    centered = x - average
    spread = jnp.mean(centered * centered, axis=-1, keepdims=True)
    inv_std = lax.rsqrt(spread + 1e-05)
    xhat_ref[...] = centered * inv_std
    inv_ref[...] = inv_std


def prepare(where, own, other):
    rows = own.shape[0]
    step = 256
    steps = rows // step
    return pl.pallas_call(
        partial(prepare_kernel, steps),
        grid=(2 * steps,),
        out_shape=(shaped(2 * rows, D, F32), shaped(2 * rows, 1, F32)),
        in_specs=[
            SMEM,
            pl.BlockSpec((step, D), lambda i: (jnp.minimum(i, steps - 1), 0)),
            pl.BlockSpec((step, D), lambda i: (jnp.maximum(i - steps, 0), 0)),
        ],
        out_specs=(
            pl.BlockSpec((step, D), lambda i: (i, 0)),
            pl.BlockSpec((step, 1), lambda i: (i, 0)),
        ),
        scratch_shapes=[pltpu.VMEM((D, D), BF), pltpu.VMEM((step, D), BF)],
        cost_estimate=cost(4 * rows * D * D, 16 * rows * D),
        name="prepare",
    )(where, own, other)


def emit_heads(value, tables, outs):
    pairs = [
        (q_ref, kv_ref, pair)
        for q_ref, kv_ref in zip(outs[::2], outs[1::2])
        for pair in range(q_ref.shape[1] // 128)
    ]
    for index, (q_ref, kv_ref, pair) in enumerate(pairs):
        first, q, k = index * 384, pair * 128, pair * 256
        q_ref[:, q : q + 128] = turn(value[:, first : first + 128], *tables).astype(BF)
        kv_ref[:, k : k + 128] = turn(value[:, first + 128 : first + 256], *tables).astype(BF)
        kv_ref[:, k + 128 : k + 256] = value[:, first + 256 : first + 384].astype(BF)


def project_first_kernel(where_ref, xhat_ref, cos_ref, forth_ref, back_ref, *refs):
    pieces, outs = refs[:4], refs[4:8]
    normed_ref, normed_t_ref, more_ref, units_ref, rows_ref, gain_ref, side_ref, bias_ref, two_ref = refs[8:]
    me, core = where_ref[0], where_ref[1]

    @pl.when(pl.program_id(0) == 0)
    def _():
        side_ref[...] = gathered(pieces, slice(768, 896)).astype(F32)
        across = side_ref[...].T
        two_ref[...] = across[:8]
        gain_ref[...] = across[0:1]
        rows_ref[...] = across[2:3] + across[3:4]
        low = lanes_low(1)

        def block(chip, owner):
            start = place_of(chip ^ me) * 64 + owner * 32 + 8
            return side_ref[pl.ds(pl.multiple_of(start, 8), 8), :]

        def pair(one, two):
            return jnp.where(low, pltpu.roll(one, HD, 1), two)

        for group in range(GROUPS):
            heads = []
            for head in range(2):
                chip = core * 8 + 2 * group + head
                zero, one = block(chip, 0), block(chip, 1)
                heads.append((zero[0:1], zero[1:2] + one[1:2], one[2:3]))
            out = bias_ref if group < 2 else more_ref
            for part in range(3):
                at = (group % 2) * 384 + part * 128
                out[:, at : at + 128] = pair(heads[0][part], heads[1][part])
        for chip in range(CHIPS):
            found = block(chip, core)
            units_ref[:, chip * 128 : chip * 128 + 128] = pair(found[3:4], found[4:5])

    normed = (xhat_ref[...] * two_ref[0:1, :] + two_ref[1:2, :]).astype(BF)
    normed_ref[...] = normed
    normed_t_ref[...] = normed.T
    value = dot(normed, gathered(pieces, slice(0, 768))) + bias_ref[...]
    emit_heads(value, (cos_ref[...], forth_ref[...], back_ref[...]), outs)


TWO_PAIRS = (shaped(1024, 128, BF), shaped(1024, 256, BF)) * 2
ONE_GROUP = (shaped(1024, 256, BF), shaped(1024, 512, BF))


def rows_spec(columns, step=256):
    return pl.BlockSpec((step, columns), lambda i: (i, 0))


def project_first(where, xhat, tables, pieces):
    small = (shaped(1, 768, F32), shaped(1, 2048, F32), shaped(1, D, F32), shaped(1, D, F32))
    return pl.pallas_call(
        project_first_kernel,
        grid=(4,),
        out_shape=TWO_PAIRS + (shaped(1024, D, BF), shaped(D, 1024, BF)) + small,
        in_specs=[SMEM, rows_spec(D)] + [rows_spec(128)] * 3 + [whole(piece) for piece in pieces],
        out_specs=tuple(rows_spec(shape.shape[1]) for shape in TWO_PAIRS)
        + (rows_spec(D), pl.BlockSpec((D, 256), lambda i: (0, i)))
        + tuple(whole(shape) for shape in small),
        scratch_shapes=[
            pltpu.VMEM((D, 128), F32),
            pltpu.VMEM((1, 768), F32),
            pltpu.VMEM((8, D), F32),
        ],
        cost_estimate=cost(2 * 1024 * D * 768, 12 * 1024 * D),
        name="project_first",
    )(where, xhat, *tables, *pieces)


def project_more_kernel(normed_ref, bias_ref, cos_ref, forth_ref, back_ref, *refs):
    value = dot(normed_ref[...], gathered(refs[:4], slice(512, 1280))) + bias_ref[...]
    emit_heads(value, (cos_ref[...], forth_ref[...], back_ref[...]), refs[4:])


def project_more(normed, bias, tables, pieces):
    return pl.pallas_call(
        project_more_kernel,
        grid=(4,),
        out_shape=ONE_GROUP,
        in_specs=[rows_spec(D), whole(bias)]
        + [rows_spec(128)] * 3
        + [whole(piece) for piece in pieces],
        out_specs=tuple(rows_spec(shape.shape[1]) for shape in ONE_GROUP),
        cost_estimate=cost(2 * 1024 * D * 768, 6 * 1024 * D),
        name="project_more",
    )(normed, bias, *tables, *pieces)


def head_rows_kernel(where_ref, *refs):
    keep_ref, give_ref, held_ref = refs[4:]
    me, core = where_ref[0], where_ref[1]
    for index, chip in enumerate(ORDER):
        array, part = LAY[index // 2]
        piece, at = refs[array], part * 128 + index % 2 * 64
        found = chip ^ me
        start = pl.multiple_of((((found // 8) ^ core) * 8 + found % 8) * 32, 32)
        held_ref[pl.ds(start, 32), : D // 2] = piece[at : at + 32, :]
        held_ref[pl.ds(start, 32), D // 2 :] = piece[at + 32 : at + 64, :]
    keep_ref[...] = held_ref[:256, :]
    give_ref[...] = held_ref[256:, :]


def head_rows(where, pieces):
    return pl.pallas_call(
        head_rows_kernel,
        out_shape=(shaped(256, D, BF),) * 2,
        grid=(1,),
        in_specs=[SMEM] + [pl.BlockSpec((256, D // 2), lambda i: (0, 0))] * 4,
        out_specs=(pl.BlockSpec((256, D), lambda i: (0, 0)),) * 2,
        scratch_shapes=[pltpu.VMEM((512, D), BF)],
        cost_estimate=cost(0, 4 * 512 * D),
        name="head_rows",
    )(where, *pieces)


def context_grad_kernel(
    where_ref, own_ref, other_ref, keep_ref, more_ref, grad_ref, heads_ref, rows_ref
):
    core = where_ref[1]
    step = pl.program_id(0)

    @pl.when(step == 0)
    def _():
        for chip in range(8):
            rows = slice(chip * 32, chip * 32 + 32)
            heads_ref[pl.ds(pl.multiple_of(chip * 64 + core * 32, 32), 32), :] = keep_ref[rows, :]
            at = pl.multiple_of(chip * 64 + (1 - core) * 32, 32)
            heads_ref[pl.ds(at, 32), :] = more_ref[rows, :]

    @pl.when(step < 2)
    def _():
        rows_ref[...] = own_ref[...]

    @pl.when(step >= 2)
    def _():
        rows_ref[...] = other_ref[...]

    grad_ref[...] = times_transposed(rows_ref[...], heads_ref[...]).astype(BF)


def context_gradient(where, own, other, keep, more):
    return pl.pallas_call(
        context_grad_kernel,
        grid=(4,),
        out_shape=(shaped(1024, D // 2, BF), shaped(D // 2, D, BF)),
        in_specs=[
            SMEM,
            pl.BlockSpec((256, D), lambda i: (jnp.minimum(i, 1), 0)),
            pl.BlockSpec((256, D), lambda i: (jnp.maximum(i - 2, 0), 0)),
            whole(keep),
            whole(more),
        ],
        out_specs=(rows_spec(D // 2), pl.BlockSpec((D // 2, D), lambda i: (0, 0))),
        scratch_shapes=[pltpu.VMEM((256, D), BF)],
        cost_estimate=cost(1024 * D * D, 6 * 1024 * D),
        name="context_grad",
    )(where, own, other, keep, more)


def attend_kernel(q_ref, do_ref, bias_ref, *refs):
    kv_refs, o_ref, dq_ref, dkv_refs = refs[:3], refs[3], refs[4], refs[5:8]
    weight_ref, probs_ref, grad_ref = refs[8:]
    rows = q_ref.shape[0]
    scaled = q_ref[...] * 0.125
    given = do_ref[...]
    given_t = given.T.astype(F32)
    low = lanes_low(rows)
    zero = jnp.zeros_like(given)

    def heads(value):
        return jnp.concatenate([jnp.where(low, value, zero), jnp.where(low, zero, value)], axis=0)

    queries, grads = heads(scaled), heads(given)
    spans = [slice(chunk * rows, chunk * rows + rows) for chunk in range(3)]
    top = None
    for here, ref in zip(spans, kv_refs):
        bias = bias_ref[0, here, :]
        scores = times_transposed(ref[:, :128], queries) + jnp.concatenate([bias, bias], axis=1)
        weight_ref[here, :] = scores
        most = jnp.max(scores, axis=0, keepdims=True)
        top = most if top is None else jnp.maximum(top, most)
    total = jnp.zeros_like(top)
    for here in spans:
        unscaled = jnp.exp(weight_ref[here, :] - top)
        weight_ref[here, :] = unscaled
        total = total + jnp.sum(unscaled, axis=0, keepdims=True)
    inverse = 1.0 / total
    for here in spans:
        probs = weight_ref[here, :] * inverse
        weight_ref[here, :] = probs
        probs_ref[here, :] = probs.astype(BF)

    def both_heads(across, right_ref):
        return jnp.concatenate(
            [dot(across[:HD], right_ref[:, :rows]), dot(across[HD:], right_ref[:, rows:])], axis=0
        )

    values_t = jnp.concatenate([ref[:, 128:] for ref in kv_refs], axis=0).T
    keys_t = jnp.concatenate([ref[:, :128] for ref in kv_refs], axis=0).T
    out_t = both_heads(values_t, probs_ref)
    product = out_t * given_t
    inner = jnp.concatenate(
        [
            jnp.sum(product[:HD], axis=0, keepdims=True),
            jnp.sum(product[HD:], axis=0, keepdims=True),
        ],
        axis=1,
    )
    for here, ref in zip(spans, kv_refs):
        prob_grad = times_transposed(ref[:, 128:], grads)
        grad_ref[here, :] = (weight_ref[here, :] * (prob_grad - inner)).astype(BF)
    dq_t = both_heads(keys_t, grad_ref)
    o_ref[...] = out_t.T.astype(BF)
    dq_ref[...] = (dq_t.T * 0.125).astype(BF)
    for here, ref in zip(spans, dkv_refs):
        ref[:, :128] = dot(grad_ref[here, :], queries).astype(ref.dtype)
        ref[:, 128:] = dot(probs_ref[here, :], grads).astype(ref.dtype)


def attend(first, query, grad, bias, kvs):
    pairs = query.shape[1] // 128
    narrow = pl.BlockSpec((256, 128), lambda b, p: (b, p))
    wide = pl.BlockSpec((256, 256), lambda b, p: (b, p))
    return pl.pallas_call(
        attend_kernel,
        grid=(4, pairs),
        out_shape=(shaped(1024, 128 * pairs, BF),) * 2
        + (shaped(1024, 256 * pairs, F32),)
        + (shaped(1024, 256 * pairs, BF),) * 2,
        in_specs=[
            narrow,
            pl.BlockSpec((256, 128), lambda b, p: (b, first + p)),
            pl.BlockSpec((1, 768, 256), lambda b, p: (b, 0, 0)),
        ]
        + [wide] * 3,
        out_specs=(narrow, narrow) + (wide,) * 3,
        scratch_shapes=[pltpu.VMEM((768, 512), dtype) for dtype in (F32, BF, BF)],
        cost_estimate=cost(
            pairs * 24 * 4 * 256 * 768 * 128, pairs * 9 * 1024 * 1024, pairs * 8 * 256 * 768
        ),
        name="attend",
    )(query, grad, bias, *kvs)


def unturn_kernel(groups, cos_ref, forth_ref, back_ref, *refs):
    cosine, forth, back = cos_ref[...], -forth_ref[...], -back_ref[...]
    out_ref, sum_ref = refs[-2:]
    first = 0
    for group in range(groups):
        dq_ref, own_ref, more_ref = refs[3 * group : 3 * group + 3]
        for pair in range(dq_ref.shape[1] // 128):
            here = slice(pair * 256, pair * 256 + 256)
            kv = (own_ref[:, here] + more_ref[:, here].astype(F32)).astype(BF)
            key = kv[:, :128].astype(F32)
            query = dq_ref[:, pair * 128 : pair * 128 + 128].astype(F32)
            out_ref[:, first : first + 128] = turn(query, cosine, forth, back).astype(BF)
            out_ref[:, first + 128 : first + 256] = turn(key, cosine, forth, back).astype(BF)
            out_ref[:, first + 256 : first + 384] = kv[:, 128:]
            first += 384

    @pl.when(pl.program_id(0) == 0)
    def _():
        sum_ref[...] = jnp.zeros_like(sum_ref)

    sum_ref[...] += jnp.sum(out_ref[...].astype(F32), axis=0, keepdims=True)


def unturn(tables, triples):
    rows = triples[0][0].shape[0]
    step = 256
    width = 3 * sum(dq.shape[1] for dq, _, _ in triples)

    def spec(columns):
        return pl.BlockSpec((step, columns), lambda i: (i, 0))

    specs, arrays = [], []
    for dq, own, more in triples:
        specs += [spec(dq.shape[1]), spec(own.shape[1]), spec(more.shape[1])]
        arrays += [dq, own, more]
    return pl.pallas_call(
        partial(unturn_kernel, len(triples)),
        grid=(rows // step,),
        out_shape=(
            jax.ShapeDtypeStruct((rows, width), BF),
            jax.ShapeDtypeStruct((1, width), F32),
        ),
        in_specs=[spec(128)] * 3 + specs,
        out_specs=(spec(width), pl.BlockSpec((1, width), lambda i: (0, 0))),
        cost_estimate=cost(rows * width * 10, rows * width * 8),
        name="unturn",
    )(*tables, *arrays)


ROOT_HALF = math.sqrt(0.5)
DENSITY = 1.0 / math.sqrt(2.0 * math.pi)


def gelu_and_slope(value):
    share = 0.5 + 0.5 * lax.erf(value * ROOT_HALF)
    return value * share, share + value * (DENSITY * jnp.exp(-0.5 * value * value))


def hidden_kernel(normed_ref, bias_ref, *refs):
    act_ref, act_t_ref, slope_ref, value_ref = refs[-4:]
    rows = 128
    value_ref[...] = dot(normed_ref[...], gathered(refs[:4])) + bias_ref[...]

    def some(i, carry):
        here = pl.ds(pl.multiple_of(i * rows, rows), rows)
        act, slope = gelu_and_slope(value_ref[here, :])
        act = act.astype(BF)
        act_ref[here, :] = act
        act_t_ref[:, here] = act.T
        slope_ref[here, :] = slope
        return carry

    lax.fori_loop(0, normed_ref.shape[0] // rows, some, 0, unroll=True)


def hidden(normed, pieces, bias):
    rows, width = normed.shape[0], bias.shape[1]
    step = 256
    column = pl.BlockSpec((rows, step), lambda j: (0, j))
    return pl.pallas_call(
        hidden_kernel,
        grid=(width // step,),
        out_shape=(shaped(rows, width, BF), shaped(width, rows, BF), shaped(rows, width, F32)),
        in_specs=[whole(normed), pl.BlockSpec((1, step), lambda j: (0, j))]
        + [pl.BlockSpec((piece.shape[0], step), lambda j: (0, j)) for piece in pieces],
        out_specs=(column, pl.BlockSpec((step, rows), lambda j: (j, 0)), column),
        scratch_shapes=[pltpu.VMEM((rows, step), F32)],
        cost_estimate=cost(2 * rows * D * width + 50 * rows * width, 9 * rows * width),
        name="hidden",
    )(normed, bias, *pieces)


def fetch_units(me, pieces, w_ref, sem):
    copies = []
    for index, chip in enumerate(ORDER):
        first = pl.multiple_of((me ^ chip) * 128, 128)
        array, part = LAY[index // 2]
        copies.append(
            pltpu.make_async_copy(
                pieces[array].at[pl.ds(part * 256 + index % 2 * 128, 128), :],
                w_ref.at[pl.ds(first, 128), :],
                sem,
            )
        )
    for copy in copies:
        copy.start()
    return copies


def unit_back_kernel(where_ref, own_ref, other_ref, slope_ref, *refs):
    hg_ref, sum_ref, w_ref, sem = refs[4:]
    j = pl.program_id(0)
    step = hg_ref.shape[1]

    @pl.when(j == 0)
    def _():
        for copy in fetch_units(where_ref[0], refs[:4], w_ref, sem):
            copy.wait()

    w = w_ref[pl.ds(pl.multiple_of(j * step, step), step), :]
    total = None
    rows = own_ref.shape[0]
    for half, g_ref in enumerate((own_ref, other_ref)):
        here = slice(half * rows, half * rows + rows)
        grad = (times_transposed(g_ref[...], w) * slope_ref[here, :]).astype(BF)
        hg_ref[here, :] = grad
        part = jnp.sum(grad.astype(F32), axis=0, keepdims=True)
        total = part if total is None else total + part
    sum_ref[...] = total


def unit_back(where, own, other, slope, pieces):
    rows, width = slope.shape
    step = 512
    column = pl.BlockSpec((rows, step), lambda j: (0, j))
    return pl.pallas_call(
        unit_back_kernel,
        grid=(width // step,),
        out_shape=(shaped(rows, width, BF), shaped(1, width, F32)),
        in_specs=[SMEM, whole(own), whole(other), column] + [ANY] * 4,
        out_specs=(column, pl.BlockSpec((1, step), lambda j: (0, j))),
        scratch_shapes=[pltpu.VMEM((width, D), BF), pltpu.SemaphoreType.DMA],
        cost_estimate=cost(2 * rows * D * width, 8 * rows * width),
        name="unit_back",
    )(where, own, other, slope, *pieces)


def unit_out_kernel(where_ref, act_ref, heads_ref, *refs):
    contexts, pieces = refs[:3], refs[3:7]
    mine_ref, theirs_ref, w_ref, total_ref, sem = refs[7:]
    step = pl.program_id(0)

    @pl.when(step == 0)
    def _():
        for copy in fetch_units(where_ref[0], pieces, w_ref, sem):
            copy.wait()

    context = jnp.concatenate([ref[...] for ref in contexts], axis=1)
    total_ref[...] = dot(act_ref[...], w_ref[...]) + dot(context, heads_ref[...])

    @pl.when(step < 2)
    def _():
        mine_ref[...] = total_ref[...]

    @pl.when(step >= 2)
    def _():
        theirs_ref[...] = total_ref[...]


def unit_out(where, act, heads, contexts, pieces):
    rows, width = act.shape
    return pl.pallas_call(
        unit_out_kernel,
        grid=(4,),
        out_shape=(shaped(rows // 2, D, F32),) * 2,
        in_specs=[SMEM, rows_spec(width), whole(heads)]
        + [rows_spec(context.shape[1]) for context in contexts]
        + [ANY] * 4,
        out_specs=(
            pl.BlockSpec((256, D), lambda i: (jnp.minimum(i, 1), 0)),
            pl.BlockSpec((256, D), lambda i: (jnp.maximum(i - 2, 0), 0)),
        ),
        scratch_shapes=[
            pltpu.VMEM((width, D), BF),
            pltpu.VMEM((256, D), F32),
            pltpu.SemaphoreType.DMA,
        ],
        cost_estimate=cost(3 * rows * D * width, 6 * rows * width),
        name="unit_out",
    )(where, act, heads, *contexts, *pieces)


def row_grads_kernel(steps, where_ref, left_ref, right_ref, *refs):
    out_refs = refs[:6] if len(refs) == 6 else refs[2:8]
    spots = [[place_of(chip) for chip in chips] for chips in BLOCKS.values()]

    @pl.when(pl.program_id(0) < steps)
    def _():
        value = dot(left_ref[...], right_ref[...]).astype(BF)
        for places, ref in zip(spots, out_refs):
            for at, place in enumerate(places):
                ref[at * 64 : at * 64 + 64, :] = value[place * 64 : place * 64 + 64]

    if len(refs) > 6:
        keep_ref, more_ref, held_ref = refs[0], refs[1], refs[-1]
        me, core = where_ref[0], where_ref[1]

        @pl.when(pl.program_id(0) >= steps)
        def _():
            held_ref[:256, :] = keep_ref[...]
            held_ref[256:, :] = more_ref[...]
            for chips, ref in zip(BLOCKS.values(), out_refs):
                for at, chip in enumerate(chips):
                    found = chip ^ me
                    start = (((found // 8) ^ core) * 8 + found % 8) * 32
                    rows = held_ref[pl.ds(pl.multiple_of(start, 32), 32), :]
                    ref[at * 64 : at * 64 + 32, :] = rows[:, : D // 2]
                    ref[at * 64 + 32 : at * 64 + 64, :] = rows[:, D // 2 :]


def row_grads(where, left, right, more=()):
    rows, tokens = left.shape
    step = 512
    steps = right.shape[1] // step
    columns = right.shape[1] + (D // 2 if more else 0)
    heights = [64 * len(chips) for chips in BLOCKS.values()]
    return pl.pallas_call(
        partial(row_grads_kernel, steps),
        grid=(columns // step,),
        out_shape=tuple(shaped(height, columns, BF) for height in heights),
        in_specs=[
            SMEM,
            whole(left),
            pl.BlockSpec((tokens, step), lambda j: (0, jnp.minimum(j, steps - 1))),
        ]
        + [whole(rows) for rows in more],
        out_specs=tuple(pl.BlockSpec((height, step), lambda j: (0, j)) for height in heights),
        scratch_shapes=[pltpu.VMEM((512, D), BF)] if more else [],
        cost_estimate=cost(2 * rows * tokens * columns, 2 * (rows * tokens + rows * columns)),
        name="row_grads",
    )(where, left, right, *more)


def unit_grads_kernel(order_ref, *refs):
    lefts, own_ref, other_ref, out_refs = refs[:4], refs[4], refs[5], refs[6:]
    left = stack(lefts)
    tokens = own_ref.shape[0]
    a, xa, b, yb, yax, xby = out_refs
    value = dot(left[:, :tokens], own_ref[...]) + dot(left[:, tokens:], other_ref[...])
    value = value.astype(BF)
    for piece, outs in enumerate(((a, xa), (b, yb), (yax,), (xby,))):

        @pl.when(pl.program_id(0) == piece)
        def _(outs=outs):
            rows = 512 // len(outs)
            for at, ref in enumerate(outs):
                ref[...] = value[at * rows : at * rows + rows]


def unit_grads(me, left, own, other):
    tokens = left.shape[1]
    order = jnp.asarray(np.array(sum(SUMS.values(), []), np.int32)) ^ me

    def block(place):
        return pl.BlockSpec((128, tokens), lambda k, order: (order[4 * k + place], 0))

    return pl.pallas_call(
        unit_grads_kernel,
        out_shape=tuple(shaped(128 * len(chips), D, BF) for chips in BLOCKS.values()),
        grid_spec=pltpu.PrefetchScalarGridSpec(
            num_scalar_prefetch=1,
            grid=(4,),
            in_specs=[block(place) for place in range(4)] + [whole(own), whole(other)],
            out_specs=tuple(
                pl.BlockSpec((128 * len(chips), D), lambda k, order: (0, 0))
                for chips in BLOCKS.values()
            ),
        ),
        cost_estimate=cost(2 * tokens * D * 2048, 4 * 2048 * D),
        name="unit_grads",
    )(order, left, left, left, left, own, other)


def out_grad_kernel(where_ref, own_ref, other_ref, *refs):
    contexts, keep_ref, give_ref, across_ref = refs[:3], refs[3], refs[4], refs[5]
    first = where_ref[1] == 0
    tokens = own_ref.shape[0]
    group = pl.program_id(0)

    @pl.when(group == 0)
    def _():
        lane = 0
        for ref in contexts:
            across_ref[lane : lane + ref.shape[1], :] = ref[...].T
            lane += ref.shape[1]

    across = across_ref[pl.ds(pl.multiple_of(group * 128, 128), 128), :]
    value = dot(across[:, :tokens], own_ref[...]) + dot(across[:, tokens:], other_ref[...])
    value = value.astype(BF)
    for head in range(2):
        zero, one = value[head * 64 : head * 64 + 32], value[head * 64 + 32 : head * 64 + 64]
        rows = slice(head * 32, head * 32 + 32)
        keep_ref[rows, :] = jnp.where(first, zero, one)
        give_ref[rows, :] = jnp.where(first, one, zero)


def out_grad(where, own, other, contexts):
    block = pl.BlockSpec((64, D), lambda i: (i, 0))
    return pl.pallas_call(
        out_grad_kernel,
        grid=(4,),
        out_shape=(shaped(256, D, BF),) * 2,
        in_specs=[SMEM, whole(own), whole(other)] + [whole(context) for context in contexts],
        out_specs=(block, block),
        scratch_shapes=[pltpu.VMEM((D // 2, 1024), BF)],
        cost_estimate=cost(1024 * D * D, 6 * 1024 * D),
        name="out_grad",
    )(where, own, other, *contexts)


def norm_grad_kernel(spans, left_ref, *refs):
    count = 4 * len(spans)
    mine_ref, theirs_ref, total_ref = refs[-3:]
    earlier = refs[count:-3]
    step = pl.program_id(0)
    first = 0
    lefts = []
    for start, end in spans:
        lefts.append(left_ref[:, first : first + end - start])
        first += end - start
    for pair in range(4):
        total = None
        for line, (left, span) in enumerate(zip(lefts, spans)):
            right = gathered(
                refs[4 * line : 4 * line + 4], slice(*span), slice(2 * pair, 2 * pair + 2)
            )
            part = times_transposed(left, right)
            total = part if total is None else total + part
        total_ref[:, 256 * pair : 256 * pair + 256] = total

    for half, out_ref in enumerate((mine_ref, theirs_ref)):

        @pl.when(step // 2 == half)
        def _(half=half, out_ref=out_ref):
            if earlier:
                out_ref[...] = total_ref[...] + earlier[half][...]
            else:
                out_ref[...] = total_ref[...]


def norm_grad(left, lines, spans, earlier=()):
    rows = left.shape[0]
    flat = [piece for line in lines for piece in line]
    halves = (
        pl.BlockSpec((256, D), lambda i: (jnp.minimum(i, 1), 0)),
        pl.BlockSpec((256, D), lambda i: (jnp.maximum(i - 2, 0), 0)),
    )
    return pl.pallas_call(
        partial(norm_grad_kernel, spans),
        grid=(4,),
        out_shape=(shaped(rows // 2, D, F32),) * 2,
        in_specs=[rows_spec(left.shape[1])]
        + [whole(piece) for piece in flat]
        + list(halves[: len(earlier)]),
        out_specs=halves,
        scratch_shapes=[pltpu.VMEM((256, D), F32)],
        cost_estimate=cost(2 * rows * D * left.shape[1], 12 * rows * D),
        name="norm_grad",
    )(left, *flat, *earlier)


def norm_back_kernel(
    where_ref, part_ref, more_ref, xhat_ref, inv_ref, gain_ref, g_ref, out_ref, sum_ref, chosen_ref
):
    @pl.when(pl.program_id(0) == 0)
    def _():
        choice_into(where_ref[0], chosen_ref)
        sum_ref[...] = jnp.zeros_like(sum_ref)

    grad = part_ref[...] + more_ref[...]
    xhat = xhat_ref[...]
    scaled = grad * gain_ref[...]
    value = (
        scaled
        - jnp.mean(scaled, axis=-1, keepdims=True)
        - xhat * jnp.mean(scaled * xhat, axis=-1, keepdims=True)
    ) * inv_ref[...]
    value = times_transposed(value.astype(BF), chosen_ref[...])
    out_ref[...] = (g_ref[...].astype(F32) + value).astype(BF)
    sum_ref[0:1, :] += jnp.sum(grad * xhat, axis=0, keepdims=True)
    sum_ref[1:2, :] += jnp.sum(grad, axis=0, keepdims=True)


def norm_back(where, part, more, xhat, inv_std, gain, grad):
    rows = grad.shape[0]
    one = pl.BlockSpec((1, D), lambda i: (0, 0))
    return pl.pallas_call(
        norm_back_kernel,
        grid=(rows // 256,),
        out_shape=(shaped(rows, D, BF), shaped(8, D, F32)),
        in_specs=[SMEM] + [rows_spec(D)] * 3 + [rows_spec(1), one, rows_spec(D)],
        out_specs=(rows_spec(D), pl.BlockSpec((8, D), lambda i: (0, 0))),
        scratch_shapes=[pltpu.VMEM((D, D), BF)],
        cost_estimate=cost(4 * rows * D * D, 16 * rows * D),
        name="norm_back",
    )(where, part, more, xhat, inv_std, gain, grad)


def paste_in_kernel(where_ref, mine_ref, other_ref, out_ref):
    core = where_ref[1]
    for owner, ref in ((core, mine_ref), (1 - core, other_ref)):
        for block in range(CHIPS):
            at = pl.multiple_of((2 * block + owner) * 128, 128)
            out_ref[:, pl.ds(at, 128)] = ref[:, block * 128 : block * 128 + 128]


def paste_qkv_kernel(where_ref, mine_ref, other_ref, out_ref):
    core = where_ref[1]
    low = lanes_low(mine_ref.shape[0])
    for owner, ref in ((core, mine_ref), (1 - core, other_ref)):
        for group in range(GROUPS):
            q, k, v = (
                ref[:, group * 384 + part * 128 : group * 384 + part * 128 + 128]
                for part in range(3)
            )
            turned = pltpu.roll(k, HD, 1)
            blocks = (jnp.where(low, q, turned), jnp.where(low, v, q), jnp.where(low, turned, v))
            for part, value in enumerate(blocks):
                at = (owner * GROUPS + group) * 384 + part * 128
                out_ref[:, pl.ds(pl.multiple_of(at, 128), 128)] = value


def paste(kernel, where, mine, other):
    return pl.pallas_call(
        kernel,
        out_shape=shaped(mine.shape[0], 2 * mine.shape[1], F32),
        in_specs=[SMEM, VMEM, VMEM],
        out_specs=VMEM,
        cost_estimate=cost(0, 16 * mine.shape[0] * mine.shape[1]),
        name="paste",
    )(where, mine, other)


def local_fast(
    hidden_in,
    document_labels,
    cotangent,
    ln_gain,
    ln_bias,
    qkv_weight,
    qkv_bias,
    out_weight,
    out_bias,
    fc_in_weight,
    fc_in_bias,
    fc_out_weight,
    fc_out_bias,
):
    local_seqs, tok_count = hidden_in.shape[:2]
    row_count = local_seqs * tok_count
    d_rows = qkv_weight.shape[0]
    f_rows = fc_out_weight.shape[0]
    units = fc_in_weight.shape[1] // 2
    pair = 2
    core = lax.axis_index("fsdp") % 2
    me = lax.axis_index("seq") * 4 + lax.axis_index("fsdp") // 2
    clock = Clock(jnp.stack([me, core]).astype(jnp.int32))
    box = {}

    waiting, deferred = [], []

    def slot(jobs, work=None, *inputs, chain=None, late=(), then=None):
        nonlocal waiting
        jobs, late = list(jobs), list(late)
        chains = chain if isinstance(chain, list) else [chain] if chain is not None else []
        gated, given, more = clock.join(
            tuple(job[2] for job in jobs + late), inputs, tuple(tuple(link[2]) for link in chains)
        )
        values = [job[3](value) for job, value in zip(jobs + late, gated)]
        made = work(*given) if work is not None else ()
        after = []
        for (name, follow, _), inputs in zip(chains, more):
            for job, value in list(zip(jobs, values)) + waiting:
                if job[1] == name:
                    after.append(follow(value, *inputs))
        for job, value in deferred:
            late.append(job)
            values.append(value)
        deferred.clear()
        if then is not None:
            started = then(made)
            late = late + started
            values = values + [job[3](job[2]) for job in started]
        ended, values, older = waiting, values[: len(jobs)], values[len(jobs) :]
        found = values + [value for _, value in ended]
        found, made, after = clock.join(tuple(found), made, after)
        for job, value in zip(jobs + [job for job, _ in ended], found):
            job[0][job[1]] = value
        waiting = list(zip(late, older))
        if chain is None:
            return made
        return made, after if isinstance(chain, list) else after[0]

    def moves(line, stage):
        return [
            (line.parts, name, line.parts[source], partial(cross, bit=bit))
            for name, source, bit in line.jobs(stage)
        ]

    def core_move(name, value):
        return (box, name, value, other_core)

    def pick(halves):
        first = core == 0
        return jnp.where(first, halves[0], halves[1]), jnp.where(first, halves[1], halves[0])

    def joined(mine, other):
        first = core == 0
        return jnp.concatenate(
            [jnp.where(first, mine, other), jnp.where(first, other, mine)], axis=0
        )

    x_own = hidden_in.reshape(row_count, D)
    g_own = cotangent.reshape(row_count, D)
    vectors = (ln_gain, ln_bias, qkv_bias, out_bias, fc_in_bias, fc_out_bias)
    keep1, give1, keep2, give2, in_keep, in_give, folded = cut(
        clock.token, qkv_weight, fc_in_weight, out_weight, vectors, document_labels
    )
    slot([core_move("give1", give1)])
    line_a = Gather(joined(keep1, box["give1"]))
    slot(moves(line_a, "far") + [core_move("x", x_own), core_move("give2", give2)])
    line_b = Gather(jnp.concatenate([folded, joined(keep2, box["give2"])], axis=1))
    line_d = Gather(fc_out_weight)
    slot(moves(line_a, "near") + moves(line_b, "far") + [core_move("in", in_give), core_move("g", g_own)])
    g_more = box["g"]
    slot(moves(line_a, "first") + moves(line_b, "near"))
    line_c = Gather(joined(in_keep, box["in"]))
    (xhat, inv_std), grad_sum, (bias, *tables) = slot(
        moves(line_a, "second") + moves(line_c, "far"),
        lambda own, other, g, a, b: (
            prepare(clock.token, own, other),
            jnp.sum(g.astype(F32), axis=0),
            marks(clock.token, a, b),
        ),
        x_own,
        box["x"],
        g_own,
        line_a.parts["a"],
        line_a.parts["b"],
    )
    a_pieces = line_a.pieces()
    made = slot(
        moves(line_b, "first") + moves(line_c, "near") + moves(line_d, "far"),
        lambda xhat, tables, pieces: project_first(clock.token, xhat, tables, pieces),
        xhat,
        tables,
        a_pieces,
    )
    queries, kvs = [made[0], made[2]], [[made[1]], [made[3]]]
    normed, normed_t, b_more, b_in, b_rows, gain = made[4:]
    moved, results, backs = {}, {}, {}

    def up(group, hop):
        return (moved, (group, hop), kvs[group][hop], partial(shift, by=1))

    def landed(*found):
        for group, hop in found:
            kvs[group].append(moved[group, hop])

    def down(group, hop):
        value = results[group][4]
        if hop == 1:
            value = (results[group][3].astype(F32) + backs[group, 0].astype(F32)).astype(BF)
        return (backs, (group, hop), value, partial(shift, by=-1))

    def attention(*groups):
        def work(*given):
            return [attend(group, *args) for group, args in zip(groups, given)]

        return work, *[
            (queries[group], context_grad, bias, tuple(kvs[group])) for group in groups
        ]

    def attended(groups, found):
        for group, result in zip(groups, found):
            results[group] = result

    line_d.parts["a"] = slot(
        moves(line_b, "second") + [up(0, 0)],
        lambda own, other: jnp.concatenate([own, other], axis=0),
        line_d.parts["s"],
        line_d.parts["f"],
        late=[up(1, 0)],
    )
    landed((0, 0))
    b_pieces = line_b.pieces()
    made, (out_keep, out_give) = slot(
        moves(line_c, "first") + [up(0, 1)],
        lambda normed, bias, tables, pieces: (
            project_more(normed, bias, tables, pieces),
            head_rows(clock.token, pieces),
        ),
        normed,
        b_more,
        tables,
        b_pieces,
    )
    landed((0, 1), (1, 0))
    queries.append(made[0])
    kvs.append([made[1]])

    def first_attention(out_more, g_own, g_more, out_keep, query, bias, kvs):
        grad, heads = context_gradient(clock.token, g_own, g_more, out_keep, out_more)
        return grad, heads, attend(0, query, grad, bias, kvs)

    _, (context_grad, out_heads, found) = slot(
        moves(line_c, "second") + moves(line_d, "near") + [up(1, 1), core_move("out", out_give)],
        chain=(
            "out",
            first_attention,
            (g_own, g_more, out_keep, queries[0], bias, tuple(kvs[0])),
        ),
    )
    results[0] = found
    landed((1, 1))
    c_pieces = line_c.pieces()
    act, act_t, slope = slot(
        moves(line_d, "first") + [up(2, 0), down(0, 0)],
        lambda normed, b_in, pieces: hidden(normed, pieces, b_in),
        normed,
        b_in,
        c_pieces,
    )
    landed((2, 0))
    work, *given = attention(1)

    def with_units(given, act_t, own, other):
        found = work(given)
        return found, unit_grads(clock.token[0], act_t, own, other), shift(found[0][4], -1)

    found, fc_parts, backs[1, 0] = slot(
        moves(line_d, "second") + [up(2, 1)],
        with_units,
        *given,
        act_t,
        g_own,
        g_more,
        late=[down(0, 1)],
    )
    attended([1], found)
    landed((2, 1))
    d_pieces = line_d.pieces()
    sum_fc = Scatter(fc_parts)
    work2, *given = attention(2)

    def last_attention(given, earlier, own, other):
        found = work2(given)
        contexts = earlier + [found[0][0]]
        return found, contexts, out_grad(clock.token, own, other, contexts)

    found, contexts, (out_keep, out_give) = slot(
        moves(sum_fc, "first") + [down(1, 1)],
        last_attention,
        *given,
        [results[group][0] for group in range(2)],
        g_own,
        g_more,
        then=lambda made: [(backs, (2, 0), made[0][0][4], partial(shift, by=-1))],
    )
    attended([2], found)

    def units_back(out_more, out_keep, normed_t, own, other, slope, pieces):
        hidden_grad, hidden_sum = unit_back(clock.token, own, other, slope, pieces)
        parts = row_grads(clock.token, normed_t, hidden_grad, (out_keep, out_more))
        box["unit_sum"] = hidden_sum
        return hidden_grad, parts

    def near_now(last, own, earlier):
        rows = own.shape[0]
        total = own.astype(F32) + earlier[:rows].astype(F32) + last.astype(F32)
        return cross(total.astype(BF), NEAR)

    def near_after(last, own, earlier):
        last, total = lax.optimization_barrier((last, box["unit_sum"]))
        return near_now(last, own, earlier), total

    _, ((hidden_grad, in_parts), (sum_fc.parts["r_b"], hidden_sum)) = slot(
        moves(sum_fc, "second") + [core_move("out_grad", out_give)],
        chain=[
            ("out_grad", units_back, (out_keep, normed_t, g_own, g_more, slope, d_pieces)),
            ("r_yb", near_after, (sum_fc.parts["b"], sum_fc.parts["r_xby"])),
        ],
    )
    sum_in = Scatter(in_parts)
    (out_mine, out_theirs), earlier = slot(
        moves(sum_in, "first") + [down(2, 1)],
        lambda act, heads, contexts, pieces, grad, c_pieces: (
            unit_out(clock.token, act, heads, contexts, pieces),
            norm_grad(grad, [c_pieces], [(0, units)]),
        ),
        act,
        out_heads,
        contexts,
        d_pieces,
        hidden_grad,
        c_pieces,
    )

    def last_grads(normed_t, tables, triples):
        projected_grad, total = unturn(tables, triples)
        return projected_grad, total, row_grads(clock.token, normed_t, projected_grad)

    def near_soon(*terms):
        deferred.append(((sum_in.parts, "r_b"), near_now(*terms)))
        return ()

    def far_soon(last, *terms):
        rows = last.shape[0]
        total = sum(term[rows // 2 : rows].astype(F32) for term in terms + (last,))
        deferred.append(((sum_in.parts, "r_far"), cross(total.astype(BF), FAR)))
        return ()

    (projected_grad, qkv_bias_sum, parts), _ = slot(
        moves(sum_in, "second") + moves(sum_fc, "far") + [core_move("out_side", out_theirs)],
        last_grads,
        normed_t,
        tables,
        [(results[group][1], results[group][2], backs[group, 1]) for group in range(3)],
        chain=[("r_yb", near_soon, (sum_in.parts["b"], sum_in.parts["r_xby"]))],
    )
    sum_qkv = Scatter(parts)
    (norm_mine, norm_theirs), _ = slot(
        moves(sum_qkv, "first"),
        lambda projected_grad, earlier, *lines: norm_grad(
            projected_grad, lines, [(0, 768), (512, 1280)], earlier
        ),
        projected_grad,
        earlier,
        a_pieces,
        b_pieces,
        chain=[("r_b", far_soon, [sum_in.parts[name] for name in ("a", "r_yax", "r_xa")])],
    )

    def finish_output(x_own, out_mine, out_more, b_rows):
        order = jnp.asarray(np.array(ORDER, np.int32)) ^ me
        spots = place_of(jnp.arange(CHIPS, dtype=jnp.int32) ^ me)
        b_rows = b_rows.reshape(CHIPS, 2 * d_rows)[spots].reshape(1, D)
        return (x_own.astype(F32) + out_mine + out_more + b_rows).astype(BF)

    def small_rows(norm_sums, qkv_bias_sum, hidden_sum, grad_sum):
        spots = place_of(jnp.arange(CHIPS, dtype=jnp.int32) ^ me)
        norm_sums = norm_sums[:2].reshape(2, CHIPS, 2, d_rows)[:, spots].reshape(2, D)
        mine = (jnp.arange(2) == core)[:, None]
        qkv_full = (
            jnp.where(mine, qkv_bias_sum, 0.0)
            .reshape(2, GROUPS, 3, pair, HD)
            .transpose(0, 1, 3, 2, 4)
            .reshape(3 * D)
        )
        in_full = jnp.where(mine[None], hidden_sum.reshape(CHIPS, 1, f_rows), 0.0)
        packed = jnp.concatenate(
            [
                vector.reshape(2 * CHIPS, -1)
                for vector in (norm_sums[0], norm_sums[1], qkv_full, grad_sum, in_full)
            ],
            axis=1,
        ).reshape(CHIPS, -1)
        order = [NEAR * (i % 2) + FAR * (i // 2 % 2) + i // 4 % 2 + Y * (i // 8) for i in range(CHIPS)]
        return packed[jnp.asarray(np.array(order, np.int32)) ^ me]

    def back_work(norm_more, norm_mine, xhat, inv_std, gain, g_own, *sums):
        input_grad, norm_sums = norm_back(
            clock.token, norm_mine, norm_more, xhat, inv_std, gain, g_own
        )
        return input_grad, small_rows(norm_sums, *sums)

    _, (input_grad, packed) = slot(
        moves(sum_qkv, "second") + [core_move("norm", norm_theirs)],
        chain=(
            "norm",
            back_work,
            (norm_mine, xhat, inv_std, gain, g_own, qkv_bias_sum, hidden_sum, grad_sum),
        ),
    )

    def fold(bit):
        return (box, "fold", packed[packed.shape[0] // 2 :], partial(cross, bit=bit))

    def half_sum():
        return packed[: packed.shape[0] // 2] + box["fold"]

    def two_folds(value, rows):
        half = rows[: rows.shape[0] // 2] + value
        give = half[half.shape[0] // 2 :]
        return half[: half.shape[0] // 2] + cross(give, X)

    in_rows = sum_in.result()
    in_keep, in_give = pick(in_rows[:, :units].reshape(2, d_rows, units))
    out_weight_grad = in_rows[:, units:].reshape(2, d_rows, D // 2)
    output, packed = slot(
        moves(sum_qkv, "near") + [fold(Y), core_move("in_rows", in_give)],
        finish_output,
        x_own,
        out_mine,
        box["out_side"],
        b_rows,
        chain=("fold", two_folds, (packed,)),
    )
    fc_in_weight_grad = slot(
        moves(sum_qkv, "far") + [fold(FAR)],
        lambda mine, other: paste(paste_in_kernel, clock.token, mine, other),
        in_keep,
        box["in_rows"],
    )
    packed = half_sum()
    qkv_keep, qkv_give = pick(sum_qkv.result().reshape(2, d_rows, -1))
    slot([core_move("qkv_rows", qkv_give), fold(NEAR)])
    sums_keep, sums_give = pick(half_sum().reshape(2, -1))
    sums = sums_keep + other_core(sums_give)
    parts = []
    first = 0
    for width in (d_rows, d_rows, 3 * d_rows, d_rows, f_rows):
        parts.append(sums[first : first + width])
        first += width
    return (
        output.reshape(local_seqs, tok_count, D),
        input_grad.reshape(local_seqs, tok_count, D),
        parts[0],
        parts[1],
        paste(paste_qkv_kernel, clock.token, qkv_keep, box["qkv_rows"]),
        parts[2],
        jnp.concatenate([out_weight_grad[0], out_weight_grad[1]], axis=1),
        parts[3],
        fc_in_weight_grad,
        parts[4],
        sum_fc.result(),
        parts[3],
    )


def solution(mesh):
    rows = P(("seq", "fsdp"))
    wide = P(("seq", "fsdp"), None)
    act = P("fsdp", "seq", None)
    placed = (act, P("fsdp", "seq"), act) + (rows, rows) + (wide, rows) * 4
    small = dict(mesh.shape) == {"seq": 4, "fsdp": 8}
    return jax.shard_map(
        local_fast if small else local_plain,
        mesh=mesh,
        in_specs=placed,
        out_specs=(act, act, rows, rows) + (wide, rows) * 4,
        check_vma=False,
    )
```
